32 devices in a mesh: dp: 2 (over x), wide: 4 (over z), narrow: 4 (over y, core).
Axes of the slice: x: 2, y: 2, z: 4, core: 2. Of those that a mesh axis runs over, the one named last changes fastest.
Arguments:
- tokens: bfloat16 [8192, 2048], P(('dp', 'wide'), 'narrow'), may hold values from -6 to 6
- continuation_lengths: int32 [2, 8], P('dp'), may hold values from 1 to 511, 2048 in all within a row
- attention_gain: float32 [2048], replicated, may hold values from 0.5 to 1.5
- query_weight: bfloat16 [2048, 2048], P('narrow', 'wide'), may hold values from -0.125 to 0.125
- key_weight: bfloat16 [2048, 1024], P('narrow', 'wide'), may hold values from -0.125 to 0.125
- value_weight: bfloat16 [2048, 1024], P('narrow', 'wide'), may hold values from -0.125 to 0.125
- head_gate: bfloat16 [2048, 16], P('narrow', 'wide'), may hold values from -0.125 to 0.125
- query_gain: float32 [128], replicated, may hold values from 0.5 to 1.5
- key_gain: float32 [128], replicated, may hold values from 0.5 to 1.5
- output_weight: bfloat16 [2048, 2048], P('wide', 'narrow'), may hold values from -2 to 2
- feedforward_gain: float32 [2048], replicated, may hold values from 0.5 to 1.5
- gate_weight: bfloat16 [2048, 6144], P('narrow', 'wide'), may hold values from -0.125 to 0.125
- up_weight: bfloat16 [2048, 6144], P('narrow', 'wide'), may hold values from -0.125 to 0.125
- down_weight: bfloat16 [6144, 2048], P('wide', 'narrow'), may hold values from -0.078125 to 0.078125
- cotangent: bfloat16 [8192, 2048], P(('dp', 'wide'), 'narrow'), may hold values from -6 to 6
Outputs:
- layer_output: bfloat16 [8192, 2048], P(('dp', 'wide'), 'narrow')
- tokens_gradient: float32 [8192, 2048], P(('dp', 'wide'), 'narrow')
- attention_gain_gradient: float32 [2048], replicated
- query_gradient: float32 [2048, 2048], P('narrow', 'wide')
- key_gradient: float32 [2048, 1024], P('narrow', 'wide')
- value_gradient: float32 [2048, 1024], P('narrow', 'wide')
- head_gate_gradient: float32 [2048, 16], P('narrow', 'wide')
- query_gain_gradient: float32 [128], replicated
- key_gain_gradient: float32 [128], replicated
- output_gradient: float32 [2048, 2048], P('wide', 'narrow')
- feedforward_gain_gradient: float32 [2048], replicated
- gate_gradient: float32 [2048, 6144], P('narrow', 'wide')
- up_gradient: float32 [2048, 6144], P('narrow', 'wide')
- down_gradient: float32 [6144, 2048], P('wide', 'narrow')
The draws below stay inside these ranges and needn't reach their ends.
Inputs may be any that keep to these rules, and one draw needn't show every extreme that they name: `continuation_lengths`: each group's 8 lengths sum to 2048, and one of them is exactly 511.
All inputs are finite; a program needn't handle non-finite values.
Results may differ from the reference program's by a relative error of at most 0.018.
Values may be sent and summed in bfloat16 or wider, within the bound.
A program may use at most 320 MiB of HBM per device.

```python
import math
import jax
import jax.numpy as jnp
import numpy as np
from jax import lax

D = 2048
HQ = 16
HK = 8
HD = 128
FF = 6144
PROMPT = 2048
CONT = 8
CLEN = 256
CMOST = 511
GROUP_TOK = 4096
GROUPS = 2
TOKENS = 8192
N_DP = 2


def shard_levels(own_key, extent, cuts, least, high):
    def one(dim, blocks):
        heights = jax.random.uniform(jax.random.fold_in(jax.random.fold_in(own_key, 6), dim), (blocks,), jnp.float32, least / len(cuts), high / len(cuts))
        return jnp.repeat(jnp.exp(heights), extent[dim] // blocks).reshape((-1,) + (1,) * (len(extent) - dim - 1))

    factor_of = one(*cuts[0])
    for cut in cuts[1:]:
        factor_of = factor_of * one(*cut)
    return factor_of


def length_profile(count, total, bound, skew):
    weights = [(1 << 20) // math.isqrt(standing ** skew) + 1 for standing in range(2, count + 1)]
    surplus, holding = total - bound - (count - 1), [1] * (count - 1)
    while surplus > 0:
        movable = [i for i in range(count - 1) if holding[i] < bound]
        mass, left = sum([weights[i] for i in movable]), surplus
        for i in movable:
            addition = min(bound - holding[i], max(1, left * weights[i] // mass), surplus)
            holding[i] = holding[i] + addition
            surplus = surplus - addition
    return np.array([bound] + holding)


def uneven(rng, count, total, reach, slope):
    if count == 2:
        one = jax.random.randint(rng, (), max(1, total - reach), min(reach, total - 1) + 1)
        return jnp.stack([one, total - one])
    sizes = jnp.asarray(length_profile(count, total, reach, slope), jnp.int32)
    couples = (count - 1) // 2
    donor, receiver = sizes[1:1 + 2 * couples:2], sizes[2:2 + 2 * couples:2]
    margin = jnp.minimum(donor - 1, reach - receiver)
    shifted = jax.random.randint(jax.random.fold_in(rng, 1), (couples,), 0, 1 << 20) % (margin + 1)
    sizes = sizes.at[1:1 + 2 * couples:2].set(donor - shifted).at[2:2 + 2 * couples:2].set(receiver + shifted)
    return sizes[jax.random.permutation(jax.random.fold_in(rng, 2), count)]


def noise(stream_key, shape, deviation, limit, cuts=(), kind=jnp.bfloat16):
    values = jax.random.normal(stream_key, shape, jnp.float32) * deviation
    if len(cuts) > 0:
        values = shard_levels(stream_key, shape, cuts, -0.22, 0.18) * values
    return jnp.clip(values, min=-limit, max=limit).astype(kind)


def setup_inputs(seed: int = 0) -> dict:
    seeds = jax.random.split(jax.random.key(seed), 16)
    return {
        "tokens": noise(seeds[0], (TOKENS, D), 1.0, 6.0, ((0, 8), (1, 4))),
        "continuation_lengths": jax.vmap(lambda own: uneven(own, CONT, CONT * CLEN, CMOST, 2))(jax.random.split(seeds[1], GROUPS)).reshape((GROUPS, CONT)).astype(jnp.int32),
        "attention_gain": jnp.clip(1.0 + 0.1 * jax.random.normal(seeds[2], (D,), jnp.float32), 0.5, 1.5),
        "query_weight": noise(seeds[3], (D, HQ * HD), D ** -0.5, 0.125, ((0, 4), (1, 4))),
        "key_weight": noise(seeds[4], (D, HK * HD), D ** -0.5, 0.125, ((0, 4), (1, 4))),
        "value_weight": noise(seeds[5], (D, HK * HD), D ** -0.5, 0.125, ((0, 4), (1, 4))),
        "head_gate": noise(seeds[6], (D, HQ), D ** -0.5, 0.125, ((0, 4), (1, 4))),
        "query_gain": jnp.clip(1.0 + 0.1 * jax.random.normal(seeds[7], (HD,), jnp.float32), 0.5, 1.5),
        "key_gain": jnp.clip(1.0 + 0.1 * jax.random.normal(seeds[8], (HD,), jnp.float32), 0.5, 1.5),
        "output_weight": noise(seeds[9], (HQ * HD, D), (max(HQ * HD // 256, 1)) ** -0.5, 2.0, ((0, 4), (1, 4))),
        "feedforward_gain": jnp.clip(1.0 + 0.1 * jax.random.normal(seeds[10], (D,), jnp.float32), 0.5, 1.5),
        "gate_weight": noise(seeds[11], (D, FF), D ** -0.5, 0.125, ((0, 4), (1, 4))),
        "up_weight": noise(seeds[12], (D, FF), D ** -0.5, 0.125, ((0, 4), (1, 4))),
        "down_weight": noise(seeds[13], (FF, D), FF ** -0.5, 0.078125, ((0, 4), (1, 4))),
        "cotangent": noise(seeds[14], (TOKENS, D), 1.0, 6.0, ((0, 8), (1, 4))),
    }


EPS = 1e-06
THETA = 1000000.0
HIGH = lax.Precision.HIGHEST

@jax.custom_vjp
def low(v):
    return lax.optimization_barrier(v.astype(jnp.bfloat16)).astype(jnp.float32)

@jax.custom_vjp
def low_back(v):
    return v

def low_keep(v):
    return (low(v), None)

def low_pass(kept, grad):
    return (grad,)

def back_keep(v):
    return (v, None)

def back_low(kept, grad):
    return (low(grad),)
low.defvjp(low_keep, low_pass)
low_back.defvjp(back_keep, back_low)

def matmul(left, right):
    return jnp.dot(left, right, precision=HIGH, preferred_element_type=jnp.float32)

def rms_norm(values, gain):
    return values * lax.rsqrt(lax.optimization_barrier(jnp.mean(values * values, axis=-1, keepdims=True)) + EPS) * gain

def head_norm(values, gain):
    return values * lax.rsqrt(lax.optimization_barrier(jnp.mean(values * values, axis=-1, keepdims=True)) + EPS) * gain

def layout(lengths):
    lengths = lengths.astype(jnp.int32)
    ends = jnp.cumsum(lengths).astype(jnp.int32)
    starts = ends - lengths
    index = jnp.arange(GROUP_TOK, dtype=jnp.int32)
    offset = index - PROMPT
    member = ((offset[:, None] >= starts[None, :]) & (offset[:, None] < ends[None, :])).astype(jnp.int32)
    numbers = jnp.arange(1, CONT + 1, dtype=jnp.int32)
    segment = lax.optimization_barrier(jnp.sum(member * numbers[None, :], axis=1)).astype(jnp.int32)
    position = (index - lax.optimization_barrier(jnp.sum(member * starts[None, :], axis=1))).astype(jnp.int32)
    return (index, segment, position)

def rope_tables(position):
    frequency = THETA ** (-2.0 * jnp.arange(HD // 2, dtype=jnp.float32) / HD)
    angle = position.astype(jnp.float32)[:, None] * frequency[None, :]
    return (jnp.cos(angle)[:, None, :], jnp.sin(angle)[:, None, :])

def rotate(values, cosine, sine):
    half = values.shape[-1] // 2
    first = values[..., :half]
    second = values[..., half:]
    return jnp.concatenate([first * cosine - second * sine, second * cosine + first * sine], axis=-1)

def attention(queries, keys, values, index, segment):
    repeat = HQ // HK
    block = 512 if GROUP_TOK % 512 == 0 else GROUP_TOK
    scale = HD ** (-0.5)

    def one_block(inputs):
        query_block, row_index, row_segment = inputs
        grouped = query_block.reshape(block, HK, repeat, HD)
        scores = low_back(scale * jnp.einsum('bkrd,tkd->krbt', grouped, keys, precision=HIGH))
        allowed = (index[None, :] <= row_index[:, None]) & ((segment[None, :] == 0) | (segment[None, :] == row_segment[:, None]))
        scores = jnp.where(allowed[None, None], scores, -1e+30)
        probs = low(jax.nn.softmax(scores, axis=-1))
        context = jnp.einsum('krbt,tkd->bkrd', probs, values, precision=HIGH)
        return context.reshape(block, HQ, HD)
    parts = lax.map(jax.checkpoint(one_block), (queries.reshape(GROUP_TOK // block, block, HQ, HD), index.reshape(GROUP_TOK // block, block), segment.reshape(GROUP_TOK // block, block)))
    return parts.reshape(GROUP_TOK, HQ, HD)

def layer(inputs, weights, index, segment, position):
    attention_gain, query_weight, key_weight, value_weight, head_gate, query_gain, key_gain, output_weight, feedforward_gain, gate_weight, up_weight, down_weight = weights
    normed = low(rms_norm(inputs, attention_gain))
    query_raw = low_back(matmul(normed, query_weight)).reshape(GROUP_TOK, HQ, HD)
    key_raw = low_back(matmul(normed, key_weight)).reshape(GROUP_TOK, HK, HD)
    value_rows = low(low_back(matmul(normed, value_weight))).reshape(GROUP_TOK, HK, HD)
    gate_logit = low_back(matmul(normed, head_gate))
    cosine, sine = rope_tables(position)
    queries = low(rotate(head_norm(query_raw, query_gain), cosine, sine))
    keys = low(rotate(head_norm(key_raw, key_gain), cosine, sine))
    context = low_back(attention(queries, keys, value_rows, index, segment))
    gated = low((context * jax.nn.sigmoid(gate_logit)[:, :, None]).reshape(GROUP_TOK, HQ * HD))
    middle = inputs + low_back(matmul(gated, output_weight))
    normed_two = low(rms_norm(middle, feedforward_gain))
    gate_pre = low_back(matmul(normed_two, gate_weight))
    up_pre = low_back(matmul(normed_two, up_weight))
    hidden = low(jax.nn.silu(gate_pre) * up_pre)
    return middle + low_back(matmul(hidden, down_weight))

def reference(tokens, continuation_lengths, attention_gain, query_weight, key_weight, value_weight, head_gate, query_gain, key_gain, output_weight, feedforward_gain, gate_weight, up_weight, down_weight, cotangent):
    params = (attention_gain.astype(jnp.float32), query_weight.astype(jnp.float32), key_weight.astype(jnp.float32), value_weight.astype(jnp.float32), head_gate.astype(jnp.float32), query_gain.astype(jnp.float32), key_gain.astype(jnp.float32), output_weight.astype(jnp.float32), feedforward_gain.astype(jnp.float32), gate_weight.astype(jnp.float32), up_weight.astype(jnp.float32), down_weight.astype(jnp.float32))
    token_groups = tokens.astype(jnp.float32).reshape(N_DP, GROUP_TOK, D)
    upstream_groups = cotangent.astype(jnp.float32).reshape(N_DP, GROUP_TOK, D)

    def one_group(totals, inputs):
        group_tokens, group_upstream, lengths = inputs
        index, segment, position = layout(lengths)

        def forward(values, *weights):
            return layer(values, weights, index, segment, position)
        result, pullback = jax.vjp(forward, group_tokens, *params)
        grads = pullback(group_upstream)
        totals = tuple((total + grad for total, grad in zip(totals, grads[1:])))
        return (totals, (result, grads[0]))
    zeros = tuple((jnp.zeros_like(param) for param in params))
    totals, (results, input_grads) = lax.scan(one_group, zeros, (token_groups, upstream_groups, continuation_lengths))
    return (results.reshape(TOKENS, D).astype(jnp.bfloat16), input_grads.reshape(TOKENS, D), totals[0], totals[1], totals[2], totals[3], totals[4], totals[5], totals[6], totals[7], totals[8], totals[9], totals[10], totals[11])
```

```python
import functools
import math

import jax
import jax.numpy as jnp
from jax import lax
from jax.experimental import pallas as pl
from jax.experimental.pallas import tpu as pltpu
from jax.sharding import PartitionSpec as P

PROMPT = 2048
EPS = 1e-06
THETA = 1000000.0
RELATIVE = (0, 2, 1, 3)
BF16 = jnp.bfloat16
F32 = jnp.float32
VMEM_LIMIT = 56 * 1024 * 1024


def dot_rows(left, right):
    return jnp.dot(left, right, preferred_element_type=F32)


def dot_trans(left, right):
    return lax.dot_general(left, right, (((1,), (1,)), ((), ())), preferred_element_type=F32)


def dot_inner(left, right):
    return lax.dot_general(left, right, (((0,), (0,)), ((), ())), preferred_element_type=F32)


def partner(values, distance, size):
    return lax.ppermute(values, "narrow", [(i, i ^ distance) for i in range(size)])


def gather_relative(values, size, axis):
    pair = jnp.concatenate([values, partner(values, 2, size)], axis=axis)
    return jnp.concatenate([pair, partner(pair, 1, size)], axis=axis)


def after(values, *others):
    return lax.optimization_barrier((values,) + others)[0]


def post_kernel(raw_ref, cos_ref, sin_ref, query_gain_ref, key_gain_ref, q_ref, kv_ref, *, heads, pairs, size, factor):
    cosine = cos_ref[...]
    sine = sin_ref[...]

    def turned(value, gain):
        inverse = lax.rsqrt(jnp.mean(value * value, axis=-1, keepdims=True) + EPS)
        normal = value * inverse * gain
        return normal * cosine + pltpu.roll(normal, size // 2, 1) * sine

    for h in range(heads):
        value = raw_ref[:, h * size : (h + 1) * size]
        q_ref[:, h * size : (h + 1) * size] = (turned(value, query_gain_ref[...]) * factor).astype(BF16)
    for h in range(pairs):
        at = (heads + h) * size
        kv_ref[:, h * size : (h + 1) * size] = turned(raw_ref[:, at : at + size], key_gain_ref[...]).astype(BF16)
        at = (heads + pairs + h) * size
        to = (pairs + h) * size
        kv_ref[:, to : to + size] = raw_ref[:, at : at + size].astype(BF16)


def post(raw, cosine, sine, query_gain, key_gain, heads, pairs, size, factor):
    rows, width = raw.shape
    step = 256
    return pl.pallas_call(
        functools.partial(post_kernel, heads=heads, pairs=pairs, size=size, factor=factor),
        grid=(rows // step,),
        in_specs=[
            pl.BlockSpec((step, width), lambda i: (i, 0)),
            pl.BlockSpec((step, size), lambda i: (i, 0)),
            pl.BlockSpec((step, size), lambda i: (i, 0)),
            pl.BlockSpec((1, size), lambda i: (0, 0)),
            pl.BlockSpec((1, size), lambda i: (0, 0)),
        ],
        out_specs=[
            pl.BlockSpec((step, heads * size), lambda i: (i, 0)),
            pl.BlockSpec((step, 2 * pairs * size), lambda i: (i, 0)),
        ],
        out_shape=[
            jax.ShapeDtypeStruct((rows, heads * size), BF16),
            jax.ShapeDtypeStruct((rows, 2 * pairs * size), BF16),
        ],
        cost_estimate=pl.CostEstimate(flops=rows * width * 20, bytes_accessed=rows * width * 8, transcendentals=0),
        name="post",
    )(raw, cosine, sine, query_gain[None], key_gain[None])


def back_kernel(
    dq_ref, dkv_ref, raw_ref, cos_ref, sin_ref, query_gain_ref, key_gain_ref, logit_ref, out_ref, gq_ref, gk_ref, *, heads, pairs, size, factor_q, factor_k
):
    cosine = cos_ref[...]
    sine = sin_ref[...]

    @pl.when(pl.program_id(0) == 0)
    def _():
        gq_ref[...] = jnp.zeros_like(gq_ref)
        gk_ref[...] = jnp.zeros_like(gk_ref)

    def back(up, value, gain, total_ref):
        up = up * cosine - pltpu.roll(up, size // 2, 1) * sine
        inverse = lax.rsqrt(jnp.mean(value * value, axis=-1, keepdims=True) + EPS)
        hat = value * inverse
        total_ref[...] += jnp.sum(up * hat, axis=0, keepdims=True)
        scaled = up * gain
        return inverse * (scaled - hat * jnp.mean(scaled * hat, axis=-1, keepdims=True))

    for h in range(heads):
        cols = slice(h * size, (h + 1) * size)
        out_ref[:, cols] = back(dq_ref[:, cols] * factor_q, raw_ref[:, cols], query_gain_ref[...], gq_ref).astype(BF16)
    for h in range(pairs):
        at = (heads + h) * size
        up = dkv_ref[:, h * size : (h + 1) * size].astype(F32) * factor_k
        out_ref[:, at : at + size] = back(up, raw_ref[:, at : at + size], key_gain_ref[...], gk_ref).astype(BF16)
        to = (pairs + h) * size
        at = (heads + pairs + h) * size
        out_ref[:, at : at + size] = dkv_ref[:, to : to + size].astype(BF16)
    at = (heads + 2 * pairs) * size
    out_ref[:, at : at + heads] = logit_ref[...].astype(BF16)


def project_back(dq, dkv, raw, cosine, sine, query_gain, key_gain, logit_grad, heads, pairs, size, factor_q, factor_k):
    rows, width = raw.shape
    step = 256
    row = lambda cols: pl.BlockSpec((step, cols), lambda i: (i, 0))
    one = pl.BlockSpec((1, size), lambda i: (0, 0))
    return pl.pallas_call(
        functools.partial(back_kernel, heads=heads, pairs=pairs, size=size, factor_q=factor_q, factor_k=factor_k),
        grid=(rows // step,),
        in_specs=[row(heads * size), row(2 * pairs * size), row(width), row(size), row(size), one, one, row(heads)],
        out_specs=[row(width), one, one],
        out_shape=[
            jax.ShapeDtypeStruct((rows, width), BF16),
            jax.ShapeDtypeStruct((1, size), F32),
            jax.ShapeDtypeStruct((1, size), F32),
        ],
        cost_estimate=pl.CostEstimate(flops=rows * width * 30, bytes_accessed=rows * width * 12, transcendentals=0),
        name="project_back",
    )(dq, dkv, raw, cosine, sine, query_gain[None], key_gain[None], logit_grad)


def forward_kernel(table_ref, q_ref, kv_ref, row_ref, start_ref, logit_ref, gated_ref, context_ref, inverse_ref, *, pairs, repeat, size, step):
    stripe = pl.program_id(0)
    wide_blocks = table_ref[stripe, 0]
    low = table_ref[stripe, 1]
    high = table_ref[stripe, 2]
    rows = row_ref[...]
    starts = start_ref[...]
    rows = jnp.concatenate([rows] * repeat, axis=0)
    starts = jnp.concatenate([starts] * repeat, axis=0)
    for k in range(pairs):
        heads = [k * repeat + r for r in range(repeat)]
        query = jnp.concatenate([q_ref[:, h * size : (h + 1) * size] for h in heads], axis=0)
        key_cols = slice(k * size, (k + 1) * size)
        value_cols = slice((pairs + k) * size, (pairs + k + 1) * size)

        def seen(i, total, length, mask):
            at = pl.ds(pl.multiple_of(i * length, length), length)
            scores = dot_trans(query, kv_ref[at, key_cols])
            weights = jnp.exp2(scores)
            if mask:
                keys = i * length + lax.broadcasted_iota(jnp.int32, scores.shape, 1)
                weights = jnp.where((keys <= rows) & (keys >= starts), weights, 0.0)
            values = kv_ref[at, value_cols]
            values = jnp.concatenate([values, jnp.ones_like(values)], axis=1)
            return total + dot_rows(weights.astype(BF16), values)

        total = jnp.zeros((query.shape[0], 2 * size), F32)
        total = lax.fori_loop(0, wide_blocks, lambda i, t: seen(i, t, 2 * step, False), total)
        total = lax.fori_loop(low, high + 1, lambda i, t: seen(i, t, step, True), total)
        inverse = 1.0 / total[:, size:]
        context = total[:, :size] * inverse
        for r, h in enumerate(heads):
            part = context[r * step : (r + 1) * step]
            cols = slice(h * size, (h + 1) * size)
            gate = jax.nn.sigmoid(logit_ref[:, h : h + 1])
            gated_ref[:, cols] = (part * gate).astype(BF16)
            context_ref[:, cols] = part
            inverse_ref[:, cols] = inverse[r * step : (r + 1) * step]


def attend(table, q, kv, rows, starts, logit, pairs, size):
    length, cols = q.shape
    heads = cols // size
    step = length // table.shape[0]
    block = lambda width: pl.BlockSpec((step, width), lambda i, t: (i, 0))
    return pl.pallas_call(
        functools.partial(forward_kernel, pairs=pairs, repeat=heads // pairs, size=size, step=step),
        grid_spec=pltpu.PrefetchScalarGridSpec(
            num_scalar_prefetch=1,
            grid=(length // step,),
            in_specs=[
                block(cols),
                pl.BlockSpec(kv.shape, lambda i, t: (0, 0), pipeline_mode=pl.Buffered(1)),
                block(1),
                block(1),
                block(heads),
            ],
            out_specs=[block(cols), block(cols), block(cols)],
        ),
        out_shape=[
            jax.ShapeDtypeStruct((length, cols), BF16),
            jax.ShapeDtypeStruct((length, cols), F32),
            jax.ShapeDtypeStruct((length, cols), F32),
        ],
        compiler_params=pltpu.CompilerParams(vmem_limit_bytes=VMEM_LIMIT),
        cost_estimate=pl.CostEstimate(flops=15 * 10**9, bytes_accessed=12 * 10**6, transcendentals=7 * 10**6),
        name="attend",
    )(table, q, kv, rows, starts, logit)


def backward_kernel(
    table_ref, q_ref, kv_ref, row_ref, start_ref, logit_ref, context_ref, inverse_ref, grad_ref,
    dq_ref, dkv_ref, dlogit_ref, sums_ref, *, pairs, repeat, size, step,
):
    stripe = pl.program_id(0)
    wide_blocks = table_ref[stripe, 0]
    low = table_ref[stripe, 1]
    high = table_ref[stripe, 2]

    @pl.when(stripe == 0)
    def _():
        sums_ref[...] = jnp.zeros_like(sums_ref)

    rows = jnp.concatenate([row_ref[0]] * repeat, axis=1)
    starts = jnp.concatenate([start_ref[0]] * repeat, axis=1)
    for k in range(pairs):
        heads = [k * repeat + r for r in range(repeat)]
        query = jnp.concatenate([q_ref[:, h * size : (h + 1) * size] for h in heads], axis=0)
        grads, inners = [], []
        for h in heads:
            cols = slice(h * size, (h + 1) * size)
            up = grad_ref[:, cols]
            gate = jax.nn.sigmoid(logit_ref[:, h : h + 1])
            product = jnp.sum(up * context_ref[:, cols], axis=1, keepdims=True)
            dlogit_ref[:, h : h + 1] = product * gate * (1.0 - gate)
            inverse = inverse_ref[:, cols]
            grads.append((up * gate * inverse).astype(BF16))
            inners.append(product * gate * inverse)
        grad = jnp.concatenate(grads, axis=0)
        inner = jnp.transpose(jnp.concatenate(inners, axis=0))[0:1]
        key_cols = slice(k * size, (k + 1) * size)
        value_cols = slice((pairs + k) * size, (pairs + k + 1) * size)

        def seen(i, total, length, mask):
            at = pl.ds(pl.multiple_of(i * length, length), length)
            keys_block = kv_ref[at, key_cols]
            weights = jnp.exp2(dot_trans(keys_block, query))
            if mask:
                keys = i * length + lax.broadcasted_iota(jnp.int32, weights.shape, 0)
                weights = jnp.where((keys <= rows) & (keys >= starts), weights, 0.0)
            changes = dot_trans(kv_ref[at, value_cols], grad)
            changes = (weights * (changes - inner)).astype(BF16)
            sums_ref[at, value_cols] += dot_rows(weights.astype(BF16), grad)
            sums_ref[at, key_cols] += dot_rows(changes, query)
            return total + dot_inner(changes, keys_block)

        total = jnp.zeros((query.shape[0], size), F32)
        total = lax.fori_loop(0, wide_blocks, lambda i, t: seen(i, t, 2 * step, False), total)
        total = lax.fori_loop(low, high + 1, lambda i, t: seen(i, t, step, True), total)
        for r, h in enumerate(heads):
            dq_ref[:, h * size : (h + 1) * size] = total[r * step : (r + 1) * step]

    @pl.when(stripe == pl.num_programs(0) - 1)
    def _():
        dkv_ref[...] = sums_ref[...].astype(BF16)


def attend_back(table, q, kv, rows, starts, logit, context, inverse, grad, pairs, size):
    length, cols = q.shape
    heads = cols // size
    step = length // table.shape[0]
    block = lambda width: pl.BlockSpec((step, width), lambda i, t: (i, 0))
    whole = pl.BlockSpec(kv.shape, lambda i, t: (0, 0), pipeline_mode=pl.Buffered(1))
    lane = pl.BlockSpec((1, 1, step), lambda i, t: (i, 0, 0))
    return pl.pallas_call(
        functools.partial(backward_kernel, pairs=pairs, repeat=heads // pairs, size=size, step=step),
        grid_spec=pltpu.PrefetchScalarGridSpec(
            num_scalar_prefetch=1,
            grid=(length // step,),
            in_specs=[block(cols), whole, lane, lane, block(heads), block(cols), block(cols), block(cols)],
            out_specs=[block(cols), whole, block(heads)],
            scratch_shapes=[pltpu.VMEM(kv.shape, F32)],
        ),
        out_shape=[
            jax.ShapeDtypeStruct((length, cols), F32),
            jax.ShapeDtypeStruct(kv.shape, BF16),
            jax.ShapeDtypeStruct((length, heads), F32),
        ],
        compiler_params=pltpu.CompilerParams(vmem_limit_bytes=VMEM_LIMIT),
        cost_estimate=pl.CostEstimate(flops=38 * 10**9, bytes_accessed=20 * 10**6, transcendentals=7 * 10**6),
        name="attend_back",
    )(table, q, kv, rows.reshape(-1, 1, step), starts.reshape(-1, 1, step), logit, context, inverse, grad)


def layout(lengths, group_rows):
    ends = jnp.cumsum(lengths)
    begins = ends - lengths
    index = jnp.arange(group_rows, dtype=jnp.int32)
    offset = index - PROMPT
    member = ((offset[:, None] >= begins[None, :]) & (offset[:, None] < ends[None, :])).astype(jnp.int32)
    shift = jnp.sum(member * begins[None, :], axis=1)
    start = jnp.where(offset >= 0, PROMPT + shift, 0)
    return index, start, index - shift


def make(sizes):
    n_dp, n_wide, n_narrow = sizes["dp"], sizes["wide"], sizes["narrow"]

    def gather_rows(values):
        return lax.all_gather(values, "wide", axis=0, tiled=True)

    def scatter_rows(values):
        return lax.psum_scatter(values.astype(BF16), "wide", scatter_dimension=0, tiled=True).astype(F32)

    def reduce_weight(first, second, axis):
        half = first.shape[axis] // 2
        come = partner(second.astype(BF16), 1, n_narrow)
        total = first + come.astype(F32)
        mine = lax.slice_in_dim(total, 0, half, axis=axis)
        theirs = lax.slice_in_dim(total, half, 2 * half, axis=axis)
        come = partner(theirs.astype(BF16), 2, n_narrow)
        total = (mine + come.astype(F32)).astype(BF16)
        if n_dp == 2:
            come = lax.ppermute(total, "dp", [(0, 1), (1, 0)])
            return total.astype(F32) + come.astype(F32)
        return lax.psum(total, "dp").astype(F32)

    def on_device(
        tokens, continuation_lengths, attention_gain, query_weight, key_weight, value_weight, head_gate, query_gain, key_gain,
        output_weight, feedforward_gain, gate_weight, up_weight, down_weight, cotangent,
    ):
        rows_wide, width_local = tokens.shape
        width = attention_gain.shape[0]
        size = query_gain.shape[0]
        heads = head_gate.shape[1]
        pairs = key_weight.shape[1] // size
        hidden_local = gate_weight.shape[1]
        group_rows = rows_wide * n_wide
        rows_local = rows_wide // n_narrow
        narrow = lax.axis_index("narrow")
        query_cols = heads * size
        key_cols = pairs * size
        scale = size ** (-0.5)
        factor = scale * math.log2(math.e)

        def to_local(values):
            send = [lax.dynamic_slice_in_dim(values, (narrow ^ r) * rows_local, rows_local) for r in RELATIVE]
            parts = [send[0]] + [partner(s, r, n_narrow) for s, r in zip(send[1:], RELATIVE[1:])]
            return jnp.concatenate(parts, axis=1)

        def from_local(values):
            out = jnp.zeros((rows_wide, width_local), values.dtype)
            for i, r in enumerate(RELATIVE):
                part = values[:, i * width_local : (i + 1) * width_local]
                if r:
                    part = partner(part, r, n_narrow)
                out = lax.dynamic_update_slice_in_dim(out, part, (narrow ^ r) * rows_local, 0)
            return out

        def relative_vector(vector):
            return jnp.concatenate(
                [lax.dynamic_slice_in_dim(vector, (narrow ^ r) * width_local, width_local) for r in RELATIVE]
            )

        def absolute_vector(vector):
            out = jnp.zeros((width,), vector.dtype)
            for i, r in enumerate(RELATIVE):
                part = vector[i * width_local : (i + 1) * width_local]
                out = lax.dynamic_update_slice_in_dim(out, part, (narrow ^ r) * width_local, 0)
            return out

        def norm(values, gain):
            inverse = lax.rsqrt(jnp.mean(values * values, axis=1, keepdims=True) + EPS)
            hat = values * inverse
            return inverse, hat, (hat * gain).astype(BF16)

        def norm_back(grad, hat, inverse, gain):
            scaled = grad * gain
            inner = jnp.mean(scaled * hat, axis=1, keepdims=True)
            return jnp.sum(grad * hat, axis=0), inverse * (scaled - hat * inner)

        inputs = to_local(tokens)
        joined = jnp.concatenate([query_weight, key_weight, value_weight, head_gate], axis=1)
        joined_weight = gather_relative(joined, n_narrow, 0)
        upstream = to_local(after(cotangent, joined_weight))
        out_weight = gather_relative(after(output_weight, joined_weight), n_narrow, 1)
        gate_up = jnp.concatenate([gate_weight, up_weight], axis=1)
        gate_up_weight = gather_relative(after(gate_up, out_weight), n_narrow, 0)
        down = gather_relative(after(down_weight, gate_up_weight), n_narrow, 1)

        index, start, position = layout(continuation_lengths[0], group_rows)

        def mine(vector):
            return lax.dynamic_slice_in_dim(
                vector.reshape(n_wide, n_narrow, rows_local), narrow, 1, axis=1
            ).reshape(rows_wide)

        my_index, my_start, my_position = mine(index), mine(start), mine(position)
        frequency = THETA ** (-2.0 * jnp.arange(size // 2, dtype=F32) / size)
        angle = my_position.astype(F32)[:, None] * frequency[None, :]
        cosine, sine = jnp.cos(angle), jnp.sin(angle)
        cosine = jnp.concatenate([cosine, cosine], axis=1)
        sine = jnp.concatenate([-sine, sine], axis=1)
        block = my_index[::rows_local] // rows_local
        first = my_start[::rows_local] // rows_local
        prompt_blocks = PROMPT // rows_local
        in_prompt = block < prompt_blocks
        table = jnp.stack(
            [
                jnp.where(in_prompt, block // 2, prompt_blocks // 2),
                jnp.where(in_prompt, block // 2 * 2, first),
                block,
            ],
            axis=1,
        ).astype(jnp.int32)

        gain_one, gain_two = relative_vector(attention_gain), relative_vector(feedforward_gain)
        inputs = inputs.astype(F32)
        inverse_one, hat_one, normed = norm(inputs, gain_one)
        normed_all = gather_rows(normed)
        upstream_all = gather_rows(after(upstream, normed_all))
        raw = dot_rows(normed_all, joined_weight)
        q, kv = post(raw, cosine, sine, query_gain, key_gain, heads, pairs, size, factor)
        logit = raw[:, query_cols + 2 * key_cols :]
        kv_parts = gather_relative(kv[None], n_narrow, 0)
        kv_all = jnp.zeros((n_wide, n_narrow, rows_local, 2 * key_cols), BF16)
        for i, r in enumerate(RELATIVE):
            kv_all = lax.dynamic_update_slice_in_dim(
                kv_all, kv_parts[i].reshape(n_wide, 1, rows_local, 2 * key_cols), narrow ^ r, 1
            )
        kv_all = kv_all.reshape(group_rows, 2 * key_cols)
        gated, context, inverse_total = attend(
            table, q, kv_all, my_index[:, None], my_start[:, None], logit, pairs, size
        )
        middle = inputs + scatter_rows(dot_rows(gated, out_weight))
        inverse_two, hat_two, normed_two = norm(middle, gain_two)
        normed_two_all = gather_rows(normed_two)
        both = dot_rows(normed_two_all, gate_up_weight)
        gate_pre, up_pre = both[:, :hidden_local], both[:, hidden_local:]
        gate_sigmoid = jax.nn.sigmoid(gate_pre)
        silu = gate_pre * gate_sigmoid
        hidden = (silu * up_pre).astype(BF16)
        hidden_grad = dot_trans(upstream_all, down)
        gate_grad = hidden_grad * up_pre * gate_sigmoid * (1.0 + gate_pre * (1.0 - gate_sigmoid))
        up_grad = hidden_grad * silu
        gate_up_low = jnp.concatenate([gate_grad, up_grad], axis=1).astype(BF16)
        normed_two_grad = scatter_rows(dot_trans(gate_up_low, gate_up_weight))
        gain_two_term, change = norm_back(normed_two_grad, hat_two, inverse_two, gain_two)
        upstream_rows = upstream.astype(F32)
        middle_grad = upstream_rows + change
        middle_low = middle_grad.astype(BF16)
        middle_all = gather_rows(middle_low)
        mlp_term = scatter_rows(after(dot_rows(hidden, down).astype(BF16), middle_all))
        layer_output = from_local((middle + mlp_term).astype(BF16))
        gated_grad = dot_trans(middle_all, out_weight)
        dq, dkv, logit_grad = attend_back(
            table, q, kv_all, my_index, my_start, logit, context, inverse_total, gated_grad, pairs, size
        )
        half = width // 2
        down_gradient = reduce_weight(
            dot_inner(hidden, upstream_all[:, :half]), dot_inner(hidden, upstream_all[:, half:]), 1
        )
        gate_up_gradient = reduce_weight(
            dot_inner(normed_two_all[:, :half], gate_up_low), dot_inner(normed_two_all[:, half:], gate_up_low), 0
        )
        output_gradient = reduce_weight(
            dot_inner(gated, middle_all[:, :half]), dot_inner(gated, middle_all[:, half:]), 1
        )
        dkv = dkv.reshape(n_wide, n_narrow, rows_local, 2 * key_cols)
        pick = lambda r: lax.dynamic_slice_in_dim(dkv, narrow ^ r, 1, axis=1).reshape(rows_wide, 2 * key_cols)
        come = partner(jnp.concatenate([pick(1), pick(3)], axis=0), 1, n_narrow).astype(F32)
        theirs = (pick(2).astype(F32) + come[rows_wide:]).astype(BF16)
        dkv_mine = pick(0).astype(F32) + come[:rows_wide] + partner(theirs, 2, n_narrow).astype(F32)
        low, query_gain_term, key_gain_term = project_back(
            dq, dkv_mine, raw, cosine, sine, query_gain, key_gain, logit_grad, heads, pairs, size, scale, math.log(2.0)
        )
        normed_grad = scatter_rows(dot_trans(low, joined_weight))
        joined_gradient = reduce_weight(
            dot_inner(normed_all[:, :half], low), dot_inner(normed_all[:, half:], low), 0
        )
        gain_one_term, change = norm_back(normed_grad, hat_one, inverse_one, gain_one)
        tokens_gradient = from_local((middle_grad + change).astype(BF16)).astype(F32)
        gains = lax.psum(
            (absolute_vector(gain_one_term), absolute_vector(gain_two_term), query_gain_term[0], key_gain_term[0]),
            ("dp", "wide", "narrow"),
        )
        return (
            layer_output,
            tokens_gradient,
            gains[0],
            joined_gradient[:, :query_cols],
            joined_gradient[:, query_cols : query_cols + key_cols],
            joined_gradient[:, query_cols + key_cols : query_cols + 2 * key_cols],
            joined_gradient[:, query_cols + 2 * key_cols :],
            gains[2],
            gains[3],
            output_gradient,
            gains[1],
            gate_up_gradient[:, :hidden_local],
            gate_up_gradient[:, hidden_local:],
            down_gradient,
        )

    return on_device


def solution(mesh):
    rows, up, down = P(("dp", "wide"), "narrow"), P("narrow", "wide"), P("wide", "narrow")
    return jax.shard_map(
        make(dict(mesh.shape)),
        mesh=mesh,
        in_specs=(rows, P("dp", None), P(), up, up, up, up, P(), P(), down, P(), up, up, down, rows),
        out_specs=(rows, rows, P(), up, up, up, up, P(), P(), down, P(), up, up, down),
        check_vma=False,
    )
```

```python
import functools
import math

import jax
import jax.numpy as jnp
from jax import lax
from jax.experimental import pallas as pl
from jax.experimental.pallas import tpu as pltpu
from jax.sharding import PartitionSpec as P

PROMPT = 2048
EPS = 1e-06
THETA = 1000000.0
RELATIVE = (0, 2, 1, 3)
BF16 = jnp.bfloat16
F32 = jnp.float32
VMEM_LIMIT = 56 * 1024 * 1024
LANES = 128


def dot_rows(left, right):
    return jnp.dot(left, right, preferred_element_type=F32)


def dot_trans(left, right):
    return lax.dot_general(left, right, (((1,), (1,)), ((), ())), preferred_element_type=F32)


def dot_inner(left, right):
    return lax.dot_general(left, right, (((0,), (0,)), ((), ())), preferred_element_type=F32)


def exchange(values, axis, distance, size):
    return lax.ppermute(values, axis, [(i, i ^ distance) for i in range(size)])


def join(parts, axis=0):
    return jnp.concatenate(parts, axis=axis)


def cut(values, at, length, axis):
    return lax.dynamic_slice_in_dim(values, at, length, axis=axis)


def turn_pairs(values):
    step = values.shape[1] // 4
    return join([values[:, i * step : (i + 1) * step] for i in (1, 0, 3, 2)], 1)


def after(values, *others):
    return lax.optimization_barrier((values,) + others)[0]


def columns(heads, pairs, size):
    query, pair = heads // 2, pairs // 2
    block = (query + 2 * pair) * size
    of = lambda i, count, before: (i // count) * block + (before + i % count) * size
    return (
        [of(h, query, 0) for h in range(heads)],
        [of(p, pair, query) for p in range(pairs)],
        [of(p, pair, query + pair) for p in range(pairs)],
        2 * block,
    )


def post_kernel(raw_ref, cos_ref, sin_ref, query_gain_ref, key_gain_ref, q_ref, kv_ref, *, heads, pairs, size, factor):
    cosine = cos_ref[...]
    sine = sin_ref[...]
    query_at, key_at, value_at, _ = columns(heads, pairs, size)

    def turned(value, gain):
        inverse = lax.rsqrt(jnp.mean(value * value, axis=-1, keepdims=True) + EPS)
        normal = value * inverse * gain
        return normal * cosine + pltpu.roll(normal, size // 2, 1) * sine

    for h, at in enumerate(query_at):
        value = raw_ref[:, at : at + size]
        q_ref[:, h * size : (h + 1) * size] = (turned(value, query_gain_ref[...]) * factor).astype(BF16)
    for p, at in enumerate(key_at):
        kv_ref[:, p * size : (p + 1) * size] = turned(raw_ref[:, at : at + size], key_gain_ref[...]).astype(BF16)
    for p, at in enumerate(value_at):
        to = (pairs + p) * size
        kv_ref[:, to : to + size] = raw_ref[:, at : at + size].astype(BF16)


def post(raw, cosine, sine, query_gain, key_gain, heads, pairs, size, factor):
    rows, width = raw.shape
    step = 256
    return pl.pallas_call(
        functools.partial(post_kernel, heads=heads, pairs=pairs, size=size, factor=factor),
        grid=(rows // step,),
        in_specs=[
            pl.BlockSpec((step, width), lambda i: (i, 0)),
            pl.BlockSpec((step, size), lambda i: (i, 0)),
            pl.BlockSpec((step, size), lambda i: (i, 0)),
            pl.BlockSpec((1, size), lambda i: (0, 0)),
            pl.BlockSpec((1, size), lambda i: (0, 0)),
        ],
        out_specs=[
            pl.BlockSpec((step, heads * size), lambda i: (i, 0)),
            pl.BlockSpec((step, 2 * pairs * size), lambda i: (i, 0)),
        ],
        out_shape=[
            jax.ShapeDtypeStruct((rows, heads * size), BF16),
            jax.ShapeDtypeStruct((rows, 2 * pairs * size), BF16),
        ],
        cost_estimate=pl.CostEstimate(flops=rows * width * 20, bytes_accessed=rows * width * 8, transcendentals=0),
        name="post",
    )(raw, cosine, sine, query_gain[None], key_gain[None])


def back_kernel(
    dq_ref, dkv_ref, raw_ref, cos_ref, sin_ref, query_gain_ref, key_gain_ref, logit_ref, out_ref, gq_ref, gk_ref, *, heads, pairs, size, factor_q, factor_k
):
    cosine = cos_ref[...]
    sine = sin_ref[...]
    query_at, key_at, value_at, logit_at = columns(heads, pairs, size)

    @pl.when(pl.program_id(0) == 0)
    def _():
        gq_ref[...] = jnp.zeros_like(gq_ref)
        gk_ref[...] = jnp.zeros_like(gk_ref)

    def back(up, value, gain, total_ref):
        up = up * cosine - pltpu.roll(up, size // 2, 1) * sine
        inverse = lax.rsqrt(jnp.mean(value * value, axis=-1, keepdims=True) + EPS)
        hat = value * inverse
        total_ref[...] += jnp.sum(up * hat, axis=0, keepdims=True)
        scaled = up * gain
        return inverse * (scaled - hat * jnp.mean(scaled * hat, axis=-1, keepdims=True))

    for h, at in enumerate(query_at):
        up = dq_ref[:, h * size : (h + 1) * size] * factor_q
        out_ref[:, at : at + size] = back(up, raw_ref[:, at : at + size], query_gain_ref[...], gq_ref).astype(BF16)
    for p, at in enumerate(key_at):
        up = dkv_ref[:, p * size : (p + 1) * size].astype(F32) * factor_k
        out_ref[:, at : at + size] = back(up, raw_ref[:, at : at + size], key_gain_ref[...], gk_ref).astype(BF16)
    for p, at in enumerate(value_at):
        to = (pairs + p) * size
        out_ref[:, at : at + size] = dkv_ref[:, to : to + size].astype(BF16)
    out_ref[:, logit_at:] = logit_ref[...].astype(BF16)


def project_back(dq, dkv, raw, cosine, sine, query_gain, key_gain, logit_grad, heads, pairs, size, factor_q, factor_k):
    rows, width = raw.shape
    step = 256
    row = lambda cols: pl.BlockSpec((step, cols), lambda i: (i, 0))
    one = pl.BlockSpec((1, size), lambda i: (0, 0))
    return pl.pallas_call(
        functools.partial(back_kernel, heads=heads, pairs=pairs, size=size, factor_q=factor_q, factor_k=factor_k),
        grid=(rows // step,),
        in_specs=[row(heads * size), row(2 * pairs * size), row(width), row(size), row(size), one, one, row(LANES)],
        out_specs=[row(width), one, one],
        out_shape=[
            jax.ShapeDtypeStruct((rows, width), BF16),
            jax.ShapeDtypeStruct((1, size), F32),
            jax.ShapeDtypeStruct((1, size), F32),
        ],
        cost_estimate=pl.CostEstimate(flops=rows * width * 30, bytes_accessed=rows * width * 12, transcendentals=0),
        name="project_back",
    )(dq, dkv, raw, cosine, sine, query_gain[None], key_gain[None], logit_grad)


def places(table_ref, stripe, step, length):
    turn = table_ref[stripe, 3]
    core = table_ref[stripe, 4]
    half = length // 2
    blocks = half // step

    def pair(i):
        at = jnp.bitwise_xor(i, turn) * step
        return pl.ds(pl.multiple_of(at, step), step), pl.ds(pl.multiple_of(at + half // 2, step), step)

    def single(b):
        part = b // blocks
        inner = b - part * blocks
        at = part * half + jnp.bitwise_xor(inner % 2, core) * (half // 2) + jnp.bitwise_xor(inner // 2, turn) * step
        return (pl.ds(pl.multiple_of(at, step), step),)

    return pair, single


def forward_kernel(table_ref, q_ref, kv_ref, row_ref, start_ref, logit_ref, gated_ref, context_ref, inverse_ref, *, pairs, repeat, size, step):
    stripe = pl.program_id(0)
    wide_blocks = table_ref[stripe, 0]
    low = table_ref[stripe, 1]
    high = table_ref[stripe, 2]
    pair, single = places(table_ref, stripe, step, kv_ref.shape[0])
    rows = row_ref[...]
    starts = start_ref[...]
    rows = jnp.concatenate([rows] * repeat, axis=0)
    starts = jnp.concatenate([starts] * repeat, axis=0)
    for k in range(pairs):
        heads = [k * repeat + r for r in range(repeat)]
        query = jnp.concatenate([q_ref[:, h * size : (h + 1) * size] for h in heads], axis=0)
        key_cols = slice(k * size, (k + 1) * size)
        value_cols = slice((pairs + k) * size, (pairs + k + 1) * size)

        def seen(total, where, first):
            keys = join([kv_ref[at, key_cols] for at in where])
            weights = jnp.exp2(dot_trans(query, keys))
            if first is not None:
                index = first + lax.broadcasted_iota(jnp.int32, weights.shape, 1)
                weights = jnp.where((index <= rows) & (index >= starts), weights, 0.0)
            values = join([kv_ref[at, value_cols] for at in where])
            values = jnp.concatenate([values, jnp.ones_like(values)], axis=1)
            return total + dot_rows(weights.astype(BF16), values)

        total = jnp.zeros((query.shape[0], 2 * size), F32)
        total = lax.fori_loop(0, wide_blocks, lambda i, t: seen(t, pair(i), None), total)
        total = lax.fori_loop(low, high + 1, lambda i, t: seen(t, single(i), i * step), total)
        inverse = 1.0 / total[:, size:]
        context = total[:, :size] * inverse
        for r, h in enumerate(heads):
            part = context[r * step : (r + 1) * step]
            cols = slice(h * size, (h + 1) * size)
            gate = jax.nn.sigmoid(logit_ref[:, h : h + 1])
            gated_ref[:, cols] = (part * gate).astype(BF16)
            context_ref[:, cols] = part
            inverse_ref[:, cols] = inverse[r * step : (r + 1) * step]


def attend(table, q, kv, rows, starts, raw, pairs, size):
    length, cols = q.shape
    heads = cols // size
    step = length // table.shape[0]
    block = lambda width: pl.BlockSpec((step, width), lambda i, t: (i, 0))
    logit_block = raw.shape[1] // LANES - 1
    return pl.pallas_call(
        functools.partial(forward_kernel, pairs=pairs, repeat=heads // pairs, size=size, step=step),
        grid_spec=pltpu.PrefetchScalarGridSpec(
            num_scalar_prefetch=1,
            grid=(length // step,),
            in_specs=[
                block(cols),
                pl.BlockSpec(kv.shape, lambda i, t: (0, 0), pipeline_mode=pl.Buffered(1)),
                block(1),
                block(1),
                pl.BlockSpec((step, LANES), lambda i, t: (i, logit_block)),
            ],
            out_specs=[block(cols), block(cols), block(cols)],
        ),
        out_shape=[
            jax.ShapeDtypeStruct((length, cols), BF16),
            jax.ShapeDtypeStruct((length, cols), F32),
            jax.ShapeDtypeStruct((length, cols), F32),
        ],
        compiler_params=pltpu.CompilerParams(vmem_limit_bytes=VMEM_LIMIT),
        cost_estimate=pl.CostEstimate(flops=20 * 10**9, bytes_accessed=12 * 10**6, transcendentals=7 * 10**6),
        name="attend",
    )(table, q, kv, rows, starts, raw)


def backward_kernel(
    table_ref, q_ref, kv_ref, row_ref, start_ref, logit_ref, context_ref, inverse_ref, grad_ref,
    dq_ref, dkv_ref, dlogit_ref, sums_ref, *, pairs, repeat, size, step,
):
    stripe = pl.program_id(0)
    wide_blocks = table_ref[stripe, 0]
    low = table_ref[stripe, 1]
    high = table_ref[stripe, 2]
    pair, single = places(table_ref, stripe, step, kv_ref.shape[0])

    @pl.when(stripe == 0)
    def _():
        sums_ref[...] = jnp.zeros_like(sums_ref)

    dlogit_ref[...] = jnp.zeros_like(dlogit_ref)
    rows = jnp.concatenate([row_ref[0]] * repeat, axis=1)
    starts = jnp.concatenate([start_ref[0]] * repeat, axis=1)
    for k in range(pairs):
        heads = [k * repeat + r for r in range(repeat)]
        query = jnp.concatenate([q_ref[:, h * size : (h + 1) * size] for h in heads], axis=0)
        grads, inners = [], []
        for h in heads:
            cols = slice(h * size, (h + 1) * size)
            up = grad_ref[:, cols]
            gate = jax.nn.sigmoid(logit_ref[:, h : h + 1])
            product = jnp.sum(up * context_ref[:, cols], axis=1, keepdims=True)
            dlogit_ref[:, h : h + 1] = product * gate * (1.0 - gate)
            inverse = inverse_ref[:, cols]
            grads.append((up * gate * inverse).astype(BF16))
            inners.append(product * gate * inverse)
        grad = jnp.concatenate(grads, axis=0)
        inner = jnp.transpose(jnp.concatenate(inners, axis=0))[0:1]
        key_cols = slice(k * size, (k + 1) * size)
        value_cols = slice((pairs + k) * size, (pairs + k + 1) * size)

        def seen(total, where, first):
            keys = join([kv_ref[at, key_cols] for at in where])
            weights = jnp.exp2(dot_trans(keys, query))
            if first is not None:
                index = first + lax.broadcasted_iota(jnp.int32, weights.shape, 0)
                weights = jnp.where((index <= rows) & (index >= starts), weights, 0.0)
            changes = dot_trans(join([kv_ref[at, value_cols] for at in where]), grad)
            changes = (weights * (changes - inner)).astype(BF16)
            value_sums = dot_rows(weights.astype(BF16), grad)
            key_sums = dot_rows(changes, query)
            for i, at in enumerate(where):
                sums_ref[at, value_cols] += value_sums[i * step : (i + 1) * step]
                sums_ref[at, key_cols] += key_sums[i * step : (i + 1) * step]
            return total + dot_inner(changes, keys)

        total = jnp.zeros((query.shape[0], size), F32)
        total = lax.fori_loop(0, wide_blocks, lambda i, t: seen(t, pair(i), None), total)
        total = lax.fori_loop(low, high + 1, lambda i, t: seen(t, single(i), i * step), total)
        for r, h in enumerate(heads):
            dq_ref[:, h * size : (h + 1) * size] = total[r * step : (r + 1) * step]

    @pl.when(stripe == pl.num_programs(0) - 1)
    def _():
        dkv_ref[...] = sums_ref[...].astype(BF16)


def attend_back(table, q, kv, rows, starts, raw, context, inverse, grad, pairs, size):
    length, cols = q.shape
    heads = cols // size
    step = length // table.shape[0]
    block = lambda width: pl.BlockSpec((step, width), lambda i, t: (i, 0))
    whole = pl.BlockSpec(kv.shape, lambda i, t: (0, 0), pipeline_mode=pl.Buffered(1))
    lane = pl.BlockSpec((1, 1, step), lambda i, t: (i, 0, 0))
    logit_block = raw.shape[1] // LANES - 1
    logit = pl.BlockSpec((step, LANES), lambda i, t: (i, logit_block))
    return pl.pallas_call(
        functools.partial(backward_kernel, pairs=pairs, repeat=heads // pairs, size=size, step=step),
        grid_spec=pltpu.PrefetchScalarGridSpec(
            num_scalar_prefetch=1,
            grid=(length // step,),
            in_specs=[block(cols), whole, lane, lane, logit, block(cols), block(cols), block(cols)],
            out_specs=[block(cols), whole, block(LANES)],
            scratch_shapes=[pltpu.VMEM(kv.shape, F32)],
        ),
        out_shape=[
            jax.ShapeDtypeStruct((length, cols), F32),
            jax.ShapeDtypeStruct(kv.shape, BF16),
            jax.ShapeDtypeStruct((length, LANES), F32),
        ],
        compiler_params=pltpu.CompilerParams(vmem_limit_bytes=VMEM_LIMIT),
        cost_estimate=pl.CostEstimate(flops=50 * 10**9, bytes_accessed=20 * 10**6, transcendentals=7 * 10**6),
        name="attend_back",
    )(table, q, kv, rows.reshape(-1, 1, step), starts.reshape(-1, 1, step), raw, context, inverse, grad)


def layout(lengths, group_rows):
    ends = jnp.cumsum(lengths)
    begins = ends - lengths
    index = jnp.arange(group_rows, dtype=jnp.int32)
    offset = index - PROMPT
    member = ((offset[:, None] >= begins[None, :]) & (offset[:, None] < ends[None, :])).astype(jnp.int32)
    shift = jnp.sum(member * begins[None, :], axis=1)
    start = jnp.where(offset >= 0, PROMPT + shift, 0)
    return index, start, index - shift


def make(sizes):
    n_dp, n_wide, n_narrow = sizes["dp"], sizes["wide"], sizes["narrow"]

    def over_y(values):
        return exchange(values, "narrow", 2, n_narrow)

    def over_core(values):
        return exchange(values, "narrow", 1, n_narrow)

    def over_z(values):
        return exchange(values, "wide", 1, n_wide)

    def over_far(values):
        return exchange(values, "wide", 2, n_wide)

    def over_x(values):
        return exchange(values, "dp", 1, n_dp)

    def gather_rows(values):
        half = values.shape[0] // 2
        first, second = values[:half], values[half:]
        turned = turn_pairs(values)
        first_y = over_y(turned[:half])
        second_z = over_z(second)
        come = over_z(join([first, first_y]))
        first_z, first_d = come[:half], come[half:]
        come = over_y(join([turned[half:], turn_pairs(second_z)]))
        second_y, second_d = come[:half], come[half:]
        return join([first, second, first_y, second_y, first_z, second_z, first_d, second_d])

    def scatter_rows(partial):
        half = partial.shape[0] // 8
        part = lambda i: partial[i * half : (i + 1) * half]
        come = over_z(join([part(4), part(6)]))
        first = part(0).astype(F32) + come[:half]
        first_y = (part(2).astype(F32) + come[half:]).astype(BF16)
        come = over_y(turn_pairs(join([part(3), part(7)])))
        second = part(1).astype(F32) + come[:half]
        second_z = (part(5).astype(F32) + come[half:]).astype(BF16)
        first = first + over_y(turn_pairs(first_y)).astype(F32)
        second = second + over_z(second_z).astype(F32)
        return join([first, second])

    def all_sum(values):
        for axis, size in (("narrow", n_narrow), ("wide", n_wide), ("dp", n_dp)):
            distance = 1
            while distance < size:
                values = values + exchange(values, axis, distance, size)
                distance *= 2
        return values

    def on_device(
        tokens, continuation_lengths, attention_gain, query_weight, key_weight, value_weight, head_gate, query_gain, key_gain,
        output_weight, feedforward_gain, gate_weight, up_weight, down_weight, cotangent,
    ):
        rows_wide, width_local = tokens.shape
        width = attention_gain.shape[0]
        size = query_gain.shape[0]
        heads = head_gate.shape[1]
        pairs = key_weight.shape[1] // size
        group_rows = rows_wide * n_wide
        rows_local = rows_wide // n_narrow
        x = lax.axis_index("dp") % 2
        z = lax.axis_index("wide")
        narrow = lax.axis_index("narrow")
        y, core = narrow // 2, narrow % 2
        z_near, z_far = z % 2, z // 2
        quarter = width_local // 2
        scale = size ** (-0.5)
        factor = scale * math.log2(math.e)
        log_two = math.log(2.0)

        def by_x(values, axis):
            half = values.shape[axis] // 2
            low = lax.slice_in_dim(values, 0, half, axis=axis)
            high = lax.slice_in_dim(values, half, 2 * half, axis=axis)
            return join([jnp.where(x == 0, low, high), jnp.where(x == 0, high, low)], axis)

        def to_local(values):
            values = by_x(values, 1)
            send = [cut(values, (narrow ^ r) * rows_local, rows_local, 0) for r in RELATIVE]
            parts = [send[0]] + [exchange(s, "narrow", r, n_narrow) for s, r in zip(send[1:], RELATIVE[1:])]
            return join(parts, 1)

        def from_local(values):
            out = jnp.zeros((rows_wide, width_local), values.dtype)
            for i, r in enumerate(RELATIVE):
                part = by_x(values[:, i * width_local : (i + 1) * width_local], 1)
                if r:
                    part = exchange(part, "narrow", r, n_narrow)
                out = lax.dynamic_update_slice_in_dim(out, part, (narrow ^ r) * rows_local, 0)
            return out

        def relative_vector(vector):
            return join([by_x(cut(vector, (narrow ^ r) * width_local, width_local, 0), 0) for r in RELATIVE])

        def absolute_vector(vector):
            out = jnp.zeros((width,), vector.dtype)
            for i, r in enumerate(RELATIVE):
                part = by_x(vector[i * width_local : (i + 1) * width_local], 0)
                out = lax.dynamic_update_slice_in_dim(out, part, (narrow ^ r) * width_local, 0)
            return out

        def norm(values, gain):
            inverse = lax.rsqrt(jnp.mean(values * values, axis=1, keepdims=True) + EPS)
            hat = values * inverse
            return inverse, hat, (hat * gain).astype(BF16)

        def norm_back(grad, hat, inverse, gain):
            scaled = grad * gain
            inner = jnp.mean(scaled * hat, axis=1, keepdims=True)
            return jnp.sum(grad * hat, axis=0), inverse * (scaled - hat * inner)

        def pieces(weights, axis):
            across = 1 - axis
            half = lambda i: join([cut(w, i * (w.shape[across] // 2), w.shape[across] // 2, across) for w in weights], across)
            mine = half(y)
            return (
                cut(mine, x * quarter, quarter, axis),
                cut(mine, (1 - x) * quarter, quarter, axis),
                cut(half(1 - y), x * quarter, quarter, axis),
            )

        def send_far(mine, from_y, axis):
            return over_far(join([mine, from_y], axis))

        def assemble(mine, rest, from_y, from_far, axis):
            far_first = lax.slice_in_dim(from_far, 0, quarter, axis=axis)
            far_second = lax.slice_in_dim(from_far, quarter, 2 * quarter, axis=axis)
            their_y, their_far = over_x(from_y), over_x(from_far)
            their_first = lax.slice_in_dim(their_far, 0, quarter, axis=axis)
            their_second = lax.slice_in_dim(their_far, quarter, 2 * quarter, axis=axis)
            own = join([mine, rest, from_y, their_y], axis)
            other = join([far_first, their_first, far_second, their_second], axis)
            block = join([own, other], 1 - axis)
            return block, over_core(block)

        def reduce_weight(first, second, axis, widths, kind=BF16):
            across = 1 - axis
            step = first.shape[axis] // 4
            piece = lambda v, i: lax.slice_in_dim(v, i * step, (i + 1) * step, axis=axis)
            total = first + over_core(second.astype(kind)).astype(F32)
            come = over_x(join([piece(total, 1), piece(total, 3)], axis).astype(kind))
            total = join([piece(total, 0), piece(total, 2)], axis) + come.astype(F32)
            distance = 2
            while distance < n_dp:
                total = total + exchange(total.astype(kind), "dp", distance, n_dp).astype(F32)
                distance *= 2
            count = sum(widths)
            come = over_far(lax.slice_in_dim(total, count, 2 * count, axis=across).astype(kind))
            total = (lax.slice_in_dim(total, 0, count, axis=across) + come.astype(F32)).astype(kind)
            ours = join([piece(total, 0), over_y(piece(total, 1))], across)
            theirs = over_x(ours)
            outs, at = [], 0
            for length in widths:
                sides = []
                for v in (ours, theirs):
                    a = lax.slice_in_dim(v, at, at + length, axis=across)
                    b = lax.slice_in_dim(v, count + at, count + at + length, axis=across)
                    sides.append(join([jnp.where(y == 0, a, b), jnp.where(y == 0, b, a)], across))
                a, b = sides
                outs.append(join([jnp.where(x == 0, a, b), jnp.where(x == 0, b, a)], axis).astype(F32))
                at += length
            return outs

        inputs = to_local(tokens)
        qkv_mine, qkv_rest, send = pieces([query_weight, key_weight, value_weight], 0)
        qkv_y = over_y(send)
        qkv_far = send_far(qkv_mine, qkv_y, 0)
        gates = lax.all_gather(lax.all_gather(head_gate, "wide", axis=1, tiled=True), "narrow", axis=0, tiled=True)
        gates = join([by_x(cut(gates, (narrow ^ r) * width_local, width_local, 0), 0) for r in RELATIVE])
        gates = join([cut(gates, v * heads + y * (heads // 2), heads // 2, 1) for v in (z, z ^ 2)], 1)
        gates = jnp.pad(gates, ((0, 0), (0, LANES - heads)))
        qkv_block, qkv_core = assemble(qkv_mine, qkv_rest, qkv_y, qkv_far, 0)
        joined_weight = join([join([qkv_block, qkv_core], 0), gates], 1)

        out_mine, out_rest, send = pieces([after(output_weight, qkv_y)], 1)
        out_y = over_y(send)
        down_mine, down_rest, send = pieces([after(down_weight, out_y)], 1)
        down_y = over_y(send)
        out_far = send_far(after(out_mine, qkv_far), out_y, 1)
        down_far = send_far(after(down_mine, out_far), down_y, 1)
        out_weight = join(assemble(out_mine, out_rest, out_y, out_far, 1), 1)
        down = join(assemble(down_mine, down_rest, down_y, down_far, 1), 1)

        index, start, position = layout(continuation_lengths[0], group_rows)
        square = [(z ^ (i // 2), narrow ^ (2 * (i % 2))) for i in range(4)]
        mine = lambda vector: join([cut(vector, (i * n_narrow + j) * rows_local, rows_local, 0) for i, j in square])
        my_index, my_start, my_position = mine(index), mine(start), mine(position)
        frequency = THETA ** (-2.0 * jnp.arange(size // 2, dtype=F32) / size)
        angle = my_position.astype(F32)[:, None] * frequency[None, :]
        cosine, sine = jnp.cos(angle), jnp.sin(angle)
        cosine = jnp.concatenate([cosine, cosine], axis=1)
        sine = jnp.concatenate([-sine, sine], axis=1)
        block = my_index[::rows_local] // rows_local
        first = my_start[::rows_local] // rows_local
        prompt_blocks = PROMPT // rows_local
        in_prompt = block < prompt_blocks
        table = jnp.stack(
            [
                jnp.where(in_prompt, block // 2, prompt_blocks // 2),
                jnp.where(in_prompt, block // 2 * 2, first),
                block,
                jnp.full_like(block, 2 * z_near + y),
                jnp.full_like(block, core),
            ],
            axis=1,
        ).astype(jnp.int32)

        gain_one, gain_two = relative_vector(attention_gain), relative_vector(feedforward_gain)
        inputs = inputs.astype(F32)
        inverse_one, hat_one, normed = norm(inputs, gain_one)
        normed_all = gather_rows(normed)
        raw = dot_rows(normed_all, joined_weight)
        q, kv = post(raw, cosine, sine, query_gain, key_gain, heads, pairs, size, factor)
        kv = after(kv, out_far, down_far)

        kv_core = over_core(kv)
        near = [i for i in range(n_wide) if i & 2 == 0]
        far_kv = lax.ppermute(turn_pairs(kv), "wide", [(i, i + 2) for i in near])
        far_core = over_core(far_kv)
        kv_all = join([jnp.where(z_far == 0, kv, far_kv), jnp.where(z_far == 0, kv_core, far_core), kv, kv_core])

        upstream = to_local(after(cotangent, kv))
        upstream_all = gather_rows(upstream)
        gate_mine, gate_rest, send = pieces([after(gate_weight, down_y)], 0)
        gate_y = over_y(send)
        up_mine, up_rest, send = pieces([after(up_weight, gate_y)], 0)
        up_y = over_y(send)
        gate_far = send_far(after(gate_mine, far_kv), gate_y, 0)
        up_far = send_far(after(up_mine, gate_far), up_y, 0)

        gated, context, inverse_total = attend(
            table, q, kv_all, my_index[:, None], my_start[:, None], raw, pairs, size
        )
        partial = dot_rows(after(gated, upstream_all, gate_far), out_weight).astype(BF16)
        middle = inputs + scatter_rows(partial)
        gate_full = join(assemble(gate_mine, gate_rest, gate_y, gate_far, 0), 0)
        up_full = join(assemble(up_mine, up_rest, up_y, up_far, 0), 0)
        inverse_two, hat_two, normed_two = norm(middle, gain_two)
        normed_two_all = gather_rows(normed_two)
        gate_pre = dot_rows(normed_two_all, gate_full)
        up_pre = dot_rows(normed_two_all, up_full)
        gate_sigmoid = jax.nn.sigmoid(gate_pre)
        silu = gate_pre * gate_sigmoid
        hidden = (silu * up_pre).astype(BF16)
        hidden_grad = dot_trans(upstream_all, down)
        gate_grad = (hidden_grad * up_pre * gate_sigmoid * (1.0 + gate_pre * (1.0 - gate_sigmoid))).astype(BF16)
        up_grad = (hidden_grad * silu).astype(BF16)
        partial = (dot_trans(gate_grad, gate_full) + dot_trans(up_grad, up_full)).astype(BF16)
        normed_two_grad = scatter_rows(partial)
        gain_two_term, change = norm_back(normed_two_grad, hat_two, inverse_two, gain_two)
        middle_grad = upstream.astype(F32) + change
        middle_low = middle_grad.astype(BF16)
        middle_all = gather_rows(middle_low)
        half = width // 2
        hidden_cols = gate_weight.shape[1] // 2
        down_gradient, = reduce_weight(
            dot_inner(hidden, upstream_all[:, :half]), dot_inner(hidden, upstream_all[:, half:]), 1, [hidden_cols]
        )
        gate_gradient, = reduce_weight(
            dot_inner(normed_two_all[:, :half], gate_grad), dot_inner(normed_two_all[:, half:], gate_grad), 0, [hidden_cols]
        )
        up_gradient, = reduce_weight(
            dot_inner(normed_two_all[:, :half], up_grad), dot_inner(normed_two_all[:, half:], up_grad), 0, [hidden_cols]
        )
        gated_grad = dot_trans(middle_all, out_weight)
        dq, dkv, logit_grad = attend_back(
            table, q, kv_all, my_index, my_start, raw, context, inverse_total, gated_grad, pairs, size
        )
        mlp_term = scatter_rows(dot_rows(after(hidden, middle_all), down).astype(BF16))
        layer_output = from_local((middle + mlp_term).astype(BF16))
        output_gradient, = reduce_weight(
            dot_inner(gated, middle_all[:, :half]), dot_inner(gated, middle_all[:, half:]), 1, [output_weight.shape[0] // 2]
        )

        part = lambda i: dkv[i * rows_wide : (i + 1) * rows_wide]
        come = over_core(join([part(1), part(3)]))
        prompt = part(0).astype(F32) + come[:rows_wide].astype(F32)
        rest = part(2).astype(F32) + come[rows_wide:].astype(F32)
        come = lax.ppermute(turn_pairs(prompt.astype(BF16)), "wide", [(i + 2, i) for i in near])
        dkv_mine = jnp.where(z_far == 0, prompt + come.astype(F32), rest)
        low, query_gain_term, key_gain_term = project_back(
            dq, dkv_mine, raw, cosine, sine, query_gain, key_gain, logit_grad, heads, pairs, size, scale, log_two
        )
        normed_grad = scatter_rows(dot_trans(low, joined_weight).astype(BF16))
        wide = low.shape[1] - LANES
        query_cols, key_cols = heads // 2 * size, pairs // 2 * size
        query_gradient, key_gradient, value_gradient = reduce_weight(
            dot_inner(normed_all[:, :half], low[:, :wide]), dot_inner(normed_all[:, half:], low[:, :wide]), 0,
            [query_cols, key_cols, key_cols],
        )
        gates_term = dot_inner(low[:, wide:], normed_all)[:heads]
        head_gate_gradient, = reduce_weight(gates_term[:, :half], gates_term[:, half:], 1, [heads // 2], F32)
        gain_one_term, change = norm_back(normed_grad, hat_one, inverse_one, gain_one)
        tokens_gradient = from_local((middle_grad + change).astype(BF16)).astype(F32)
        gains = all_sum(
            join([absolute_vector(gain_one_term), absolute_vector(gain_two_term), query_gain_term[0], key_gain_term[0]])
        )
        return (
            layer_output,
            tokens_gradient,
            gains[:width],
            query_gradient,
            key_gradient,
            value_gradient,
            head_gate_gradient.T,
            gains[2 * width : 2 * width + size],
            gains[2 * width + size :],
            output_gradient,
            gains[width : 2 * width],
            gate_gradient,
            up_gradient,
            down_gradient,
        )

    return on_device


def solution(mesh):
    rows, up, down = P(("dp", "wide"), "narrow"), P("narrow", "wide"), P("wide", "narrow")
    return jax.shard_map(
        make(dict(mesh.shape)),
        mesh=mesh,
        in_specs=(rows, P("dp", None), P(), up, up, up, up, P(), P(), down, P(), up, up, down, rows),
        out_specs=(rows, rows, P(), up, up, up, up, P(), P(), down, P(), up, up, down),
        check_vma=False,
    )
```

```python
import functools
import math

import jax
import jax.numpy as jnp
from jax import lax
from jax.experimental import pallas as pl
from jax.experimental.pallas import tpu as pltpu
from jax.sharding import PartitionSpec as P

PROMPT = 2048
EPS = 1e-06
THETA = 1000000.0
RELATIVE = (0, 2, 1, 3)
BF16 = jnp.bfloat16
F32 = jnp.float32
VMEM_LIMIT = 56 * 1024 * 1024
LANES = 128


def dot_rows(left, right):
    return jnp.dot(left, right, preferred_element_type=F32)


def dot_trans(left, right):
    return lax.dot_general(left, right, (((1,), (1,)), ((), ())), preferred_element_type=F32)


def dot_inner(left, right):
    return lax.dot_general(left, right, (((0,), (0,)), ((), ())), preferred_element_type=F32)


def exchange(values, axis, distance, size):
    return lax.ppermute(values, axis, [(i, i ^ distance) for i in range(size)])


def join(parts, axis=0):
    return jnp.concatenate(parts, axis=axis)


def cut(values, at, length, axis):
    return lax.dynamic_slice_in_dim(values, at, length, axis=axis)


def turn_pairs(values):
    step = values.shape[1] // 4
    return join([values[:, i * step : (i + 1) * step] for i in (1, 0, 3, 2)], 1)


def after(values, *others):
    return lax.optimization_barrier((values,) + others)[0]


def columns(heads, pairs, size):
    query, pair = heads // 2, pairs // 2
    block = (query + 2 * pair) * size + LANES
    of = lambda i, count, before: (i // count) * block + (before + i % count) * size
    return (
        [of(h, query, 0) for h in range(heads)],
        [of(p, pair, query) for p in range(pairs)],
        [of(p, pair, query + pair) for p in range(pairs)],
        [block - LANES, 2 * block - LANES],
    )


def post_kernel(raw_ref, cos_ref, sin_ref, query_gain_ref, key_gain_ref, q_ref, kv_ref, *, heads, pairs, size, factor):
    cosine = cos_ref[...]
    sine = sin_ref[...]
    query_at, key_at, value_at, _ = columns(heads, pairs, size)

    def turned(value, gain):
        inverse = lax.rsqrt(jnp.mean(value * value, axis=-1, keepdims=True) + EPS)
        normal = value * inverse * gain
        return normal * cosine + pltpu.roll(normal, size // 2, 1) * sine

    for h, at in enumerate(query_at):
        value = raw_ref[:, at : at + size]
        q_ref[:, h * size : (h + 1) * size] = (turned(value, query_gain_ref[...]) * factor).astype(BF16)
    for p, at in enumerate(key_at):
        kv_ref[:, p * size : (p + 1) * size] = turned(raw_ref[:, at : at + size], key_gain_ref[...]).astype(BF16)
    for p, at in enumerate(value_at):
        to = (pairs + p) * size
        kv_ref[:, to : to + size] = raw_ref[:, at : at + size].astype(BF16)


def post(raw, cosine, sine, query_gain, key_gain, heads, pairs, size, factor):
    rows, width = raw.shape
    step = 256
    return pl.pallas_call(
        functools.partial(post_kernel, heads=heads, pairs=pairs, size=size, factor=factor),
        grid=(rows // step,),
        in_specs=[
            pl.BlockSpec((step, width), lambda i: (i, 0)),
            pl.BlockSpec((step, size), lambda i: (i, 0)),
            pl.BlockSpec((step, size), lambda i: (i, 0)),
            pl.BlockSpec((1, size), lambda i: (0, 0)),
            pl.BlockSpec((1, size), lambda i: (0, 0)),
        ],
        out_specs=[
            pl.BlockSpec((step, heads * size), lambda i: (i, 0)),
            pl.BlockSpec((step, 2 * pairs * size), lambda i: (i, 0)),
        ],
        out_shape=[
            jax.ShapeDtypeStruct((rows, heads * size), BF16),
            jax.ShapeDtypeStruct((rows, 2 * pairs * size), BF16),
        ],
        cost_estimate=pl.CostEstimate(flops=rows * width * 20, bytes_accessed=rows * width * 8, transcendentals=0),
        name="post",
    )(raw, cosine, sine, query_gain[None], key_gain[None])


def back_kernel(
    dq_ref, dkv_ref, raw_ref, cos_ref, sin_ref, query_gain_ref, key_gain_ref, logit_ref, out_ref, gq_ref, gk_ref, *, heads, pairs, size, factor_q, factor_k
):
    cosine = cos_ref[...]
    sine = sin_ref[...]
    query_at, key_at, value_at, logit_at = columns(heads, pairs, size)

    @pl.when(pl.program_id(0) == 0)
    def _():
        gq_ref[...] = jnp.zeros_like(gq_ref)
        gk_ref[...] = jnp.zeros_like(gk_ref)

    def back(up, value, gain, total_ref):
        up = up * cosine - pltpu.roll(up, size // 2, 1) * sine
        inverse = lax.rsqrt(jnp.mean(value * value, axis=-1, keepdims=True) + EPS)
        hat = value * inverse
        total_ref[...] += jnp.sum(up * hat, axis=0, keepdims=True)
        scaled = up * gain
        return inverse * (scaled - hat * jnp.mean(scaled * hat, axis=-1, keepdims=True))

    for h, at in enumerate(query_at):
        up = dq_ref[:, h * size : (h + 1) * size] * factor_q
        out_ref[:, at : at + size] = back(up, raw_ref[:, at : at + size], query_gain_ref[...], gq_ref).astype(BF16)
    for p, at in enumerate(key_at):
        up = dkv_ref[:, p * size : (p + 1) * size].astype(F32) * factor_k
        out_ref[:, at : at + size] = back(up, raw_ref[:, at : at + size], key_gain_ref[...], gk_ref).astype(BF16)
    for p, at in enumerate(value_at):
        to = (pairs + p) * size
        out_ref[:, at : at + size] = dkv_ref[:, to : to + size].astype(BF16)
    for i, at in enumerate(logit_at):
        out_ref[:, at : at + LANES] = logit_ref[:, i * LANES : (i + 1) * LANES].astype(BF16)


def project_back(dq, dkv, raw, cosine, sine, query_gain, key_gain, logit_grad, heads, pairs, size, factor_q, factor_k):
    rows, width = raw.shape
    step = 256
    row = lambda cols: pl.BlockSpec((step, cols), lambda i: (i, 0))
    one = pl.BlockSpec((1, size), lambda i: (0, 0))
    return pl.pallas_call(
        functools.partial(back_kernel, heads=heads, pairs=pairs, size=size, factor_q=factor_q, factor_k=factor_k),
        grid=(rows // step,),
        in_specs=[row(heads * size), row(2 * pairs * size), row(width), row(size), row(size), one, one, row(2 * LANES)],
        out_specs=[row(width), one, one],
        out_shape=[
            jax.ShapeDtypeStruct((rows, width), BF16),
            jax.ShapeDtypeStruct((1, size), F32),
            jax.ShapeDtypeStruct((1, size), F32),
        ],
        cost_estimate=pl.CostEstimate(flops=rows * width * 30, bytes_accessed=rows * width * 12, transcendentals=0),
        name="project_back",
    )(dq, dkv, raw, cosine, sine, query_gain[None], key_gain[None], logit_grad)


def places(table_ref, stripe, step, length):
    turn = table_ref[stripe, 3]
    core = table_ref[stripe, 4]
    half = length // 2
    blocks = half // step

    def pair(i):
        at = jnp.bitwise_xor(i, turn) * step
        return pl.ds(pl.multiple_of(at, step), step), pl.ds(pl.multiple_of(at + half // 2, step), step)

    def single(b):
        part = b // blocks
        inner = b - part * blocks
        at = part * half + jnp.bitwise_xor(inner % 2, core) * (half // 2) + jnp.bitwise_xor(inner // 2, turn) * step
        return (pl.ds(pl.multiple_of(at, step), step),)

    return pair, single


def logit_of(head, heads, own_ref, other_ref):
    half = heads // 2
    at = head % half
    return (own_ref if head < half else other_ref)[:, at : at + 1]


def logit_specs(raw, heads, pairs, size, step):
    spec = lambda i: pl.BlockSpec((step, LANES), lambda s, t: (s, i))
    return [spec(at // LANES) for at in columns(heads, pairs, size)[3]]


def forward_kernel(table_ref, q_ref, kv_ref, row_ref, start_ref, own_ref, other_ref, gated_ref, context_ref, inverse_ref, *, pairs, repeat, size, step):
    stripe = pl.program_id(0)
    wide_blocks = table_ref[stripe, 0]
    low = table_ref[stripe, 1]
    high = table_ref[stripe, 2]
    pair, single = places(table_ref, stripe, step, kv_ref.shape[0])
    rows = row_ref[...]
    starts = start_ref[...]
    rows = jnp.concatenate([rows] * repeat, axis=0)
    starts = jnp.concatenate([starts] * repeat, axis=0)
    for k in range(pairs):
        heads = [k * repeat + r for r in range(repeat)]
        query = jnp.concatenate([q_ref[:, h * size : (h + 1) * size] for h in heads], axis=0)
        key_cols = slice(k * size, (k + 1) * size)
        value_cols = slice((pairs + k) * size, (pairs + k + 1) * size)

        def seen(total, where, first):
            keys = join([kv_ref[at, key_cols] for at in where])
            weights = jnp.exp2(dot_trans(query, keys))
            if first is not None:
                index = first + lax.broadcasted_iota(jnp.int32, weights.shape, 1)
                weights = jnp.where((index <= rows) & (index >= starts), weights, 0.0)
            values = join([kv_ref[at, value_cols] for at in where])
            values = jnp.concatenate([values, jnp.ones_like(values)], axis=1)
            return total + dot_rows(weights.astype(BF16), values)

        total = jnp.zeros((query.shape[0], 2 * size), F32)
        total = lax.fori_loop(0, wide_blocks, lambda i, t: seen(t, pair(i), None), total)
        total = lax.fori_loop(low, high + 1, lambda i, t: seen(t, single(i), i * step), total)
        inverse = 1.0 / total[:, size:]
        context = total[:, :size] * inverse
        for r, h in enumerate(heads):
            part = context[r * step : (r + 1) * step]
            cols = slice(h * size, (h + 1) * size)
            gate = jax.nn.sigmoid(logit_of(h, pairs * repeat, own_ref, other_ref))
            gated_ref[:, cols] = (part * gate).astype(BF16)
            context_ref[:, cols] = part
            inverse_ref[:, cols] = inverse[r * step : (r + 1) * step]


def attend(table, q, kv, rows, starts, raw, pairs, size):
    length, cols = q.shape
    heads = cols // size
    step = length // table.shape[0]
    block = lambda width: pl.BlockSpec((step, width), lambda i, t: (i, 0))
    return pl.pallas_call(
        functools.partial(forward_kernel, pairs=pairs, repeat=heads // pairs, size=size, step=step),
        grid_spec=pltpu.PrefetchScalarGridSpec(
            num_scalar_prefetch=1,
            grid=(length // step,),
            in_specs=[
                block(cols),
                pl.BlockSpec(kv.shape, lambda i, t: (0, 0), pipeline_mode=pl.Buffered(1)),
                block(1),
                block(1),
                *logit_specs(raw, heads, pairs, size, step),
            ],
            out_specs=[block(cols), block(cols), block(cols)],
        ),
        out_shape=[
            jax.ShapeDtypeStruct((length, cols), BF16),
            jax.ShapeDtypeStruct((length, cols), F32),
            jax.ShapeDtypeStruct((length, cols), F32),
        ],
        compiler_params=pltpu.CompilerParams(vmem_limit_bytes=VMEM_LIMIT),
        cost_estimate=pl.CostEstimate(flops=20 * 10**9, bytes_accessed=12 * 10**6, transcendentals=7 * 10**6),
        name="attend",
    )(table, q, kv, rows, starts, raw, raw)


def backward_kernel(
    table_ref, q_ref, kv_ref, row_ref, start_ref, own_ref, other_ref, context_ref, inverse_ref, grad_ref,
    dq_ref, dkv_ref, dlogit_ref, sums_ref, *, pairs, repeat, size, step,
):
    stripe = pl.program_id(0)
    wide_blocks = table_ref[stripe, 0]
    low = table_ref[stripe, 1]
    high = table_ref[stripe, 2]
    pair, single = places(table_ref, stripe, step, kv_ref.shape[0])

    @pl.when(stripe == 0)
    def _():
        sums_ref[...] = jnp.zeros_like(sums_ref)

    dlogit_ref[...] = jnp.zeros_like(dlogit_ref)
    rows = jnp.concatenate([row_ref[0]] * repeat, axis=1)
    starts = jnp.concatenate([start_ref[0]] * repeat, axis=1)
    for k in range(pairs):
        heads = [k * repeat + r for r in range(repeat)]
        query = jnp.concatenate([q_ref[:, h * size : (h + 1) * size] for h in heads], axis=0)
        grads, inners = [], []
        for h in heads:
            cols = slice(h * size, (h + 1) * size)
            up = grad_ref[:, cols]
            gate = jax.nn.sigmoid(logit_of(h, pairs * repeat, own_ref, other_ref))
            product = jnp.sum(up * context_ref[:, cols], axis=1, keepdims=True)
            half = pairs * repeat // 2
            at = h // half * LANES + h % half
            dlogit_ref[:, at : at + 1] = product * gate * (1.0 - gate)
            inverse = inverse_ref[:, cols]
            grads.append((up * gate * inverse).astype(BF16))
            inners.append(product * gate * inverse)
        grad = jnp.concatenate(grads, axis=0)
        inner = jnp.transpose(jnp.concatenate(inners, axis=0))[0:1]
        key_cols = slice(k * size, (k + 1) * size)
        value_cols = slice((pairs + k) * size, (pairs + k + 1) * size)

        def seen(total, where, first):
            keys = join([kv_ref[at, key_cols] for at in where])
            weights = jnp.exp2(dot_trans(keys, query))
            if first is not None:
                index = first + lax.broadcasted_iota(jnp.int32, weights.shape, 0)
                weights = jnp.where((index <= rows) & (index >= starts), weights, 0.0)
            changes = dot_trans(join([kv_ref[at, value_cols] for at in where]), grad)
            changes = (weights * (changes - inner)).astype(BF16)
            value_sums = dot_rows(weights.astype(BF16), grad)
            key_sums = dot_rows(changes, query)
            for i, at in enumerate(where):
                sums_ref[at, value_cols] += value_sums[i * step : (i + 1) * step]
                sums_ref[at, key_cols] += key_sums[i * step : (i + 1) * step]
            return total + dot_inner(changes, keys)

        total = jnp.zeros((query.shape[0], size), F32)
        total = lax.fori_loop(0, wide_blocks, lambda i, t: seen(t, pair(i), None), total)
        total = lax.fori_loop(low, high + 1, lambda i, t: seen(t, single(i), i * step), total)
        for r, h in enumerate(heads):
            dq_ref[:, h * size : (h + 1) * size] = total[r * step : (r + 1) * step]

    @pl.when(stripe == pl.num_programs(0) - 1)
    def _():
        dkv_ref[...] = sums_ref[...].astype(BF16)


def attend_back(table, q, kv, rows, starts, raw, context, inverse, grad, pairs, size):
    length, cols = q.shape
    heads = cols // size
    step = length // table.shape[0]
    block = lambda width: pl.BlockSpec((step, width), lambda i, t: (i, 0))
    whole = pl.BlockSpec(kv.shape, lambda i, t: (0, 0), pipeline_mode=pl.Buffered(1))
    lane = pl.BlockSpec((1, 1, step), lambda i, t: (i, 0, 0))
    logits = logit_specs(raw, heads, pairs, size, step)
    return pl.pallas_call(
        functools.partial(backward_kernel, pairs=pairs, repeat=heads // pairs, size=size, step=step),
        grid_spec=pltpu.PrefetchScalarGridSpec(
            num_scalar_prefetch=1,
            grid=(length // step,),
            in_specs=[block(cols), whole, lane, lane, *logits, block(cols), block(cols), block(cols)],
            out_specs=[block(cols), whole, block(2 * LANES)],
            scratch_shapes=[pltpu.VMEM(kv.shape, F32)],
        ),
        out_shape=[
            jax.ShapeDtypeStruct((length, cols), F32),
            jax.ShapeDtypeStruct(kv.shape, BF16),
            jax.ShapeDtypeStruct((length, 2 * LANES), F32),
        ],
        compiler_params=pltpu.CompilerParams(vmem_limit_bytes=VMEM_LIMIT),
        cost_estimate=pl.CostEstimate(flops=50 * 10**9, bytes_accessed=20 * 10**6, transcendentals=7 * 10**6),
        name="attend_back",
    )(table, q, kv, rows.reshape(-1, 1, step), starts.reshape(-1, 1, step), raw, raw, context, inverse, grad)


class Wires:
    def __init__(self, send_sems, recv_sems, local_sems, sizes):
        self.send_sems, self.recv_sems, self.local_sems = send_sems, recv_sems, local_sems
        self.sizes = sizes
        self.sent, self.local, self.open = [], [], []
        self.locals_used = 0
        self.dp, self.wide, self.narrow = (lax.axis_index(a) for a in ("dp", "wide", "narrow"))
        self.y, self.core = self.narrow // 2, self.narrow % 2
        self.x, self.far = self.dp % 2, self.wide // 2

    def peer(self, axis, distance):
        at = {"dp": self.dp, "wide": self.wide, "narrow": self.narrow}[axis]
        bit = at // distance % 2
        return {axis: at + distance * (1 - 2 * bit) if distance < 3 else 3 - at}

    def greet(self, peers):
        barrier = pltpu.get_barrier_semaphore()
        for to in peers:
            pl.semaphore_signal(barrier, inc=1, device_id=self.peer(*to), device_id_type=pl.DeviceIdType.MESH)
        pl.semaphore_wait(barrier, len(peers))

    def make(self, source, target, to):
        i = len(self.sent)
        copy = pltpu.make_async_remote_copy(
            src_ref=source, dst_ref=target, send_sem=self.send_sems.at[i], recv_sem=self.recv_sems.at[i],
            device_id=self.peer(*to), device_id_type=pl.DeviceIdType.MESH,
        )
        self.sent.append(copy)
        return copy

    def send(self, source, target, to):
        copy = self.make(source, target, to)
        copy.start()
        self.open.append(copy)
        return copy

    def arrived(self, copy):
        copy.wait_recv()
        self.open = [other for other in self.open if other is not copy]

    def copy(self, source, target):
        copy = pltpu.make_async_copy(source, target, self.local_sems.at[self.locals_used])
        self.locals_used += 1
        copy.start()
        self.local.append(copy)
        return copy

    def finish(self):
        for copy in list(self.open):
            self.arrived(copy)
        for copy in self.sent:
            copy.wait_send()
        for copy in self.local:
            copy.wait()


Y, CORE, CORNER, NEAR, FAR, X = ("narrow", 2), ("narrow", 1), ("narrow", 3), ("wide", 1), ("wide", 2), ("dp", 1)


def local_flow(net, values_ref, rows_ref):
    rows, width = rows_ref.shape[0], values_ref.shape[1]
    half = width // 2
    out = []
    for distance, to in ((0, None), (1, CORE), (2, Y), (3, CORNER)):
        target = net.narrow if to is None else net.peer(*to)["narrow"]
        at = (2 * (distance % 2) + net.y) * width
        for j in range(2):
            sub = net.x if j == 0 else 1 - net.x
            source = values_ref.at[pl.ds(pl.multiple_of(target * rows, rows), rows), pl.ds(pl.multiple_of(sub * half, half), half)]
            goal = rows_ref.at[:, pl.ds(pl.multiple_of(at + j * half, half), half)]
            out.append(net.copy(source, goal) if to is None else net.send(source, goal, to))
    return out


def gather_flow(net, values_ref, all_ref):
    rows = values_ref.shape[0]
    half = rows // 2
    part = lambda i: all_ref.at[pl.ds(i * half, half), :]
    first, second = values_ref.at[pl.ds(0, half), :], values_ref.at[pl.ds(half, half), :]
    first_y = net.send(first, part(2), Y)
    second_z = net.send(second, part(5), NEAR)
    net.send(first, part(4), NEAR)
    net.send(second, part(3), Y)
    net.copy(values_ref, all_ref.at[pl.ds(0, rows), :])
    yield
    net.arrived(first_y)
    net.send(part(2), part(6), NEAR)
    yield
    net.arrived(second_z)
    net.send(part(5), part(7), Y)
    yield


def weight_flow(net, source_ref, out_ref, axis, own, other, across, from_y=None, from_far=None):
    step = source_ref.shape[axis] // 2
    count = source_ref.shape[axis]

    def window(ref, at, start):
        long, wide = pl.ds(pl.multiple_of(at, step), step), pl.ds(start, across)
        return ref.at[long, wide] if axis == 0 else ref.at[wide, long]

    y, x = net.y, net.x
    piece = lambda sub, half: window(source_ref, sub * step, pl.multiple_of(half * across, across))
    place = lambda slot, j, start: window(out_ref, slot * count + j * step, start)
    mine, rest = piece(x, y), piece(1 - x, y)
    net.copy(mine, place(y, 0, own))
    net.copy(rest, place(y, 1, own))
    if from_y is None:
        come_y = net.send(piece(x, 1 - y), place(y, 0, own), Y)
    else:
        net.copy(from_y, place(1 - y, 0, own))
    if from_far is None:
        come_far = net.send(mine, place(y, 0, other), FAR)
    else:
        net.copy(from_far, place(y, 0, other))
    net.send(mine, place(2 + y, 0, own), CORE)
    net.send(rest, place(2 + y, 1, own), CORE)
    if from_y is None:
        yield
        net.arrived(come_y)
        from_y = place(1 - y, 0, own)
    come_both = net.send(from_y, place(1 - y, 0, other), FAR)
    their_y = net.send(from_y, place(1 - y, 1, own), X)
    net.send(from_y, place(3 - y, 0, own), CORE)
    if from_far is None:
        yield
        net.arrived(come_far)
        from_far = place(y, 0, other)
    their_far = net.send(from_far, place(y, 1, other), X)
    net.send(from_far, place(2 + y, 0, other), CORE)
    yield
    net.arrived(come_both)
    both = place(1 - y, 0, other)
    their_both = net.send(both, place(1 - y, 1, other), X)
    net.send(both, place(3 - y, 0, other), CORE)
    yield
    for copy, slot, start in ((their_y, 1 - y, own), (their_far, y, other), (their_both, 1 - y, other)):
        net.arrived(copy)
        net.send(place(slot, 1, start), place(slot + 2, 1, start), CORE)
    yield


def run(flow):
    return next(flow, None)


def by_rows(count, body):
    step = 16
    lax.fori_loop(0, count // step, lambda i, _: (body(pl.ds(pl.multiple_of(i * step, step), step)), 0)[1], 0)


def begin_kernel(tokens_ref, gain_ref, qkv_ref, out_ref, x_ref, all_ref, joined_ref, output_ref, here, normed, send, recv, local, *, sizes):
    net = Wires(send, recv, local, sizes)
    net.greet([Y, CORE, CORNER, NEAR, FAR, X])
    rows = local_flow(net, tokens_ref, here)
    across = qkv_ref.shape[1] // 2
    joined = weight_flow(net, qkv_ref, joined_ref, 0, 0, across, across)
    run(joined)
    rows[0].wait()
    rows[1].wait()
    net.local = net.local[2:]
    for copy in rows[2:]:
        net.arrived(copy)

    def norm(at):
        values = here[at, :].astype(F32)
        inverse = lax.rsqrt(jnp.mean(values * values, axis=1, keepdims=True) + EPS)
        normed[at, :] = (values * inverse * gain_ref[...]).astype(BF16)
        x_ref[at, :] = here[at, :]

    by_rows(here.shape[0], norm)
    gather = gather_flow(net, normed, all_ref)
    run(gather)
    across = out_ref.shape[0] // 2
    output = weight_flow(net, out_ref, output_ref, 1, 0, across, across)
    for flow in (joined, output, gather, joined, gather, joined, output, joined, output, output, output):
        run(flow)
    net.finish()


ANY = pl.BlockSpec(memory_space=pl.ANY)
VMEM = pl.BlockSpec(memory_space=pltpu.VMEM)


def sems(sends, locals_):
    return [pltpu.SemaphoreType.DMA((sends,)), pltpu.SemaphoreType.DMA((sends,)), pltpu.SemaphoreType.DMA((locals_,))]


def wire_call(kernel, name, number, specs, out_specs, shapes, scratch, sizes, cost, *args):
    return pl.pallas_call(
        functools.partial(kernel, sizes=sizes),
        in_specs=specs,
        out_specs=out_specs,
        out_shape=[jax.ShapeDtypeStruct(*shape) for shape in shapes],
        scratch_shapes=scratch,
        compiler_params=pltpu.CompilerParams(collective_id=number, has_side_effects=True, vmem_limit_bytes=VMEM_LIMIT),
        cost_estimate=pl.CostEstimate(flops=0, bytes_accessed=cost * 3 * 10**6, transcendentals=0),
        name=name,
    )(*args)


def begin(tokens, gain, qkv, out, sizes):
    rows, width = tokens.shape[0] // sizes["narrow"], gain.shape[0]
    return wire_call(
        begin_kernel, "begin", 1, [ANY, VMEM, VMEM, VMEM], [VMEM, ANY, ANY, ANY],
        [((rows, width), BF16), ((4 * rows, width), BF16), ((width, qkv.shape[1]), BF16), ((out.shape[0], width), BF16)],
        [pltpu.VMEM((rows, width), BF16), pltpu.VMEM((rows, width), BF16), *sems(48, 8)], sizes, 55,
        tokens, gain[None], qkv, out,
    )


def keys_kernel(kv_ref, cotangent_ref, keys_ref, rows_ref, all_ref, here, send, recv, local, *, sizes):
    net = Wires(send, recv, local, sizes)
    net.greet([Y, CORE, CORNER, NEAR, FAR])
    count, width = kv_ref.shape
    size = width // 4
    part = lambda i, j: keys_ref.at[pl.ds(i, count), pl.ds(j * size, size)]
    base = pl.multiple_of(net.far * 2 * count, count)
    far = [net.make(kv_ref.at[:, pl.ds(j * size, size)], part(0, j ^ 1), FAR) for j in range(4)]

    @pl.when(net.far == 0)
    def _():
        for copy in far:
            copy.start()

    rows = local_flow(net, cotangent_ref, here)
    net.copy(kv_ref, keys_ref.at[pl.ds(base, count), :])
    net.send(kv_ref, keys_ref.at[pl.ds(base + count, count), :], CORE)
    rows[0].wait()
    rows[1].wait()
    net.local = net.local[2:]
    for copy in rows[2:]:
        net.arrived(copy)
    net.copy(here, rows_ref)
    gather = gather_flow(net, here, all_ref)
    for _ in range(3):
        run(gather)
    on = [net.make(part(0, j ^ 1), part(count, j ^ 1), CORE) for j in range(4)]

    @pl.when(net.far == 1)
    def _():
        for copy, forward in zip(far, on):
            copy.wait_recv()
            forward.start()
        for forward in on:
            forward.wait()

    @pl.when(net.far == 0)
    def _():
        for copy in far:
            copy.wait_send()

    net.sent = [copy for copy in net.sent if all(copy is not other for other in far + on)]
    net.finish()


def exchange_keys(kv, cotangent, width, sizes):
    rows = cotangent.shape[0] // sizes["narrow"]
    return wire_call(
        keys_kernel, "keys", 2, [VMEM, ANY], [ANY, ANY, ANY],
        [((4 * kv.shape[0], kv.shape[1]), BF16), ((rows, width), BF16), ((4 * rows, width), BF16)],
        [pltpu.VMEM((rows, width), BF16), *sems(24, 8)], sizes, 55, kv, cotangent,
    )


def scatter_flow(net, partial_ref, first_ref, second_ref, send_ref, last_ref, total_ref):
    half = partial_ref.shape[0] // 8
    part = lambda i: partial_ref.at[pl.ds(i * half, half), :]
    slot = lambda ref, i: ref.at[pl.ds(i * half, half), :]
    to_z = [net.send(part(6), slot(first_ref, 1), NEAR), net.send(part(4), slot(first_ref, 0), NEAR)]
    to_y = [net.send(part(7), slot(second_ref, 1), Y), net.send(part(3), slot(second_ref, 0), Y)]
    yield

    def add(out_ref, to, i, ref, j):
        def body(at):
            move = lambda start: pl.ds(pl.multiple_of(at.start + start, 16), at.size)
            value = partial_ref[move(i * half), :].astype(F32) + ref[move(j * half), :].astype(F32)
            out_ref[move(to), :] = value.astype(out_ref.dtype)

        by_rows(half, body)

    net.arrived(to_z[0])
    add(send_ref, 0, 2, first_ref, 1)
    last_y = net.send(slot(send_ref, 0), slot(last_ref, 0), Y)
    net.arrived(to_y[0])
    add(send_ref, half, 5, second_ref, 1)
    last_z = net.send(slot(send_ref, 1), slot(last_ref, 1), NEAR)
    yield
    net.arrived(to_z[1])
    add(total_ref, 0, 0, first_ref, 0)
    net.arrived(to_y[1])
    add(total_ref, half, 1, second_ref, 0)
    yield
    net.arrived(last_y)
    net.arrived(last_z)
    yield


def middle_kernel(
    partial_ref, x_ref, gain_ref, gate_ref, up_ref, down_ref, gate_y_ref, up_y_ref, down_y_ref, gate_far_ref, up_far_ref, down_far_ref,
    middle_ref, all_ref, both_ref, last_ref,
    first, second, sums, last, total, normed, send, recv, local, *, sizes,
):
    net = Wires(send, recv, local, sizes)
    net.greet([Y, CORE, NEAR, FAR, X])
    scatter = scatter_flow(net, partial_ref, first, second, sums, last, total)
    run(scatter)
    across = gate_ref.shape[1] // 2
    flows = [
        weight_flow(net, gate_ref, both_ref, 0, 0, across, across, gate_y_ref, gate_far_ref),
        weight_flow(net, up_ref, both_ref, 0, 2 * across, 3 * across, across, up_y_ref, up_far_ref),
        weight_flow(net, down_ref, last_ref, 1, 0, across, across, down_y_ref, down_far_ref),
    ]
    for flow in flows:
        run(flow)
    run(scatter)
    run(scatter)
    run(scatter)

    def norm(at):
        values = x_ref[at, :].astype(F32) + total[at, :] + last[at, :].astype(F32)
        middle_ref[at, :] = values
        inverse = lax.rsqrt(jnp.mean(values * values, axis=1, keepdims=True) + EPS)
        normed[at, :] = (values * inverse * gain_ref[...]).astype(BF16)

    by_rows(normed.shape[0], norm)
    gather = gather_flow(net, normed, all_ref)
    run(gather)
    run(flows[0])
    run(gather)
    run(gather)
    run(flows[1])
    run(flows[2])
    for flow in flows:
        run(flow)
    net.finish()


def to_middle(partial, x, gain, gate, up, down, pieces, sizes):
    rows, width = x.shape
    buffer = lambda n, kind: pltpu.VMEM((n, width), kind)
    return wire_call(
        middle_kernel, "middle", 3, [VMEM] * 12, [VMEM, ANY, ANY, ANY],
        [((rows, width), F32), ((4 * rows, width), BF16), ((width, 2 * gate.shape[1]), BF16), ((down.shape[0], width), BF16)],
        [
            buffer(rows, BF16), buffer(rows, BF16), buffer(rows, BF16), buffer(rows, BF16), buffer(rows, F32), buffer(rows, BF16),
            *sems(64, 16),
        ],
        sizes, 80, partial, x, gain[None], gate, up, down, *pieces,
    )


def layout(lengths, group_rows):
    ends = jnp.cumsum(lengths)
    begins = ends - lengths
    index = jnp.arange(group_rows, dtype=jnp.int32)
    offset = index - PROMPT
    member = ((offset[:, None] >= begins[None, :]) & (offset[:, None] < ends[None, :])).astype(jnp.int32)
    shift = jnp.sum(member * begins[None, :], axis=1)
    start = jnp.where(offset >= 0, PROMPT + shift, 0)
    return index, start, index - shift


def make(sizes):
    n_dp, n_wide, n_narrow = sizes["dp"], sizes["wide"], sizes["narrow"]

    def over_y(values):
        return exchange(values, "narrow", 2, n_narrow)

    def over_core(values):
        return exchange(values, "narrow", 1, n_narrow)

    def over_z(values):
        return exchange(values, "wide", 1, n_wide)

    def over_far(values):
        return exchange(values, "wide", 2, n_wide)

    def over_x(values):
        return exchange(values, "dp", 1, n_dp)

    def gather_rows(values):
        half = values.shape[0] // 2
        first, second = values[:half], values[half:]
        first_y, second_z = over_y(first), over_z(second)
        come = over_z(join([first, first_y]))
        first_z, first_d = come[:half], come[half:]
        come = over_y(join([second, second_z]))
        second_y, second_d = come[:half], come[half:]
        return join([first, second, first_y, second_y, first_z, second_z, first_d, second_d])

    def scatter_rows(partial):
        half = partial.shape[0] // 8
        part = lambda i: partial[i * half : (i + 1) * half]
        come = over_z(join([part(4), part(6)]))
        first = part(0).astype(F32) + come[:half]
        first_y = (part(2).astype(F32) + come[half:]).astype(BF16)
        come = over_y(join([part(3), part(7)]))
        second = part(1).astype(F32) + come[:half]
        second_z = (part(5).astype(F32) + come[half:]).astype(BF16)
        first = first + over_y(first_y).astype(F32)
        second = second + over_z(second_z).astype(F32)
        return join([first, second])

    def all_sum(values):
        for axis, size in (("dp", n_dp), ("narrow", n_narrow), ("wide", n_wide)):
            distance = 1
            while distance < size:
                values = values + exchange(values, axis, distance, size)
                distance *= 2
        return values

    def on_device(
        tokens, continuation_lengths, attention_gain, query_weight, key_weight, value_weight, head_gate, query_gain, key_gain,
        output_weight, feedforward_gain, gate_weight, up_weight, down_weight, cotangent,
    ):
        rows_wide, width_local = tokens.shape
        width = attention_gain.shape[0]
        size = query_gain.shape[0]
        heads = head_gate.shape[1]
        pairs = key_weight.shape[1] // size
        group_rows = rows_wide * n_wide
        rows_local = rows_wide // n_narrow
        x = lax.axis_index("dp") % 2
        z = lax.axis_index("wide")
        narrow = lax.axis_index("narrow")
        y, core = narrow // 2, narrow % 2
        z_near, z_far = z % 2, z // 2
        quarter = width_local // 2
        scale = size ** (-0.5)
        factor = scale * math.log2(math.e)
        log_two = math.log(2.0)

        def by_x(values, axis):
            half = values.shape[axis] // 2
            low = lax.slice_in_dim(values, 0, half, axis=axis)
            high = lax.slice_in_dim(values, half, 2 * half, axis=axis)
            return join([jnp.where(x == 0, low, high), jnp.where(x == 0, high, low)], axis)

        owners = [2 * (i % 2) + (core ^ (i // 2)) for i in range(4)]

        def from_local(values):
            out = jnp.zeros((rows_wide, width_local), values.dtype)
            for r in RELATIVE:
                slot = 2 * (r % 2) + (y ^ (r // 2))
                part = by_x(cut(values, slot * width_local, width_local, 1), 1)
                if r:
                    part = exchange(part, "narrow", r, n_narrow)
                out = lax.dynamic_update_slice_in_dim(out, part, (narrow ^ r) * rows_local, 0)
            return out

        def relative_vector(vector):
            return join([by_x(cut(vector, i * width_local, width_local, 0), 0) for i in owners])

        def absolute_vector(vector):
            out = jnp.zeros((width,), vector.dtype)
            for at, i in enumerate(owners):
                part = by_x(vector[at * width_local : (at + 1) * width_local], 0)
                out = lax.dynamic_update_slice_in_dim(out, part, i * width_local, 0)
            return out

        def norm(values, gain):
            inverse = lax.rsqrt(jnp.mean(values * values, axis=1, keepdims=True) + EPS)
            hat = values * inverse
            return inverse, hat, (hat * gain).astype(BF16)

        def norm_back(grad, hat, inverse, gain):
            scaled = grad * gain
            inner = jnp.mean(scaled * hat, axis=1, keepdims=True)
            return jnp.sum(grad * hat, axis=0), inverse * (scaled - hat * inner)

        def piece_of(weight, i, axis):
            half = weight.shape[1 - axis] // 2
            return cut(cut(weight, x * quarter, quarter, axis), i * half, half, 1 - axis)

        def reduce_first(first, second, axis, *ready):
            step = first.shape[axis] // 4
            piece = lambda v, i: lax.slice_in_dim(v, i * step, (i + 1) * step, axis=axis)
            total = first + over_core(second.astype(BF16)).astype(F32)
            send = join([piece(total, 1), piece(total, 3)], axis).astype(BF16)
            come = over_x(after(send, *ready) if ready else send)
            total = join([piece(total, 0), piece(total, 2)], axis) + come.astype(F32)
            distance = 2
            while distance < n_dp:
                total = total + exchange(total.astype(BF16), "dp", distance, n_dp).astype(F32)
                distance *= 2
            return total, come

        def reduce_second(total, axis, *ready):
            across = 1 - axis
            count = total.shape[across] // 2
            send = lax.slice_in_dim(total, count, 2 * count, axis=across).astype(BF16)
            come = over_far(after(send, *ready) if ready else send)
            return (lax.slice_in_dim(total, 0, count, axis=across) + come.astype(F32)).astype(BF16)

        def reduce_third(total, axis, *ready):
            step = total.shape[axis] // 2
            piece = lambda i: cut(total, i * step, step, axis)
            send = piece(1 - y)
            ours = join([piece(y), over_y(after(send, *ready) if ready else send)], 1 - axis)
            return ours, over_x(ours)

        def reduce_last(ours, theirs, axis, widths):
            across = 1 - axis
            outs, at = [], 0
            count = sum(widths)
            for length in widths:
                sides = []
                for v in (ours, theirs):
                    a = lax.slice_in_dim(v, at, at + length, axis=across)
                    b = lax.slice_in_dim(v, count + at, count + at + length, axis=across)
                    sides.append(join([jnp.where(y == 0, a, b), jnp.where(y == 0, b, a)], across))
                a, b = sides
                outs.append(join([jnp.where(x == 0, a, b), jnp.where(x == 0, b, a)], axis).astype(F32))
                at += length
            return outs

        gain_one, gain_two = relative_vector(attention_gain), relative_vector(feedforward_gain)
        lane_pad = ((0, 0), (0, LANES - heads // 2))
        halves = lambda w, i: w[:, i * (w.shape[1] // 2) : (i + 1) * (w.shape[1] // 2)]
        packed = join(
            [v for i in range(2) for v in (
                halves(query_weight, i), halves(key_weight, i), halves(value_weight, i), jnp.pad(halves(head_gate, i), lane_pad)
            )], 1
        )
        inputs, normed_all, joined_weight, out_weight = begin(tokens, gain_one, packed, output_weight, sizes)

        index, start, position = layout(continuation_lengths[0], group_rows)
        square = [(z ^ (i // 2), narrow ^ (2 * (i % 2))) for i in range(4)]
        mine = lambda vector: join([cut(vector, (i * n_narrow + j) * rows_local, rows_local, 0) for i, j in square])
        my_index, my_start, my_position = mine(index), mine(start), mine(position)
        frequency = THETA ** (-2.0 * jnp.arange(size // 2, dtype=F32) / size)
        angle = my_position.astype(F32)[:, None] * frequency[None, :]
        cosine, sine = jnp.cos(angle), jnp.sin(angle)
        cosine = jnp.concatenate([cosine, cosine], axis=1)
        sine = jnp.concatenate([-sine, sine], axis=1)
        block = my_index[::rows_local] // rows_local
        first = my_start[::rows_local] // rows_local
        prompt_blocks = PROMPT // rows_local
        in_prompt = block < prompt_blocks
        table = jnp.stack(
            [
                jnp.where(in_prompt, block // 2, prompt_blocks // 2),
                jnp.where(in_prompt, block // 2 * 2, first),
                block,
                jnp.full_like(block, 2 * z_near + y),
                jnp.full_like(block, core),
            ],
            axis=1,
        ).astype(jnp.int32)

        raw = dot_rows(normed_all, joined_weight)
        q, kv = post(raw, cosine, sine, query_gain, key_gain, heads, pairs, size, factor)
        send = after((gate_weight, up_weight, down_weight), normed_all)
        axes = (0, 0, 1)
        from_y = [over_y(piece_of(w, 1 - y, axis)) for w, axis in zip(send, axes)]
        near = [i for i in range(n_wide) if i & 2 == 0]
        kv_all, upstream, upstream_all = exchange_keys(after(kv, *from_y), cotangent, width, sizes)
        send = after((gate_weight, up_weight, down_weight), kv_all)
        from_far = [over_far(piece_of(w, y, axis)) for w, axis in zip(send, axes)]

        gated, context, inverse_total = attend(
            table, q, kv_all, my_index[:, None], my_start[:, None], raw, pairs, size
        )
        partial = dot_rows(gated, out_weight).astype(BF16)
        middle, normed_two_all, gate_up, down = to_middle(
            partial, inputs, gain_two, gate_weight, up_weight, down_weight, from_y + from_far, sizes
        )
        inputs = inputs.astype(F32)
        inverse_one, hat_one, _ = norm(inputs, gain_one)
        inverse_two, hat_two, _ = norm(middle, gain_two)
        both = dot_rows(normed_two_all, gate_up)
        hidden_cols = gate_weight.shape[1]
        gate_pre, up_pre = both[:, :hidden_cols], both[:, hidden_cols:]
        gate_sigmoid = jax.nn.sigmoid(gate_pre)
        silu = gate_pre * gate_sigmoid
        hidden = (silu * up_pre).astype(BF16)
        hidden_grad = dot_trans(upstream_all, down)
        gate_grad = hidden_grad * up_pre * gate_sigmoid * (1.0 + gate_pre * (1.0 - gate_sigmoid))
        up_grad = hidden_grad * silu
        gate_up_low = join([gate_grad, up_grad], 1).astype(BF16)
        normed_two_grad = scatter_rows(dot_trans(gate_up_low, gate_up).astype(BF16))
        gain_two_term, change = norm_back(normed_two_grad, hat_two, inverse_two, gain_two)
        middle_grad = upstream.astype(F32) + change
        middle_low = middle_grad.astype(BF16)
        middle_all = gather_rows(middle_low)
        half = width // 2
        down_total, down_x = reduce_first(
            dot_inner(hidden, upstream_all[:, :half]), dot_inner(hidden, upstream_all[:, half:]), 1
        )
        gate_low, up_low = gate_up_low[:, :hidden_cols], gate_up_low[:, hidden_cols:]
        gate_total, gate_x = reduce_first(
            dot_inner(normed_two_all[:, :half], gate_low), dot_inner(normed_two_all[:, half:], gate_low), 0, down_x
        )
        up_total, up_x = reduce_first(
            dot_inner(normed_two_all[:, :half], up_low), dot_inner(normed_two_all[:, half:], up_low), 0, gate_x
        )
        gated_grad = dot_trans(middle_all, out_weight)
        dq, dkv, logit_grad = attend_back(
            table, q, kv_all, my_index, my_start, raw, context, inverse_total, gated_grad, pairs, size
        )
        down_total = reduce_second(down_total, 1)
        gate_total = reduce_second(gate_total, 0, down_total)
        mlp_term = scatter_rows(dot_rows(after(hidden, middle_all), down).astype(BF16))
        layer_output = from_local((middle + mlp_term).astype(BF16))
        out_total, _ = reduce_first(
            dot_inner(gated, middle_all[:, :half]), dot_inner(gated, middle_all[:, half:]), 1, up_x
        )

        part = lambda i: dkv[i * rows_wide : (i + 1) * rows_wide]
        come = over_core(join([part(1), part(3)]))
        prompt = part(0).astype(F32) + come[:rows_wide].astype(F32)
        rest = part(2).astype(F32) + come[rows_wide:].astype(F32)
        far_grad = lax.ppermute(turn_pairs(prompt.astype(BF16)), "wide", [(i + 2, i) for i in near])
        down_ours, down_theirs = reduce_third(down_total, 1, dkv)
        gate_ours, gate_theirs = reduce_third(gate_total, 0, down_ours)
        far_grad = after(far_grad, down_theirs, gate_theirs)
        dkv_mine = jnp.where(z_far == 0, prompt + far_grad.astype(F32), rest)
        low, query_gain_term, key_gain_term = project_back(
            dq, dkv_mine, raw, cosine, sine, query_gain, key_gain, logit_grad, heads, pairs, size, scale, log_two
        )
        up_total = reduce_second(up_total, 0, far_grad)
        out_total = reduce_second(out_total, 1, far_grad)
        normed_grad = scatter_rows(dot_trans(low, joined_weight).astype(BF16))
        qkv_total, _ = reduce_first(
            dot_inner(normed_all[:, :half], low), dot_inner(normed_all[:, half:], low), 0
        )
        qkv_total = reduce_second(qkv_total, 0, up_total, out_total)
        up_ours, up_theirs = reduce_third(up_total, 0, low)
        out_ours, out_theirs = reduce_third(out_total, 1, low)
        gain_one_term, change = norm_back(normed_grad, hat_one, inverse_one, gain_one)
        tokens_gradient = from_local((middle_grad + change).astype(BF16)).astype(F32)
        gains = all_sum(
            join([absolute_vector(gain_one_term), absolute_vector(gain_two_term), query_gain_term[0], key_gain_term[0]])
        )
        qkv_ours, qkv_theirs = reduce_third(qkv_total, 0)
        query_gradient, key_gradient, value_gradient, gates_gradient = reduce_last(
            qkv_ours, qkv_theirs, 0, [heads // 2 * size, pairs // 2 * size, pairs // 2 * size, LANES]
        )
        head_gate_gradient = join([gates_gradient[:, : heads // 2], gates_gradient[:, LANES : LANES + heads // 2]], 1)
        down_gradient, = reduce_last(down_ours, down_theirs, 1, [hidden_cols // 2])
        gate_gradient, = reduce_last(gate_ours, gate_theirs, 0, [hidden_cols // 2])
        up_gradient, = reduce_last(up_ours, up_theirs, 0, [hidden_cols // 2])
        output_gradient, = reduce_last(out_ours, out_theirs, 1, [output_weight.shape[0] // 2])
        return (
            layer_output,
            tokens_gradient,
            gains[:width],
            query_gradient,
            key_gradient,
            value_gradient,
            head_gate_gradient,
            gains[2 * width : 2 * width + size],
            gains[2 * width + size :],
            output_gradient,
            gains[width : 2 * width],
            gate_gradient,
            up_gradient,
            down_gradient,
        )

    return on_device


def solution(mesh):
    rows, up, down = P(("dp", "wide"), "narrow"), P("narrow", "wide"), P("wide", "narrow")
    return jax.shard_map(
        make(dict(mesh.shape)),
        mesh=mesh,
        in_specs=(rows, P("dp", None), P(), up, up, up, up, P(), P(), down, P(), up, up, down, rows),
        out_specs=(rows, rows, P(), up, up, up, up, P(), P(), down, P(), up, up, down),
        check_vma=False,
    )
```

```python
import functools
import math

import jax
import jax.numpy as jnp
from jax import lax
from jax.experimental import pallas as pl
from jax.experimental.pallas import tpu as pltpu
from jax.sharding import PartitionSpec as P

PROMPT = 2048
EPS = 1e-06
THETA = 1000000.0
RELATIVE = (0, 2, 1, 3)
BF16 = jnp.bfloat16
F32 = jnp.float32
VMEM_LIMIT = 56 * 1024 * 1024
LANES = 128


def dot_rows(left, right):
    return jnp.dot(left, right, preferred_element_type=F32)


def dot_trans(left, right):
    return lax.dot_general(left, right, (((1,), (1,)), ((), ())), preferred_element_type=F32)


def dot_inner(left, right):
    return lax.dot_general(left, right, (((0,), (0,)), ((), ())), preferred_element_type=F32)


def exchange(values, axis, distance, size):
    return lax.ppermute(values, axis, [(i, i ^ distance) for i in range(size)])


def join(parts, axis=0):
    return jnp.concatenate(parts, axis=axis)


def cut(values, at, length, axis):
    return lax.dynamic_slice_in_dim(values, at, length, axis=axis)


def turn_pairs(values):
    step = values.shape[1] // 4
    return join([values[:, i * step : (i + 1) * step] for i in (1, 0, 3, 2)], 1)


def after(values, *others):
    return lax.optimization_barrier((values,) + others)[0]


def columns(heads, pairs, size):
    query, pair = heads // 2, pairs // 2
    block = (query + 2 * pair) * size + LANES
    of = lambda i, count, before: (i // count) * block + (before + i % count) * size
    return (
        [of(h, query, 0) for h in range(heads)],
        [of(p, pair, query) for p in range(pairs)],
        [of(p, pair, query + pair) for p in range(pairs)],
        [block - LANES, 2 * block - LANES],
    )


def post_kernel(raw_ref, cos_ref, sin_ref, query_gain_ref, key_gain_ref, q_ref, kv_ref, *, heads, pairs, size, factor):
    cosine = cos_ref[...]
    sine = sin_ref[...]
    query_at, key_at, value_at, _ = columns(heads, pairs, size)

    def turned(value, gain):
        inverse = lax.rsqrt(jnp.mean(value * value, axis=-1, keepdims=True) + EPS)
        normal = value * inverse * gain
        return normal * cosine + pltpu.roll(normal, size // 2, 1) * sine

    for h, at in enumerate(query_at):
        value = raw_ref[:, at : at + size]
        q_ref[:, h * size : (h + 1) * size] = (turned(value, query_gain_ref[...]) * factor).astype(BF16)
    for p, at in enumerate(key_at):
        kv_ref[:, p * size : (p + 1) * size] = turned(raw_ref[:, at : at + size], key_gain_ref[...]).astype(BF16)
    for p, at in enumerate(value_at):
        to = (pairs + p) * size
        kv_ref[:, to : to + size] = raw_ref[:, at : at + size].astype(BF16)


def post(raw, cosine, sine, query_gain, key_gain, heads, pairs, size, factor):
    rows, width = raw.shape
    step = 256
    return pl.pallas_call(
        functools.partial(post_kernel, heads=heads, pairs=pairs, size=size, factor=factor),
        grid=(rows // step,),
        in_specs=[
            pl.BlockSpec((step, width), lambda i: (i, 0)),
            pl.BlockSpec((step, size), lambda i: (i, 0)),
            pl.BlockSpec((step, size), lambda i: (i, 0)),
            pl.BlockSpec((1, size), lambda i: (0, 0)),
            pl.BlockSpec((1, size), lambda i: (0, 0)),
        ],
        out_specs=[
            pl.BlockSpec((step, heads * size), lambda i: (i, 0)),
            pl.BlockSpec((step, 2 * pairs * size), lambda i: (i, 0)),
        ],
        out_shape=[
            jax.ShapeDtypeStruct((rows, heads * size), BF16),
            jax.ShapeDtypeStruct((rows, 2 * pairs * size), BF16),
        ],
        cost_estimate=pl.CostEstimate(flops=rows * width * 20, bytes_accessed=rows * width * 8, transcendentals=0),
        name="post",
    )(raw, cosine, sine, query_gain[None], key_gain[None])


def back_kernel(
    dq_ref, dkv_ref, raw_ref, cos_ref, sin_ref, query_gain_ref, key_gain_ref, logit_ref, out_ref, gq_ref, gk_ref, *, heads, pairs, size, factor_q, factor_k
):
    cosine = cos_ref[...]
    sine = sin_ref[...]
    query_at, key_at, value_at, logit_at = columns(heads, pairs, size)

    @pl.when(pl.program_id(0) == 0)
    def _():
        gq_ref[...] = jnp.zeros_like(gq_ref)
        gk_ref[...] = jnp.zeros_like(gk_ref)

    def back(up, value, gain, total_ref):
        up = up * cosine - pltpu.roll(up, size // 2, 1) * sine
        inverse = lax.rsqrt(jnp.mean(value * value, axis=-1, keepdims=True) + EPS)
        hat = value * inverse
        total_ref[...] += jnp.sum(up * hat, axis=0, keepdims=True)
        scaled = up * gain
        return inverse * (scaled - hat * jnp.mean(scaled * hat, axis=-1, keepdims=True))

    for h, at in enumerate(query_at):
        up = dq_ref[:, h * size : (h + 1) * size] * factor_q
        out_ref[:, at : at + size] = back(up, raw_ref[:, at : at + size], query_gain_ref[...], gq_ref).astype(BF16)
    for p, at in enumerate(key_at):
        up = dkv_ref[:, p * size : (p + 1) * size].astype(F32) * factor_k
        out_ref[:, at : at + size] = back(up, raw_ref[:, at : at + size], key_gain_ref[...], gk_ref).astype(BF16)
    for p, at in enumerate(value_at):
        to = (pairs + p) * size
        out_ref[:, at : at + size] = dkv_ref[:, to : to + size].astype(BF16)
    for i, at in enumerate(logit_at):
        out_ref[:, at : at + LANES] = logit_ref[:, i * LANES : (i + 1) * LANES].astype(BF16)


def project_back(dq, dkv, raw, cosine, sine, query_gain, key_gain, logit_grad, heads, pairs, size, factor_q, factor_k):
    rows, width = raw.shape
    step = 256
    row = lambda cols: pl.BlockSpec((step, cols), lambda i: (i, 0))
    one = pl.BlockSpec((1, size), lambda i: (0, 0))
    return pl.pallas_call(
        functools.partial(back_kernel, heads=heads, pairs=pairs, size=size, factor_q=factor_q, factor_k=factor_k),
        grid=(rows // step,),
        in_specs=[row(heads * size), row(2 * pairs * size), row(width), row(size), row(size), one, one, row(2 * LANES)],
        out_specs=[row(width), one, one],
        out_shape=[
            jax.ShapeDtypeStruct((rows, width), BF16),
            jax.ShapeDtypeStruct((1, size), F32),
            jax.ShapeDtypeStruct((1, size), F32),
        ],
        cost_estimate=pl.CostEstimate(flops=rows * width * 30, bytes_accessed=rows * width * 12, transcendentals=0),
        name="project_back",
    )(dq, dkv, raw, cosine, sine, query_gain[None], key_gain[None], logit_grad)


def places(table_ref, stripe, step, length):
    turn = table_ref[stripe, 3]
    core = table_ref[stripe, 4]
    half = length // 2
    blocks = half // step

    def pair(i):
        at = jnp.bitwise_xor(i, turn) * step
        return pl.ds(pl.multiple_of(at, step), step), pl.ds(pl.multiple_of(at + half // 2, step), step)

    def single(b):
        part = b // blocks
        inner = b - part * blocks
        at = part * half + jnp.bitwise_xor(inner % 2, core) * (half // 2) + jnp.bitwise_xor(inner // 2, turn) * step
        return (pl.ds(pl.multiple_of(at, step), step),)

    return pair, single


def logit_of(head, heads, own_ref, other_ref):
    half = heads // 2
    at = head % half
    return (own_ref if head < half else other_ref)[:, at : at + 1]


def logit_specs(raw, heads, pairs, size, step):
    spec = lambda i: pl.BlockSpec((step, LANES), lambda s, t: (s, i))
    return [spec(at // LANES) for at in columns(heads, pairs, size)[3]]


def forward_kernel(table_ref, q_ref, kv_ref, row_ref, start_ref, own_ref, other_ref, gated_ref, context_ref, inverse_ref, *, pairs, repeat, size, step):
    stripe = pl.program_id(0)
    wide_blocks = table_ref[stripe, 0]
    low = table_ref[stripe, 1]
    high = table_ref[stripe, 2]
    pair, single = places(table_ref, stripe, step, kv_ref.shape[0])
    rows = row_ref[...]
    starts = start_ref[...]
    rows = jnp.concatenate([rows] * repeat, axis=0)
    starts = jnp.concatenate([starts] * repeat, axis=0)
    for k in range(pairs):
        heads = [k * repeat + r for r in range(repeat)]
        query = jnp.concatenate([q_ref[:, h * size : (h + 1) * size] for h in heads], axis=0)
        key_cols = slice(k * size, (k + 1) * size)
        value_cols = slice((pairs + k) * size, (pairs + k + 1) * size)

        def seen(total, where, first):
            keys = join([kv_ref[at, key_cols] for at in where])
            weights = jnp.exp2(dot_trans(query, keys))
            if first is not None:
                index = first + lax.broadcasted_iota(jnp.int32, weights.shape, 1)
                weights = jnp.where((index <= rows) & (index >= starts), weights, 0.0)
            values = join([kv_ref[at, value_cols] for at in where])
            values = jnp.concatenate([values, jnp.ones_like(values)], axis=1)
            return total + dot_rows(weights.astype(BF16), values)

        total = jnp.zeros((query.shape[0], 2 * size), F32)
        total = lax.fori_loop(0, wide_blocks, lambda i, t: seen(t, pair(i), None), total)
        total = lax.fori_loop(low, high + 1, lambda i, t: seen(t, single(i), i * step), total)
        inverse = 1.0 / total[:, size:]
        context = total[:, :size] * inverse
        for r, h in enumerate(heads):
            part = context[r * step : (r + 1) * step]
            cols = slice(h * size, (h + 1) * size)
            gate = jax.nn.sigmoid(logit_of(h, pairs * repeat, own_ref, other_ref))
            gated_ref[:, cols] = (part * gate).astype(BF16)
            context_ref[:, cols] = part
            inverse_ref[:, cols] = inverse[r * step : (r + 1) * step]


def attend(table, q, kv, rows, starts, raw, pairs, size):
    length, cols = q.shape
    heads = cols // size
    step = length // table.shape[0]
    block = lambda width: pl.BlockSpec((step, width), lambda i, t: (i, 0))
    return pl.pallas_call(
        functools.partial(forward_kernel, pairs=pairs, repeat=heads // pairs, size=size, step=step),
        grid_spec=pltpu.PrefetchScalarGridSpec(
            num_scalar_prefetch=1,
            grid=(length // step,),
            in_specs=[
                block(cols),
                pl.BlockSpec(kv.shape, lambda i, t: (0, 0), pipeline_mode=pl.Buffered(1)),
                block(1),
                block(1),
                *logit_specs(raw, heads, pairs, size, step),
            ],
            out_specs=[block(cols), block(cols), block(cols)],
        ),
        out_shape=[
            jax.ShapeDtypeStruct((length, cols), BF16),
            jax.ShapeDtypeStruct((length, cols), F32),
            jax.ShapeDtypeStruct((length, cols), F32),
        ],
        compiler_params=pltpu.CompilerParams(vmem_limit_bytes=VMEM_LIMIT),
        cost_estimate=pl.CostEstimate(flops=20 * 10**9, bytes_accessed=12 * 10**6, transcendentals=7 * 10**6),
        name="attend",
    )(table, q, kv, rows, starts, raw, raw)


def backward_kernel(
    table_ref, q_ref, kv_ref, row_ref, start_ref, own_ref, other_ref, context_ref, inverse_ref, grad_ref,
    dq_ref, dkv_ref, dlogit_ref, sums_ref, *, pairs, repeat, size, step,
):
    stripe = pl.program_id(0)
    wide_blocks = table_ref[stripe, 0]
    low = table_ref[stripe, 1]
    high = table_ref[stripe, 2]
    pair, single = places(table_ref, stripe, step, kv_ref.shape[0])

    @pl.when(stripe == 0)
    def _():
        sums_ref[...] = jnp.zeros_like(sums_ref)

    dlogit_ref[...] = jnp.zeros_like(dlogit_ref)
    rows = jnp.concatenate([row_ref[0]] * repeat, axis=1)
    starts = jnp.concatenate([start_ref[0]] * repeat, axis=1)
    for k in range(pairs):
        heads = [k * repeat + r for r in range(repeat)]
        query = jnp.concatenate([q_ref[:, h * size : (h + 1) * size] for h in heads], axis=0)
        grads, inners = [], []
        for h in heads:
            cols = slice(h * size, (h + 1) * size)
            up = grad_ref[:, cols]
            gate = jax.nn.sigmoid(logit_of(h, pairs * repeat, own_ref, other_ref))
            product = jnp.sum(up * context_ref[:, cols], axis=1, keepdims=True)
            half = pairs * repeat // 2
            at = h // half * LANES + h % half
            dlogit_ref[:, at : at + 1] = product * gate * (1.0 - gate)
            inverse = inverse_ref[:, cols]
            grads.append((up * gate * inverse).astype(BF16))
            inners.append(product * gate * inverse)
        grad = jnp.concatenate(grads, axis=0)
        inner = jnp.transpose(jnp.concatenate(inners, axis=0))[0:1]
        key_cols = slice(k * size, (k + 1) * size)
        value_cols = slice((pairs + k) * size, (pairs + k + 1) * size)

        def seen(total, where, first):
            keys = join([kv_ref[at, key_cols] for at in where])
            weights = jnp.exp2(dot_trans(keys, query))
            if first is not None:
                index = first + lax.broadcasted_iota(jnp.int32, weights.shape, 0)
                weights = jnp.where((index <= rows) & (index >= starts), weights, 0.0)
            changes = dot_trans(join([kv_ref[at, value_cols] for at in where]), grad)
            changes = (weights * (changes - inner)).astype(BF16)
            value_sums = dot_rows(weights.astype(BF16), grad)
            key_sums = dot_rows(changes, query)
            for i, at in enumerate(where):
                sums_ref[at, value_cols] += value_sums[i * step : (i + 1) * step]
                sums_ref[at, key_cols] += key_sums[i * step : (i + 1) * step]
            return total + dot_inner(changes, keys)

        total = jnp.zeros((query.shape[0], size), F32)
        total = lax.fori_loop(0, wide_blocks, lambda i, t: seen(t, pair(i), None), total)
        total = lax.fori_loop(low, high + 1, lambda i, t: seen(t, single(i), i * step), total)
        for r, h in enumerate(heads):
            dq_ref[:, h * size : (h + 1) * size] = total[r * step : (r + 1) * step]

    @pl.when(stripe == pl.num_programs(0) - 1)
    def _():
        dkv_ref[...] = sums_ref[...].astype(BF16)


def attend_back(table, q, kv, rows, starts, raw, context, inverse, grad, pairs, size):
    length, cols = q.shape
    heads = cols // size
    step = length // table.shape[0]
    block = lambda width: pl.BlockSpec((step, width), lambda i, t: (i, 0))
    whole = pl.BlockSpec(kv.shape, lambda i, t: (0, 0), pipeline_mode=pl.Buffered(1))
    lane = pl.BlockSpec((1, 1, step), lambda i, t: (i, 0, 0))
    logits = logit_specs(raw, heads, pairs, size, step)
    return pl.pallas_call(
        functools.partial(backward_kernel, pairs=pairs, repeat=heads // pairs, size=size, step=step),
        grid_spec=pltpu.PrefetchScalarGridSpec(
            num_scalar_prefetch=1,
            grid=(length // step,),
            in_specs=[block(cols), whole, lane, lane, *logits, block(cols), block(cols), block(cols)],
            out_specs=[block(cols), whole, block(2 * LANES)],
            scratch_shapes=[pltpu.VMEM(kv.shape, F32)],
        ),
        out_shape=[
            jax.ShapeDtypeStruct((length, cols), F32),
            jax.ShapeDtypeStruct(kv.shape, BF16),
            jax.ShapeDtypeStruct((length, 2 * LANES), F32),
        ],
        compiler_params=pltpu.CompilerParams(vmem_limit_bytes=VMEM_LIMIT),
        cost_estimate=pl.CostEstimate(flops=50 * 10**9, bytes_accessed=20 * 10**6, transcendentals=7 * 10**6),
        name="attend_back",
    )(table, q, kv, rows.reshape(-1, 1, step), starts.reshape(-1, 1, step), raw, raw, context, inverse, grad)


class Wires:
    def __init__(self, send_sems, recv_sems, local_sems, sizes):
        self.send_sems, self.recv_sems, self.local_sems = send_sems, recv_sems, local_sems
        self.sizes = sizes
        self.sent, self.local, self.open = [], [], []
        self.locals_used, self.sends_used = 0, 0
        self.dp, self.wide, self.narrow = (lax.axis_index(a) for a in ("dp", "wide", "narrow"))
        self.y, self.core = self.narrow // 2, self.narrow % 2
        self.x, self.far = self.dp % 2, self.wide // 2

    def peer(self, axis, distance):
        at = {"dp": self.dp, "wide": self.wide, "narrow": self.narrow}[axis]
        bit = at // distance % 2
        return {axis: at + distance * (1 - 2 * bit) if distance < 3 else 3 - at}

    def greet(self, peers):
        barrier = pltpu.get_barrier_semaphore()
        for to in peers:
            pl.semaphore_signal(barrier, inc=1, device_id=self.peer(*to), device_id_type=pl.DeviceIdType.MESH)
        pl.semaphore_wait(barrier, len(peers))

    def make(self, source, target, to):
        i = self.sends_used
        self.sends_used += 1
        copy = pltpu.make_async_remote_copy(
            src_ref=source, dst_ref=target, send_sem=self.send_sems.at[i], recv_sem=self.recv_sems.at[i],
            device_id=self.peer(*to), device_id_type=pl.DeviceIdType.MESH,
        )
        self.sent.append(copy)
        return copy

    def send(self, source, target, to):
        copy = self.make(source, target, to)
        copy.start()
        self.open.append(copy)
        return copy

    def arrived(self, copy):
        copy.wait_recv()
        self.open = [other for other in self.open if other is not copy]

    def copy(self, source, target):
        copy = pltpu.make_async_copy(source, target, self.local_sems.at[self.locals_used])
        self.locals_used += 1
        copy.start()
        self.local.append(copy)
        return copy

    def finish(self):
        for copy in list(self.open):
            self.arrived(copy)
        for copy in self.sent:
            copy.wait_send()
        for copy in self.local:
            copy.wait()


Y, CORE, CORNER, NEAR, FAR, X = ("narrow", 2), ("narrow", 1), ("narrow", 3), ("wide", 1), ("wide", 2), ("dp", 1)


def local_flow(net, values_ref, rows_ref):
    rows, width = rows_ref.shape[0], values_ref.shape[1]
    half = width // 2
    out = []
    for distance, to in ((0, None), (1, CORE), (2, Y), (3, CORNER)):
        target = net.narrow if to is None else net.peer(*to)["narrow"]
        at = (2 * (distance % 2) + net.y) * width
        for j in range(2):
            sub = net.x if j == 0 else 1 - net.x
            source = values_ref.at[pl.ds(pl.multiple_of(target * rows, rows), rows), pl.ds(pl.multiple_of(sub * half, half), half)]
            goal = rows_ref.at[:, pl.ds(pl.multiple_of(at + j * half, half), half)]
            out.append(net.copy(source, goal) if to is None else net.send(source, goal, to))
    return out


def gather_flow(net, values_ref, all_ref):
    rows = values_ref.shape[0]
    half = rows // 2
    part = lambda i: all_ref.at[pl.ds(i * half, half), :]
    first, second = values_ref.at[pl.ds(0, half), :], values_ref.at[pl.ds(half, half), :]
    first_y = net.send(first, part(2), Y)
    second_z = net.send(second, part(5), NEAR)
    net.send(first, part(4), NEAR)
    net.send(second, part(3), Y)
    net.copy(values_ref, all_ref.at[pl.ds(0, rows), :])
    yield
    net.arrived(first_y)
    net.send(part(2), part(6), NEAR)
    yield
    net.arrived(second_z)
    net.send(part(5), part(7), Y)
    yield


def weight_flow(net, source_ref, out_ref, axis, own, other, across, from_y=None, from_far=None):
    step = source_ref.shape[axis] // 2
    count = source_ref.shape[axis]

    def window(ref, at, start):
        long, wide = pl.ds(pl.multiple_of(at, step), step), pl.ds(start, across)
        return ref.at[long, wide] if axis == 0 else ref.at[wide, long]

    y, x = net.y, net.x
    piece = lambda sub, half: window(source_ref, sub * step, pl.multiple_of(half * across, across))
    place = lambda slot, j, start: window(out_ref, slot * count + j * step, start)
    mine, rest = piece(x, y), piece(1 - x, y)
    net.copy(mine, place(y, 0, own))
    net.copy(rest, place(y, 1, own))
    if from_y is None:
        come_y = net.send(piece(x, 1 - y), place(y, 0, own), Y)
    else:
        net.copy(from_y, place(1 - y, 0, own))
    if from_far is None:
        come_far = net.send(mine, place(y, 0, other), FAR)
    else:
        net.copy(from_far, place(y, 0, other))
    net.send(mine, place(2 + y, 0, own), CORE)
    net.send(rest, place(2 + y, 1, own), CORE)
    if from_y is None:
        yield
        net.arrived(come_y)
        from_y = place(1 - y, 0, own)
    come_both = net.send(from_y, place(1 - y, 0, other), FAR)
    their_y = net.send(from_y, place(1 - y, 1, own), X)
    net.send(from_y, place(3 - y, 0, own), CORE)
    if from_far is None:
        yield
        net.arrived(come_far)
        from_far = place(y, 0, other)
    their_far = net.send(from_far, place(y, 1, other), X)
    net.send(from_far, place(2 + y, 0, other), CORE)
    yield
    net.arrived(come_both)
    both = place(1 - y, 0, other)
    their_both = net.send(both, place(1 - y, 1, other), X)
    net.send(both, place(3 - y, 0, other), CORE)
    yield
    for copy, slot, start in ((their_y, 1 - y, own), (their_far, y, other), (their_both, 1 - y, other)):
        net.arrived(copy)
        net.send(place(slot, 1, start), place(slot + 2, 1, start), CORE)
    yield


def run(flow):
    return next(flow, None)


def by_rows(count, body):
    step = 16
    lax.fori_loop(0, count // step, lambda i, _: (body(pl.ds(pl.multiple_of(i * step, step), step)), 0)[1], 0)


def begin_kernel(tokens_ref, gain_ref, qkv_ref, out_ref, x_ref, all_ref, joined_ref, output_ref, here, normed, send, recv, local, *, sizes):
    net = Wires(send, recv, local, sizes)
    net.greet([Y, CORE, CORNER, NEAR, FAR, X])
    rows = local_flow(net, tokens_ref, here)
    across = qkv_ref.shape[1] // 2
    joined = weight_flow(net, qkv_ref, joined_ref, 0, 0, across, across)
    run(joined)
    rows[0].wait()
    rows[1].wait()
    net.local = net.local[2:]
    for copy in rows[2:]:
        net.arrived(copy)

    def norm(at):
        values = here[at, :].astype(F32)
        inverse = lax.rsqrt(jnp.mean(values * values, axis=1, keepdims=True) + EPS)
        normed[at, :] = (values * inverse * gain_ref[...]).astype(BF16)
        x_ref[at, :] = here[at, :]

    by_rows(here.shape[0], norm)
    gather = gather_flow(net, normed, all_ref)
    run(gather)
    across = out_ref.shape[0] // 2
    output = weight_flow(net, out_ref, output_ref, 1, 0, across, across)
    for flow in (joined, output, gather, joined, gather, joined, output, joined, output, output, output):
        run(flow)
    net.finish()


ANY = pl.BlockSpec(memory_space=pl.ANY)
VMEM = pl.BlockSpec(memory_space=pltpu.VMEM)


def sems(sends, locals_):
    return [pltpu.SemaphoreType.DMA((sends,)), pltpu.SemaphoreType.DMA((sends,)), pltpu.SemaphoreType.DMA((locals_,))]


def wire_call(kernel, name, number, specs, out_specs, shapes, scratch, sizes, cost, *args):
    return pl.pallas_call(
        functools.partial(kernel, sizes=sizes),
        in_specs=specs,
        out_specs=out_specs,
        out_shape=[jax.ShapeDtypeStruct(*shape) for shape in shapes],
        scratch_shapes=scratch,
        compiler_params=pltpu.CompilerParams(collective_id=number, has_side_effects=True, vmem_limit_bytes=VMEM_LIMIT),
        cost_estimate=pl.CostEstimate(flops=0, bytes_accessed=cost * 3 * 10**6, transcendentals=0),
        name=name,
    )(*args)


def begin(tokens, gain, qkv, out, sizes):
    rows, width = tokens.shape[0] // sizes["narrow"], gain.shape[0]
    return wire_call(
        begin_kernel, "begin", 1, [ANY, VMEM, VMEM, VMEM], [VMEM, ANY, ANY, ANY],
        [((rows, width), BF16), ((4 * rows, width), BF16), ((width, qkv.shape[1]), BF16), ((out.shape[0], width), BF16)],
        [pltpu.VMEM((rows, width), BF16), pltpu.VMEM((rows, width), BF16), *sems(48, 8)], sizes, 55,
        tokens, gain[None], qkv, out,
    )


def keys_kernel(kv_ref, cotangent_ref, keys_ref, rows_ref, all_ref, here, send, recv, local, *, sizes):
    net = Wires(send, recv, local, sizes)
    net.greet([Y, CORE, CORNER, NEAR, FAR])
    count, width = kv_ref.shape
    size = width // 4
    part = lambda i, j: keys_ref.at[pl.ds(i, count), pl.ds(j * size, size)]
    base = pl.multiple_of(net.far * 2 * count, count)
    far = [net.make(kv_ref.at[:, pl.ds(j * size, size)], part(0, j ^ 1), FAR) for j in range(4)]

    @pl.when(net.far == 0)
    def _():
        for copy in far:
            copy.start()

    rows = local_flow(net, cotangent_ref, here)
    net.copy(kv_ref, keys_ref.at[pl.ds(base, count), :])
    net.send(kv_ref, keys_ref.at[pl.ds(base + count, count), :], CORE)
    rows[0].wait()
    rows[1].wait()
    net.local = net.local[2:]
    for copy in rows[2:]:
        net.arrived(copy)
    net.copy(here, rows_ref)
    gather = gather_flow(net, here, all_ref)
    for _ in range(3):
        run(gather)
    on = [net.make(part(0, j ^ 1), part(count, j ^ 1), CORE) for j in range(4)]

    @pl.when(net.far == 1)
    def _():
        for copy, forward in zip(far, on):
            copy.wait_recv()
            forward.start()
        for forward in on:
            forward.wait()

    @pl.when(net.far == 0)
    def _():
        for copy in far:
            copy.wait_send()

    net.sent = [copy for copy in net.sent if all(copy is not other for other in far + on)]
    net.finish()


def exchange_keys(kv, cotangent, width, sizes):
    rows = cotangent.shape[0] // sizes["narrow"]
    return wire_call(
        keys_kernel, "keys", 2, [VMEM, ANY], [ANY, ANY, ANY],
        [((4 * kv.shape[0], kv.shape[1]), BF16), ((rows, width), BF16), ((4 * rows, width), BF16)],
        [pltpu.VMEM((rows, width), BF16), *sems(24, 8)], sizes, 55, kv, cotangent,
    )


def scatter_flow(net, partial_ref, first_ref, second_ref, send_ref, last_ref, total_ref):
    half = partial_ref.shape[0] // 8
    part = lambda i: partial_ref.at[pl.ds(i * half, half), :]
    slot = lambda ref, i: ref.at[pl.ds(i * half, half), :]
    to_z = [net.send(part(6), slot(first_ref, 1), NEAR), net.send(part(4), slot(first_ref, 0), NEAR)]
    to_y = [net.send(part(7), slot(second_ref, 1), Y), net.send(part(3), slot(second_ref, 0), Y)]
    yield

    def add(out_ref, to, i, ref, j):
        def body(at):
            move = lambda start: pl.ds(pl.multiple_of(at.start + start, 16), at.size)
            value = partial_ref[move(i * half), :].astype(F32) + ref[move(j * half), :].astype(F32)
            out_ref[move(to), :] = value.astype(out_ref.dtype)

        by_rows(half, body)

    net.arrived(to_z[0])
    add(send_ref, 0, 2, first_ref, 1)
    last_y = net.send(slot(send_ref, 0), slot(last_ref, 0), Y)
    net.arrived(to_y[0])
    add(send_ref, half, 5, second_ref, 1)
    last_z = net.send(slot(send_ref, 1), slot(last_ref, 1), NEAR)
    yield
    net.arrived(to_z[1])
    add(total_ref, 0, 0, first_ref, 0)
    net.arrived(to_y[1])
    add(total_ref, half, 1, second_ref, 0)
    yield
    net.arrived(last_y)
    net.arrived(last_z)
    yield


def middle_kernel(
    partial_ref, x_ref, gain_ref, gate_ref, up_ref, down_ref, gate_y_ref, up_y_ref, down_y_ref, gate_far_ref, up_far_ref, down_far_ref,
    middle_ref, all_ref, both_ref, last_ref,
    first, second, sums, last, total, normed, send, recv, local, *, sizes,
):
    net = Wires(send, recv, local, sizes)
    net.greet([Y, CORE, NEAR, FAR, X])
    scatter = scatter_flow(net, partial_ref, first, second, sums, last, total)
    run(scatter)
    across = gate_ref.shape[1] // 2
    flows = [
        weight_flow(net, gate_ref, both_ref, 0, 0, across, across, gate_y_ref, gate_far_ref),
        weight_flow(net, up_ref, both_ref, 0, 2 * across, 3 * across, across, up_y_ref, up_far_ref),
        weight_flow(net, down_ref, last_ref, 1, 0, across, across, down_y_ref, down_far_ref),
    ]
    for flow in flows:
        run(flow)
    run(scatter)
    run(scatter)
    run(scatter)

    def norm(at):
        values = x_ref[at, :].astype(F32) + total[at, :] + last[at, :].astype(F32)
        middle_ref[at, :] = values
        inverse = lax.rsqrt(jnp.mean(values * values, axis=1, keepdims=True) + EPS)
        normed[at, :] = (values * inverse * gain_ref[...]).astype(BF16)

    by_rows(normed.shape[0], norm)
    gather = gather_flow(net, normed, all_ref)
    run(gather)
    run(flows[0])
    run(gather)
    run(gather)
    run(flows[1])
    run(flows[2])
    for flow in flows:
        run(flow)
    net.finish()


def to_middle(partial, x, gain, gate, up, down, pieces, sizes):
    rows, width = x.shape
    buffer = lambda n, kind: pltpu.VMEM((n, width), kind)
    return wire_call(
        middle_kernel, "middle", 3, [VMEM] * 12, [VMEM, ANY, ANY, ANY],
        [((rows, width), F32), ((4 * rows, width), BF16), ((width, 2 * gate.shape[1]), BF16), ((down.shape[0], width), BF16)],
        [
            buffer(rows, BF16), buffer(rows, BF16), buffer(rows, BF16), buffer(rows, BF16), buffer(rows, F32), buffer(rows, BF16),
            *sems(64, 16),
        ],
        sizes, 80, partial, x, gain[None], gate, up, down, *pieces,
    )


def spread_flow(net, rows_ref, out_ref):
    rows, width = rows_ref.shape[0], out_ref.shape[1]
    half = width // 2
    base = pl.multiple_of(net.narrow * rows, rows)
    for distance, to in ((3, CORNER), (2, Y), (1, CORE), (0, None)):
        target = net.narrow if to is None else net.peer(*to)["narrow"]
        at = (2 * (distance % 2) + target // 2) * width
        for j in range(2):
            sub = net.x if j == 0 else 1 - net.x
            source = rows_ref.at[:, pl.ds(pl.multiple_of(at + j * half, half), half)]
            goal = out_ref.at[pl.ds(base, rows), pl.ds(pl.multiple_of(sub * half, half), half)]
            if to is None:
                net.copy(source, goal)
            else:
                net.send(source, goal, to)


class Gradient:
    def __init__(self, net, axis, acc, from_core=None, from_x=None, from_far=None, out=None, result=None):
        self.net, self.axis = net, axis
        self.acc, self.from_core, self.from_x, self.from_far, self.out = acc, from_core, from_x, from_far, out
        self.result = acc if result is None else result
        self.step = (from_far if from_far is not None else acc).shape[axis] // 2
        self.across = (from_far if from_far is not None else acc).shape[1 - axis]

    def window(self, ref, at, start, count, length=None):
        along, wide = pl.ds(at, self.step if length is None else length), pl.ds(start, count)
        return (along, wide) if self.axis == 0 else (wide, along)

    def view(self, ref, *place):
        return ref.at[self.window(ref, *place)]

    def add(self, to, other, ref, result=None):
        (rows, cols), (rows_b, cols_b) = to, other

        def body(at):
            move = lambda r: pl.ds(pl.multiple_of(at.start + r.start, 16), at.size)
            value = (self.acc[move(rows), cols].astype(F32) + ref[move(rows_b), cols_b].astype(F32)).astype(BF16)
            if result is None:
                self.acc[move(rows), cols] = value
            else:
                result[move(rows_b), cols_b] = value

        by_rows(rows.size, body)

    def start(self, g_ref):
        count = 4 * self.step
        own, other = (self.window(g_ref, i * count, 0, 2 * self.across, count) for i in range(2))
        self.loaded = self.net.copy(g_ref.at[own], self.acc)
        self.core = self.net.send(g_ref.at[other], self.from_core, CORE)

    def after_core(self):
        self.loaded.wait()
        self.net.local = [copy for copy in self.net.local if copy is not self.loaded]
        self.net.arrived(self.core)
        self.x = []
        for slot in range(2):
            place = self.window(self.acc, (2 * slot + 1) * self.step, 0, 2 * self.across)
            self.add(place, place, self.from_core)
            self.x.append(
                self.net.send(self.acc.at[place], self.view(self.from_x, slot * self.step, 0, 2 * self.across), X)
            )
        for slot in range(2):
            place = self.window(self.acc, 2 * slot * self.step, 0, 2 * self.across)
            self.add(place, place, self.from_core)

    def after_x(self):
        for slot in range(2):
            self.net.arrived(self.x[slot])
            to = self.window(self.acc, 2 * slot * self.step, 0, 2 * self.across)
            self.add(to, self.window(self.from_x, slot * self.step, 0, 2 * self.across), self.from_x)

    def send_far(self, stride=2):
        self.stride = stride
        self.far = []
        for slot in range(2):
            source = self.view(self.acc, stride * slot * self.step, self.across, self.across)
            self.far.append(self.net.send(source, self.view(self.from_far, slot * self.step, 0, self.across), FAR))

    def after_far(self):
        for slot in range(2):
            self.net.arrived(self.far[slot])
            to = self.window(self.acc, self.stride * slot * self.step, 0, self.across)
            result = None if self.result is self.acc else self.result
            self.add(to, self.window(self.from_far, slot * self.step, 0, self.across), self.from_far, result)

    def send_y(self, stride=2):
        net, step, across = self.net, self.step, self.across
        at = lambda slot: pl.multiple_of(stride * slot * step, step)
        base, start = pl.multiple_of(net.x * step, step), pl.multiple_of(net.y * across, across)
        goal = self.view(self.out, base, start, across)
        mine = self.view(self.result, at(net.y), 0, across)
        self.y = net.send(self.view(self.result, at(1 - net.y), 0, across), goal, Y)
        net.copy(mine, goal)
        net.send(mine, goal, X)

    def after_y(self):
        net, across = self.net, self.across
        self.net.arrived(self.y)
        start = pl.multiple_of((1 - net.y) * across, across)
        place = self.view(self.out, pl.multiple_of(net.x * self.step, self.step), start, across)
        net.send(place, place, X)


def row_back(grad, values, gain):
    inverse = lax.rsqrt(jnp.mean(values * values, axis=1, keepdims=True) + EPS)
    hat = values * inverse
    scaled = grad * gain
    inner = jnp.mean(scaled * hat, axis=1, keepdims=True)
    return jnp.sum(grad * hat, axis=0, keepdims=True), inverse * (scaled - hat * inner)


def turn_kernel(
    partial_ref, middle_ref, upstream_ref, gain_ref, down_ref, gate_ref, up_ref,
    grad_ref, all_ref, term_ref, down_out, gate_out, up_out,
    first, second, sums, last, total, low, *rest, sizes,
):
    buffers, (send, recv, local) = rest[:-3], rest[-3:]
    net = Wires(send, recv, local, sizes)
    net.greet([Y, CORE, NEAR, FAR, X])
    scatter = scatter_flow(net, partial_ref, first, second, sums, last, total)
    run(scatter)
    down = Gradient(net, 1, *buffers[0:4])
    gate = Gradient(net, 0, *buffers[4:8])
    up = Gradient(net, 0, *buffers[8:12])
    for flow, ref in ((down, down_ref), (gate, gate_ref), (up, up_ref)):
        flow.start(ref)
    down.after_core()
    run(scatter)
    gate.after_core()
    run(scatter)
    run(scatter)
    term_ref[...] = jnp.zeros_like(term_ref)

    def rows(at):
        grad = total[at, :] + last[at, :].astype(F32)
        term, change = row_back(grad, middle_ref[at, :], gain_ref[...])
        term_ref[...] += term
        value = upstream_ref[at, :].astype(F32) + change
        grad_ref[at, :] = value
        low[at, :] = value.astype(BF16)

    by_rows(low.shape[0], rows)
    gather = gather_flow(net, low, all_ref)
    run(gather)
    down.after_x()
    down.send_far()
    run(gather)
    up.after_core()
    run(gather)
    gate.after_x()
    gate.send_far()
    down.after_far()
    up.after_x()
    gate.after_far()
    for flow, ref, wide in ((down, down_out, 1), (gate, gate_out, 1), (up, up_out, 2)):
        for slot in range(2):
            source = flow.view(flow.acc, 2 * slot * flow.step, 0, wide * flow.across)
            net.copy(source, flow.view(ref, slot * flow.step, 0, wide * flow.across))
    net.finish()


def gradient_buffers(size, across, axis, whole=True):
    shape = lambda a, b: pltpu.VMEM((a, b) if axis == 0 else (b, a), BF16)
    first = [shape(2 * size, 2 * across), shape(2 * size, 2 * across), shape(size, 2 * across)]
    return first + [shape(size, across)] if whole else first[:1]


def scatter_buffers(rows, width):
    buffer = lambda kind: pltpu.VMEM((rows, width), kind)
    return [buffer(BF16), buffer(BF16), buffer(BF16), buffer(BF16), buffer(F32)]


def turn(partial, middle, upstream, gain, down, gate, up, sizes):
    rows, width = middle.shape
    size, across = width // sizes["narrow"], down.shape[0] // 2
    return wire_call(
        turn_kernel, "turn", 4, [VMEM] * 4 + [ANY] * 3, [VMEM, ANY, VMEM, ANY, ANY, ANY],
        [
            ((rows, width), F32), ((4 * rows, width), BF16), ((1, width), F32),
            ((across, size), BF16), ((size, across), BF16), ((size, 2 * across), BF16),
        ],
        [
            *scatter_buffers(rows, width), pltpu.VMEM((rows, width), BF16),
            *gradient_buffers(size, across, 1), *gradient_buffers(size, across, 0), *gradient_buffers(size, across, 0), *sems(40, 16),
        ],
        sizes, 105, partial, middle, upstream, gain[None], down, gate, up,
    )


def owner_kernel(
    dkv_ref, partial_ref, middle_ref, down_ref, gate_ref, up_ref,
    mine_ref, layer_ref, down_out, gate_out, up_out,
    prompt_core, rest_core, prompt, prompt_far, first, second, sums, last, total, rows_low, up_far, up_sums, send, recv, local, *, sizes,
):
    net = Wires(send, recv, local, sizes)
    net.greet([Y, CORE, CORNER, NEAR, FAR, X])
    count, width = prompt.shape
    size = width // 4
    region = lambda i: dkv_ref.at[pl.ds(i * count, count), :]
    come = net.send(region(1), prompt_core, CORE)
    rest = net.send(region(3), rest_core, CORE)
    scatter = scatter_flow(net, partial_ref, first, second, sums, last, total)
    run(scatter)
    down, gate = Gradient(net, 1, down_ref, out=down_out), Gradient(net, 0, gate_ref, out=gate_out)
    up = Gradient(net, 0, up_ref, from_far=up_far, out=up_out, result=up_sums)
    net.arrived(come)

    def add(at):
        prompt[at, :] = (dkv_ref[at, :].astype(F32) + prompt_core[at, :].astype(F32)).astype(BF16)

    by_rows(count, add)
    cols = lambda ref, j: ref.at[:, pl.ds(j * size, size)]
    far = [net.make(cols(prompt, j), cols(prompt_far, j ^ 1), FAR) for j in range(4)]

    @pl.when(net.far == 1)
    def _():
        for copy in far:
            copy.start()

    up.send_far(1)
    down.send_y(1)
    run(scatter)
    gate.send_y(1)
    run(scatter)
    run(scatter)

    def rows(at):
        rows_low[at, :] = (middle_ref[at, :] + total[at, :] + last[at, :].astype(F32)).astype(BF16)

    by_rows(rows_low.shape[0], rows)
    spread_flow(net, rows_low, layer_ref)
    down.after_y()
    gate.after_y()
    net.arrived(rest)

    @pl.when(net.far == 1)
    def _():
        def add(at):
            move = pl.ds(pl.multiple_of(at.start + 2 * count, 16), at.size)
            mine_ref[at, :] = dkv_ref[move, :].astype(F32) + rest_core[at, :].astype(F32)

        by_rows(count, add)
        for copy in far:
            copy.wait_send()

    @pl.when(net.far == 0)
    def _():
        for copy in far:
            copy.wait_recv()

        def add(at):
            mine_ref[at, :] = dkv_ref[at, :].astype(F32) + prompt_core[at, :].astype(F32) + prompt_far[at, :].astype(F32)

        by_rows(count, add)

    net.sent = [copy for copy in net.sent if all(copy is not other for other in far)]
    up.after_far()
    up.send_y(1)
    up.after_y()
    net.finish()


def to_owner(dkv, partial, middle, down, gate, up, sizes):
    rows, width = middle.shape
    size, across = width // sizes["narrow"], gate.shape[1]
    count = dkv.shape[0] // 4
    block = lambda: pltpu.VMEM((count, dkv.shape[1]), BF16)
    return wire_call(
        owner_kernel, "owner", 5, [VMEM] * 6, [VMEM, ANY, ANY, ANY, ANY],
        [
            ((count, dkv.shape[1]), F32), ((sizes["narrow"] * rows, size), BF16),
            ((2 * across, size), BF16), ((size, 2 * across), BF16), ((size, 2 * across), BF16),
        ],
        [
            block(), block(), block(), block(), *scatter_buffers(rows, width), pltpu.VMEM((rows, width), BF16),
            pltpu.VMEM((size, across), BF16), pltpu.VMEM((size, across), BF16), *sems(40, 16),
        ],
        sizes, 80, dkv, partial, middle, down, gate, up,
    )


SUMS = [X, CORE, Y, NEAR, FAR]


def end_kernel(
    partial_ref, x_ref, gain_ref, grad_ref, two_ref, query_ref, key_ref, qkv_ref, out_ref,
    tokens_ref, gains_ref, qkv_out, out_out,
    first, second, sums, last, total, rows_low, vectors, *rest, sizes,
):
    buffers, (send, recv, local) = rest[:-3], rest[-3:]
    net = Wires(send, recv, local, sizes)
    net.greet([Y, CORE, CORNER, NEAR, FAR, X])
    qkv = Gradient(net, 0, *buffers[0:4], out=qkv_out)
    out = Gradient(net, 1, *buffers[4:8], out=out_out)
    qkv.start(qkv_ref)
    out.start(out_ref)
    scatter = scatter_flow(net, partial_ref, first, second, sums, last, total)
    run(scatter)
    qkv.after_core()
    out.after_core()
    run(scatter)
    run(scatter)
    run(scatter)
    width = x_ref.shape[1]
    size = query_ref.shape[1]
    block = width // sizes["narrow"]
    half = block // 2
    gains_ref[...] = jnp.zeros_like(gains_ref)

    def rows(at):
        grad = total[at, :] + last[at, :].astype(F32)
        term, change = row_back(grad, x_ref[at, :].astype(F32), gain_ref[...])
        gains_ref[:, :width] += term
        rows_low[at, :] = (grad_ref[at, :] + change).astype(BF16)

    by_rows(rows_low.shape[0], rows)
    spread_flow(net, rows_low, tokens_ref)
    for i, ref in enumerate((gains_ref, two_ref)):
        for slot in range(4):
            to = (2 * (slot % 2) + jnp.bitwise_xor(net.core, slot // 2)) * block + i * width
            for j in range(2):
                sub = net.x if j == 0 else 1 - net.x
                at = slot * block + j * half
                vectors[0, :, pl.ds(pl.multiple_of(to + sub * half, half), half)] = ref[:, at : at + half]
    vectors[0, :, 2 * width : 2 * width + size] = query_ref[...]
    vectors[0, :, 2 * width + size :] = key_ref[...]
    qkv.after_x()
    qkv.send_far()
    out.after_x()
    out.send_far()
    for i, to in enumerate(SUMS):
        copy = net.send(vectors.at[i], vectors.at[len(SUMS) + 1 + i], to)
        net.arrived(copy)
        vectors[i + 1] = vectors[i] + vectors[len(SUMS) + 1 + i]
    gains_ref[...] = vectors[len(SUMS)]
    qkv.after_far()
    qkv.send_y()
    out.after_far()
    out.send_y()
    qkv.after_y()
    out.after_y()
    net.finish()


def end(partial, x, gain, grad, two, query, key, qkv, out, sizes):
    rows, width = x.shape
    size = width // sizes["narrow"]
    wide, deep = qkv.shape[1], out.shape[0]
    length = 2 * width + 2 * query.shape[1]
    return wire_call(
        end_kernel, "end", 6, [VMEM] * 7 + [ANY] * 2, [ANY, VMEM, ANY, ANY],
        [((sizes["narrow"] * rows, size), BF16), ((1, length), F32), ((size, wide), BF16), ((deep, size), BF16)],
        [
            *scatter_buffers(rows, width), pltpu.VMEM((rows, width), BF16), pltpu.VMEM((2 * len(SUMS) + 1, 1, length), F32),
            *gradient_buffers(size, wide // 2, 0), *gradient_buffers(size, deep // 2, 1), *sems(40, 16),
        ],
        sizes, 90, partial, x, gain[None], grad, two, query, key, qkv, out,
    )


def layout(lengths, group_rows):
    ends = jnp.cumsum(lengths)
    begins = ends - lengths
    index = jnp.arange(group_rows, dtype=jnp.int32)
    offset = index - PROMPT
    member = ((offset[:, None] >= begins[None, :]) & (offset[:, None] < ends[None, :])).astype(jnp.int32)
    shift = jnp.sum(member * begins[None, :], axis=1)
    start = jnp.where(offset >= 0, PROMPT + shift, 0)
    return index, start, index - shift


def make(sizes):
    n_dp, n_wide, n_narrow = sizes["dp"], sizes["wide"], sizes["narrow"]

    def over_y(values):
        return exchange(values, "narrow", 2, n_narrow)

    def over_far(values):
        return exchange(values, "wide", 2, n_wide)

    def over_groups(values, kind):
        distance = 2
        while distance < n_dp:
            values = values.astype(F32) + exchange(values.astype(kind), "dp", distance, n_dp).astype(F32)
            distance *= 2
        return values.astype(F32)

    def on_device(
        tokens, continuation_lengths, attention_gain, query_weight, key_weight, value_weight, head_gate, query_gain, key_gain,
        output_weight, feedforward_gain, gate_weight, up_weight, down_weight, cotangent,
    ):
        rows_wide, width_local = tokens.shape
        width = attention_gain.shape[0]
        size = query_gain.shape[0]
        heads = head_gate.shape[1]
        pairs = key_weight.shape[1] // size
        group_rows = rows_wide * n_wide
        rows_local = rows_wide // n_narrow
        x = lax.axis_index("dp") % 2
        z = lax.axis_index("wide")
        narrow = lax.axis_index("narrow")
        y, core = narrow // 2, narrow % 2
        z_near, z_far = z % 2, z // 2
        quarter = width_local // 2
        scale = size ** (-0.5)
        factor = scale * math.log2(math.e)
        log_two = math.log(2.0)

        def by_x(values, axis):
            half = values.shape[axis] // 2
            low = lax.slice_in_dim(values, 0, half, axis=axis)
            high = lax.slice_in_dim(values, half, 2 * half, axis=axis)
            return join([jnp.where(x == 0, low, high), jnp.where(x == 0, high, low)], axis)

        owners = [2 * (i % 2) + (core ^ (i // 2)) for i in range(4)]

        def relative_vector(vector):
            return join([by_x(cut(vector, i * width_local, width_local, 0), 0) for i in owners])

        def piece_of(weight, i, axis):
            half = weight.shape[1 - axis] // 2
            return cut(cut(weight, x * quarter, quarter, axis), i * half, half, 1 - axis)

        gain_one, gain_two = relative_vector(attention_gain), relative_vector(feedforward_gain)
        lane_pad = ((0, 0), (0, LANES - heads // 2))
        halves = lambda w, i: w[:, i * (w.shape[1] // 2) : (i + 1) * (w.shape[1] // 2)]
        packed = join(
            [v for i in range(2) for v in (
                halves(query_weight, i), halves(key_weight, i), halves(value_weight, i), jnp.pad(halves(head_gate, i), lane_pad)
            )], 1
        )
        inputs, normed_all, joined_weight, out_weight = begin(tokens, gain_one, packed, output_weight, sizes)

        index, start, position = layout(continuation_lengths[0], group_rows)
        square = [(z ^ (i // 2), narrow ^ (2 * (i % 2))) for i in range(4)]
        mine = lambda vector: join([cut(vector, (i * n_narrow + j) * rows_local, rows_local, 0) for i, j in square])
        my_index, my_start, my_position = mine(index), mine(start), mine(position)
        frequency = THETA ** (-2.0 * jnp.arange(size // 2, dtype=F32) / size)
        angle = my_position.astype(F32)[:, None] * frequency[None, :]
        cosine, sine = jnp.cos(angle), jnp.sin(angle)
        cosine = jnp.concatenate([cosine, cosine], axis=1)
        sine = jnp.concatenate([-sine, sine], axis=1)
        block = my_index[::rows_local] // rows_local
        first = my_start[::rows_local] // rows_local
        prompt_blocks = PROMPT // rows_local
        in_prompt = block < prompt_blocks
        table = jnp.stack(
            [
                jnp.where(in_prompt, block // 2, prompt_blocks // 2),
                jnp.where(in_prompt, block // 2 * 2, first),
                block,
                jnp.full_like(block, 2 * z_near + y),
                jnp.full_like(block, core),
            ],
            axis=1,
        ).astype(jnp.int32)

        raw = dot_rows(normed_all, joined_weight)
        q, kv = post(raw, cosine, sine, query_gain, key_gain, heads, pairs, size, factor)
        send = after((gate_weight, up_weight, down_weight), normed_all)
        axes = (0, 0, 1)
        from_y = [over_y(piece_of(w, 1 - y, axis)) for w, axis in zip(send, axes)]
        near = [i for i in range(n_wide) if i & 2 == 0]
        kv_all, upstream, upstream_all = exchange_keys(after(kv, *from_y), cotangent, width, sizes)
        send = after((gate_weight, up_weight, down_weight), kv_all)
        from_far = [over_far(piece_of(w, y, axis)) for w, axis in zip(send, axes)]

        gated, context, inverse_total = attend(
            table, q, kv_all, my_index[:, None], my_start[:, None], raw, pairs, size
        )
        partial = dot_rows(gated, out_weight).astype(BF16)
        middle, normed_two_all, gate_up, down = to_middle(
            partial, inputs, gain_two, gate_weight, up_weight, down_weight, from_y + from_far, sizes
        )
        both = dot_rows(normed_two_all, gate_up)
        hidden_cols = gate_weight.shape[1]
        gate_pre, up_pre = both[:, :hidden_cols], both[:, hidden_cols:]
        gate_sigmoid = jax.nn.sigmoid(gate_pre)
        silu = gate_pre * gate_sigmoid
        hidden = (silu * up_pre).astype(BF16)
        hidden_grad = dot_trans(upstream_all, down)
        gate_grad = hidden_grad * up_pre * gate_sigmoid * (1.0 + gate_pre * (1.0 - gate_sigmoid))
        up_grad = hidden_grad * silu
        gate_up_low = join([gate_grad, up_grad], 1).astype(BF16)
        partial = dot_trans(gate_up_low, gate_up).astype(BF16)
        gate_low, up_low = gate_up_low[:, :hidden_cols], gate_up_low[:, hidden_cols:]
        down_sums = dot_inner(hidden, upstream_all).astype(BF16)
        gate_sums = dot_inner(normed_two_all, gate_low).astype(BF16)
        up_sums = dot_inner(normed_two_all, up_low).astype(BF16)
        middle_grad, middle_all, two_term, down_part, gate_part, up_part = turn(
            partial, middle, upstream, gain_two, down_sums, gate_sums, up_sums, sizes
        )
        gated_grad = dot_trans(middle_all, out_weight)
        dq, dkv, logit_grad = attend_back(
            table, q, kv_all, my_index, my_start, raw, context, inverse_total, gated_grad, pairs, size
        )
        partial = dot_rows(hidden, down).astype(BF16)
        dkv_mine, layer_output, down_gradient, gate_gradient, up_gradient = to_owner(
            dkv, partial, middle, down_part, gate_part, up_part, sizes
        )
        low, query_term, key_term = project_back(
            dq, dkv_mine, raw, cosine, sine, query_gain, key_gain, logit_grad, heads, pairs, size, scale, log_two
        )
        partial = dot_trans(low, joined_weight).astype(BF16)
        qkv_sums = dot_inner(normed_all, low).astype(BF16)
        out_sums = dot_inner(gated, middle_all).astype(BF16)
        tokens_gradient, gains, qkv_gradient, output_gradient = end(
            partial, inputs, gain_one, middle_grad, two_term, query_term, key_term, qkv_sums, out_sums, sizes
        )
        tokens_gradient = tokens_gradient.astype(F32)
        gains = over_groups(gains[0], F32)
        qkv_gradient = over_groups(qkv_gradient, BF16)
        down_gradient, gate_gradient, up_gradient, output_gradient = (
            over_groups(v, BF16) for v in (down_gradient, gate_gradient, up_gradient, output_gradient)
        )
        block = qkv_gradient.shape[1] // 2
        query_cols, key_cols = heads // 2 * size, pairs // 2 * size
        take = lambda at, count: join([qkv_gradient[:, at + i * block : at + i * block + count] for i in range(2)], 1)
        query_gradient = take(0, query_cols)
        key_gradient = take(query_cols, key_cols)
        value_gradient = take(query_cols + key_cols, key_cols)
        head_gate_gradient = take(query_cols + 2 * key_cols, heads // 2)
        return (
            layer_output,
            tokens_gradient,
            gains[:width],
            query_gradient,
            key_gradient,
            value_gradient,
            head_gate_gradient,
            gains[2 * width : 2 * width + size],
            gains[2 * width + size :],
            output_gradient,
            gains[width : 2 * width],
            gate_gradient,
            up_gradient,
            down_gradient,
        )

    return on_device


def solution(mesh):
    rows, up, down = P(("dp", "wide"), "narrow"), P("narrow", "wide"), P("wide", "narrow")
    return jax.shard_map(
        make(dict(mesh.shape)),
        mesh=mesh,
        in_specs=(rows, P("dp", None), P(), up, up, up, up, P(), P(), down, P(), up, up, down, rows),
        out_specs=(rows, rows, P(), up, up, up, up, P(), P(), down, P(), up, up, down),
        check_vma=False,
    )
```

```python
import functools
import math

import jax
import jax.numpy as jnp
from jax import lax
from jax.experimental import pallas as pl
from jax.experimental.pallas import tpu as pltpu
from jax.sharding import PartitionSpec as P

PROMPT = 2048
EPS = 1e-06
THETA = 1000000.0
RELATIVE = (0, 2, 1, 3)
BF16 = jnp.bfloat16
F32 = jnp.float32
VMEM_LIMIT = 56 * 1024 * 1024
LANES = 128


def dot_rows(left, right):
    return jnp.dot(left, right, preferred_element_type=F32)


def dot_trans(left, right):
    return lax.dot_general(left, right, (((1,), (1,)), ((), ())), preferred_element_type=F32)


def dot_inner(left, right):
    return lax.dot_general(left, right, (((0,), (0,)), ((), ())), preferred_element_type=F32)


def exchange(values, axis, distance, size):
    return lax.ppermute(values, axis, [(i, i ^ distance) for i in range(size)])


def join(parts, axis=0):
    return jnp.concatenate(parts, axis=axis)


def cut(values, at, length, axis):
    return lax.dynamic_slice_in_dim(values, at, length, axis=axis)


def turn_pairs(values):
    step = values.shape[1] // 4
    return join([values[:, i * step : (i + 1) * step] for i in (1, 0, 3, 2)], 1)


def after(values, *others):
    return lax.optimization_barrier((values,) + others)[0]


def columns(heads, pairs, size):
    query, pair = heads // 2, pairs // 2
    block = (query + 2 * pair) * size + LANES
    of = lambda i, count, before: (i // count) * block + (before + i % count) * size
    return (
        [of(h, query, 0) for h in range(heads)],
        [of(p, pair, query) for p in range(pairs)],
        [of(p, pair, query + pair) for p in range(pairs)],
        [block - LANES, 2 * block - LANES],
    )


def post_kernel(raw_ref, cos_ref, sin_ref, query_gain_ref, key_gain_ref, q_ref, kv_ref, *, heads, pairs, size, factor):
    cosine = cos_ref[...]
    sine = sin_ref[...]
    query_at, key_at, value_at, _ = columns(heads, pairs, size)

    def turned(value, gain):
        inverse = lax.rsqrt(jnp.mean(value * value, axis=-1, keepdims=True) + EPS)
        normal = value * inverse * gain
        return normal * cosine + pltpu.roll(normal, size // 2, 1) * sine

    for h, at in enumerate(query_at):
        value = raw_ref[:, at : at + size]
        q_ref[:, h * size : (h + 1) * size] = (turned(value, query_gain_ref[...]) * factor).astype(BF16)
    for p, at in enumerate(key_at):
        kv_ref[:, p * size : (p + 1) * size] = turned(raw_ref[:, at : at + size], key_gain_ref[...]).astype(BF16)
    for p, at in enumerate(value_at):
        to = (pairs + p) * size
        kv_ref[:, to : to + size] = raw_ref[:, at : at + size].astype(BF16)


def post(raw, cosine, sine, query_gain, key_gain, heads, pairs, size, factor):
    rows, width = raw.shape
    step = 256
    return pl.pallas_call(
        functools.partial(post_kernel, heads=heads, pairs=pairs, size=size, factor=factor),
        grid=(rows // step,),
        in_specs=[
            pl.BlockSpec((step, width), lambda i: (i, 0)),
            pl.BlockSpec((step, size), lambda i: (i, 0)),
            pl.BlockSpec((step, size), lambda i: (i, 0)),
            pl.BlockSpec((1, size), lambda i: (0, 0)),
            pl.BlockSpec((1, size), lambda i: (0, 0)),
        ],
        out_specs=[
            pl.BlockSpec((step, heads * size), lambda i: (i, 0)),
            pl.BlockSpec((step, 2 * pairs * size), lambda i: (i, 0)),
        ],
        out_shape=[
            jax.ShapeDtypeStruct((rows, heads * size), BF16),
            jax.ShapeDtypeStruct((rows, 2 * pairs * size), BF16),
        ],
        cost_estimate=pl.CostEstimate(flops=rows * width * 20, bytes_accessed=rows * width * 8, transcendentals=0),
        name="post",
    )(raw, cosine, sine, query_gain[None], key_gain[None])


def back_kernel(
    dq_ref, dkv_ref, raw_ref, cos_ref, sin_ref, query_gain_ref, key_gain_ref, logit_ref, out_ref, gq_ref, gk_ref, *, heads, pairs, size, factor_q, factor_k
):
    cosine = cos_ref[...]
    sine = sin_ref[...]
    query_at, key_at, value_at, logit_at = columns(heads, pairs, size)

    @pl.when(pl.program_id(0) == 0)
    def _():
        gq_ref[...] = jnp.zeros_like(gq_ref)
        gk_ref[...] = jnp.zeros_like(gk_ref)

    def back(up, value, gain, total_ref):
        up = up * cosine - pltpu.roll(up, size // 2, 1) * sine
        inverse = lax.rsqrt(jnp.mean(value * value, axis=-1, keepdims=True) + EPS)
        hat = value * inverse
        total_ref[...] += jnp.sum(up * hat, axis=0, keepdims=True)
        scaled = up * gain
        return inverse * (scaled - hat * jnp.mean(scaled * hat, axis=-1, keepdims=True))

    for h, at in enumerate(query_at):
        up = dq_ref[:, h * size : (h + 1) * size] * factor_q
        out_ref[:, at : at + size] = back(up, raw_ref[:, at : at + size], query_gain_ref[...], gq_ref).astype(BF16)
    for p, at in enumerate(key_at):
        up = dkv_ref[:, p * size : (p + 1) * size].astype(F32) * factor_k
        out_ref[:, at : at + size] = back(up, raw_ref[:, at : at + size], key_gain_ref[...], gk_ref).astype(BF16)
    for p, at in enumerate(value_at):
        to = (pairs + p) * size
        out_ref[:, at : at + size] = dkv_ref[:, to : to + size].astype(BF16)
    for i, at in enumerate(logit_at):
        out_ref[:, at : at + LANES] = logit_ref[:, i * LANES : (i + 1) * LANES].astype(BF16)


def project_back(dq, dkv, raw, cosine, sine, query_gain, key_gain, logit_grad, heads, pairs, size, factor_q, factor_k):
    rows, width = raw.shape
    step = 256
    row = lambda cols: pl.BlockSpec((step, cols), lambda i: (i, 0))
    one = pl.BlockSpec((1, size), lambda i: (0, 0))
    return pl.pallas_call(
        functools.partial(back_kernel, heads=heads, pairs=pairs, size=size, factor_q=factor_q, factor_k=factor_k),
        grid=(rows // step,),
        in_specs=[row(heads * size), row(2 * pairs * size), row(width), row(size), row(size), one, one, row(2 * LANES)],
        out_specs=[row(width), one, one],
        out_shape=[
            jax.ShapeDtypeStruct((rows, width), BF16),
            jax.ShapeDtypeStruct((1, size), F32),
            jax.ShapeDtypeStruct((1, size), F32),
        ],
        cost_estimate=pl.CostEstimate(flops=rows * width * 30, bytes_accessed=rows * width * 12, transcendentals=0),
        name="project_back",
    )(dq, dkv, raw, cosine, sine, query_gain[None], key_gain[None], logit_grad)


def places(table_ref, stripe, step, length):
    turn = table_ref[stripe, 3]
    core = table_ref[stripe, 4]
    half = length // 2
    blocks = half // step

    def pair(i):
        at = jnp.bitwise_xor(i, turn) * step
        return pl.ds(pl.multiple_of(at, step), step), pl.ds(pl.multiple_of(at + half // 2, step), step)

    def single(b):
        part = b // blocks
        inner = b - part * blocks
        at = part * half + jnp.bitwise_xor(inner % 2, core) * (half // 2) + jnp.bitwise_xor(inner // 2, turn) * step
        return (pl.ds(pl.multiple_of(at, step), step),)

    return pair, single


def logit_of(head, heads, own_ref, other_ref):
    half = heads // 2
    at = head % half
    return (own_ref if head < half else other_ref)[:, at : at + 1]


def logit_specs(raw, heads, pairs, size, step):
    spec = lambda i: pl.BlockSpec((step, LANES), lambda s, t: (s, i))
    return [spec(at // LANES) for at in columns(heads, pairs, size)[3]]


def forward_kernel(table_ref, q_ref, kv_ref, row_ref, start_ref, own_ref, other_ref, gated_ref, context_ref, inverse_ref, *, pairs, repeat, size, step):
    stripe = pl.program_id(0)
    wide_blocks = table_ref[stripe, 0]
    low = table_ref[stripe, 1]
    high = table_ref[stripe, 2]
    pair, single = places(table_ref, stripe, step, kv_ref.shape[0])
    rows = row_ref[...]
    starts = start_ref[...]
    rows = jnp.concatenate([rows] * repeat, axis=0)
    starts = jnp.concatenate([starts] * repeat, axis=0)
    for k in range(pairs):
        heads = [k * repeat + r for r in range(repeat)]
        query = jnp.concatenate([q_ref[:, h * size : (h + 1) * size] for h in heads], axis=0)
        key_cols = slice(k * size, (k + 1) * size)
        value_cols = slice((pairs + k) * size, (pairs + k + 1) * size)

        def seen(total, where, first):
            keys = join([kv_ref[at, key_cols] for at in where])
            weights = jnp.exp2(dot_trans(query, keys))
            if first is not None:
                index = first + lax.broadcasted_iota(jnp.int32, weights.shape, 1)
                weights = jnp.where((index <= rows) & (index >= starts), weights, 0.0)
            values = join([kv_ref[at, value_cols] for at in where])
            values = jnp.concatenate([values, jnp.ones_like(values)], axis=1)
            return total + dot_rows(weights.astype(BF16), values)

        total = jnp.zeros((query.shape[0], 2 * size), F32)
        total = lax.fori_loop(0, wide_blocks, lambda i, t: seen(t, pair(i), None), total)
        total = lax.fori_loop(low, high + 1, lambda i, t: seen(t, single(i), i * step), total)
        inverse = 1.0 / total[:, size:]
        context = total[:, :size] * inverse
        for r, h in enumerate(heads):
            part = context[r * step : (r + 1) * step]
            cols = slice(h * size, (h + 1) * size)
            gate = jax.nn.sigmoid(logit_of(h, pairs * repeat, own_ref, other_ref))
            gated_ref[:, cols] = (part * gate).astype(BF16)
            context_ref[:, cols] = part
            inverse_ref[:, cols] = inverse[r * step : (r + 1) * step]


def attend(table, q, kv, rows, starts, raw, pairs, size):
    length, cols = q.shape
    heads = cols // size
    step = length // table.shape[0]
    block = lambda width: pl.BlockSpec((step, width), lambda i, t: (i, 0))
    return pl.pallas_call(
        functools.partial(forward_kernel, pairs=pairs, repeat=heads // pairs, size=size, step=step),
        grid_spec=pltpu.PrefetchScalarGridSpec(
            num_scalar_prefetch=1,
            grid=(length // step,),
            in_specs=[
                block(cols),
                pl.BlockSpec(kv.shape, lambda i, t: (0, 0), pipeline_mode=pl.Buffered(1)),
                block(1),
                block(1),
                *logit_specs(raw, heads, pairs, size, step),
            ],
            out_specs=[block(cols), block(cols), block(cols)],
        ),
        out_shape=[
            jax.ShapeDtypeStruct((length, cols), BF16),
            jax.ShapeDtypeStruct((length, cols), F32),
            jax.ShapeDtypeStruct((length, cols), F32),
        ],
        compiler_params=pltpu.CompilerParams(vmem_limit_bytes=VMEM_LIMIT),
        cost_estimate=pl.CostEstimate(flops=20 * 10**9, bytes_accessed=12 * 10**6, transcendentals=7 * 10**6),
        name="attend",
    )(table, q, kv, rows, starts, raw, raw)


def backward_kernel(
    table_ref, q_ref, kv_ref, row_ref, start_ref, own_ref, other_ref, context_ref, inverse_ref, grad_ref,
    dq_ref, dkv_ref, dlogit_ref, sums_ref, *, pairs, repeat, size, step,
):
    stripe = pl.program_id(0)
    wide_blocks = table_ref[stripe, 0]
    low = table_ref[stripe, 1]
    high = table_ref[stripe, 2]
    pair, single = places(table_ref, stripe, step, kv_ref.shape[0])

    @pl.when(stripe == 0)
    def _():
        sums_ref[...] = jnp.zeros_like(sums_ref)

    dlogit_ref[...] = jnp.zeros_like(dlogit_ref)
    rows = jnp.concatenate([row_ref[0]] * repeat, axis=1)
    starts = jnp.concatenate([start_ref[0]] * repeat, axis=1)
    for k in range(pairs):
        heads = [k * repeat + r for r in range(repeat)]
        query = jnp.concatenate([q_ref[:, h * size : (h + 1) * size] for h in heads], axis=0)
        grads, inners = [], []
        for h in heads:
            cols = slice(h * size, (h + 1) * size)
            up = grad_ref[:, cols]
            gate = jax.nn.sigmoid(logit_of(h, pairs * repeat, own_ref, other_ref))
            product = jnp.sum(up * context_ref[:, cols], axis=1, keepdims=True)
            half = pairs * repeat // 2
            at = h // half * LANES + h % half
            dlogit_ref[:, at : at + 1] = product * gate * (1.0 - gate)
            inverse = inverse_ref[:, cols]
            grads.append((up * gate * inverse).astype(BF16))
            inners.append(product * gate * inverse)
        grad = jnp.concatenate(grads, axis=0)
        inner = jnp.transpose(jnp.concatenate(inners, axis=0))[0:1]
        key_cols = slice(k * size, (k + 1) * size)
        value_cols = slice((pairs + k) * size, (pairs + k + 1) * size)

        def seen(total, where, first):
            keys = join([kv_ref[at, key_cols] for at in where])
            weights = jnp.exp2(dot_trans(keys, query))
            if first is not None:
                index = first + lax.broadcasted_iota(jnp.int32, weights.shape, 0)
                weights = jnp.where((index <= rows) & (index >= starts), weights, 0.0)
            changes = dot_trans(join([kv_ref[at, value_cols] for at in where]), grad)
            changes = (weights * (changes - inner)).astype(BF16)
            value_sums = dot_rows(weights.astype(BF16), grad)
            key_sums = dot_rows(changes, query)
            for i, at in enumerate(where):
                sums_ref[at, value_cols] += value_sums[i * step : (i + 1) * step]
                sums_ref[at, key_cols] += key_sums[i * step : (i + 1) * step]
            return total + dot_inner(changes, keys)

        total = jnp.zeros((query.shape[0], size), F32)
        total = lax.fori_loop(0, wide_blocks, lambda i, t: seen(t, pair(i), None), total)
        total = lax.fori_loop(low, high + 1, lambda i, t: seen(t, single(i), i * step), total)
        for r, h in enumerate(heads):
            dq_ref[:, h * size : (h + 1) * size] = total[r * step : (r + 1) * step]

    @pl.when(stripe == pl.num_programs(0) - 1)
    def _():
        dkv_ref[...] = sums_ref[...].astype(BF16)


def attend_back(table, q, kv, rows, starts, raw, context, inverse, grad, pairs, size):
    length, cols = q.shape
    heads = cols // size
    step = length // table.shape[0]
    block = lambda width: pl.BlockSpec((step, width), lambda i, t: (i, 0))
    whole = pl.BlockSpec(kv.shape, lambda i, t: (0, 0), pipeline_mode=pl.Buffered(1))
    lane = pl.BlockSpec((1, 1, step), lambda i, t: (i, 0, 0))
    logits = logit_specs(raw, heads, pairs, size, step)
    return pl.pallas_call(
        functools.partial(backward_kernel, pairs=pairs, repeat=heads // pairs, size=size, step=step),
        grid_spec=pltpu.PrefetchScalarGridSpec(
            num_scalar_prefetch=1,
            grid=(length // step,),
            in_specs=[block(cols), whole, lane, lane, *logits, block(cols), block(cols), block(cols)],
            out_specs=[block(cols), whole, block(2 * LANES)],
            scratch_shapes=[pltpu.VMEM(kv.shape, F32)],
        ),
        out_shape=[
            jax.ShapeDtypeStruct((length, cols), F32),
            jax.ShapeDtypeStruct(kv.shape, BF16),
            jax.ShapeDtypeStruct((length, 2 * LANES), F32),
        ],
        compiler_params=pltpu.CompilerParams(vmem_limit_bytes=VMEM_LIMIT),
        cost_estimate=pl.CostEstimate(flops=50 * 10**9, bytes_accessed=20 * 10**6, transcendentals=7 * 10**6),
        name="attend_back",
    )(table, q, kv, rows.reshape(-1, 1, step), starts.reshape(-1, 1, step), raw, raw, context, inverse, grad)


class Wires:
    def __init__(self, send_sems, recv_sems, local_sems, sizes):
        self.send_sems, self.recv_sems, self.local_sems = send_sems, recv_sems, local_sems
        self.sizes = sizes
        self.sent, self.local, self.open = [], [], []
        self.locals_used, self.sends_used = 0, 0
        self.dp, self.wide, self.narrow = (lax.axis_index(a) for a in ("dp", "wide", "narrow"))
        self.y, self.core = self.narrow // 2, self.narrow % 2
        self.x, self.far = self.dp % 2, self.wide // 2

    def peer(self, axis, distance):
        at = {"dp": self.dp, "wide": self.wide, "narrow": self.narrow}[axis]
        bit = at // distance % 2
        return {axis: at + distance * (1 - 2 * bit) if distance < 3 else 3 - at}

    def greet(self, peers):
        barrier = pltpu.get_barrier_semaphore()
        for to in peers:
            pl.semaphore_signal(barrier, inc=1, device_id=self.peer(*to), device_id_type=pl.DeviceIdType.MESH)
        pl.semaphore_wait(barrier, len(peers))

    def make(self, source, target, to):
        i = self.sends_used
        self.sends_used += 1
        copy = pltpu.make_async_remote_copy(
            src_ref=source, dst_ref=target, send_sem=self.send_sems.at[i], recv_sem=self.recv_sems.at[i],
            device_id=self.peer(*to), device_id_type=pl.DeviceIdType.MESH,
        )
        self.sent.append(copy)
        return copy

    def send(self, source, target, to):
        copy = self.make(source, target, to)
        copy.start()
        self.open.append(copy)
        return copy

    def arrived(self, copy):
        copy.wait_recv()
        self.open = [other for other in self.open if other is not copy]

    def copy(self, source, target):
        copy = pltpu.make_async_copy(source, target, self.local_sems.at[self.locals_used])
        self.locals_used += 1
        copy.start()
        self.local.append(copy)
        return copy

    def finish(self):
        for copy in list(self.open):
            self.arrived(copy)
        for copy in self.sent:
            copy.wait_send()
        for copy in self.local:
            copy.wait()


Y, CORE, CORNER, NEAR, FAR, X = ("narrow", 2), ("narrow", 1), ("narrow", 3), ("wide", 1), ("wide", 2), ("dp", 1)


def local_flow(net, values_ref, rows_ref):
    rows, width = rows_ref.shape[0], values_ref.shape[1]
    half = width // 2
    out = []
    for distance, to in ((0, None), (1, CORE), (2, Y), (3, CORNER)):
        target = net.narrow if to is None else net.peer(*to)["narrow"]
        at = (2 * (distance % 2) + net.y) * width
        for j in range(2):
            sub = net.x if j == 0 else 1 - net.x
            source = values_ref.at[pl.ds(pl.multiple_of(target * rows, rows), rows), pl.ds(pl.multiple_of(sub * half, half), half)]
            goal = rows_ref.at[:, pl.ds(pl.multiple_of(at + j * half, half), half)]
            out.append(net.copy(source, goal) if to is None else net.send(source, goal, to))
    return out


def gather_flow(net, values_ref, all_ref):
    rows = values_ref.shape[0]
    half = rows // 2
    part = lambda i: all_ref.at[pl.ds(i * half, half), :]
    first, second = values_ref.at[pl.ds(0, half), :], values_ref.at[pl.ds(half, half), :]
    first_y = net.send(first, part(2), Y)
    second_z = net.send(second, part(5), NEAR)
    net.send(first, part(4), NEAR)
    net.send(second, part(3), Y)
    net.copy(values_ref, all_ref.at[pl.ds(0, rows), :])
    yield
    net.arrived(first_y)
    net.send(part(2), part(6), NEAR)
    yield
    net.arrived(second_z)
    net.send(part(5), part(7), Y)
    yield


def weight_flow(net, source_ref, out_ref, axis, own, other, across, from_y=None, from_far=None):
    step = source_ref.shape[axis] // 2
    count = source_ref.shape[axis]

    def window(ref, at, start):
        long, wide = pl.ds(pl.multiple_of(at, step), step), pl.ds(start, across)
        return ref.at[long, wide] if axis == 0 else ref.at[wide, long]

    y, x = net.y, net.x
    piece = lambda sub, half: window(source_ref, sub * step, pl.multiple_of(half * across, across))
    place = lambda slot, j, start: window(out_ref, slot * count + j * step, start)
    mine, rest = piece(x, y), piece(1 - x, y)
    net.copy(mine, place(y, 0, own))
    net.copy(rest, place(y, 1, own))
    if from_y is None:
        come_y = net.send(piece(x, 1 - y), place(y, 0, own), Y)
    else:
        net.copy(from_y, place(1 - y, 0, own))
    if from_far is None:
        come_far = net.send(mine, place(y, 0, other), FAR)
    else:
        net.copy(from_far, place(y, 0, other))
    net.send(mine, place(2 + y, 0, own), CORE)
    net.send(rest, place(2 + y, 1, own), CORE)
    if from_y is None:
        yield
        net.arrived(come_y)
        from_y = place(1 - y, 0, own)
    come_both = net.send(from_y, place(1 - y, 0, other), FAR)
    their_y = net.send(from_y, place(1 - y, 1, own), X)
    net.send(from_y, place(3 - y, 0, own), CORE)
    if from_far is None:
        yield
        net.arrived(come_far)
        from_far = place(y, 0, other)
    their_far = net.send(from_far, place(y, 1, other), X)
    net.send(from_far, place(2 + y, 0, other), CORE)
    yield
    net.arrived(come_both)
    both = place(1 - y, 0, other)
    their_both = net.send(both, place(1 - y, 1, other), X)
    net.send(both, place(3 - y, 0, other), CORE)
    yield
    for copy, slot, start in ((their_y, 1 - y, own), (their_far, y, other), (their_both, 1 - y, other)):
        net.arrived(copy)
        net.send(place(slot, 1, start), place(slot + 2, 1, start), CORE)
    yield


def run(flow):
    return next(flow, None)


def by_rows(count, body):
    step = 16
    lax.fori_loop(0, count // step, lambda i, _: (body(pl.ds(pl.multiple_of(i * step, step), step)), 0)[1], 0)


def begin_kernel(
    tokens_ref, cotangent_ref, gain_ref, qkv_ref, out_ref, x_ref, rows_ref, all_ref, joined_ref, output_ref,
    here, normed, there, send, recv, local, *, sizes,
):
    net = Wires(send, recv, local, sizes)
    net.greet([Y, CORE, CORNER, NEAR, FAR, X])
    rows = local_flow(net, tokens_ref, here)
    across = qkv_ref.shape[1] // 2
    joined = weight_flow(net, qkv_ref, joined_ref, 0, 0, across, across)
    run(joined)
    rows[0].wait()
    rows[1].wait()
    net.local = net.local[2:]
    for copy in rows[2:]:
        net.arrived(copy)

    def norm(at):
        values = here[at, :].astype(F32)
        inverse = lax.rsqrt(jnp.mean(values * values, axis=1, keepdims=True) + EPS)
        normed[at, :] = (values * inverse * gain_ref[...]).astype(BF16)
        x_ref[at, :] = here[at, :]

    by_rows(here.shape[0], norm)
    gather = gather_flow(net, normed, all_ref)
    run(gather)
    across = out_ref.shape[0] // 2
    output = weight_flow(net, out_ref, output_ref, 1, 0, across, across)
    for flow in (joined, gather, output, joined, gather):
        run(flow)
    rows = local_flow(net, cotangent_ref, there)
    for flow in (joined, output, joined, output, output, output):
        run(flow)
    for copy in rows[:2]:
        copy.wait()
    net.local = [copy for copy in net.local if all(copy is not other for other in rows[:2])]
    for copy in rows[2:]:
        net.arrived(copy)
    net.copy(there, rows_ref)
    net.finish()


ANY = pl.BlockSpec(memory_space=pl.ANY)
VMEM = pl.BlockSpec(memory_space=pltpu.VMEM)


def sems(sends, locals_):
    return [pltpu.SemaphoreType.DMA((sends,)), pltpu.SemaphoreType.DMA((sends,)), pltpu.SemaphoreType.DMA((locals_,))]


def wire_call(kernel, name, number, specs, out_specs, shapes, scratch, sizes, cost, *args):
    return pl.pallas_call(
        functools.partial(kernel, sizes=sizes),
        in_specs=specs,
        out_specs=out_specs,
        out_shape=[jax.ShapeDtypeStruct(*shape) for shape in shapes],
        scratch_shapes=scratch,
        compiler_params=pltpu.CompilerParams(collective_id=number, has_side_effects=True, vmem_limit_bytes=VMEM_LIMIT),
        cost_estimate=pl.CostEstimate(flops=0, bytes_accessed=cost * 3 * 10**6, transcendentals=0),
        name=name,
    )(*args)


def begin(tokens, cotangent, gain, qkv, out, sizes):
    rows, width = tokens.shape[0] // sizes["narrow"], gain.shape[0]
    row = pltpu.VMEM((rows, width), BF16)
    return wire_call(
        begin_kernel, "begin", 1, [ANY, ANY, VMEM, VMEM, VMEM], [VMEM, ANY, ANY, ANY, ANY],
        [
            ((rows, width), BF16), ((rows, width), BF16), ((4 * rows, width), BF16), ((width, qkv.shape[1]), BF16),
            ((out.shape[0], width), BF16),
        ],
        [row, row, row, *sems(48, 16)], sizes, 55, tokens, cotangent, gain[None], qkv, out,
    )


def keys_kernel(kv_ref, keys_ref, send, recv, local, *, sizes):
    net = Wires(send, recv, local, sizes)
    net.greet([CORE, FAR])
    count, width = kv_ref.shape
    size = width // 4
    part = lambda i, j: keys_ref.at[pl.ds(i, count), pl.ds(j * size, size)]
    base = pl.multiple_of(net.far * 2 * count, count)
    far = [net.make(kv_ref.at[:, pl.ds(j * size, size)], part(0, j ^ 1), FAR) for j in range(4)]
    on = [net.make(part(0, j ^ 1), part(count, j ^ 1), CORE) for j in range(4)]

    @pl.when(net.far == 0)
    def _():
        for copy in far:
            copy.start()

    net.copy(kv_ref, keys_ref.at[pl.ds(base, count), :])
    net.send(kv_ref, keys_ref.at[pl.ds(base + count, count), :], CORE)

    @pl.when(net.far == 1)
    def _():
        for copy, forward in zip(far, on):
            copy.wait_recv()
            forward.start()
        for forward in on:
            forward.wait()

    @pl.when(net.far == 0)
    def _():
        for copy in far:
            copy.wait_send()

    net.sent = [copy for copy in net.sent if all(copy is not other for other in far + on)]
    net.finish()


def exchange_keys(kv, sizes):
    return wire_call(
        keys_kernel, "keys", 2, [VMEM], [ANY], [((4 * kv.shape[0], kv.shape[1]), BF16)], [*sems(16, 4)], sizes, 45, kv,
    )[0]


def scatter_flow(net, partial_ref, first_ref, second_ref, send_ref, last_ref, total_ref):
    half = partial_ref.shape[0] // 8
    part = lambda i: partial_ref.at[pl.ds(i * half, half), :]
    slot = lambda ref, i: ref.at[pl.ds(i * half, half), :]
    to_z = [net.send(part(6), slot(first_ref, 1), NEAR), net.send(part(4), slot(first_ref, 0), NEAR)]
    to_y = [net.send(part(7), slot(second_ref, 1), Y), net.send(part(3), slot(second_ref, 0), Y)]
    yield

    def add(out_ref, to, i, ref, j):
        def body(at):
            move = lambda start: pl.ds(pl.multiple_of(at.start + start, 16), at.size)
            value = partial_ref[move(i * half), :].astype(F32) + ref[move(j * half), :].astype(F32)
            out_ref[move(to), :] = value.astype(out_ref.dtype)

        by_rows(half, body)

    net.arrived(to_z[0])
    add(send_ref, 0, 2, first_ref, 1)
    last_y = net.send(slot(send_ref, 0), slot(last_ref, 0), Y)
    net.arrived(to_y[0])
    add(send_ref, half, 5, second_ref, 1)
    last_z = net.send(slot(send_ref, 1), slot(last_ref, 1), NEAR)
    yield
    net.arrived(to_z[1])
    add(total_ref, 0, 0, first_ref, 0)
    net.arrived(to_y[1])
    add(total_ref, half, 1, second_ref, 0)
    yield
    net.arrived(last_y)
    net.arrived(last_z)
    yield


def middle_kernel(
    partial_ref, x_ref, gain_ref, gate_ref, up_ref, down_ref, gate_y_ref, up_y_ref, down_y_ref, gate_far_ref, up_far_ref, down_far_ref,
    middle_ref, all_ref, both_ref, last_ref,
    first, second, sums, last, total, normed, send, recv, local, *, sizes,
):
    net = Wires(send, recv, local, sizes)
    net.greet([Y, CORE, NEAR, FAR, X])
    scatter = scatter_flow(net, partial_ref, first, second, sums, last, total)
    run(scatter)
    across = gate_ref.shape[1] // 2
    flows = [
        weight_flow(net, gate_ref, both_ref, 0, 0, across, across, gate_y_ref, gate_far_ref),
        weight_flow(net, up_ref, both_ref, 0, 2 * across, 3 * across, across, up_y_ref, up_far_ref),
        weight_flow(net, down_ref, last_ref, 1, 0, across, across, down_y_ref, down_far_ref),
    ]
    for flow in flows:
        run(flow)
    run(scatter)
    run(scatter)
    run(scatter)

    def norm(at):
        values = x_ref[at, :].astype(F32) + total[at, :] + last[at, :].astype(F32)
        middle_ref[at, :] = values
        inverse = lax.rsqrt(jnp.mean(values * values, axis=1, keepdims=True) + EPS)
        normed[at, :] = (values * inverse * gain_ref[...]).astype(BF16)

    by_rows(normed.shape[0], norm)
    gather = gather_flow(net, normed, all_ref)
    run(gather)
    run(flows[0])
    run(flows[1])
    run(gather)
    run(flows[2])
    run(gather)
    for flow in flows:
        run(flow)
    net.finish()


def to_middle(partial, x, gain, gate, up, down, pieces, sizes):
    rows, width = x.shape
    buffer = lambda n, kind: pltpu.VMEM((n, width), kind)
    return wire_call(
        middle_kernel, "middle", 3, [VMEM] * 12, [VMEM, ANY, ANY, ANY],
        [((rows, width), F32), ((4 * rows, width), BF16), ((width, 2 * gate.shape[1]), BF16), ((down.shape[0], width), BF16)],
        [
            buffer(rows, BF16), buffer(rows, BF16), buffer(rows, BF16), buffer(rows, BF16), buffer(rows, F32), buffer(rows, BF16),
            *sems(64, 16),
        ],
        sizes, 80, partial, x, gain[None], gate, up, down, *pieces,
    )


def spread_flow(net, rows_ref, out_ref):
    rows, width = rows_ref.shape[0], out_ref.shape[1]
    half = width // 2
    base = pl.multiple_of(net.narrow * rows, rows)
    for distance, to in ((3, CORNER), (2, Y), (1, CORE), (0, None)):
        target = net.narrow if to is None else net.peer(*to)["narrow"]
        at = (2 * (distance % 2) + target // 2) * width
        for j in range(2):
            sub = net.x if j == 0 else 1 - net.x
            source = rows_ref.at[:, pl.ds(pl.multiple_of(at + j * half, half), half)]
            goal = out_ref.at[pl.ds(base, rows), pl.ds(pl.multiple_of(sub * half, half), half)]
            if to is None:
                net.copy(source, goal)
            else:
                net.send(source, goal, to)


def add_rows(target, terms):
    ref, (rows, cols) = target

    def body(at):
        move = lambda r: pl.ds(pl.multiple_of(at.start + r.start, 16), at.size)
        value = sum(term[move(r), c].astype(F32) for term, (r, c) in terms)
        ref[move(rows), cols] = value.astype(BF16)

    by_rows(rows.size, body)


class Gradient:
    def __init__(self, net, axis, step, across):
        self.net, self.axis, self.step, self.across = net, axis, step, across
        self.order = (1 - net.y, net.y)
        self.x, self.far = [], []

    def window(self, at, start, count, length=None):
        step = self.step if length is None else length
        hint = lambda v, unit: v if isinstance(v, int) else pl.multiple_of(v, unit)
        along, wide = pl.ds(hint(at, self.step), step), pl.ds(hint(start, self.across), count)
        return (along, wide) if self.axis == 0 else (wide, along)

    def start(self, g_ref, acc, from_core):
        self.acc, self.from_core = acc, from_core
        count = 4 * self.step
        own, other = (self.window(i * count, 0, 2 * self.across, count) for i in range(2))
        self.loaded = self.net.copy(g_ref.at[own], acc)
        self.core = self.net.send(g_ref.at[other], from_core, CORE)

    def wait_core(self):
        self.loaded.wait()
        self.net.local = [copy for copy in self.net.local if copy is not self.loaded]
        self.net.arrived(self.core)

    def core_to_x(self, from_x):
        self.wait_core()
        self.from_x = from_x
        for slot in self.order:
            place = self.window((2 * slot + 1) * self.step, 0, 2 * self.across)
            add_rows((self.acc, place), [(self.acc, place), (self.from_core, place)])
            goal = from_x.at[self.window(slot * self.step, 0, 2 * self.across)]
            self.x.append(self.net.send(self.acc.at[place], goal, X))

    def x_end(self, k, from_far=None):
        slot = self.order[k]
        self.net.arrived(self.x[k])
        for start in (self.across, 0):
            place = self.window(2 * slot * self.step, start, self.across)
            come = self.window(slot * self.step, start, self.across)
            add_rows((self.acc, place), [(self.acc, place), (self.from_core, place), (self.from_x, come)])
            if start and from_far is not None:
                self.from_far = from_far
                goal = from_far.at[self.window(slot * self.step, 0, self.across)]
                self.far.append(self.net.send(self.acc.at[place], goal, FAR))

    def far_end(self, k, result=None):
        slot = self.order[k]
        self.net.arrived(self.far[k])
        place = self.window(2 * slot * self.step, 0, self.across)
        come = self.window(slot * self.step, 0, self.across)
        add_rows((self.acc, place), [(self.acc, place), (self.from_far, come)])

    def to_owner(self, k, source, out):
        net, across = self.net, self.across
        goal = out.at[self.window(net.x * self.step, net.y * across, across)]
        if k == 0:
            self.out = out
            self.y = net.send(source, goal, Y)
        else:
            net.copy(source, goal)
            net.send(source, goal, X)

    def after_y(self):
        net, across = self.net, self.across
        net.arrived(self.y)
        place = self.out.at[self.window(net.x * self.step, (1 - net.y) * across, across)]
        net.send(place, place, X)

    def slot(self, k, stride, start, count):
        return self.window(stride * self.order[k] * self.step, start, count)


def row_back(grad, values, gain):
    inverse = lax.rsqrt(jnp.mean(values * values, axis=1, keepdims=True) + EPS)
    hat = values * inverse
    scaled = grad * gain
    inner = jnp.mean(scaled * hat, axis=1, keepdims=True)
    return jnp.sum(grad * hat, axis=0, keepdims=True), inverse * (scaled - hat * inner)


def turn_kernel(
    partial_ref, middle_ref, upstream_ref, gain_ref, down_ref, gate_ref, up_ref,
    grad_ref, all_ref, term_ref, down_out, gate_out, up_keep, up_send,
    first, second, sums, last, total, low, *rest, sizes,
):
    buffers, (send, recv, local) = rest[:-3], rest[-3:]
    net = Wires(send, recv, local, sizes)
    net.greet([Y, CORE, NEAR, FAR, X])
    scatter = scatter_flow(net, partial_ref, first, second, sums, last, total)
    run(scatter)
    step, across = low.shape[1] // sizes["narrow"] // 2, gate_ref.shape[1] // 2
    down, gate, up = (Gradient(net, axis, step, across) for axis in (1, 0, 0))
    down.start(down_ref, *buffers[0:2])
    gate.start(gate_ref, *buffers[4:6])
    up.start(up_ref, *buffers[7:9])
    down.core_to_x(buffers[2])
    gate.core_to_x(buffers[6])
    run(scatter)
    down.x_end(0, buffers[3])
    run(scatter)
    run(scatter)
    term_ref[...] = jnp.zeros_like(term_ref)

    def rows(at):
        grad = total[at, :] + last[at, :].astype(F32)
        term, change = row_back(grad, middle_ref[at, :], gain_ref[...])
        term_ref[...] += term
        value = upstream_ref[at, :].astype(F32) + change
        grad_ref[at, :] = value
        low[at, :] = value.astype(BF16)

    by_rows(low.shape[0], rows)
    gather = gather_flow(net, low, all_ref)
    run(gather)
    down.x_end(1, buffers[3])
    run(gather)
    run(gather)
    up.wait_core()
    for slot in range(2):
        for j, ref in ((1, up_send), (0, up_keep)):
            place = up.window((2 * slot + j) * step, 0, 2 * across)
            add_rows((up.acc, place), [(up.acc, place), (up.from_core, place)])
            net.copy(up.acc.at[place], ref.at[up.window(slot * step, 0, 2 * across)])
    for k in range(2):
        gate.x_end(k)
        net.copy(gate.acc.at[gate.slot(k, 2, 0, 2 * across)], gate_out.at[gate.slot(k, 1, 0, 2 * across)])
    for k in range(2):
        down.far_end(k)
        net.copy(down.acc.at[down.slot(k, 2, 0, across)], down_out.at[down.slot(k, 1, 0, across)])
    net.finish()


def gradient_buffers(size, across, axis, count=4):
    shape = lambda a, b: pltpu.VMEM((a, b) if axis == 0 else (b, a), BF16)
    every = [shape(2 * size, 2 * across), shape(2 * size, 2 * across), shape(size, 2 * across), shape(size, across)]
    return every[:count]


def scatter_buffers(rows, width):
    buffer = lambda kind: pltpu.VMEM((rows, width), kind)
    return [buffer(BF16), buffer(BF16), buffer(BF16), buffer(BF16), buffer(F32)]


def turn(partial, middle, upstream, gain, down, gate, up, sizes):
    rows, width = middle.shape
    size, across = width // sizes["narrow"], down.shape[0] // 2
    return wire_call(
        turn_kernel, "turn", 4, [VMEM] * 4 + [ANY] * 3, [VMEM, ANY, VMEM, ANY, ANY, ANY, ANY],
        [
            ((rows, width), F32), ((4 * rows, width), BF16), ((1, width), F32),
            ((across, size), BF16), ((size, 2 * across), BF16), ((size, 2 * across), BF16), ((size, 2 * across), BF16),
        ],
        [
            *scatter_buffers(rows, width), pltpu.VMEM((rows, width), BF16),
            *gradient_buffers(size, across, 1), *gradient_buffers(size, across, 0, 3), *gradient_buffers(size, across, 0, 2), *sems(40, 16),
        ],
        sizes, 80, partial, middle, upstream, gain[None], down, gate, up,
    )


def owner_kernel(
    dkv_ref, partial_ref, middle_ref, down_ref, gate_ref, gate_far_ref, up_ref, up_x_ref,
    mine_ref, layer_ref, down_out, gate_out, up_out,
    prompt_core, rest_core, prompt, prompt_far, first, second, sums, last, total, rows_low, gate_sums, up_acc, up_far, up_sums,
    send, recv, local, *, sizes,
):
    net = Wires(send, recv, local, sizes)
    net.greet([Y, CORE, CORNER, NEAR, FAR, X])
    count, width = prompt.shape
    size = width // 4
    region = lambda i: dkv_ref.at[pl.ds(i * count, count), :]
    come = net.send(region(1), prompt_core, CORE)
    rest = net.send(region(3), rest_core, CORE)
    scatter = scatter_flow(net, partial_ref, first, second, sums, last, total)
    run(scatter)
    step, across = down_ref.shape[1] // 2, down_ref.shape[0]
    down, gate, up = (Gradient(net, axis, step, across) for axis in (1, 0, 0))
    for k in range(2):
        down.to_owner(k, down_ref.at[down.slot(k, 1, 0, across)], down_out)
    net.arrived(come)

    def add(at):
        prompt[at, :] = (dkv_ref[at, :].astype(F32) + prompt_core[at, :].astype(F32)).astype(BF16)

    by_rows(count, add)
    cols = lambda ref, j: ref.at[:, pl.ds(j * size, size)]
    far = [net.make(cols(prompt, j), cols(prompt_far, j ^ 1), FAR) for j in range(4)]

    @pl.when(net.far == 1)
    def _():
        for copy in far:
            copy.start()

    for k in range(2):
        for start in (across, 0):
            place = up.slot(k, 1, start, across)
            add_rows((up_acc, place), [(up_ref, place), (up_x_ref, place)])
            if start:
                up.far.append(net.send(up_acc.at[place], up_far.at[up.slot(k, 1, 0, across)], FAR))
    for k in range(2):
        place = gate.slot(k, 1, 0, across)
        add_rows((gate_sums, place), [(gate_ref, place), (gate_far_ref, place)])
        gate.to_owner(k, gate_sums.at[place], gate_out)
    run(scatter)
    run(scatter)
    run(scatter)

    def rows(at):
        rows_low[at, :] = (middle_ref[at, :] + total[at, :] + last[at, :].astype(F32)).astype(BF16)

    by_rows(rows_low.shape[0], rows)
    spread_flow(net, rows_low, layer_ref)
    down.after_y()
    gate.after_y()
    net.arrived(rest)

    @pl.when(net.far == 1)
    def _():
        def add(at):
            move = pl.ds(pl.multiple_of(at.start + 2 * count, 16), at.size)
            mine_ref[at, :] = dkv_ref[move, :].astype(F32) + rest_core[at, :].astype(F32)

        by_rows(count, add)
        for copy in far:
            copy.wait_send()

    @pl.when(net.far == 0)
    def _():
        for copy in far:
            copy.wait_recv()

        def add(at):
            mine_ref[at, :] = dkv_ref[at, :].astype(F32) + prompt_core[at, :].astype(F32) + prompt_far[at, :].astype(F32)

        by_rows(count, add)

    net.sent = [copy for copy in net.sent if all(copy is not other for other in far)]
    for k in range(2):
        net.arrived(up.far[k])
        place = up.slot(k, 1, 0, across)
        add_rows((up_sums, place), [(up_acc, place), (up_far, place)])
        up.to_owner(k, up_sums.at[place], up_out)
    up.after_y()
    net.finish()


def to_owner(dkv, partial, middle, down, gate, gate_far, up, up_x, sizes):
    rows, width = middle.shape
    size, across = width // sizes["narrow"], gate_far.shape[1]
    count = dkv.shape[0] // 4
    block = lambda: pltpu.VMEM((count, dkv.shape[1]), BF16)
    part = lambda wide: pltpu.VMEM((size, wide), BF16)
    return wire_call(
        owner_kernel, "owner", 5, [VMEM] * 8, [VMEM, ANY, ANY, ANY, ANY],
        [
            ((count, dkv.shape[1]), F32), ((sizes["narrow"] * rows, size), BF16),
            ((2 * across, size), BF16), ((size, 2 * across), BF16), ((size, 2 * across), BF16),
        ],
        [
            block(), block(), block(), block(), *scatter_buffers(rows, width), pltpu.VMEM((rows, width), BF16),
            part(across), part(2 * across), part(across), part(across), *sems(40, 16),
        ],
        sizes, 80, dkv, partial, middle, down, gate, gate_far, up, up_x,
    )


SUMS = [CORE, Y, NEAR, X, FAR]


def end_kernel(
    partial_ref, x_ref, gain_ref, grad_ref, two_ref, query_ref, key_ref, qkv_ref, out_ref,
    tokens_ref, gains_ref, qkv_out, out_out,
    first, second, sums, last, total, rows_low, vectors, *rest, sizes,
):
    buffers, (send, recv, local) = rest[:-3], rest[-3:]
    net = Wires(send, recv, local, sizes)
    net.greet([Y, CORE, CORNER, NEAR, FAR, X])
    step = x_ref.shape[1] // sizes["narrow"] // 2
    qkv = Gradient(net, 0, step, qkv_ref.shape[1] // 2)
    out = Gradient(net, 1, step, out_ref.shape[0] // 2)
    qkv.start(qkv_ref, *buffers[0:2])
    out.start(out_ref, *buffers[4:6])
    scatter = scatter_flow(net, partial_ref, first, second, sums, last, total)
    run(scatter)
    qkv.core_to_x(buffers[2])
    out.core_to_x(buffers[6])
    run(scatter)
    qkv.x_end(0, buffers[3])
    run(scatter)
    qkv.x_end(1, buffers[3])
    run(scatter)
    width = x_ref.shape[1]
    size = query_ref.shape[1]
    block = width // sizes["narrow"]
    half = block // 2
    gains_ref[...] = jnp.zeros_like(gains_ref)

    def rows(at):
        grad = total[at, :] + last[at, :].astype(F32)
        term, change = row_back(grad, x_ref[at, :].astype(F32), gain_ref[...])
        gains_ref[:, :width] += term
        rows_low[at, :] = (grad_ref[at, :] + change).astype(BF16)

    by_rows(rows_low.shape[0], rows)
    for i, ref in enumerate((gains_ref, two_ref)):
        for slot in range(4):
            to = (2 * (slot % 2) + jnp.bitwise_xor(net.core, slot // 2)) * block + i * width
            for j in range(2):
                sub = net.x if j == 0 else 1 - net.x
                at = slot * block + j * half
                vectors[0, :, pl.ds(pl.multiple_of(to + sub * half, half), half)] = ref[:, at : at + half]
    vectors[0, :, 2 * width : 2 * width + size] = query_ref[...]
    vectors[0, :, 2 * width + size :] = key_ref[...]

    def add_gains():
        for i, to in enumerate(SUMS):
            copy = net.send(vectors.at[i], vectors.at[len(SUMS) + 1 + i], to)
            yield
            net.arrived(copy)
            vectors[i + 1] = vectors[i] + vectors[len(SUMS) + 1 + i]
        gains_ref[...] = vectors[len(SUMS)]
        yield

    def own(flow, k, ref):
        flow.far_end(k)
        flow.to_owner(k, flow.acc.at[flow.slot(k, 2, 0, flow.across)], ref)

    gains = add_gains()
    run(gains)
    out.x_end(0, buffers[7])
    out.x_end(1, buffers[7])
    run(gains)
    own(qkv, 0, qkv_out)
    run(gains)
    spread_flow(net, rows_low, tokens_ref)
    run(gains)
    own(qkv, 1, qkv_out)
    run(gains)
    own(out, 0, out_out)
    own(out, 1, out_out)
    qkv.after_y()
    out.after_y()
    run(gains)
    net.finish()


def end(partial, x, gain, grad, two, query, key, qkv, out, sizes):
    rows, width = x.shape
    size = width // sizes["narrow"]
    wide, deep = qkv.shape[1], out.shape[0]
    length = 2 * width + 2 * query.shape[1]
    return wire_call(
        end_kernel, "end", 6, [VMEM] * 7 + [ANY] * 2, [ANY, VMEM, ANY, ANY],
        [((sizes["narrow"] * rows, size), BF16), ((1, length), F32), ((size, wide), BF16), ((deep, size), BF16)],
        [
            *scatter_buffers(rows, width), pltpu.VMEM((rows, width), BF16), pltpu.VMEM((2 * len(SUMS) + 1, 1, length), F32),
            *gradient_buffers(size, wide // 2, 0), *gradient_buffers(size, deep // 2, 1), *sems(40, 16),
        ],
        sizes, 90, partial, x, gain[None], grad, two, query, key, qkv, out,
    )


def layout(lengths, index):
    order = jnp.arange(lengths.shape[0])
    ends = jnp.sum(jnp.where(order[None, :] <= order[:, None], lengths[None, :], 0), axis=1)[None, :]
    begins = ends - lengths[None, :]
    offset = index - PROMPT
    shift = jnp.sum(jnp.where((offset >= begins) & (offset < ends), begins, 0), axis=1, keepdims=True)
    return jnp.where(offset >= 0, PROMPT + shift, 0), index - shift


def make(sizes):
    n_dp, n_wide, n_narrow = sizes["dp"], sizes["wide"], sizes["narrow"]

    def over_y(values):
        return exchange(values, "narrow", 2, n_narrow)

    def over_z(values):
        return exchange(values, "wide", 1, n_wide)

    def over_x(values):
        return exchange(values, "dp", 1, n_dp)

    def over_far(values):
        return exchange(values, "wide", 2, n_wide)

    def over_groups(values, kind):
        distance = 2
        while distance < n_dp:
            values = values.astype(F32) + exchange(values.astype(kind), "dp", distance, n_dp).astype(F32)
            distance *= 2
        return values.astype(F32)

    def on_device(
        tokens, continuation_lengths, attention_gain, query_weight, key_weight, value_weight, head_gate, query_gain, key_gain,
        output_weight, feedforward_gain, gate_weight, up_weight, down_weight, cotangent,
    ):
        rows_wide, width_local = tokens.shape
        width = attention_gain.shape[0]
        size = query_gain.shape[0]
        heads = head_gate.shape[1]
        pairs = key_weight.shape[1] // size
        group_rows = rows_wide * n_wide
        rows_local = rows_wide // n_narrow
        x = lax.axis_index("dp") % 2
        z = lax.axis_index("wide")
        narrow = lax.axis_index("narrow")
        y, core = narrow // 2, narrow % 2
        z_near, z_far = z % 2, z // 2
        quarter = width_local // 2
        scale = size ** (-0.5)
        factor = scale * math.log2(math.e)
        log_two = math.log(2.0)

        def relative_vector(vector):
            values = jnp.transpose(vector.reshape(2, 2, 2, quarter), (1, 0, 2, 3))
            values = jnp.where(core == 0, values, values[::-1])
            return jnp.where(x == 0, values, values[:, :, ::-1]).reshape(width)

        def piece_of(weight, i, axis):
            half = weight.shape[1 - axis] // 2
            return cut(cut(weight, x * quarter, quarter, axis), i * half, half, 1 - axis)

        gain_one, gain_two = relative_vector(attention_gain), relative_vector(feedforward_gain)
        lane_pad = ((0, 0), (0, LANES - heads // 2))
        halves = lambda w, i: w[:, i * (w.shape[1] // 2) : (i + 1) * (w.shape[1] // 2)]
        packed = join(
            [v for i in range(2) for v in (
                halves(query_weight, i), halves(key_weight, i), halves(value_weight, i), jnp.pad(halves(head_gate, i), lane_pad)
            )], 1
        )
        inputs, upstream, normed_all, joined_weight, out_weight = begin(tokens, cotangent, gain_one, packed, output_weight, sizes)

        def indices(row):
            part, at = row // rows_local, row % rows_local
            return ((z ^ (part // 2)) * n_narrow + (narrow ^ (2 * (part % 2)))) * rows_local + at

        my_index = indices(lax.broadcasted_iota(jnp.int32, (4 * rows_local, 1), 0))
        my_start, my_position = layout(continuation_lengths[0], my_index)
        frequency = THETA ** (-2.0 * jnp.arange(size // 2, dtype=F32) / size)
        angle = my_position.astype(F32) * frequency[None, :]
        cosine, sine = jnp.cos(angle), jnp.sin(angle)
        cosine = jnp.concatenate([cosine, cosine], axis=1)
        sine = jnp.concatenate([-sine, sine], axis=1)
        heads_index = indices(lax.broadcasted_iota(jnp.int32, (4, 1), 0) * rows_local)
        block = heads_index // rows_local
        first = layout(continuation_lengths[0], heads_index)[0] // rows_local
        prompt_blocks = PROMPT // rows_local
        in_prompt = block < prompt_blocks
        column = lax.broadcasted_iota(jnp.int32, (4, 5), 1)
        pick = lambda values: functools.reduce(lambda acc, item: jnp.where(column == item[0], item[1], acc), enumerate(values), 0)
        table = pick(
            [
                jnp.where(in_prompt, block // 2, prompt_blocks // 2),
                jnp.where(in_prompt, block // 2 * 2, first),
                block,
                2 * z_near + y,
                core,
            ]
        ).astype(jnp.int32)

        raw = dot_rows(normed_all, joined_weight)
        q, kv = post(raw, cosine, sine, query_gain, key_gain, heads, pairs, size, factor)
        send = after((gate_weight, up_weight, down_weight), normed_all)
        axes = (0, 0, 1)
        from_y = [over_y(piece_of(w, 1 - y, axis)) for w, axis in zip(send, axes)]
        part = rows_local // 2
        upstream_y, upstream_z = over_y(upstream[:part]), over_z(upstream[part:])
        kv_all = exchange_keys(after(kv, *from_y, upstream_y, upstream_z), sizes)
        send = after((gate_weight, up_weight, down_weight), kv_all)
        from_far = [over_far(piece_of(w, y, axis)) for w, axis in zip(send, axes)]
        come_z = over_z(join([upstream[:part], after(upstream_y, kv_all)]))
        come_y = over_y(join([upstream[part:], after(upstream_z, kv_all)]))
        upstream_all = join(
            [upstream, upstream_y, come_y[:part], come_z[:part], upstream_z, come_z[part:], come_y[part:]]
        )

        gated, context, inverse_total = attend(
            table, q, kv_all, my_index, my_start, raw, pairs, size
        )
        partial = dot_rows(gated, out_weight).astype(BF16)
        middle, normed_two_all, gate_up, down = to_middle(
            partial, inputs, gain_two, gate_weight, up_weight, down_weight, from_y + from_far, sizes
        )
        both = dot_rows(normed_two_all, gate_up)
        hidden_cols = gate_weight.shape[1]
        gate_pre, up_pre = both[:, :hidden_cols], both[:, hidden_cols:]
        gate_sigmoid = jax.nn.sigmoid(gate_pre)
        silu = gate_pre * gate_sigmoid
        hidden = (silu * up_pre).astype(BF16)
        hidden_grad = dot_trans(upstream_all, down)
        gate_grad = hidden_grad * up_pre * gate_sigmoid * (1.0 + gate_pre * (1.0 - gate_sigmoid))
        up_grad = hidden_grad * silu
        gate_up_low = join([gate_grad, up_grad], 1).astype(BF16)
        partial = dot_trans(gate_up_low, gate_up).astype(BF16)
        gate_low, up_low = gate_up_low[:, :hidden_cols], gate_up_low[:, hidden_cols:]
        down_sums = dot_inner(hidden, upstream_all).astype(BF16)
        gate_sums = dot_inner(normed_two_all, gate_low).astype(BF16)
        up_sums = dot_inner(normed_two_all, up_low).astype(BF16)
        middle_grad, middle_all, two_term, down_part, gate_part, up_keep, up_send = turn(
            partial, middle, upstream, gain_two, down_sums, gate_sums, up_sums, sizes
        )
        gate_far = over_far(gate_part[:, hidden_cols // 2 :])
        up_come = over_x(up_send)
        gated_grad = dot_trans(middle_all, out_weight)
        dq, dkv, logit_grad = attend_back(
            table, q, kv_all, my_index, my_start, raw, context, inverse_total, gated_grad, pairs, size
        )
        partial = dot_rows(hidden, down).astype(BF16)
        dkv_mine, layer_output, down_gradient, gate_gradient, up_gradient = to_owner(
            dkv, partial, middle, down_part, gate_part, gate_far, up_keep, up_come, sizes
        )
        low, query_term, key_term = project_back(
            dq, dkv_mine, raw, cosine, sine, query_gain, key_gain, logit_grad, heads, pairs, size, scale, log_two
        )
        partial = dot_trans(low, joined_weight).astype(BF16)
        qkv_sums = dot_inner(normed_all, low).astype(BF16)
        out_sums = dot_inner(gated, middle_all).astype(BF16)
        tokens_gradient, gains, qkv_gradient, output_gradient = end(
            partial, inputs, gain_one, middle_grad, two_term, query_term, key_term, qkv_sums, out_sums, sizes
        )
        tokens_gradient = tokens_gradient.astype(F32)
        gains = over_groups(gains[0], F32)
        qkv_gradient = over_groups(qkv_gradient, BF16)
        down_gradient, gate_gradient, up_gradient, output_gradient = (
            over_groups(v, BF16) for v in (down_gradient, gate_gradient, up_gradient, output_gradient)
        )
        block = qkv_gradient.shape[1] // 2
        query_cols, key_cols = heads // 2 * size, pairs // 2 * size
        take = lambda at, count: join([qkv_gradient[:, at + i * block : at + i * block + count] for i in range(2)], 1)
        query_gradient = take(0, query_cols)
        key_gradient = take(query_cols, key_cols)
        value_gradient = take(query_cols + key_cols, key_cols)
        head_gate_gradient = take(query_cols + 2 * key_cols, heads // 2)
        return (
            layer_output,
            tokens_gradient,
            gains[:width],
            query_gradient,
            key_gradient,
            value_gradient,
            head_gate_gradient,
            gains[2 * width : 2 * width + size],
            gains[2 * width + size :],
            output_gradient,
            gains[width : 2 * width],
            gate_gradient,
            up_gradient,
            down_gradient,
        )

    return on_device


def solution(mesh):
    rows, up, down = P(("dp", "wide"), "narrow"), P("narrow", "wide"), P("wide", "narrow")
    return jax.shard_map(
        make(dict(mesh.shape)),
        mesh=mesh,
        in_specs=(rows, P("dp", None), P(), up, up, up, up, P(), P(), down, P(), up, up, down, rows),
        out_specs=(rows, rows, P(), up, up, up, up, P(), P(), down, P(), up, up, down),
        check_vma=False,
    )
```

```python
import functools
import math

import jax
import jax.numpy as jnp
from jax import lax
from jax.experimental import pallas as pl
from jax.experimental.pallas import tpu as pltpu
from jax.sharding import PartitionSpec as P

PROMPT = 2048
EPS = 1e-06
THETA = 1000000.0
RELATIVE = (0, 2, 1, 3)
BF16 = jnp.bfloat16
F32 = jnp.float32
VMEM_LIMIT = 56 * 1024 * 1024
LANES = 128


def dot_rows(left, right):
    return jnp.dot(left, right, preferred_element_type=F32)


def dot_trans(left, right):
    return lax.dot_general(left, right, (((1,), (1,)), ((), ())), preferred_element_type=F32)


def dot_inner(left, right):
    return lax.dot_general(left, right, (((0,), (0,)), ((), ())), preferred_element_type=F32)


def exchange(values, axis, distance, size):
    return lax.ppermute(values, axis, [(i, i ^ distance) for i in range(size)])


def join(parts, axis=0):
    return jnp.concatenate(parts, axis=axis)


def cut(values, at, length, axis):
    return lax.dynamic_slice_in_dim(values, at, length, axis=axis)


def turn_pairs(values):
    step = values.shape[1] // 4
    return join([values[:, i * step : (i + 1) * step] for i in (1, 0, 3, 2)], 1)


def after(values, *others):
    return lax.optimization_barrier((values,) + others)[0]


def columns(heads, pairs, size):
    query, pair = heads // 2, pairs // 2
    block = (query + 2 * pair) * size + LANES
    of = lambda i, count, before: (i // count) * block + (before + i % count) * size
    return (
        [of(h, query, 0) for h in range(heads)],
        [of(p, pair, query) for p in range(pairs)],
        [of(p, pair, query + pair) for p in range(pairs)],
        [block - LANES, 2 * block - LANES],
    )


def post_kernel(raw_ref, cos_ref, sin_ref, query_gain_ref, key_gain_ref, q_ref, kv_ref, *, heads, pairs, size, factor):
    cosine = cos_ref[...]
    sine = sin_ref[...]
    query_at, key_at, value_at, _ = columns(heads, pairs, size)

    def turned(value, gain):
        inverse = lax.rsqrt(jnp.mean(value * value, axis=-1, keepdims=True) + EPS)
        normal = value * inverse * gain
        return normal * cosine + pltpu.roll(normal, size // 2, 1) * sine

    for h, at in enumerate(query_at):
        value = raw_ref[:, at : at + size]
        q_ref[:, h * size : (h + 1) * size] = (turned(value, query_gain_ref[...]) * factor).astype(BF16)
    for p, at in enumerate(key_at):
        kv_ref[:, p * size : (p + 1) * size] = turned(raw_ref[:, at : at + size], key_gain_ref[...]).astype(BF16)
    for p, at in enumerate(value_at):
        to = (pairs + p) * size
        kv_ref[:, to : to + size] = raw_ref[:, at : at + size].astype(BF16)


def post(raw, cosine, sine, query_gain, key_gain, heads, pairs, size, factor):
    rows, width = raw.shape
    step = 256
    return pl.pallas_call(
        functools.partial(post_kernel, heads=heads, pairs=pairs, size=size, factor=factor),
        grid=(rows // step,),
        in_specs=[
            pl.BlockSpec((step, width), lambda i: (i, 0)),
            pl.BlockSpec((step, size), lambda i: (i, 0)),
            pl.BlockSpec((step, size), lambda i: (i, 0)),
            pl.BlockSpec((1, size), lambda i: (0, 0)),
            pl.BlockSpec((1, size), lambda i: (0, 0)),
        ],
        out_specs=[
            pl.BlockSpec((step, heads * size), lambda i: (i, 0)),
            pl.BlockSpec((step, 2 * pairs * size), lambda i: (i, 0)),
        ],
        out_shape=[
            jax.ShapeDtypeStruct((rows, heads * size), BF16),
            jax.ShapeDtypeStruct((rows, 2 * pairs * size), BF16),
        ],
        cost_estimate=pl.CostEstimate(flops=rows * width * 20, bytes_accessed=rows * width * 8, transcendentals=0),
        name="post",
    )(raw, cosine, sine, query_gain[None], key_gain[None])


def back_kernel(
    dq_ref, dkv_ref, raw_ref, cos_ref, sin_ref, query_gain_ref, key_gain_ref, logit_ref, out_ref, gq_ref, gk_ref, *, heads, pairs, size, factor_q, factor_k
):
    cosine = cos_ref[...]
    sine = sin_ref[...]
    query_at, key_at, value_at, logit_at = columns(heads, pairs, size)

    @pl.when(pl.program_id(0) == 0)
    def _():
        gq_ref[...] = jnp.zeros_like(gq_ref)
        gk_ref[...] = jnp.zeros_like(gk_ref)

    def back(up, value, gain, total_ref):
        up = up * cosine - pltpu.roll(up, size // 2, 1) * sine
        inverse = lax.rsqrt(jnp.mean(value * value, axis=-1, keepdims=True) + EPS)
        hat = value * inverse
        total_ref[...] += jnp.sum(up * hat, axis=0, keepdims=True)
        scaled = up * gain
        return inverse * (scaled - hat * jnp.mean(scaled * hat, axis=-1, keepdims=True))

    for h, at in enumerate(query_at):
        up = dq_ref[:, h * size : (h + 1) * size] * factor_q
        out_ref[:, at : at + size] = back(up, raw_ref[:, at : at + size], query_gain_ref[...], gq_ref).astype(BF16)
    for p, at in enumerate(key_at):
        up = dkv_ref[:, p * size : (p + 1) * size].astype(F32) * factor_k
        out_ref[:, at : at + size] = back(up, raw_ref[:, at : at + size], key_gain_ref[...], gk_ref).astype(BF16)
    for p, at in enumerate(value_at):
        to = (pairs + p) * size
        out_ref[:, at : at + size] = dkv_ref[:, to : to + size].astype(BF16)
    for i, at in enumerate(logit_at):
        out_ref[:, at : at + LANES] = logit_ref[:, i * LANES : (i + 1) * LANES].astype(BF16)


def project_back(dq, dkv, raw, cosine, sine, query_gain, key_gain, logit_grad, heads, pairs, size, factor_q, factor_k):
    rows, width = raw.shape
    step = 256
    row = lambda cols: pl.BlockSpec((step, cols), lambda i: (i, 0))
    one = pl.BlockSpec((1, size), lambda i: (0, 0))
    return pl.pallas_call(
        functools.partial(back_kernel, heads=heads, pairs=pairs, size=size, factor_q=factor_q, factor_k=factor_k),
        grid=(rows // step,),
        in_specs=[row(heads * size), row(2 * pairs * size), row(width), row(size), row(size), one, one, row(2 * LANES)],
        out_specs=[row(width), one, one],
        out_shape=[
            jax.ShapeDtypeStruct((rows, width), BF16),
            jax.ShapeDtypeStruct((1, size), F32),
            jax.ShapeDtypeStruct((1, size), F32),
        ],
        cost_estimate=pl.CostEstimate(flops=rows * width * 30, bytes_accessed=rows * width * 12, transcendentals=0),
        name="project_back",
    )(dq, dkv, raw, cosine, sine, query_gain[None], key_gain[None], logit_grad)


def places(table_ref, stripe, step, length):
    turn = table_ref[stripe, 3]
    core = table_ref[stripe, 4]
    half = length // 2
    blocks = half // step

    def pair(i):
        at = jnp.bitwise_xor(i, turn) * step
        return pl.ds(pl.multiple_of(at, step), step), pl.ds(pl.multiple_of(at + half // 2, step), step)

    def single(b):
        part = b // blocks
        inner = b - part * blocks
        at = part * half + jnp.bitwise_xor(inner % 2, core) * (half // 2) + jnp.bitwise_xor(inner // 2, turn) * step
        return (pl.ds(pl.multiple_of(at, step), step),)

    return pair, single


def logit_of(head, heads, own_ref, other_ref):
    half = heads // 2
    at = head % half
    return (own_ref if head < half else other_ref)[:, at : at + 1]


def logit_specs(raw, heads, pairs, size, step):
    spec = lambda i: pl.BlockSpec((step, LANES), lambda s, t: (s, i))
    return [spec(at // LANES) for at in columns(heads, pairs, size)[3]]


def forward_kernel(table_ref, q_ref, kv_ref, row_ref, start_ref, own_ref, other_ref, gated_ref, context_ref, inverse_ref, *, pairs, repeat, size, step):
    stripe = pl.program_id(0)
    wide_blocks = table_ref[stripe, 0]
    low = table_ref[stripe, 1]
    high = table_ref[stripe, 2]
    pair, single = places(table_ref, stripe, step, kv_ref.shape[0])
    rows = row_ref[...]
    starts = start_ref[...]
    rows = jnp.concatenate([rows] * repeat, axis=0)
    starts = jnp.concatenate([starts] * repeat, axis=0)
    queries = [
        jnp.concatenate([q_ref[:, h * size : (h + 1) * size] for h in range(k * repeat, (k + 1) * repeat)], axis=0)
        for k in range(pairs)
    ]

    def seen(totals, where, first):
        outs = []
        for k in range(pairs):
            keys = join([kv_ref[at, k * size : (k + 1) * size] for at in where])
            weights = jnp.exp2(dot_trans(queries[k], keys))
            if first is not None:
                index = first + lax.broadcasted_iota(jnp.int32, weights.shape, 1)
                weights = jnp.where((index <= rows) & (index >= starts), weights, 0.0)
            values = join([kv_ref[at, (pairs + k) * size : (pairs + k + 1) * size] for at in where])
            values = jnp.concatenate([values, jnp.ones_like(values)], axis=1)
            outs.append(totals[k] + dot_rows(weights.astype(BF16), values))
        return tuple(outs)

    totals = tuple(jnp.zeros((query.shape[0], 2 * size), F32) for query in queries)
    totals = lax.fori_loop(0, wide_blocks, lambda i, t: seen(t, pair(i), None), totals)
    totals = lax.fori_loop(low, high + 1, lambda i, t: seen(t, single(i), i * step), totals)
    for k, total in enumerate(totals):
        inverse = 1.0 / total[:, size:]
        context = total[:, :size] * inverse
        for r in range(repeat):
            h = k * repeat + r
            part = context[r * step : (r + 1) * step]
            cols = slice(h * size, (h + 1) * size)
            gate = jax.nn.sigmoid(logit_of(h, pairs * repeat, own_ref, other_ref))
            gated_ref[:, cols] = (part * gate).astype(BF16)
            context_ref[:, cols] = part
            inverse_ref[:, cols] = inverse[r * step : (r + 1) * step]


def attend(table, q, kv, rows, starts, raw, pairs, size):
    length, cols = q.shape
    heads = cols // size
    step = length // table.shape[0]
    block = lambda width: pl.BlockSpec((step, width), lambda i, t: (i, 0))
    return pl.pallas_call(
        functools.partial(forward_kernel, pairs=pairs, repeat=heads // pairs, size=size, step=step),
        grid_spec=pltpu.PrefetchScalarGridSpec(
            num_scalar_prefetch=1,
            grid=(length // step,),
            in_specs=[
                block(cols),
                pl.BlockSpec(kv.shape, lambda i, t: (0, 0), pipeline_mode=pl.Buffered(1)),
                block(1),
                block(1),
                *logit_specs(raw, heads, pairs, size, step),
            ],
            out_specs=[block(cols), block(cols), block(cols)],
        ),
        out_shape=[
            jax.ShapeDtypeStruct((length, cols), BF16),
            jax.ShapeDtypeStruct((length, cols), F32),
            jax.ShapeDtypeStruct((length, cols), F32),
        ],
        compiler_params=pltpu.CompilerParams(vmem_limit_bytes=VMEM_LIMIT),
        cost_estimate=pl.CostEstimate(flops=20 * 10**9, bytes_accessed=12 * 10**6, transcendentals=7 * 10**6),
        name="attend",
    )(table, q, kv, rows, starts, raw, raw)


def backward_kernel(
    table_ref, q_ref, kv_ref, row_ref, start_ref, own_ref, other_ref, context_ref, inverse_ref, grad_ref,
    dq_ref, dkv_ref, dlogit_ref, sums_ref, *, pairs, repeat, size, step,
):
    stripe = pl.program_id(0)
    wide_blocks = table_ref[stripe, 0]
    low = table_ref[stripe, 1]
    high = table_ref[stripe, 2]
    pair, single = places(table_ref, stripe, step, kv_ref.shape[0])

    @pl.when(stripe == 0)
    def _():
        sums_ref[...] = jnp.zeros_like(sums_ref)

    dlogit_ref[...] = jnp.zeros_like(dlogit_ref)
    rows = jnp.concatenate([row_ref[0]] * repeat, axis=1)
    starts = jnp.concatenate([start_ref[0]] * repeat, axis=1)
    for k in range(pairs):
        heads = [k * repeat + r for r in range(repeat)]
        query = jnp.concatenate([q_ref[:, h * size : (h + 1) * size] for h in heads], axis=0)
        grads, inners = [], []
        for h in heads:
            cols = slice(h * size, (h + 1) * size)
            up = grad_ref[:, cols]
            gate = jax.nn.sigmoid(logit_of(h, pairs * repeat, own_ref, other_ref))
            product = jnp.sum(up * context_ref[:, cols], axis=1, keepdims=True)
            half = pairs * repeat // 2
            at = h // half * LANES + h % half
            dlogit_ref[:, at : at + 1] = product * gate * (1.0 - gate)
            inverse = inverse_ref[:, cols]
            grads.append((up * gate * inverse).astype(BF16))
            inners.append(product * gate * inverse)
        grad = jnp.concatenate(grads, axis=0)
        inner = jnp.transpose(jnp.concatenate(inners, axis=0))[0:1]
        key_cols = slice(k * size, (k + 1) * size)
        value_cols = slice((pairs + k) * size, (pairs + k + 1) * size)

        def seen(total, where, first):
            keys = join([kv_ref[at, key_cols] for at in where])
            weights = jnp.exp2(dot_trans(keys, query))
            if first is not None:
                index = first + lax.broadcasted_iota(jnp.int32, weights.shape, 0)
                weights = jnp.where((index <= rows) & (index >= starts), weights, 0.0)
            changes = dot_trans(join([kv_ref[at, value_cols] for at in where]), grad)
            changes = (weights * (changes - inner)).astype(BF16)
            value_sums = dot_rows(weights.astype(BF16), grad)
            key_sums = dot_rows(changes, query)
            for i, at in enumerate(where):
                sums_ref[at, value_cols] += value_sums[i * step : (i + 1) * step]
                sums_ref[at, key_cols] += key_sums[i * step : (i + 1) * step]
            return total + dot_inner(changes, keys)

        total = jnp.zeros((query.shape[0], size), F32)
        total = lax.fori_loop(0, wide_blocks, lambda i, t: seen(t, pair(i), None), total)
        total = lax.fori_loop(low, high + 1, lambda i, t: seen(t, single(i), i * step), total)
        for r, h in enumerate(heads):
            dq_ref[:, h * size : (h + 1) * size] = total[r * step : (r + 1) * step]

    @pl.when(stripe == pl.num_programs(0) - 1)
    def _():
        dkv_ref[...] = sums_ref[...].astype(BF16)


def attend_back(table, q, kv, rows, starts, raw, context, inverse, grad, pairs, size):
    length, cols = q.shape
    heads = cols // size
    step = length // table.shape[0]
    block = lambda width: pl.BlockSpec((step, width), lambda i, t: (i, 0))
    whole = pl.BlockSpec(kv.shape, lambda i, t: (0, 0), pipeline_mode=pl.Buffered(1))
    lane = pl.BlockSpec((1, 1, step), lambda i, t: (i, 0, 0))
    logits = logit_specs(raw, heads, pairs, size, step)
    return pl.pallas_call(
        functools.partial(backward_kernel, pairs=pairs, repeat=heads // pairs, size=size, step=step),
        grid_spec=pltpu.PrefetchScalarGridSpec(
            num_scalar_prefetch=1,
            grid=(length // step,),
            in_specs=[block(cols), whole, lane, lane, *logits, block(cols), block(cols), block(cols)],
            out_specs=[block(cols), whole, block(2 * LANES)],
            scratch_shapes=[pltpu.VMEM(kv.shape, F32)],
        ),
        out_shape=[
            jax.ShapeDtypeStruct((length, cols), F32),
            jax.ShapeDtypeStruct(kv.shape, BF16),
            jax.ShapeDtypeStruct((length, 2 * LANES), F32),
        ],
        compiler_params=pltpu.CompilerParams(vmem_limit_bytes=VMEM_LIMIT),
        cost_estimate=pl.CostEstimate(flops=50 * 10**9, bytes_accessed=20 * 10**6, transcendentals=7 * 10**6),
        name="attend_back",
    )(table, q, kv, rows.reshape(-1, 1, step), starts.reshape(-1, 1, step), raw, raw, context, inverse, grad)


class Wires:
    def __init__(self, send_sems, recv_sems, local_sems, sizes):
        self.send_sems, self.recv_sems, self.local_sems = send_sems, recv_sems, local_sems
        self.sizes = sizes
        self.sent, self.local, self.open = [], [], []
        self.locals_used, self.sends_used = 0, 0
        self.dp, self.wide, self.narrow = (lax.axis_index(a) for a in ("dp", "wide", "narrow"))
        self.y, self.core = self.narrow // 2, self.narrow % 2
        self.x, self.far = self.dp % 2, self.wide // 2

    def peer(self, *to):
        if isinstance(to[0], tuple):
            return {axis: at for part in to for axis, at in self.peer(*part).items()}
        axis, distance = to
        at = {"dp": self.dp, "wide": self.wide, "narrow": self.narrow}[axis]
        bit = at // distance % 2
        return {axis: at + distance * (1 - 2 * bit) if distance < 3 else 3 - at}

    def greet(self, peers):
        barrier = pltpu.get_barrier_semaphore()
        for to in peers:
            pl.semaphore_signal(barrier, inc=1, device_id=self.peer(*to), device_id_type=pl.DeviceIdType.MESH)
        pl.semaphore_wait(barrier, len(peers))

    def make(self, source, target, to):
        i = self.sends_used
        self.sends_used += 1
        copy = pltpu.make_async_remote_copy(
            src_ref=source, dst_ref=target, send_sem=self.send_sems.at[i], recv_sem=self.recv_sems.at[i],
            device_id=self.peer(*to), device_id_type=pl.DeviceIdType.MESH,
        )
        self.sent.append(copy)
        return copy

    def send(self, source, target, to):
        copy = self.make(source, target, to)
        copy.start()
        self.open.append(copy)
        return copy

    def arrived(self, copy):
        copy.wait_recv()
        self.open = [other for other in self.open if other is not copy]

    def copy(self, source, target):
        copy = pltpu.make_async_copy(source, target, self.local_sems.at[self.locals_used])
        self.locals_used += 1
        copy.start()
        self.local.append(copy)
        return copy

    def finish(self):
        for copy in list(self.open):
            self.arrived(copy)
        for copy in self.sent:
            copy.wait_send()
        for copy in self.local:
            copy.wait()


Y, CORE, CORNER, NEAR, FAR, X = ("narrow", 2), ("narrow", 1), ("narrow", 3), ("wide", 1), ("wide", 2), ("dp", 1)


def local_flow(net, values_ref, rows_ref):
    rows, width = rows_ref.shape[0], values_ref.shape[1]
    half = width // 2
    out = []
    for distance, to in ((0, None), (1, CORE), (2, Y), (3, CORNER)):
        target = net.narrow if to is None else net.peer(*to)["narrow"]
        at = (2 * (distance % 2) + net.y) * width
        for j in range(2):
            sub = net.x if j == 0 else 1 - net.x
            source = values_ref.at[pl.ds(pl.multiple_of(target * rows, rows), rows), pl.ds(pl.multiple_of(sub * half, half), half)]
            goal = rows_ref.at[:, pl.ds(pl.multiple_of(at + j * half, half), half)]
            out.append(net.copy(source, goal) if to is None else net.send(source, goal, to))
    return out


def gather_flow(net, values_ref, all_ref):
    rows = values_ref.shape[0]
    half = rows // 2
    part = lambda i: all_ref.at[pl.ds(i * half, half), :]
    first, second = values_ref.at[pl.ds(0, half), :], values_ref.at[pl.ds(half, half), :]
    first_y = net.send(first, part(2), Y)
    second_z = net.send(second, part(5), NEAR)
    net.send(first, part(4), NEAR)
    net.send(second, part(3), Y)
    net.copy(values_ref, all_ref.at[pl.ds(0, rows), :])
    yield
    net.arrived(first_y)
    net.send(part(2), part(6), NEAR)
    yield
    net.arrived(second_z)
    net.send(part(5), part(7), Y)
    yield


def weight_flow(net, source_ref, out_ref, axis, own, other, across, from_y=None, from_far=None, from_both=None):
    step = source_ref.shape[axis] // 2
    count = source_ref.shape[axis]

    def window(ref, at, start):
        long, wide = pl.ds(pl.multiple_of(at, step), step), pl.ds(start, across)
        return ref.at[long, wide] if axis == 0 else ref.at[wide, long]

    y, x = net.y, net.x
    piece = lambda sub, half: window(source_ref, sub * step, pl.multiple_of(half * across, across))
    place = lambda slot, j, start: window(out_ref, slot * count + j * step, start)
    mine, rest = piece(x, y), piece(1 - x, y)
    net.copy(mine, place(y, 0, own))
    net.copy(rest, place(y, 1, own))
    if from_y is None:
        come_y = net.send(piece(x, 1 - y), place(y, 0, own), Y)
    else:
        net.copy(from_y, place(1 - y, 0, own))
    if from_far is None:
        come_far = net.send(mine, place(y, 0, other), FAR)
    else:
        net.copy(from_far, place(y, 0, other))
    net.send(mine, place(2 + y, 0, own), CORE)
    net.send(rest, place(2 + y, 1, own), CORE)
    if from_y is None:
        yield
        net.arrived(come_y)
        from_y = place(1 - y, 0, own)
    if from_both is None:
        come_both = net.send(from_y, place(1 - y, 0, other), FAR)
    else:
        net.copy(from_both, place(1 - y, 0, other))
    their_y = net.send(from_y, place(1 - y, 1, own), X)
    net.send(from_y, place(3 - y, 0, own), CORE)
    if from_far is None:
        yield
        net.arrived(come_far)
        from_far = place(y, 0, other)
    their_far = net.send(from_far, place(y, 1, other), X)
    net.send(from_far, place(2 + y, 0, other), CORE)
    if from_both is None:
        yield
        net.arrived(come_both)
        from_both = place(1 - y, 0, other)
    their_both = net.send(from_both, place(1 - y, 1, other), X)
    net.send(from_both, place(3 - y, 0, other), CORE)
    yield
    for copy, slot, start in ((their_y, 1 - y, own), (their_far, y, other), (their_both, 1 - y, other)):
        net.arrived(copy)
        net.send(place(slot, 1, start), place(slot + 2, 1, start), CORE)
    yield


def run(flow):
    return next(flow, None)


def by_rows(count, body):
    step = 16
    lax.fori_loop(0, count // step, lambda i, _: (body(pl.ds(pl.multiple_of(i * step, step), step)), 0)[1], 0)


def begin_kernel(
    tokens_ref, cotangent_ref, gain_ref, qkv_ref, out_ref, x_ref, rows_ref, all_ref, joined_ref, output_ref,
    here, normed, there, send, recv, local, *, sizes,
):
    net = Wires(send, recv, local, sizes)
    net.greet([Y, CORE, CORNER, NEAR, FAR, X])
    rows = local_flow(net, tokens_ref, here)
    across = qkv_ref.shape[1] // 2
    joined = weight_flow(net, qkv_ref, joined_ref, 0, 0, across, across)
    run(joined)
    rows[0].wait()
    rows[1].wait()
    net.local = net.local[2:]
    for copy in rows[2:]:
        net.arrived(copy)

    def norm(at):
        values = here[at, :].astype(F32)
        inverse = lax.rsqrt(jnp.mean(values * values, axis=1, keepdims=True) + EPS)
        normed[at, :] = (values * inverse * gain_ref[...]).astype(BF16)
        x_ref[at, :] = here[at, :]

    by_rows(here.shape[0], norm)
    gather = gather_flow(net, normed, all_ref)
    run(gather)
    across = out_ref.shape[0] // 2
    output = weight_flow(net, out_ref, output_ref, 1, 0, across, across)
    for flow in (joined, gather, output, joined, gather):
        run(flow)
    rows = local_flow(net, cotangent_ref, there)
    for flow in (joined, output, joined, output, output, output):
        run(flow)
    for copy in rows[:2]:
        copy.wait()
    net.local = [copy for copy in net.local if all(copy is not other for other in rows[:2])]
    for copy in rows[2:]:
        net.arrived(copy)
    net.copy(there, rows_ref)
    net.finish()


ANY = pl.BlockSpec(memory_space=pl.ANY)
VMEM = pl.BlockSpec(memory_space=pltpu.VMEM)


def sems(sends, locals_):
    return [pltpu.SemaphoreType.DMA((sends,)), pltpu.SemaphoreType.DMA((sends,)), pltpu.SemaphoreType.DMA((locals_,))]


def wire_call(kernel, name, number, specs, out_specs, shapes, scratch, sizes, cost, *args):
    return pl.pallas_call(
        functools.partial(kernel, sizes=sizes),
        in_specs=specs,
        out_specs=out_specs,
        out_shape=[jax.ShapeDtypeStruct(*shape) for shape in shapes],
        scratch_shapes=scratch,
        compiler_params=pltpu.CompilerParams(collective_id=number, has_side_effects=True, vmem_limit_bytes=VMEM_LIMIT),
        cost_estimate=pl.CostEstimate(flops=0, bytes_accessed=cost * 3 * 10**6, transcendentals=0),
        name=name,
    )(*args)


def begin(tokens, cotangent, gain, qkv, out, sizes):
    rows, width = tokens.shape[0] // sizes["narrow"], gain.shape[0]
    row = pltpu.VMEM((rows, width), BF16)
    return wire_call(
        begin_kernel, "begin", 1, [ANY, ANY, VMEM, VMEM, VMEM], [VMEM, ANY, ANY, ANY, ANY],
        [
            ((rows, width), BF16), ((rows, width), BF16), ((4 * rows, width), BF16), ((width, qkv.shape[1]), BF16),
            ((out.shape[0], width), BF16),
        ],
        [row, row, row, *sems(48, 16)], sizes, 55, tokens, cotangent, gain[None], qkv, out,
    )


def keys_kernel(kv_ref, keys_ref, done, send, recv, local, *, sizes):
    net = Wires(send, recv, local, sizes)
    across = [FAR, ("wide", 3), (FAR, CORE), (("wide", 3), CORE)]
    net.greet([CORE] + across)
    count, width = kv_ref.shape
    size = width // 4
    part = lambda i, j: keys_ref.at[pl.ds(i, count), pl.ds(j * size, size)]
    base = pl.multiple_of(net.far * 2 * count, count)
    far = [net.make(kv_ref.at[:, pl.ds(j * size, size)], part(0, j ^ 1), FAR) for j in range(4)]
    on = [net.make(part(0, j ^ 1), part(count, j ^ 1), CORE) for j in range(4)]

    @pl.when(net.far == 0)
    def _():
        for copy in far:
            copy.start()

    net.copy(kv_ref, keys_ref.at[pl.ds(base, count), :])
    net.send(kv_ref, keys_ref.at[pl.ds(base + count, count), :], CORE)

    @pl.when(net.far == 1)
    def _():
        for copy, forward in zip(far, on):
            copy.wait_recv()
            forward.start()
        for to in across:
            pl.semaphore_signal(done, inc=1, device_id=net.peer(*to), device_id_type=pl.DeviceIdType.MESH)
        for forward in on:
            forward.wait()

    @pl.when(net.far == 0)
    def _():
        for copy in far:
            copy.wait_send()
        pl.semaphore_wait(done, len(across))

    net.sent = [copy for copy in net.sent if all(copy is not other for other in far + on)]
    net.finish()


def exchange_keys(kv, sizes):
    return wire_call(
        keys_kernel, "keys", 2, [VMEM], [ANY], [((4 * kv.shape[0], kv.shape[1]), BF16)],
        [pltpu.SemaphoreType.REGULAR, *sems(16, 4)], sizes, 45, kv,
    )[0]


def scatter_flow(net, partial_ref, first_ref, second_ref, send_ref, last_ref, total_ref):
    half = partial_ref.shape[0] // 8
    part = lambda i: partial_ref.at[pl.ds(i * half, half), :]
    slot = lambda ref, i: ref.at[pl.ds(i * half, half), :]
    to_z = [net.send(part(6), slot(first_ref, 1), NEAR), net.send(part(4), slot(first_ref, 0), NEAR)]
    to_y = [net.send(part(7), slot(second_ref, 1), Y), net.send(part(3), slot(second_ref, 0), Y)]
    yield

    def add(out_ref, to, i, ref, j):
        def body(at):
            move = lambda start: pl.ds(pl.multiple_of(at.start + start, 16), at.size)
            value = partial_ref[move(i * half), :].astype(F32) + ref[move(j * half), :].astype(F32)
            out_ref[move(to), :] = value.astype(out_ref.dtype)

        by_rows(half, body)

    net.arrived(to_z[0])
    add(send_ref, 0, 2, first_ref, 1)
    last_y = net.send(slot(send_ref, 0), slot(last_ref, 0), Y)
    net.arrived(to_y[0])
    add(send_ref, half, 5, second_ref, 1)
    last_z = net.send(slot(send_ref, 1), slot(last_ref, 1), NEAR)
    yield
    net.arrived(to_z[1])
    add(total_ref, 0, 0, first_ref, 0)
    net.arrived(to_y[1])
    add(total_ref, half, 1, second_ref, 0)
    yield
    net.arrived(last_y)
    net.arrived(last_z)
    yield


def middle_kernel(
    partial_ref, x_ref, gain_ref, gate_ref, up_ref, down_ref, gate_y_ref, up_y_ref, down_y_ref, gate_far_ref, up_far_ref, down_far_ref,
    gate_both_ref, up_both_ref, down_both_ref, middle_ref, all_ref, both_ref, last_ref,
    first, second, sums, last, total, normed, send, recv, local, *, sizes,
):
    net = Wires(send, recv, local, sizes)
    net.greet([Y, CORE, NEAR, FAR, X])
    scatter = scatter_flow(net, partial_ref, first, second, sums, last, total)
    run(scatter)
    across = gate_ref.shape[1] // 2
    flows = [
        weight_flow(net, gate_ref, both_ref, 0, 0, across, across, gate_y_ref, gate_far_ref, gate_both_ref),
        weight_flow(net, up_ref, both_ref, 0, 2 * across, 3 * across, across, up_y_ref, up_far_ref, up_both_ref),
        weight_flow(net, down_ref, last_ref, 1, 0, across, across, down_y_ref, down_far_ref, down_both_ref),
    ]
    for flow in flows:
        run(flow)
    run(scatter)
    run(scatter)
    run(scatter)

    def norm(at):
        values = x_ref[at, :].astype(F32) + total[at, :] + last[at, :].astype(F32)
        middle_ref[at, :] = values
        inverse = lax.rsqrt(jnp.mean(values * values, axis=1, keepdims=True) + EPS)
        normed[at, :] = (values * inverse * gain_ref[...]).astype(BF16)

    by_rows(normed.shape[0], norm)
    gather = gather_flow(net, normed, all_ref)
    run(gather)
    run(flows[0])
    run(gather)
    run(gather)
    run(flows[1])
    run(flows[2])
    net.finish()


def to_middle(partial, x, gain, gate, up, down, pieces, sizes):
    rows, width = x.shape
    buffer = lambda n, kind: pltpu.VMEM((n, width), kind)
    return wire_call(
        middle_kernel, "middle", 3, [VMEM] * 15, [VMEM, ANY, ANY, ANY],
        [((rows, width), F32), ((4 * rows, width), BF16), ((width, 2 * gate.shape[1]), BF16), ((down.shape[0], width), BF16)],
        [
            buffer(rows, BF16), buffer(rows, BF16), buffer(rows, BF16), buffer(rows, BF16), buffer(rows, F32), buffer(rows, BF16),
            *sems(64, 24),
        ],
        sizes, 80, partial, x, gain[None], gate, up, down, *pieces,
    )


def spread_flow(net, rows_ref, out_ref):
    rows, width = rows_ref.shape[0], out_ref.shape[1]
    half = width // 2
    base = pl.multiple_of(net.narrow * rows, rows)
    for distance, to in ((3, CORNER), (2, Y), (1, CORE), (0, None)):
        target = net.narrow if to is None else net.peer(*to)["narrow"]
        at = (2 * (distance % 2) + target // 2) * width
        for j in range(2):
            sub = net.x if j == 0 else 1 - net.x
            source = rows_ref.at[:, pl.ds(pl.multiple_of(at + j * half, half), half)]
            goal = out_ref.at[pl.ds(base, rows), pl.ds(pl.multiple_of(sub * half, half), half)]
            if to is None:
                net.copy(source, goal)
            else:
                net.send(source, goal, to)


def add_rows(target, terms):
    ref, (rows, cols) = target

    def body(at):
        move = lambda r: pl.ds(pl.multiple_of(at.start + r.start, 16), at.size)
        value = sum(term[move(r), c].astype(F32) for term, (r, c) in terms)
        ref[move(rows), cols] = value.astype(BF16)

    by_rows(rows.size, body)


class Gradient:
    def __init__(self, net, axis, step, across):
        self.net, self.axis, self.step, self.across = net, axis, step, across
        self.order = (1 - net.y, net.y)
        self.x, self.far = [], []

    def window(self, at, start, count, length=None):
        step = self.step if length is None else length
        hint = lambda v, unit: v if isinstance(v, int) else pl.multiple_of(v, unit)
        along, wide = pl.ds(hint(at, self.step), step), pl.ds(hint(start, self.across), count)
        return (along, wide) if self.axis == 0 else (wide, along)

    def start(self, g_ref, acc, from_core):
        self.acc, self.from_core = acc, from_core
        count = 4 * self.step
        own, other = (self.window(i * count, 0, 2 * self.across, count) for i in range(2))
        self.loaded = self.net.copy(g_ref.at[own], acc)
        self.core = self.net.send(g_ref.at[other], from_core, CORE)

    def wait_core(self):
        self.loaded.wait()
        self.net.local = [copy for copy in self.net.local if copy is not self.loaded]
        self.net.arrived(self.core)

    def core_to_x(self, from_x):
        self.wait_core()
        self.from_x = from_x
        for slot in self.order:
            place = self.window((2 * slot + 1) * self.step, 0, 2 * self.across)
            add_rows((self.acc, place), [(self.acc, place), (self.from_core, place)])
            goal = from_x.at[self.window(slot * self.step, 0, 2 * self.across)]
            self.x.append(self.net.send(self.acc.at[place], goal, X))

    def x_end(self, k, from_far=None):
        slot = self.order[k]
        self.net.arrived(self.x[k])
        for start in (self.across, 0):
            place = self.window(2 * slot * self.step, start, self.across)
            come = self.window(slot * self.step, start, self.across)
            add_rows((self.acc, place), [(self.acc, place), (self.from_core, place), (self.from_x, come)])
            if start and from_far is not None:
                self.from_far = from_far
                goal = from_far.at[self.window(slot * self.step, 0, self.across)]
                self.far.append(self.net.send(self.acc.at[place], goal, FAR))

    def far_end(self, k, result=None):
        slot = self.order[k]
        self.net.arrived(self.far[k])
        place = self.window(2 * slot * self.step, 0, self.across)
        come = self.window(slot * self.step, 0, self.across)
        add_rows((self.acc, place), [(self.acc, place), (self.from_far, come)])

    def to_owner(self, k, source, out):
        net, across = self.net, self.across
        goal = out.at[self.window(net.x * self.step, net.y * across, across)]
        if k == 0:
            self.out = out
            self.y = net.send(source, goal, Y)
        else:
            net.copy(source, goal)
            net.send(source, goal, X)

    def after_y(self):
        net, across = self.net, self.across
        net.arrived(self.y)
        place = self.out.at[self.window(net.x * self.step, (1 - net.y) * across, across)]
        net.send(place, place, X)

    def slot(self, k, stride, start, count):
        return self.window(stride * self.order[k] * self.step, start, count)


def row_back(grad, values, gain):
    inverse = lax.rsqrt(jnp.mean(values * values, axis=1, keepdims=True) + EPS)
    hat = values * inverse
    scaled = grad * gain
    inner = jnp.mean(scaled * hat, axis=1, keepdims=True)
    return jnp.sum(grad * hat, axis=0, keepdims=True), inverse * (scaled - hat * inner)


def turn_kernel(
    partial_ref, middle_ref, upstream_ref, gain_ref, down_ref, gate_ref, up_ref,
    grad_ref, all_ref, term_ref, down_out, gate_out, up_keep, up_send,
    first, second, sums, last, total, low, *rest, sizes,
):
    buffers, (send, recv, local) = rest[:-3], rest[-3:]
    net = Wires(send, recv, local, sizes)
    net.greet([Y, CORE, NEAR, FAR, X])
    scatter = scatter_flow(net, partial_ref, first, second, sums, last, total)
    run(scatter)
    step, across = low.shape[1] // sizes["narrow"] // 2, gate_ref.shape[1] // 2
    down, gate, up = (Gradient(net, axis, step, across) for axis in (1, 0, 0))
    down.start(down_ref, *buffers[0:2])
    gate.start(gate_ref, *buffers[3:5])
    up.start(up_ref, *buffers[6:8])
    down.core_to_x(buffers[2])
    gate.core_to_x(buffers[5])
    run(scatter)
    run(scatter)
    run(scatter)
    term_ref[...] = jnp.zeros_like(term_ref)

    def rows(at):
        grad = total[at, :] + last[at, :].astype(F32)
        term, change = row_back(grad, middle_ref[at, :], gain_ref[...])
        term_ref[...] += term
        value = upstream_ref[at, :].astype(F32) + change
        grad_ref[at, :] = value
        low[at, :] = value.astype(BF16)

    by_rows(low.shape[0], rows)
    gather = gather_flow(net, low, all_ref)
    run(gather)
    for k in range(2):
        down.x_end(k)
        net.copy(down.acc.at[down.slot(k, 2, 0, 2 * across)], down_out.at[down.slot(k, 1, 0, 2 * across)])
    run(gather)
    run(gather)
    up.wait_core()
    for slot in range(2):
        for j, ref in ((1, up_send), (0, up_keep)):
            place = up.window((2 * slot + j) * step, 0, 2 * across)
            add_rows((up.acc, place), [(up.acc, place), (up.from_core, place)])
            net.copy(up.acc.at[place], ref.at[up.window(slot * step, 0, 2 * across)])
    for k in range(2):
        gate.x_end(k)
        net.copy(gate.acc.at[gate.slot(k, 2, 0, 2 * across)], gate_out.at[gate.slot(k, 1, 0, 2 * across)])
    net.finish()


def gradient_buffers(size, across, axis, count=4):
    shape = lambda a, b: pltpu.VMEM((a, b) if axis == 0 else (b, a), BF16)
    every = [shape(2 * size, 2 * across), shape(2 * size, 2 * across), shape(size, 2 * across), shape(size, across)]
    return every[:count]


def scatter_buffers(rows, width):
    buffer = lambda kind: pltpu.VMEM((rows, width), kind)
    return [buffer(BF16), buffer(BF16), buffer(BF16), buffer(BF16), buffer(F32)]


def turn(partial, middle, upstream, gain, down, gate, up, sizes):
    rows, width = middle.shape
    size, across = width // sizes["narrow"], down.shape[0] // 2
    return wire_call(
        turn_kernel, "turn", 4, [VMEM] * 4 + [ANY] * 3, [VMEM, ANY, VMEM, ANY, ANY, ANY, ANY],
        [
            ((rows, width), F32), ((4 * rows, width), BF16), ((1, width), F32),
            ((2 * across, size), BF16), ((size, 2 * across), BF16), ((size, 2 * across), BF16), ((size, 2 * across), BF16),
        ],
        [
            *scatter_buffers(rows, width), pltpu.VMEM((rows, width), BF16),
            *gradient_buffers(size, across, 1, 3), *gradient_buffers(size, across, 0, 3), *gradient_buffers(size, across, 0, 2), *sems(40, 16),
        ],
        sizes, 80, partial, middle, upstream, gain[None], down, gate, up,
    )


def owner_kernel(
    dkv_ref, partial_ref, middle_ref, down_ref, down_far_ref, gate_ref, gate_far_ref,
    mine_ref, layer_ref, down_out, gate_out,
    prompt_core, rest_core, prompt, prompt_far, first, second, sums, last, total, rows_low, down_sums, gate_sums,
    send, recv, local, *, sizes,
):
    net = Wires(send, recv, local, sizes)
    net.greet([Y, CORE, CORNER, NEAR, FAR, X])
    count, width = prompt.shape
    size = width // 4
    region = lambda i: dkv_ref.at[pl.ds(i * count, count), :]
    come = net.send(region(1), prompt_core, CORE)
    rest = net.send(region(3), rest_core, CORE)
    scatter = scatter_flow(net, partial_ref, first, second, sums, last, total)
    run(scatter)
    step, across = down_far_ref.shape[1] // 2, down_far_ref.shape[0]
    down, gate = (Gradient(net, axis, step, across) for axis in (1, 0))
    net.arrived(come)

    def add(at):
        prompt[at, :] = (dkv_ref[at, :].astype(F32) + prompt_core[at, :].astype(F32)).astype(BF16)

    by_rows(count, add)
    cols = lambda ref, j: ref.at[:, pl.ds(j * size, size)]
    far = [net.make(cols(prompt, j), cols(prompt_far, j ^ 1), FAR) for j in range(4)]

    @pl.when(net.far == 1)
    def _():
        for copy in far:
            copy.start()

    parts = ((down, down_sums, down_ref, down_far_ref, down_out), (gate, gate_sums, gate_ref, gate_far_ref, gate_out))
    for flow, total_ref, ref, far_ref, goal in parts:
        for k in range(2):
            place = flow.slot(k, 1, 0, across)
            add_rows((total_ref, place), [(ref, place), (far_ref, place)])
            flow.to_owner(k, total_ref.at[place], goal)
    run(scatter)
    run(scatter)
    run(scatter)

    def rows(at):
        rows_low[at, :] = (middle_ref[at, :] + total[at, :] + last[at, :].astype(F32)).astype(BF16)

    by_rows(rows_low.shape[0], rows)
    spread_flow(net, rows_low, layer_ref)
    down.after_y()
    gate.after_y()
    net.arrived(rest)

    @pl.when(net.far == 1)
    def _():
        def add(at):
            move = pl.ds(pl.multiple_of(at.start + 2 * count, 16), at.size)
            mine_ref[at, :] = dkv_ref[move, :].astype(F32) + rest_core[at, :].astype(F32)

        by_rows(count, add)
        for copy in far:
            copy.wait_send()

    @pl.when(net.far == 0)
    def _():
        for copy in far:
            copy.wait_recv()

        def add(at):
            mine_ref[at, :] = dkv_ref[at, :].astype(F32) + prompt_core[at, :].astype(F32) + prompt_far[at, :].astype(F32)

        by_rows(count, add)

    net.sent = [copy for copy in net.sent if all(copy is not other for other in far)]
    net.finish()


def to_owner(dkv, partial, middle, down, down_far, gate, gate_far, sizes):
    rows, width = middle.shape
    size, across = width // sizes["narrow"], gate_far.shape[1]
    count = dkv.shape[0] // 4
    block = lambda: pltpu.VMEM((count, dkv.shape[1]), BF16)
    return wire_call(
        owner_kernel, "owner", 5, [VMEM] * 7, [VMEM, ANY, ANY, ANY],
        [
            ((count, dkv.shape[1]), F32), ((sizes["narrow"] * rows, size), BF16), ((2 * across, size), BF16),
            ((size, 2 * across), BF16),
        ],
        [
            block(), block(), block(), block(), *scatter_buffers(rows, width), pltpu.VMEM((rows, width), BF16),
            pltpu.VMEM((across, size), BF16), pltpu.VMEM((size, across), BF16), *sems(40, 16),
        ],
        sizes, 80, dkv, partial, middle, down, down_far, gate, gate_far,
    )


SUMS = [CORE, Y, NEAR, X, FAR]


def end_kernel(
    partial_ref, x_ref, gain_ref, grad_ref, two_ref, query_ref, key_ref, up_ref, up_far_ref, qkv_ref, out_ref,
    tokens_ref, gains_ref, qkv_out, out_out, up_out,
    first, second, sums, last, total, rows_low, vectors, up_sums, *rest, sizes,
):
    buffers, (send, recv, local) = rest[:-3], rest[-3:]
    net = Wires(send, recv, local, sizes)
    net.greet([Y, CORE, CORNER, NEAR, FAR, X])
    step = x_ref.shape[1] // sizes["narrow"] // 2
    qkv = Gradient(net, 0, step, qkv_ref.shape[1] // 2)
    out = Gradient(net, 1, step, out_ref.shape[0] // 2)
    qkv.start(qkv_ref, *buffers[0:2])
    out.start(out_ref, *buffers[4:6])
    scatter = scatter_flow(net, partial_ref, first, second, sums, last, total)
    run(scatter)
    up = Gradient(net, 0, step, up_far_ref.shape[1])
    qkv.core_to_x(buffers[2])
    out.core_to_x(buffers[6])
    for k in range(2):
        place = up.slot(k, 1, 0, up.across)
        add_rows((up_sums, place), [(up_ref, place), (up_far_ref, place)])
        up.to_owner(k, up_sums.at[place], up_out)
    run(scatter)
    qkv.x_end(0, buffers[3])
    run(scatter)
    qkv.x_end(1, buffers[3])
    run(scatter)
    width = x_ref.shape[1]
    size = query_ref.shape[1]
    block = width // sizes["narrow"]
    half = block // 2
    gains_ref[...] = jnp.zeros_like(gains_ref)

    def rows(at):
        grad = total[at, :] + last[at, :].astype(F32)
        term, change = row_back(grad, x_ref[at, :].astype(F32), gain_ref[...])
        gains_ref[:, :width] += term
        rows_low[at, :] = (grad_ref[at, :] + change).astype(BF16)

    by_rows(rows_low.shape[0], rows)
    for i, ref in enumerate((gains_ref, two_ref)):
        for slot in range(4):
            to = (2 * (slot % 2) + jnp.bitwise_xor(net.core, slot // 2)) * block + i * width
            for j in range(2):
                sub = net.x if j == 0 else 1 - net.x
                at = slot * block + j * half
                vectors[0, :, pl.ds(pl.multiple_of(to + sub * half, half), half)] = ref[:, at : at + half]
    vectors[0, :, 2 * width : 2 * width + size] = query_ref[...]
    vectors[0, :, 2 * width + size :] = key_ref[...]

    def add_gains():
        for i, to in enumerate(SUMS):
            copy = net.send(vectors.at[i], vectors.at[len(SUMS) + 1 + i], to)
            yield
            net.arrived(copy)
            vectors[i + 1] = vectors[i] + vectors[len(SUMS) + 1 + i]
        gains_ref[...] = vectors[len(SUMS)]
        yield

    def own(flow, k, ref):
        flow.far_end(k)
        flow.to_owner(k, flow.acc.at[flow.slot(k, 2, 0, flow.across)], ref)

    gains = add_gains()
    run(gains)
    out.x_end(0, buffers[7])
    out.x_end(1, buffers[7])
    run(gains)
    own(qkv, 0, qkv_out)
    run(gains)
    spread_flow(net, rows_low, tokens_ref)
    run(gains)
    own(qkv, 1, qkv_out)
    run(gains)
    own(out, 0, out_out)
    own(out, 1, out_out)
    up.after_y()
    qkv.after_y()
    out.after_y()
    run(gains)
    net.finish()


def end(partial, x, gain, grad, two, query, key, up, up_far, qkv, out, sizes):
    rows, width = x.shape
    size = width // sizes["narrow"]
    wide, deep = qkv.shape[1], out.shape[0]
    length = 2 * width + 2 * query.shape[1]
    return wire_call(
        end_kernel, "end", 6, [VMEM] * 9 + [ANY] * 2, [ANY, VMEM, ANY, ANY, ANY],
        [((sizes["narrow"] * rows, size), BF16), ((1, length), F32), ((size, wide), BF16), ((deep, size), BF16),
         ((size, 2 * up_far.shape[1]), BF16)],
        [
            *scatter_buffers(rows, width), pltpu.VMEM((rows, width), BF16), pltpu.VMEM((2 * len(SUMS) + 1, 1, length), F32),
            pltpu.VMEM(up_far.shape, BF16),
            *gradient_buffers(size, wide // 2, 0), *gradient_buffers(size, deep // 2, 1), *sems(40, 16),
        ],
        sizes, 90, partial, x, gain[None], grad, two, query, key, up, up_far, qkv, out,
    )


def layout(lengths, index):
    order = jnp.arange(lengths.shape[0])
    ends = jnp.sum(jnp.where(order[None, :] <= order[:, None], lengths[None, :], 0), axis=1)[None, :]
    begins = ends - lengths[None, :]
    offset = index - PROMPT
    shift = jnp.sum(jnp.where((offset >= begins) & (offset < ends), begins, 0), axis=1, keepdims=True)
    return jnp.where(offset >= 0, PROMPT + shift, 0), index - shift


def make(sizes):
    n_dp, n_wide, n_narrow = sizes["dp"], sizes["wide"], sizes["narrow"]

    def over_y(values):
        return exchange(values, "narrow", 2, n_narrow)

    def over_z(values):
        return exchange(values, "wide", 1, n_wide)

    def over_x(values):
        return exchange(values, "dp", 1, n_dp)

    def over_far(values):
        return exchange(values, "wide", 2, n_wide)

    def over_groups(values, kind):
        distance = 2
        while distance < n_dp:
            values = values.astype(F32) + exchange(values.astype(kind), "dp", distance, n_dp).astype(F32)
            distance *= 2
        return values.astype(F32)

    def on_device(
        tokens, continuation_lengths, attention_gain, query_weight, key_weight, value_weight, head_gate, query_gain, key_gain,
        output_weight, feedforward_gain, gate_weight, up_weight, down_weight, cotangent,
    ):
        rows_wide, width_local = tokens.shape
        width = attention_gain.shape[0]
        size = query_gain.shape[0]
        heads = head_gate.shape[1]
        pairs = key_weight.shape[1] // size
        group_rows = rows_wide * n_wide
        rows_local = rows_wide // n_narrow
        x = lax.axis_index("dp") % 2
        z = lax.axis_index("wide")
        narrow = lax.axis_index("narrow")
        y, core = narrow // 2, narrow % 2
        z_near, z_far = z % 2, z // 2
        quarter = width_local // 2
        scale = size ** (-0.5)
        factor = scale * math.log2(math.e)
        log_two = math.log(2.0)

        def relative_vector(vector):
            values = jnp.transpose(vector.reshape(2, 2, 2, quarter), (1, 0, 2, 3))
            values = jnp.where(core == 0, values, values[::-1])
            return jnp.where(x == 0, values, values[:, :, ::-1]).reshape(width)

        def piece_of(weight, i, axis):
            half = weight.shape[1 - axis] // 2
            return cut(cut(weight, x * quarter, quarter, axis), i * half, half, 1 - axis)

        gain_one, gain_two = relative_vector(attention_gain), relative_vector(feedforward_gain)
        lane_pad = ((0, 0), (0, LANES - heads // 2))
        halves = lambda w, i: w[:, i * (w.shape[1] // 2) : (i + 1) * (w.shape[1] // 2)]
        packed = join(
            [v for i in range(2) for v in (
                halves(query_weight, i), halves(key_weight, i), halves(value_weight, i), jnp.pad(halves(head_gate, i), lane_pad)
            )], 1
        )
        inputs, upstream, normed_all, joined_weight, out_weight = begin(tokens, cotangent, gain_one, packed, output_weight, sizes)

        def indices(row):
            part, at = row // rows_local, row % rows_local
            return ((z ^ (part // 2)) * n_narrow + (narrow ^ (2 * (part % 2)))) * rows_local + at

        my_index = indices(lax.broadcasted_iota(jnp.int32, (4 * rows_local, 1), 0))
        my_start, my_position = layout(continuation_lengths[0], my_index)
        frequency = THETA ** (-2.0 * jnp.arange(size // 2, dtype=F32) / size)
        angle = my_position.astype(F32) * frequency[None, :]
        cosine, sine = jnp.cos(angle), jnp.sin(angle)
        cosine = jnp.concatenate([cosine, cosine], axis=1)
        sine = jnp.concatenate([-sine, sine], axis=1)
        heads_index = indices(lax.broadcasted_iota(jnp.int32, (4, 1), 0) * rows_local)
        block = heads_index // rows_local
        first = layout(continuation_lengths[0], heads_index)[0] // rows_local
        prompt_blocks = PROMPT // rows_local
        in_prompt = block < prompt_blocks
        column = lax.broadcasted_iota(jnp.int32, (4, 5), 1)
        pick = lambda values: functools.reduce(lambda acc, item: jnp.where(column == item[0], item[1], acc), enumerate(values), 0)
        table = pick(
            [
                jnp.where(in_prompt, block // 2, prompt_blocks // 2),
                jnp.where(in_prompt, block // 2 * 2, first),
                block,
                2 * z_near + y,
                core,
            ]
        ).astype(jnp.int32)

        raw = dot_rows(normed_all, joined_weight)
        q, kv = post(raw, cosine, sine, query_gain, key_gain, heads, pairs, size, factor)
        send = after((gate_weight, up_weight, down_weight), normed_all)
        axes = (0, 0, 1)
        from_y = [over_y(piece_of(w, 1 - y, axis)) for w, axis in zip(send, axes)]
        from_far = [over_far(piece_of(w, y, axis)) for w, axis in zip(send, axes)]
        part = rows_local // 2
        upstream_y, upstream_z = over_y(upstream[:part]), over_z(upstream[part:])
        kv_all = exchange_keys(after(kv, *from_y, *from_far, upstream_y, upstream_z), sizes)
        from_both = [over_far(after(v, kv_all)) for v in from_y]
        come_z = over_z(join([upstream[:part], after(upstream_y, kv_all)]))
        come_y = over_y(join([upstream[part:], after(upstream_z, kv_all)]))
        upstream_all = join(
            [upstream, upstream_y, come_y[:part], come_z[:part], upstream_z, come_z[part:], come_y[part:]]
        )

        gated, context, inverse_total = attend(
            table, q, kv_all, my_index, my_start, raw, pairs, size
        )
        partial = dot_rows(gated, out_weight).astype(BF16)
        middle, normed_two_all, gate_up, down = to_middle(
            partial, inputs, gain_two, gate_weight, up_weight, down_weight, from_y + from_far + from_both, sizes
        )
        both = dot_rows(normed_two_all, gate_up)
        hidden_cols = gate_weight.shape[1]
        gate_pre, up_pre = both[:, :hidden_cols], both[:, hidden_cols:]
        gate_sigmoid = jax.nn.sigmoid(gate_pre)
        silu = gate_pre * gate_sigmoid
        hidden = (silu * up_pre).astype(BF16)
        hidden_grad = dot_trans(upstream_all, down)
        gate_grad = hidden_grad * up_pre * gate_sigmoid * (1.0 + gate_pre * (1.0 - gate_sigmoid))
        up_grad = hidden_grad * silu
        gate_up_low = join([gate_grad, up_grad], 1).astype(BF16)
        partial = dot_trans(gate_up_low, gate_up).astype(BF16)
        gate_low, up_low = gate_up_low[:, :hidden_cols], gate_up_low[:, hidden_cols:]
        down_sums = dot_inner(hidden, upstream_all).astype(BF16)
        gate_sums = dot_inner(normed_two_all, gate_low).astype(BF16)
        up_sums = dot_inner(normed_two_all, up_low).astype(BF16)
        middle_grad, middle_all, two_term, down_part, gate_part, up_keep, up_send = turn(
            partial, middle, upstream, gain_two, down_sums, gate_sums, up_sums, sizes
        )
        down_far = over_far(down_part[hidden_cols // 2 :])
        gate_far = over_far(gate_part[:, hidden_cols // 2 :])
        up_come = over_x(up_send)
        gated_grad = dot_trans(middle_all, out_weight)
        dq, dkv, logit_grad = attend_back(
            table, q, kv_all, my_index, my_start, raw, context, inverse_total, gated_grad, pairs, size
        )
        partial = dot_rows(hidden, down).astype(BF16)
        up_part = (up_keep.astype(F32) + up_come.astype(F32)).astype(BF16)
        dkv_mine, layer_output, down_gradient, gate_gradient = to_owner(
            dkv, partial, middle, down_part, down_far, gate_part, gate_far, sizes
        )
        up_far = over_far(after(up_part[:, hidden_cols // 2 :], dkv_mine))
        low, query_term, key_term = project_back(
            dq, dkv_mine, raw, cosine, sine, query_gain, key_gain, logit_grad, heads, pairs, size, scale, log_two
        )
        partial = dot_trans(low, joined_weight).astype(BF16)
        qkv_sums = dot_inner(normed_all, low).astype(BF16)
        out_sums = dot_inner(gated, middle_all).astype(BF16)
        tokens_gradient, gains, qkv_gradient, output_gradient, up_gradient = end(
            partial, inputs, gain_one, middle_grad, two_term, query_term, key_term, up_part[:, : hidden_cols // 2], up_far,
            qkv_sums, out_sums, sizes
        )
        tokens_gradient = tokens_gradient.astype(F32)
        gains = over_groups(gains[0], F32)
        qkv_gradient = over_groups(qkv_gradient, BF16)
        down_gradient, gate_gradient, up_gradient, output_gradient = (
            over_groups(v, BF16) for v in (down_gradient, gate_gradient, up_gradient, output_gradient)
        )
        block = qkv_gradient.shape[1] // 2
        query_cols, key_cols = heads // 2 * size, pairs // 2 * size
        take = lambda at, count: join([qkv_gradient[:, at + i * block : at + i * block + count] for i in range(2)], 1)
        query_gradient = take(0, query_cols)
        key_gradient = take(query_cols, key_cols)
        value_gradient = take(query_cols + key_cols, key_cols)
        head_gate_gradient = take(query_cols + 2 * key_cols, heads // 2)
        return (
            layer_output,
            tokens_gradient,
            gains[:width],
            query_gradient,
            key_gradient,
            value_gradient,
            head_gate_gradient,
            gains[2 * width : 2 * width + size],
            gains[2 * width + size :],
            output_gradient,
            gains[width : 2 * width],
            gate_gradient,
            up_gradient,
            down_gradient,
        )

    return on_device


def solution(mesh):
    rows, up, down = P(("dp", "wide"), "narrow"), P("narrow", "wide"), P("wide", "narrow")
    return jax.shard_map(
        make(dict(mesh.shape)),
        mesh=mesh,
        in_specs=(rows, P("dp", None), P(), up, up, up, up, P(), P(), down, P(), up, up, down, rows),
        out_specs=(rows, rows, P(), up, up, up, up, P(), P(), down, P(), up, up, down),
        check_vma=False,
    )
```

```python
import functools
import math

import jax
import jax.numpy as jnp
from jax import lax
from jax.experimental import pallas as pl
from jax.experimental.pallas import tpu as pltpu
from jax.sharding import PartitionSpec as P

PROMPT = 2048
EPS = 1e-06
THETA = 1000000.0
RELATIVE = (0, 2, 1, 3)
BF16 = jnp.bfloat16
F32 = jnp.float32
VMEM_LIMIT = 56 * 1024 * 1024
LANES = 128


def dot_rows(left, right):
    return jnp.dot(left, right, preferred_element_type=F32)


def dot_trans(left, right):
    return lax.dot_general(left, right, (((1,), (1,)), ((), ())), preferred_element_type=F32)


def dot_inner(left, right):
    return lax.dot_general(left, right, (((0,), (0,)), ((), ())), preferred_element_type=F32)


def exchange(values, axis, distance, size):
    return lax.ppermute(values, axis, [(i, i ^ distance) for i in range(size)])


def join(parts, axis=0):
    return jnp.concatenate(parts, axis=axis)


def cut(values, at, length, axis):
    return lax.dynamic_slice_in_dim(values, at, length, axis=axis)


def turn_pairs(values):
    step = values.shape[1] // 4
    return join([values[:, i * step : (i + 1) * step] for i in (1, 0, 3, 2)], 1)


def after(values, *others):
    return lax.optimization_barrier((values,) + others)[0]


def columns(heads, pairs, size):
    query, pair = heads // 2, pairs // 2
    block = (query + 2 * pair) * size + LANES
    of = lambda i, count, before: (i // count) * block + (before + i % count) * size
    return (
        [of(h, query, 0) for h in range(heads)],
        [of(p, pair, query) for p in range(pairs)],
        [of(p, pair, query + pair) for p in range(pairs)],
        [block - LANES, 2 * block - LANES],
    )


def post_kernel(raw_ref, cos_ref, sin_ref, query_gain_ref, key_gain_ref, q_ref, kv_ref, *, heads, pairs, size, factor):
    cosine = cos_ref[...]
    sine = sin_ref[...]
    query_at, key_at, value_at, _ = columns(heads, pairs, size)

    def turned(value, gain):
        inverse = lax.rsqrt(jnp.mean(value * value, axis=-1, keepdims=True) + EPS)
        normal = value * inverse * gain
        return normal * cosine + pltpu.roll(normal, size // 2, 1) * sine

    for h, at in enumerate(query_at):
        value = raw_ref[:, at : at + size]
        q_ref[:, h * size : (h + 1) * size] = (turned(value, query_gain_ref[...]) * factor).astype(BF16)
    for p, at in enumerate(key_at):
        kv_ref[:, p * size : (p + 1) * size] = turned(raw_ref[:, at : at + size], key_gain_ref[...]).astype(BF16)
    for p, at in enumerate(value_at):
        to = (pairs + p) * size
        kv_ref[:, to : to + size] = raw_ref[:, at : at + size].astype(BF16)


def post(raw, cosine, sine, query_gain, key_gain, heads, pairs, size, factor):
    rows, width = raw.shape
    step = 256
    return pl.pallas_call(
        functools.partial(post_kernel, heads=heads, pairs=pairs, size=size, factor=factor),
        grid=(rows // step,),
        in_specs=[
            pl.BlockSpec((step, width), lambda i: (i, 0)),
            pl.BlockSpec((step, size), lambda i: (i, 0)),
            pl.BlockSpec((step, size), lambda i: (i, 0)),
            pl.BlockSpec((1, size), lambda i: (0, 0)),
            pl.BlockSpec((1, size), lambda i: (0, 0)),
        ],
        out_specs=[
            pl.BlockSpec((step, heads * size), lambda i: (i, 0)),
            pl.BlockSpec((step, 2 * pairs * size), lambda i: (i, 0)),
        ],
        out_shape=[
            jax.ShapeDtypeStruct((rows, heads * size), BF16),
            jax.ShapeDtypeStruct((rows, 2 * pairs * size), BF16),
        ],
        cost_estimate=pl.CostEstimate(flops=rows * width * 20, bytes_accessed=rows * width * 8, transcendentals=0),
        name="post",
    )(raw, cosine, sine, query_gain[None], key_gain[None])


def back_kernel(
    dq_ref, dkv_ref, raw_ref, cos_ref, sin_ref, query_gain_ref, key_gain_ref, logit_ref, out_ref, gq_ref, gk_ref, *, heads, pairs, size, factor_q, factor_k
):
    cosine = cos_ref[...]
    sine = sin_ref[...]
    query_at, key_at, value_at, logit_at = columns(heads, pairs, size)

    @pl.when(pl.program_id(0) == 0)
    def _():
        gq_ref[...] = jnp.zeros_like(gq_ref)
        gk_ref[...] = jnp.zeros_like(gk_ref)

    def back(up, value, gain, total_ref):
        up = up * cosine - pltpu.roll(up, size // 2, 1) * sine
        inverse = lax.rsqrt(jnp.mean(value * value, axis=-1, keepdims=True) + EPS)
        hat = value * inverse
        total_ref[...] += jnp.sum(up * hat, axis=0, keepdims=True)
        scaled = up * gain
        return inverse * (scaled - hat * jnp.mean(scaled * hat, axis=-1, keepdims=True))

    for h, at in enumerate(query_at):
        up = dq_ref[:, h * size : (h + 1) * size] * factor_q
        out_ref[:, at : at + size] = back(up, raw_ref[:, at : at + size], query_gain_ref[...], gq_ref).astype(BF16)
    for p, at in enumerate(key_at):
        up = dkv_ref[:, p * size : (p + 1) * size].astype(F32) * factor_k
        out_ref[:, at : at + size] = back(up, raw_ref[:, at : at + size], key_gain_ref[...], gk_ref).astype(BF16)
    for p, at in enumerate(value_at):
        to = (pairs + p) * size
        out_ref[:, at : at + size] = dkv_ref[:, to : to + size].astype(BF16)
    for i, at in enumerate(logit_at):
        out_ref[:, at : at + LANES] = logit_ref[:, i * LANES : (i + 1) * LANES].astype(BF16)


def project_back(dq, dkv, raw, cosine, sine, query_gain, key_gain, logit_grad, heads, pairs, size, factor_q, factor_k):
    rows, width = raw.shape
    step = 256
    row = lambda cols: pl.BlockSpec((step, cols), lambda i: (i, 0))
    one = pl.BlockSpec((1, size), lambda i: (0, 0))
    return pl.pallas_call(
        functools.partial(back_kernel, heads=heads, pairs=pairs, size=size, factor_q=factor_q, factor_k=factor_k),
        grid=(rows // step,),
        in_specs=[row(heads * size), row(2 * pairs * size), row(width), row(size), row(size), one, one, row(2 * LANES)],
        out_specs=[row(width), one, one],
        out_shape=[
            jax.ShapeDtypeStruct((rows, width), BF16),
            jax.ShapeDtypeStruct((1, size), F32),
            jax.ShapeDtypeStruct((1, size), F32),
        ],
        cost_estimate=pl.CostEstimate(flops=rows * width * 30, bytes_accessed=rows * width * 12, transcendentals=0),
        name="project_back",
    )(dq, dkv, raw, cosine, sine, query_gain[None], key_gain[None], logit_grad)


def places(table_ref, stripe, step, length):
    turn = table_ref[stripe, 3]
    core = table_ref[stripe, 4]
    half = length // 2
    blocks = half // step

    def pair(i):
        at = jnp.bitwise_xor(i, turn) * step
        return pl.ds(pl.multiple_of(at, step), step), pl.ds(pl.multiple_of(at + half // 2, step), step)

    def single(b):
        part = b // blocks
        inner = b - part * blocks
        at = part * half + jnp.bitwise_xor(inner % 2, core) * (half // 2) + jnp.bitwise_xor(inner // 2, turn) * step
        return (pl.ds(pl.multiple_of(at, step), step),)

    return pair, single


def logit_of(head, heads, own_ref, other_ref):
    half = heads // 2
    at = head % half
    return (own_ref if head < half else other_ref)[:, at : at + 1]


def logit_specs(raw, heads, pairs, size, step):
    spec = lambda i: pl.BlockSpec((step, LANES), lambda s, t: (s, i))
    return [spec(at // LANES) for at in columns(heads, pairs, size)[3]]


def forward_kernel(table_ref, q_ref, kv_ref, row_ref, start_ref, own_ref, other_ref, gated_ref, context_ref, inverse_ref, *, pairs, repeat, size, step):
    stripe = pl.program_id(0)
    wide_blocks = table_ref[stripe, 0]
    low = table_ref[stripe, 1]
    high = table_ref[stripe, 2]
    pair, single = places(table_ref, stripe, step, kv_ref.shape[0])
    rows = row_ref[...]
    starts = start_ref[...]
    rows = jnp.concatenate([rows] * repeat, axis=0)
    starts = jnp.concatenate([starts] * repeat, axis=0)
    queries = [
        jnp.concatenate([q_ref[:, h * size : (h + 1) * size] for h in range(k * repeat, (k + 1) * repeat)], axis=0)
        for k in range(pairs)
    ]

    def seen(totals, where, first):
        outs = []
        for k in range(pairs):
            keys = join([kv_ref[at, k * size : (k + 1) * size] for at in where])
            weights = jnp.exp2(dot_trans(queries[k], keys))
            if first is not None:
                index = first + lax.broadcasted_iota(jnp.int32, weights.shape, 1)
                weights = jnp.where((index <= rows) & (index >= starts), weights, 0.0)
            values = join([kv_ref[at, (pairs + k) * size : (pairs + k + 1) * size] for at in where])
            values = jnp.concatenate([values, jnp.ones_like(values)], axis=1)
            outs.append(totals[k] + dot_rows(weights.astype(BF16), values))
        return tuple(outs)

    totals = tuple(jnp.zeros((query.shape[0], 2 * size), F32) for query in queries)
    totals = lax.fori_loop(0, wide_blocks, lambda i, t: seen(t, pair(i), None), totals)
    totals = lax.fori_loop(low, high + 1, lambda i, t: seen(t, single(i), i * step), totals)
    for k, total in enumerate(totals):
        inverse = 1.0 / total[:, size:]
        context = total[:, :size] * inverse
        for r in range(repeat):
            h = k * repeat + r
            part = context[r * step : (r + 1) * step]
            cols = slice(h * size, (h + 1) * size)
            gate = jax.nn.sigmoid(logit_of(h, pairs * repeat, own_ref, other_ref))
            gated_ref[:, cols] = (part * gate).astype(BF16)
            context_ref[:, cols] = part
            inverse_ref[:, cols] = inverse[r * step : (r + 1) * step]


def attend(table, q, kv, rows, starts, raw, pairs, size):
    length, cols = q.shape
    heads = cols // size
    step = length // table.shape[0]
    block = lambda width: pl.BlockSpec((step, width), lambda i, t: (i, 0))
    return pl.pallas_call(
        functools.partial(forward_kernel, pairs=pairs, repeat=heads // pairs, size=size, step=step),
        grid_spec=pltpu.PrefetchScalarGridSpec(
            num_scalar_prefetch=1,
            grid=(length // step,),
            in_specs=[
                block(cols),
                pl.BlockSpec(kv.shape, lambda i, t: (0, 0), pipeline_mode=pl.Buffered(1)),
                block(1),
                block(1),
                *logit_specs(raw, heads, pairs, size, step),
            ],
            out_specs=[block(cols), block(cols), block(cols)],
        ),
        out_shape=[
            jax.ShapeDtypeStruct((length, cols), BF16),
            jax.ShapeDtypeStruct((length, cols), F32),
            jax.ShapeDtypeStruct((length, cols), F32),
        ],
        compiler_params=pltpu.CompilerParams(vmem_limit_bytes=VMEM_LIMIT),
        cost_estimate=pl.CostEstimate(flops=20 * 10**9, bytes_accessed=12 * 10**6, transcendentals=7 * 10**6),
        name="attend",
    )(table, q, kv, rows, starts, raw, raw)


def backward_kernel(
    table_ref, q_ref, kv_ref, row_ref, start_ref, own_ref, other_ref, context_ref, inverse_ref, grad_ref,
    dq_ref, dkv_ref, dlogit_ref, sums_ref, *, pairs, repeat, size, step,
):
    stripe = pl.program_id(0)
    wide_blocks = table_ref[stripe, 0]
    low = table_ref[stripe, 1]
    high = table_ref[stripe, 2]
    pair, single = places(table_ref, stripe, step, kv_ref.shape[0])

    @pl.when(stripe == 0)
    def _():
        sums_ref[...] = jnp.zeros_like(sums_ref)

    dlogit_ref[...] = jnp.zeros_like(dlogit_ref)
    rows = jnp.concatenate([row_ref[0]] * repeat, axis=1)
    starts = jnp.concatenate([start_ref[0]] * repeat, axis=1)
    queries, all_grads, all_inners = [], [], []
    for k in range(pairs):
        heads = [k * repeat + r for r in range(repeat)]
        queries.append(jnp.concatenate([q_ref[:, h * size : (h + 1) * size] for h in heads], axis=0))
        grads, inners = [], []
        for h in heads:
            cols = slice(h * size, (h + 1) * size)
            up = grad_ref[:, cols]
            gate = jax.nn.sigmoid(logit_of(h, pairs * repeat, own_ref, other_ref))
            product = jnp.sum(up * context_ref[:, cols], axis=1, keepdims=True)
            half = pairs * repeat // 2
            at = h // half * LANES + h % half
            dlogit_ref[:, at : at + 1] = product * gate * (1.0 - gate)
            inverse = inverse_ref[:, cols]
            grads.append((up * gate * inverse).astype(BF16))
            inners.append(product * gate * inverse)
        all_grads.append(jnp.concatenate(grads, axis=0))
        all_inners.append(jnp.transpose(jnp.concatenate(inners, axis=0))[0:1])

    def seen(totals, where, first):
        outs = []
        for k in range(pairs):
            key_cols = slice(k * size, (k + 1) * size)
            value_cols = slice((pairs + k) * size, (pairs + k + 1) * size)
            keys = join([kv_ref[at, key_cols] for at in where])
            weights = jnp.exp2(dot_trans(keys, queries[k]))
            if first is not None:
                index = first + lax.broadcasted_iota(jnp.int32, weights.shape, 0)
                weights = jnp.where((index <= rows) & (index >= starts), weights, 0.0)
            changes = dot_trans(join([kv_ref[at, value_cols] for at in where]), all_grads[k])
            changes = (weights * (changes - all_inners[k])).astype(BF16)
            value_sums = dot_rows(weights.astype(BF16), all_grads[k])
            key_sums = dot_rows(changes, queries[k])
            for i, at in enumerate(where):
                sums_ref[at, value_cols] += value_sums[i * step : (i + 1) * step]
                sums_ref[at, key_cols] += key_sums[i * step : (i + 1) * step]
            outs.append(totals[k] + dot_inner(changes, keys))
        return tuple(outs)

    totals = tuple(jnp.zeros((query.shape[0], size), F32) for query in queries)
    totals = lax.fori_loop(0, wide_blocks, lambda i, t: seen(t, pair(i), None), totals)
    totals = lax.fori_loop(low, high + 1, lambda i, t: seen(t, single(i), i * step), totals)
    for k, total in enumerate(totals):
        for r in range(repeat):
            h = k * repeat + r
            dq_ref[:, h * size : (h + 1) * size] = total[r * step : (r + 1) * step]

    @pl.when(stripe == pl.num_programs(0) - 1)
    def _():
        dkv_ref[...] = sums_ref[...].astype(BF16)


def attend_back(table, q, kv, rows, starts, raw, context, inverse, grad, pairs, size):
    length, cols = q.shape
    heads = cols // size
    step = length // table.shape[0]
    block = lambda width: pl.BlockSpec((step, width), lambda i, t: (i, 0))
    whole = pl.BlockSpec(kv.shape, lambda i, t: (0, 0), pipeline_mode=pl.Buffered(1))
    lane = pl.BlockSpec((1, 1, step), lambda i, t: (i, 0, 0))
    logits = logit_specs(raw, heads, pairs, size, step)
    return pl.pallas_call(
        functools.partial(backward_kernel, pairs=pairs, repeat=heads // pairs, size=size, step=step),
        grid_spec=pltpu.PrefetchScalarGridSpec(
            num_scalar_prefetch=1,
            grid=(length // step,),
            in_specs=[block(cols), whole, lane, lane, *logits, block(cols), block(cols), block(cols)],
            out_specs=[block(cols), whole, block(2 * LANES)],
            scratch_shapes=[pltpu.VMEM(kv.shape, F32)],
        ),
        out_shape=[
            jax.ShapeDtypeStruct((length, cols), F32),
            jax.ShapeDtypeStruct(kv.shape, BF16),
            jax.ShapeDtypeStruct((length, 2 * LANES), F32),
        ],
        compiler_params=pltpu.CompilerParams(vmem_limit_bytes=VMEM_LIMIT),
        cost_estimate=pl.CostEstimate(flops=50 * 10**9, bytes_accessed=20 * 10**6, transcendentals=7 * 10**6),
        name="attend_back",
    )(table, q, kv, rows.reshape(-1, 1, step), starts.reshape(-1, 1, step), raw, raw, context, inverse, grad)


class Wires:
    def __init__(self, send_sems, recv_sems, local_sems, sizes):
        self.send_sems, self.recv_sems, self.local_sems = send_sems, recv_sems, local_sems
        self.sizes = sizes
        self.sent, self.local, self.open = [], [], []
        self.locals_used, self.sends_used = 0, 0
        self.dp, self.wide, self.narrow = (lax.axis_index(a) for a in ("dp", "wide", "narrow"))
        self.y, self.core = self.narrow // 2, self.narrow % 2
        self.x, self.far = self.dp % 2, self.wide // 2

    def peer(self, *to):
        if isinstance(to[0], tuple):
            return {axis: at for part in to for axis, at in self.peer(*part).items()}
        axis, distance = to
        at = {"dp": self.dp, "wide": self.wide, "narrow": self.narrow}[axis]
        bit = at // distance % 2
        return {axis: at + distance * (1 - 2 * bit) if distance < 3 else 3 - at}

    def greet(self, peers):
        barrier = pltpu.get_barrier_semaphore()
        for to in peers:
            pl.semaphore_signal(barrier, inc=1, device_id=self.peer(*to), device_id_type=pl.DeviceIdType.MESH)
        pl.semaphore_wait(barrier, len(peers))

    def make(self, source, target, to):
        i = self.sends_used
        self.sends_used += 1
        copy = pltpu.make_async_remote_copy(
            src_ref=source, dst_ref=target, send_sem=self.send_sems.at[i], recv_sem=self.recv_sems.at[i],
            device_id=self.peer(*to), device_id_type=pl.DeviceIdType.MESH,
        )
        self.sent.append(copy)
        return copy

    def send(self, source, target, to):
        copy = self.make(source, target, to)
        copy.start()
        self.open.append(copy)
        return copy

    def arrived(self, copy):
        copy.wait_recv()
        self.open = [other for other in self.open if other is not copy]

    def copy(self, source, target):
        copy = pltpu.make_async_copy(source, target, self.local_sems.at[self.locals_used])
        self.locals_used += 1
        copy.start()
        self.local.append(copy)
        return copy

    def finish(self):
        for copy in list(self.open):
            self.arrived(copy)
        for copy in self.sent:
            copy.wait_send()
        for copy in self.local:
            copy.wait()


Y, CORE, CORNER, NEAR, FAR, X = ("narrow", 2), ("narrow", 1), ("narrow", 3), ("wide", 1), ("wide", 2), ("dp", 1)


def local_flow(net, values_ref, rows_ref):
    rows, width = rows_ref.shape[0], values_ref.shape[1]
    half = width // 2
    out = []
    for distance, to in ((0, None), (1, CORE), (2, Y), (3, CORNER)):
        target = net.narrow if to is None else net.peer(*to)["narrow"]
        at = (2 * (distance % 2) + net.y) * width
        for j in range(2):
            sub = net.x if j == 0 else 1 - net.x
            source = values_ref.at[pl.ds(pl.multiple_of(target * rows, rows), rows), pl.ds(pl.multiple_of(sub * half, half), half)]
            goal = rows_ref.at[:, pl.ds(pl.multiple_of(at + j * half, half), half)]
            out.append(net.copy(source, goal) if to is None else net.send(source, goal, to))
    return out


def gather_flow(net, values_ref, all_ref):
    rows = values_ref.shape[0]
    half = rows // 2
    part = lambda i: all_ref.at[pl.ds(i * half, half), :]
    first, second = values_ref.at[pl.ds(0, half), :], values_ref.at[pl.ds(half, half), :]
    first_y = net.send(first, part(2), Y)
    second_z = net.send(second, part(5), NEAR)
    net.send(first, part(4), NEAR)
    net.send(second, part(3), Y)
    net.copy(values_ref, all_ref.at[pl.ds(0, rows), :])
    yield
    net.arrived(first_y)
    net.send(part(2), part(6), NEAR)
    yield
    net.arrived(second_z)
    net.send(part(5), part(7), Y)
    yield


def weight_flow(net, source_ref, out_ref, axis, own, other, across, from_y=None, from_far=None, from_both=None, their_y=None, their_far=None):
    step = source_ref.shape[axis] // 2
    count = source_ref.shape[axis]

    def window(ref, at, start):
        long, wide = pl.ds(pl.multiple_of(at, step), step), pl.ds(start, across)
        return ref.at[long, wide] if axis == 0 else ref.at[wide, long]

    y, x = net.y, net.x
    piece = lambda sub, half: window(source_ref, sub * step, pl.multiple_of(half * across, across))
    place = lambda slot, j, start: window(out_ref, slot * count + j * step, start)
    mine, rest = piece(x, y), piece(1 - x, y)
    net.copy(mine, place(y, 0, own))
    net.copy(rest, place(y, 1, own))
    if from_y is None:
        come_y = net.send(piece(x, 1 - y), place(y, 0, own), Y)
    else:
        net.copy(from_y, place(1 - y, 0, own))
    if from_far is None:
        come_far = net.send(mine, place(y, 0, other), FAR)
    else:
        net.copy(from_far, place(y, 0, other))
    net.send(mine, place(2 + y, 0, own), CORE)
    net.send(rest, place(2 + y, 1, own), CORE)
    if from_y is None:
        yield
        net.arrived(come_y)
        from_y = place(1 - y, 0, own)
    if from_both is None:
        come_both = net.send(from_y, place(1 - y, 0, other), FAR)
    else:
        net.copy(from_both, place(1 - y, 0, other))
    given = their_y is not None
    if given:
        for ref, slot, start in ((their_y, 1 - y, own), (their_far, y, other)):
            net.copy(ref, place(slot, 1, start))
            net.send(ref, place(slot + 2, 1, start), CORE)
    else:
        their_y = net.send(from_y, place(1 - y, 1, own), X)
    net.send(from_y, place(3 - y, 0, own), CORE)
    if from_far is None:
        yield
        net.arrived(come_far)
        from_far = place(y, 0, other)
    if not given:
        their_far = net.send(from_far, place(y, 1, other), X)
    net.send(from_far, place(2 + y, 0, other), CORE)
    if from_both is None:
        yield
        net.arrived(come_both)
        from_both = place(1 - y, 0, other)
    their_both = net.send(from_both, place(1 - y, 1, other), X)
    net.send(from_both, place(3 - y, 0, other), CORE)
    yield
    waiting = ((their_y, 1 - y, own), (their_far, y, other), (their_both, 1 - y, other))
    for copy, slot, start in waiting[2 * given :]:
        net.arrived(copy)
        net.send(place(slot, 1, start), place(slot + 2, 1, start), CORE)
    yield


def run(flow):
    return next(flow, None)


def by_rows(count, body):
    step = 16
    lax.fori_loop(0, count // step, lambda i, _: (body(pl.ds(pl.multiple_of(i * step, step), step)), 0)[1], 0)


def begin_kernel(
    tokens_ref, cotangent_ref, gain_ref, qkv_ref, out_ref, x_ref, rows_ref, all_ref, joined_ref, output_ref,
    here, normed, there, send, recv, local, *, sizes,
):
    net = Wires(send, recv, local, sizes)
    net.greet([Y, CORE, CORNER, NEAR, FAR, X])
    rows = local_flow(net, tokens_ref, here)
    across = qkv_ref.shape[1] // 2
    joined = weight_flow(net, qkv_ref, joined_ref, 0, 0, across, across)
    run(joined)
    rows[0].wait()
    rows[1].wait()
    net.local = net.local[2:]
    for copy in rows[2:]:
        net.arrived(copy)

    def norm(at):
        values = here[at, :].astype(F32)
        inverse = lax.rsqrt(jnp.mean(values * values, axis=1, keepdims=True) + EPS)
        normed[at, :] = (values * inverse * gain_ref[...]).astype(BF16)
        x_ref[at, :] = here[at, :]

    by_rows(here.shape[0], norm)
    gather = gather_flow(net, normed, all_ref)
    run(gather)
    across = out_ref.shape[0] // 2
    output = weight_flow(net, out_ref, output_ref, 1, 0, across, across)
    for flow in (joined, gather, output, joined, gather):
        run(flow)
    rows = local_flow(net, cotangent_ref, there)
    for flow in (joined, output, joined, output, output, output):
        run(flow)
    for copy in rows[:2]:
        copy.wait()
    net.local = [copy for copy in net.local if all(copy is not other for other in rows[:2])]
    for copy in rows[2:]:
        net.arrived(copy)
    net.copy(there, rows_ref)
    net.finish()


ANY = pl.BlockSpec(memory_space=pl.ANY)
VMEM = pl.BlockSpec(memory_space=pltpu.VMEM)


def sems(sends, locals_):
    return [pltpu.SemaphoreType.DMA((sends,)), pltpu.SemaphoreType.DMA((sends,)), pltpu.SemaphoreType.DMA((locals_,))]


def wire_call(kernel, name, number, specs, out_specs, shapes, scratch, sizes, cost, *args):
    return pl.pallas_call(
        functools.partial(kernel, sizes=sizes),
        in_specs=specs,
        out_specs=out_specs,
        out_shape=[jax.ShapeDtypeStruct(*shape) for shape in shapes],
        scratch_shapes=scratch,
        compiler_params=pltpu.CompilerParams(collective_id=number, has_side_effects=True, vmem_limit_bytes=VMEM_LIMIT),
        cost_estimate=pl.CostEstimate(flops=0, bytes_accessed=cost * 3 * 10**6, transcendentals=0),
        name=name,
    )(*args)


def begin(tokens, cotangent, gain, qkv, out, sizes):
    rows, width = tokens.shape[0] // sizes["narrow"], gain.shape[0]
    row = pltpu.VMEM((rows, width), BF16)
    return wire_call(
        begin_kernel, "begin", 1, [ANY, ANY, VMEM, VMEM, VMEM], [VMEM, ANY, ANY, ANY, ANY],
        [
            ((rows, width), BF16), ((rows, width), BF16), ((4 * rows, width), BF16), ((width, qkv.shape[1]), BF16),
            ((out.shape[0], width), BF16),
        ],
        [row, row, row, *sems(48, 16)], sizes, 55, tokens, cotangent, gain[None], qkv, out,
    )


def keys_kernel(kv_ref, keys_ref, done, send, recv, local, *, sizes):
    net = Wires(send, recv, local, sizes)
    across = [FAR, ("wide", 3), (FAR, CORE), (("wide", 3), CORE)]
    net.greet([CORE] + across)
    count, width = kv_ref.shape
    size = width // 4
    part = lambda i, j: keys_ref.at[pl.ds(i, count), pl.ds(j * size, size)]
    base = pl.multiple_of(net.far * 2 * count, count)
    far = [net.make(kv_ref.at[:, pl.ds(j * size, size)], part(0, j ^ 1), FAR) for j in range(4)]
    on = [net.make(part(0, j ^ 1), part(count, j ^ 1), CORE) for j in range(4)]

    @pl.when(net.far == 0)
    def _():
        for copy in far:
            copy.start()

    net.copy(kv_ref, keys_ref.at[pl.ds(base, count), :])
    net.send(kv_ref, keys_ref.at[pl.ds(base + count, count), :], CORE)

    @pl.when(net.far == 1)
    def _():
        for copy, forward in zip(far, on):
            copy.wait_recv()
            forward.start()
        for to in across:
            pl.semaphore_signal(done, inc=1, device_id=net.peer(*to), device_id_type=pl.DeviceIdType.MESH)
        for forward in on:
            forward.wait()

    @pl.when(net.far == 0)
    def _():
        for copy in far:
            copy.wait_send()
        pl.semaphore_wait(done, len(across))

    net.sent = [copy for copy in net.sent if all(copy is not other for other in far + on)]
    net.finish()


def exchange_keys(kv, sizes):
    return wire_call(
        keys_kernel, "keys", 2, [VMEM], [ANY], [((4 * kv.shape[0], kv.shape[1]), BF16)],
        [pltpu.SemaphoreType.REGULAR, *sems(16, 4)], sizes, 45, kv,
    )[0]


def scatter_flow(net, partial_ref, first_ref, second_ref, send_ref, last_ref, total_ref):
    half = partial_ref.shape[0] // 8
    part = lambda i: partial_ref.at[pl.ds(i * half, half), :]
    slot = lambda ref, i: ref.at[pl.ds(i * half, half), :]
    to_z = [net.send(part(6), slot(first_ref, 1), NEAR), net.send(part(4), slot(first_ref, 0), NEAR)]
    to_y = [net.send(part(7), slot(second_ref, 1), Y), net.send(part(3), slot(second_ref, 0), Y)]
    yield

    def add(out_ref, to, i, ref, j):
        def body(at):
            move = lambda start: pl.ds(pl.multiple_of(at.start + start, 16), at.size)
            value = partial_ref[move(i * half), :].astype(F32) + ref[move(j * half), :].astype(F32)
            out_ref[move(to), :] = value.astype(out_ref.dtype)

        by_rows(half, body)

    net.arrived(to_z[0])
    add(send_ref, 0, 2, first_ref, 1)
    last_y = net.send(slot(send_ref, 0), slot(last_ref, 0), Y)
    net.arrived(to_y[0])
    add(send_ref, half, 5, second_ref, 1)
    last_z = net.send(slot(send_ref, 1), slot(last_ref, 1), NEAR)
    yield
    net.arrived(to_z[1])
    add(total_ref, 0, 0, first_ref, 0)
    net.arrived(to_y[1])
    add(total_ref, half, 1, second_ref, 0)
    yield
    net.arrived(last_y)
    net.arrived(last_z)
    yield


def middle_kernel(
    partial_ref, x_ref, gain_ref, gate_ref, up_ref, down_ref, gate_y_ref, up_y_ref, down_y_ref, gate_far_ref, up_far_ref, down_far_ref,
    gate_both_ref, up_both_ref, down_both_ref, wide_x_ref, down_x_ref, middle_ref, all_ref, both_ref, last_ref,
    first, second, sums, last, total, normed, send, recv, local, *, sizes,
):
    net = Wires(send, recv, local, sizes)
    net.greet([Y, CORE, NEAR, FAR, X])
    scatter = scatter_flow(net, partial_ref, first, second, sums, last, total)
    run(scatter)
    across = gate_ref.shape[1] // 2
    step = gate_ref.shape[0] // 2
    their = [wide_x_ref.at[pl.ds(i * step, step), :] for i in range(4)] + [down_x_ref.at[:, pl.ds(i * step, step)] for i in range(2)]
    flows = [
        weight_flow(net, gate_ref, both_ref, 0, 0, across, across, gate_y_ref, gate_far_ref, gate_both_ref, their[0], their[2]),
        weight_flow(net, up_ref, both_ref, 0, 2 * across, 3 * across, across, up_y_ref, up_far_ref, up_both_ref, their[1], their[3]),
        weight_flow(net, down_ref, last_ref, 1, 0, across, across, down_y_ref, down_far_ref, down_both_ref, their[4], their[5]),
    ]
    for flow in flows:
        run(flow)
    run(scatter)
    run(scatter)
    run(scatter)

    def norm(at):
        values = x_ref[at, :].astype(F32) + total[at, :] + last[at, :].astype(F32)
        middle_ref[at, :] = values
        inverse = lax.rsqrt(jnp.mean(values * values, axis=1, keepdims=True) + EPS)
        normed[at, :] = (values * inverse * gain_ref[...]).astype(BF16)

    by_rows(normed.shape[0], norm)
    gather = gather_flow(net, normed, all_ref)
    run(gather)
    run(flows[0])
    run(gather)
    run(gather)
    run(flows[1])
    run(flows[2])
    net.finish()


def to_middle(partial, x, gain, gate, up, down, pieces, sizes):
    rows, width = x.shape
    buffer = lambda n, kind: pltpu.VMEM((n, width), kind)
    return wire_call(
        middle_kernel, "middle", 3, [VMEM] * 17, [VMEM, ANY, ANY, ANY],
        [((rows, width), F32), ((4 * rows, width), BF16), ((width, 2 * gate.shape[1]), BF16), ((down.shape[0], width), BF16)],
        [
            buffer(rows, BF16), buffer(rows, BF16), buffer(rows, BF16), buffer(rows, BF16), buffer(rows, F32), buffer(rows, BF16),
            *sems(64, 32),
        ],
        sizes, 80, partial, x, gain[None], gate, up, down, *pieces,
    )


def spread_flow(net, rows_ref, out_ref):
    rows, width = rows_ref.shape[0], out_ref.shape[1]
    half = width // 2
    base = pl.multiple_of(net.narrow * rows, rows)
    for distance, to in ((3, CORNER), (2, Y), (1, CORE), (0, None)):
        target = net.narrow if to is None else net.peer(*to)["narrow"]
        at = (2 * (distance % 2) + target // 2) * width
        for j in range(2):
            sub = net.x if j == 0 else 1 - net.x
            source = rows_ref.at[:, pl.ds(pl.multiple_of(at + j * half, half), half)]
            goal = out_ref.at[pl.ds(base, rows), pl.ds(pl.multiple_of(sub * half, half), half)]
            if to is None:
                net.copy(source, goal)
            else:
                net.send(source, goal, to)


def add_rows(target, terms):
    ref, (rows, cols) = target

    def body(at):
        move = lambda r: pl.ds(pl.multiple_of(at.start + r.start, 16), at.size)
        value = sum(term[move(r), c].astype(F32) for term, (r, c) in terms)
        ref[move(rows), cols] = value.astype(BF16)

    by_rows(rows.size, body)


class Gradient:
    def __init__(self, net, axis, step, across):
        self.net, self.axis, self.step, self.across = net, axis, step, across
        self.order = (1 - net.y, net.y)
        self.x, self.far = [], []

    def window(self, at, start, count, length=None):
        step = self.step if length is None else length
        hint = lambda v, unit: v if isinstance(v, int) else pl.multiple_of(v, unit)
        along, wide = pl.ds(hint(at, self.step), step), pl.ds(hint(start, self.across), count)
        return (along, wide) if self.axis == 0 else (wide, along)

    def start(self, g_ref, acc, from_core, given=False):
        self.acc, self.from_core = acc, from_core
        count = 4 * self.step
        own, other = (self.window(i * count, 0, 2 * self.across, count) for i in range(2))
        self.loaded = self.net.copy(g_ref.at[own], acc)
        self.core = None if given else self.net.send(g_ref.at[other], from_core, CORE)

    def wait_core(self):
        self.loaded.wait()
        self.net.local = [copy for copy in self.net.local if copy is not self.loaded]
        if self.core is not None:
            self.net.arrived(self.core)

    def core_to_x(self, from_x):
        self.wait_core()
        self.from_x = from_x
        for slot in self.order:
            place = self.window((2 * slot + 1) * self.step, 0, 2 * self.across)
            add_rows((self.acc, place), [(self.acc, place), (self.from_core, place)])
            goal = from_x.at[self.window(slot * self.step, 0, 2 * self.across)]
            self.x.append(self.net.send(self.acc.at[place], goal, X))

    def x_end(self, k, from_far=None):
        slot = self.order[k]
        self.net.arrived(self.x[k])
        for start in (self.across, 0):
            place = self.window(2 * slot * self.step, start, self.across)
            come = self.window(slot * self.step, start, self.across)
            add_rows((self.acc, place), [(self.acc, place), (self.from_core, place), (self.from_x, come)])
            if start and from_far is not None:
                self.from_far = from_far
                goal = from_far.at[self.window(slot * self.step, 0, self.across)]
                self.far.append(self.net.send(self.acc.at[place], goal, FAR))

    def far_end(self, k, result=None):
        slot = self.order[k]
        self.net.arrived(self.far[k])
        place = self.window(2 * slot * self.step, 0, self.across)
        come = self.window(slot * self.step, 0, self.across)
        add_rows((self.acc, place), [(self.acc, place), (self.from_far, come)])

    def to_owner(self, k, source, out):
        net, across = self.net, self.across
        goal = out.at[self.window(net.x * self.step, net.y * across, across)]
        if k == 0:
            self.out = out
            self.y = net.send(source, goal, Y)
        else:
            net.copy(source, goal)
            net.send(source, goal, X)

    def after_y(self):
        net, across = self.net, self.across
        net.arrived(self.y)
        place = self.out.at[self.window(net.x * self.step, (1 - net.y) * across, across)]
        net.send(place, place, X)

    def slot(self, k, stride, start, count):
        return self.window(stride * self.order[k] * self.step, start, count)


def row_back(grad, values, gain):
    inverse = lax.rsqrt(jnp.mean(values * values, axis=1, keepdims=True) + EPS)
    hat = values * inverse
    scaled = grad * gain
    inner = jnp.mean(scaled * hat, axis=1, keepdims=True)
    return jnp.sum(grad * hat, axis=0, keepdims=True), inverse * (scaled - hat * inner)


def turn_kernel(
    partial_ref, middle_ref, upstream_ref, gain_ref, down_ref, gate_ref, up_ref,
    grad_ref, all_ref, term_ref, down_out, gate_out, up_keep, up_send,
    first, second, sums, last, total, low, *rest, sizes,
):
    buffers, (send, recv, local) = rest[:-3], rest[-3:]
    net = Wires(send, recv, local, sizes)
    net.greet([Y, CORE, NEAR, FAR, X])
    scatter = scatter_flow(net, partial_ref, first, second, sums, last, total)
    run(scatter)
    step, across = low.shape[1] // sizes["narrow"] // 2, gate_ref.shape[1] // 2
    down, gate, up = (Gradient(net, axis, step, across) for axis in (1, 0, 0))
    down.start(down_ref, *buffers[0:2])
    gate.start(gate_ref, *buffers[3:5])
    up.start(up_ref, *buffers[6:8])
    down.core_to_x(buffers[2])
    gate.core_to_x(buffers[5])
    run(scatter)
    run(scatter)
    run(scatter)
    term_ref[...] = jnp.zeros_like(term_ref)

    def rows(at):
        grad = total[at, :] + last[at, :].astype(F32)
        term, change = row_back(grad, middle_ref[at, :], gain_ref[...])
        term_ref[...] += term
        value = upstream_ref[at, :].astype(F32) + change
        grad_ref[at, :] = value
        low[at, :] = value.astype(BF16)

    by_rows(low.shape[0], rows)
    gather = gather_flow(net, low, all_ref)
    run(gather)
    for k in range(2):
        down.x_end(k)
        net.copy(down.acc.at[down.slot(k, 2, 0, 2 * across)], down_out.at[down.slot(k, 1, 0, 2 * across)])
    run(gather)
    run(gather)
    up.wait_core()
    for slot in range(2):
        for j, ref in ((1, up_send), (0, up_keep)):
            place = up.window((2 * slot + j) * step, 0, 2 * across)
            add_rows((up.acc, place), [(up.acc, place), (up.from_core, place)])
            net.copy(up.acc.at[place], ref.at[up.window(slot * step, 0, 2 * across)])
    for k in range(2):
        gate.x_end(k)
        net.copy(gate.acc.at[gate.slot(k, 2, 0, 2 * across)], gate_out.at[gate.slot(k, 1, 0, 2 * across)])
    net.finish()


def gradient_buffers(size, across, axis, count=4):
    shape = lambda a, b: pltpu.VMEM((a, b) if axis == 0 else (b, a), BF16)
    every = [shape(2 * size, 2 * across), shape(2 * size, 2 * across), shape(size, 2 * across), shape(size, across)]
    return every[:count]


def scatter_buffers(rows, width):
    buffer = lambda kind: pltpu.VMEM((rows, width), kind)
    return [buffer(BF16), buffer(BF16), buffer(BF16), buffer(BF16), buffer(F32)]


def turn(partial, middle, upstream, gain, down, gate, up, sizes):
    rows, width = middle.shape
    size, across = width // sizes["narrow"], down.shape[0] // 2
    return wire_call(
        turn_kernel, "turn", 4, [VMEM] * 4 + [ANY] * 3, [VMEM, ANY, VMEM, ANY, ANY, ANY, ANY],
        [
            ((rows, width), F32), ((4 * rows, width), BF16), ((1, width), F32),
            ((2 * across, size), BF16), ((size, 2 * across), BF16), ((size, 2 * across), BF16), ((size, 2 * across), BF16),
        ],
        [
            *scatter_buffers(rows, width), pltpu.VMEM((rows, width), BF16),
            *gradient_buffers(size, across, 1, 3), *gradient_buffers(size, across, 0, 3), *gradient_buffers(size, across, 0, 2), *sems(40, 16),
        ],
        sizes, 80, partial, middle, upstream, gain[None], down, gate, up,
    )


def owner_kernel(
    dkv_ref, partial_ref, middle_ref, down_ref, down_far_ref, gate_ref, gate_far_ref,
    mine_ref, layer_ref, down_out, gate_out,
    prompt_core, rest_core, prompt, prompt_far, first, second, sums, last, total, rows_low, down_sums, gate_sums,
    send, recv, local, *, sizes,
):
    net = Wires(send, recv, local, sizes)
    net.greet([Y, CORE, CORNER, NEAR, FAR, X])
    count, width = prompt.shape
    size = width // 4
    region = lambda i: dkv_ref.at[pl.ds(i * count, count), :]
    come = net.send(region(1), prompt_core, CORE)
    rest = net.send(region(3), rest_core, CORE)
    scatter = scatter_flow(net, partial_ref, first, second, sums, last, total)
    run(scatter)
    step, across = down_far_ref.shape[1] // 2, down_far_ref.shape[0]
    down, gate = (Gradient(net, axis, step, across) for axis in (1, 0))
    net.arrived(come)

    def add(at):
        prompt[at, :] = (dkv_ref[at, :].astype(F32) + prompt_core[at, :].astype(F32)).astype(BF16)

    by_rows(count, add)
    cols = lambda ref, j: ref.at[:, pl.ds(j * size, size)]
    far = [net.make(cols(prompt, j), cols(prompt_far, j ^ 1), FAR) for j in range(4)]

    @pl.when(net.far == 1)
    def _():
        for copy in far:
            copy.start()

    parts = ((down, down_sums, down_ref, down_far_ref, down_out), (gate, gate_sums, gate_ref, gate_far_ref, gate_out))
    for flow, total_ref, ref, far_ref, goal in parts:
        for k in range(2):
            place = flow.slot(k, 1, 0, across)
            add_rows((total_ref, place), [(ref, place), (far_ref, place)])
            flow.to_owner(k, total_ref.at[place], goal)
    run(scatter)
    run(scatter)
    run(scatter)

    def rows(at):
        rows_low[at, :] = (middle_ref[at, :] + total[at, :] + last[at, :].astype(F32)).astype(BF16)

    by_rows(rows_low.shape[0], rows)
    spread_flow(net, rows_low, layer_ref)
    down.after_y()
    gate.after_y()
    net.arrived(rest)

    @pl.when(net.far == 1)
    def _():
        def add(at):
            move = pl.ds(pl.multiple_of(at.start + 2 * count, 16), at.size)
            mine_ref[at, :] = dkv_ref[move, :].astype(F32) + rest_core[at, :].astype(F32)

        by_rows(count, add)
        for copy in far:
            copy.wait_send()

    @pl.when(net.far == 0)
    def _():
        for copy in far:
            copy.wait_recv()

        def add(at):
            mine_ref[at, :] = dkv_ref[at, :].astype(F32) + prompt_core[at, :].astype(F32) + prompt_far[at, :].astype(F32)

        by_rows(count, add)

    net.sent = [copy for copy in net.sent if all(copy is not other for other in far)]
    net.finish()


def to_owner(dkv, partial, middle, down, down_far, gate, gate_far, sizes):
    rows, width = middle.shape
    size, across = width // sizes["narrow"], gate_far.shape[1]
    count = dkv.shape[0] // 4
    block = lambda: pltpu.VMEM((count, dkv.shape[1]), BF16)
    return wire_call(
        owner_kernel, "owner", 5, [VMEM] * 7, [VMEM, ANY, ANY, ANY],
        [
            ((count, dkv.shape[1]), F32), ((sizes["narrow"] * rows, size), BF16), ((2 * across, size), BF16),
            ((size, 2 * across), BF16),
        ],
        [
            block(), block(), block(), block(), *scatter_buffers(rows, width), pltpu.VMEM((rows, width), BF16),
            pltpu.VMEM((across, size), BF16), pltpu.VMEM((size, across), BF16), *sems(40, 16),
        ],
        sizes, 80, dkv, partial, middle, down, down_far, gate, gate_far,
    )


SUMS = [CORE, Y, NEAR, X, FAR]


def end_kernel(
    partial_ref, x_ref, gain_ref, grad_ref, two_ref, query_ref, key_ref, up_ref, up_far_ref, qkv_core_ref, qkv_ref, out_ref,
    tokens_ref, gains_ref, qkv_out, out_out, up_out,
    first, second, sums, last, total, rows_low, vectors, up_sums, *rest, sizes,
):
    buffers, (send, recv, local) = rest[:-3], rest[-3:]
    net = Wires(send, recv, local, sizes)
    net.greet([Y, CORE, CORNER, NEAR, FAR, X])
    step = x_ref.shape[1] // sizes["narrow"] // 2
    qkv = Gradient(net, 0, step, qkv_ref.shape[1] // 2)
    out = Gradient(net, 1, step, out_ref.shape[0] // 2)
    qkv.start(qkv_ref, buffers[0], qkv_core_ref, True)
    out.start(out_ref, *buffers[3:5])
    scatter = scatter_flow(net, partial_ref, first, second, sums, last, total)
    run(scatter)
    up = Gradient(net, 0, step, up_far_ref.shape[1])
    qkv.core_to_x(buffers[1])
    out.core_to_x(buffers[5])
    for k in range(2):
        place = up.slot(k, 1, 0, up.across)
        add_rows((up_sums, place), [(up_ref, place), (up_far_ref, place)])
        up.to_owner(k, up_sums.at[place], up_out)
    run(scatter)
    qkv.x_end(0, buffers[2])
    run(scatter)
    qkv.x_end(1, buffers[2])
    run(scatter)
    width = x_ref.shape[1]
    size = query_ref.shape[1]
    block = width // sizes["narrow"]
    half = block // 2
    gains_ref[...] = jnp.zeros_like(gains_ref)

    def rows(at):
        grad = total[at, :] + last[at, :].astype(F32)
        term, change = row_back(grad, x_ref[at, :].astype(F32), gain_ref[...])
        gains_ref[:, :width] += term
        rows_low[at, :] = (grad_ref[at, :] + change).astype(BF16)

    by_rows(rows_low.shape[0], rows)
    for i, ref in enumerate((gains_ref, two_ref)):
        for slot in range(4):
            to = (2 * (slot % 2) + jnp.bitwise_xor(net.core, slot // 2)) * block + i * width
            for j in range(2):
                sub = net.x if j == 0 else 1 - net.x
                at = slot * block + j * half
                vectors[0, :, pl.ds(pl.multiple_of(to + sub * half, half), half)] = ref[:, at : at + half]
    vectors[0, :, 2 * width : 2 * width + size] = query_ref[...]
    vectors[0, :, 2 * width + size :] = key_ref[...]

    def add_gains():
        for i, to in enumerate(SUMS):
            copy = net.send(vectors.at[i], vectors.at[len(SUMS) + 1 + i], to)
            yield
            net.arrived(copy)
            vectors[i + 1] = vectors[i] + vectors[len(SUMS) + 1 + i]
        gains_ref[...] = vectors[len(SUMS)]
        yield

    def own(flow, k, ref):
        flow.far_end(k)
        flow.to_owner(k, flow.acc.at[flow.slot(k, 2, 0, flow.across)], ref)

    gains = add_gains()
    run(gains)
    out.x_end(0, buffers[6])
    out.x_end(1, buffers[6])
    run(gains)
    own(qkv, 0, qkv_out)
    run(gains)
    spread_flow(net, rows_low, tokens_ref)
    run(gains)
    own(qkv, 1, qkv_out)
    run(gains)
    own(out, 0, out_out)
    own(out, 1, out_out)
    up.after_y()
    qkv.after_y()
    out.after_y()
    run(gains)
    net.finish()


def end(partial, x, gain, grad, two, query, key, up, up_far, qkv_core, qkv, out, sizes):
    rows, width = x.shape
    size = width // sizes["narrow"]
    wide, deep = qkv.shape[1], out.shape[0]
    length = 2 * width + 2 * query.shape[1]
    return wire_call(
        end_kernel, "end", 6, [VMEM] * 10 + [ANY] * 2, [ANY, VMEM, ANY, ANY, ANY],
        [((sizes["narrow"] * rows, size), BF16), ((1, length), F32), ((size, wide), BF16), ((deep, size), BF16),
         ((size, 2 * up_far.shape[1]), BF16)],
        [
            *scatter_buffers(rows, width), pltpu.VMEM((rows, width), BF16), pltpu.VMEM((2 * len(SUMS) + 1, 1, length), F32),
            pltpu.VMEM(up_far.shape, BF16),
            *(v for i, v in enumerate(gradient_buffers(size, wide // 2, 0)) if i != 1), *gradient_buffers(size, deep // 2, 1),
            *sems(40, 16),
        ],
        sizes, 90, partial, x, gain[None], grad, two, query, key, up, up_far, qkv_core, qkv, out,
    )


def layout(lengths, index):
    order = jnp.arange(lengths.shape[0])
    ends = jnp.sum(jnp.where(order[None, :] <= order[:, None], lengths[None, :], 0), axis=1)[None, :]
    begins = ends - lengths[None, :]
    offset = index - PROMPT
    shift = jnp.sum(jnp.where((offset >= begins) & (offset < ends), begins, 0), axis=1, keepdims=True)
    return jnp.where(offset >= 0, PROMPT + shift, 0), index - shift


def make(sizes):
    n_dp, n_wide, n_narrow = sizes["dp"], sizes["wide"], sizes["narrow"]

    def over_y(values):
        return exchange(values, "narrow", 2, n_narrow)

    def over_z(values):
        return exchange(values, "wide", 1, n_wide)

    def over_x(values):
        return exchange(values, "dp", 1, n_dp)

    def over_core(values):
        return exchange(values, "narrow", 1, n_narrow)

    def over_far(values):
        return exchange(values, "wide", 2, n_wide)

    def over_groups(values, kind):
        distance = 2
        while distance < n_dp:
            values = values.astype(F32) + exchange(values.astype(kind), "dp", distance, n_dp).astype(F32)
            distance *= 2
        return values.astype(F32)

    def on_device(
        tokens, continuation_lengths, attention_gain, query_weight, key_weight, value_weight, head_gate, query_gain, key_gain,
        output_weight, feedforward_gain, gate_weight, up_weight, down_weight, cotangent,
    ):
        rows_wide, width_local = tokens.shape
        width = attention_gain.shape[0]
        size = query_gain.shape[0]
        heads = head_gate.shape[1]
        pairs = key_weight.shape[1] // size
        group_rows = rows_wide * n_wide
        rows_local = rows_wide // n_narrow
        x = lax.axis_index("dp") % 2
        z = lax.axis_index("wide")
        narrow = lax.axis_index("narrow")
        y, core = narrow // 2, narrow % 2
        z_near, z_far = z % 2, z // 2
        quarter = width_local // 2
        scale = size ** (-0.5)
        factor = scale * math.log2(math.e)
        log_two = math.log(2.0)

        def relative_vector(vector):
            values = jnp.transpose(vector.reshape(2, 2, 2, quarter), (1, 0, 2, 3))
            values = jnp.where(core == 0, values, values[::-1])
            return jnp.where(x == 0, values, values[:, :, ::-1]).reshape(width)

        def piece_of(weight, i, axis):
            half = weight.shape[1 - axis] // 2
            return cut(cut(weight, x * quarter, quarter, axis), i * half, half, 1 - axis)

        gain_one, gain_two = relative_vector(attention_gain), relative_vector(feedforward_gain)
        lane_pad = ((0, 0), (0, LANES - heads // 2))
        halves = lambda w, i: w[:, i * (w.shape[1] // 2) : (i + 1) * (w.shape[1] // 2)]
        packed = join(
            [v for i in range(2) for v in (
                halves(query_weight, i), halves(key_weight, i), halves(value_weight, i), jnp.pad(halves(head_gate, i), lane_pad)
            )], 1
        )
        inputs, upstream, normed_all, joined_weight, out_weight = begin(tokens, cotangent, gain_one, packed, output_weight, sizes)

        def indices(row):
            part, at = row // rows_local, row % rows_local
            return ((z ^ (part // 2)) * n_narrow + (narrow ^ (2 * (part % 2)))) * rows_local + at

        my_index = indices(lax.broadcasted_iota(jnp.int32, (4 * rows_local, 1), 0))
        my_start, my_position = layout(continuation_lengths[0], my_index)
        frequency = THETA ** (-2.0 * jnp.arange(size // 2, dtype=F32) / size)
        angle = my_position.astype(F32) * frequency[None, :]
        cosine, sine = jnp.cos(angle), jnp.sin(angle)
        cosine = jnp.concatenate([cosine, cosine], axis=1)
        sine = jnp.concatenate([-sine, sine], axis=1)
        heads_index = indices(lax.broadcasted_iota(jnp.int32, (4, 1), 0) * rows_local)
        block = heads_index // rows_local
        first = layout(continuation_lengths[0], heads_index)[0] // rows_local
        prompt_blocks = PROMPT // rows_local
        in_prompt = block < prompt_blocks
        column = lax.broadcasted_iota(jnp.int32, (4, 5), 1)
        pick = lambda values: functools.reduce(lambda acc, item: jnp.where(column == item[0], item[1], acc), enumerate(values), 0)
        table = pick(
            [
                jnp.where(in_prompt, block // 2, prompt_blocks // 2),
                jnp.where(in_prompt, block // 2 * 2, first),
                block,
                2 * z_near + y,
                core,
            ]
        ).astype(jnp.int32)

        raw = dot_rows(normed_all, joined_weight)
        q, kv = post(raw, cosine, sine, query_gain, key_gain, heads, pairs, size, factor)
        send = after((gate_weight, up_weight, down_weight), normed_all)
        axes = (0, 0, 1)
        from_y = [over_y(piece_of(w, 1 - y, axis)) for w, axis in zip(send, axes)]
        from_far = [over_far(piece_of(w, y, axis)) for w, axis in zip(send, axes)]
        part = rows_local // 2
        kv_all = exchange_keys(after(kv, *from_y, *from_far), sizes)
        upstream_y, upstream_z = over_y(after(upstream[:part], kv_all)), over_z(after(upstream[part:], kv_all))
        from_both = [over_far(after(v, kv_all)) for v in from_y]
        their_parts = [
            over_x(after(join(from_y[:2] + from_far[:2]), kv_all)),
            over_x(after(join([from_y[2], from_far[2]], 1), kv_all)),
        ]

        gated, context, inverse_total = attend(
            table, q, kv_all, my_index, my_start, raw, pairs, size
        )
        partial = dot_rows(after(gated, their_parts[0], upstream_y, upstream_z), out_weight).astype(BF16)
        middle, normed_two_all, gate_up, down = to_middle(
            partial, inputs, gain_two, gate_weight, up_weight, down_weight, from_y + from_far + from_both + their_parts, sizes
        )
        come_z = over_z(join([upstream[:part], after(upstream_y, normed_two_all)]))
        come_y = over_y(join([upstream[part:], after(upstream_z, normed_two_all)]))
        upstream_all = join(
            [upstream, upstream_y, come_y[:part], come_z[:part], upstream_z, come_z[part:], come_y[part:]]
        )
        both = dot_rows(normed_two_all, gate_up)
        hidden_cols = gate_weight.shape[1]
        gate_pre, up_pre = both[:, :hidden_cols], both[:, hidden_cols:]
        gate_sigmoid = jax.nn.sigmoid(gate_pre)
        silu = gate_pre * gate_sigmoid
        hidden = (silu * up_pre).astype(BF16)
        hidden_grad = dot_trans(upstream_all, down)
        gate_grad = hidden_grad * up_pre * gate_sigmoid * (1.0 + gate_pre * (1.0 - gate_sigmoid))
        up_grad = hidden_grad * silu
        gate_up_low = join([gate_grad, up_grad], 1).astype(BF16)
        partial = dot_trans(gate_up_low, gate_up).astype(BF16)
        gate_low, up_low = gate_up_low[:, :hidden_cols], gate_up_low[:, hidden_cols:]
        down_sums = dot_inner(hidden, upstream_all).astype(BF16)
        gate_sums = dot_inner(normed_two_all, gate_low).astype(BF16)
        up_sums = dot_inner(normed_two_all, up_low).astype(BF16)
        middle_grad, middle_all, two_term, down_part, gate_part, up_keep, up_send = turn(
            partial, middle, upstream, gain_two, down_sums, gate_sums, up_sums, sizes
        )
        down_far = over_far(down_part[hidden_cols // 2 :])
        far_part = gate_part[:, hidden_cols // 2 :]
        gate_far = [over_far(far_part[i * quarter : (i + 1) * quarter]) for i in range(2)]
        up_come = over_x(up_send)
        gated_grad = dot_trans(middle_all, out_weight)
        mlp_partial = dot_rows(after(hidden, gated_grad), down).astype(BF16)
        gated_grad = after(gated_grad, gate_far[0], mlp_partial)
        dq, dkv, logit_grad = attend_back(
            table, q, kv_all, my_index, my_start, raw, context, inverse_total, gated_grad, pairs, size
        )
        up_part = (up_keep.astype(F32) + up_come.astype(F32)).astype(BF16)
        dkv_mine, layer_output, down_gradient, gate_gradient = to_owner(
            dkv, mlp_partial, middle, down_part, down_far, gate_part, join(gate_far), sizes
        )
        far_part = after(up_part[:, hidden_cols // 2 :], dkv_mine)
        up_far = [over_far(far_part[i * quarter : (i + 1) * quarter]) for i in range(2)]
        low, query_term, key_term = project_back(
            dq, dkv_mine, raw, cosine, sine, query_gain, key_gain, logit_grad, heads, pairs, size, scale, log_two
        )
        half = width // 2
        low = after(low, up_far[0])
        qkv_sums = dot_inner(normed_all, low).astype(BF16)
        qkv_core = over_core(qkv_sums[half:])
        partial = dot_trans(after(low, qkv_sums), joined_weight).astype(BF16)
        out_sums = dot_inner(after(gated, dkv_mine), middle_all).astype(BF16)
        tokens_gradient, gains, qkv_gradient, output_gradient, up_gradient = end(
            partial, inputs, gain_one, middle_grad, two_term, query_term, key_term, up_part[:, : hidden_cols // 2], join(up_far),
            qkv_core, qkv_sums, out_sums, sizes
        )
        tokens_gradient = tokens_gradient.astype(F32)
        gains = over_groups(gains[0], F32)
        qkv_gradient = over_groups(qkv_gradient, BF16)
        down_gradient, gate_gradient, up_gradient, output_gradient = (
            over_groups(v, BF16) for v in (down_gradient, gate_gradient, up_gradient, output_gradient)
        )
        block = qkv_gradient.shape[1] // 2
        query_cols, key_cols = heads // 2 * size, pairs // 2 * size
        take = lambda at, count: join([qkv_gradient[:, at + i * block : at + i * block + count] for i in range(2)], 1)
        query_gradient = take(0, query_cols)
        key_gradient = take(query_cols, key_cols)
        value_gradient = take(query_cols + key_cols, key_cols)
        head_gate_gradient = take(query_cols + 2 * key_cols, heads // 2)
        return (
            layer_output,
            tokens_gradient,
            gains[:width],
            query_gradient,
            key_gradient,
            value_gradient,
            head_gate_gradient,
            gains[2 * width : 2 * width + size],
            gains[2 * width + size :],
            output_gradient,
            gains[width : 2 * width],
            gate_gradient,
            up_gradient,
            down_gradient,
        )

    return on_device


def solution(mesh):
    rows, up, down = P(("dp", "wide"), "narrow"), P("narrow", "wide"), P("wide", "narrow")
    return jax.shard_map(
        make(dict(mesh.shape)),
        mesh=mesh,
        in_specs=(rows, P("dp", None), P(), up, up, up, up, P(), P(), down, P(), up, up, down, rows),
        out_specs=(rows, rows, P(), up, up, up, up, P(), P(), down, P(), up, up, down),
        check_vma=False,
    )
```

```python
import functools
import math

import jax
import jax.numpy as jnp
from jax import lax
from jax.experimental import pallas as pl
from jax.experimental.pallas import tpu as pltpu
from jax.sharding import PartitionSpec as P

PROMPT = 2048
EPS = 1e-06
THETA = 1000000.0
RELATIVE = (0, 2, 1, 3)
BF16 = jnp.bfloat16
F32 = jnp.float32
VMEM_LIMIT = 56 * 1024 * 1024
LANES = 128


def dot_rows(left, right):
    return jnp.dot(left, right, preferred_element_type=F32)


def dot_trans(left, right):
    return lax.dot_general(left, right, (((1,), (1,)), ((), ())), preferred_element_type=F32)


def dot_inner(left, right):
    return lax.dot_general(left, right, (((0,), (0,)), ((), ())), preferred_element_type=F32)


def exchange(values, axis, distance, size):
    return lax.ppermute(values, axis, [(i, i ^ distance) for i in range(size)])


def join(parts, axis=0):
    return jnp.concatenate(parts, axis=axis)


def cut(values, at, length, axis):
    return lax.dynamic_slice_in_dim(values, at, length, axis=axis)


def turn_pairs(values):
    step = values.shape[1] // 4
    return join([values[:, i * step : (i + 1) * step] for i in (1, 0, 3, 2)], 1)


def after(values, *others):
    return lax.optimization_barrier((values,) + others)[0]


def columns(heads, pairs, size):
    query, pair = heads // 2, pairs // 2
    block = (query + 2 * pair) * size + LANES
    of = lambda i, count, before: (i // count) * block + (before + i % count) * size
    return (
        [of(h, query, 0) for h in range(heads)],
        [of(p, pair, query) for p in range(pairs)],
        [of(p, pair, query + pair) for p in range(pairs)],
        [block - LANES, 2 * block - LANES],
    )


def post_kernel(raw_ref, cos_ref, sin_ref, query_gain_ref, key_gain_ref, q_ref, kv_ref, *, heads, pairs, size, factor):
    cosine = cos_ref[...]
    sine = sin_ref[...]
    query_at, key_at, value_at, _ = columns(heads, pairs, size)

    def turned(value, gain):
        inverse = lax.rsqrt(jnp.mean(value * value, axis=-1, keepdims=True) + EPS)
        normal = value * inverse * gain
        return normal * cosine + pltpu.roll(normal, size // 2, 1) * sine

    for h, at in enumerate(query_at):
        value = raw_ref[:, at : at + size]
        q_ref[:, h * size : (h + 1) * size] = (turned(value, query_gain_ref[...]) * factor).astype(BF16)
    for p, at in enumerate(key_at):
        kv_ref[:, p * size : (p + 1) * size] = turned(raw_ref[:, at : at + size], key_gain_ref[...]).astype(BF16)
    for p, at in enumerate(value_at):
        to = (pairs + p) * size
        kv_ref[:, to : to + size] = raw_ref[:, at : at + size].astype(BF16)


def post(raw, cosine, sine, query_gain, key_gain, heads, pairs, size, factor):
    rows, width = raw.shape
    step = 256
    return pl.pallas_call(
        functools.partial(post_kernel, heads=heads, pairs=pairs, size=size, factor=factor),
        grid=(rows // step,),
        in_specs=[
            pl.BlockSpec((step, width), lambda i: (i, 0)),
            pl.BlockSpec((step, size), lambda i: (i, 0)),
            pl.BlockSpec((step, size), lambda i: (i, 0)),
            pl.BlockSpec((1, size), lambda i: (0, 0)),
            pl.BlockSpec((1, size), lambda i: (0, 0)),
        ],
        out_specs=[
            pl.BlockSpec((step, heads * size), lambda i: (i, 0)),
            pl.BlockSpec((step, 2 * pairs * size), lambda i: (i, 0)),
        ],
        out_shape=[
            jax.ShapeDtypeStruct((rows, heads * size), BF16),
            jax.ShapeDtypeStruct((rows, 2 * pairs * size), BF16),
        ],
        cost_estimate=pl.CostEstimate(flops=rows * width * 20, bytes_accessed=rows * width * 8, transcendentals=0),
        name="post",
    )(raw, cosine, sine, query_gain[None], key_gain[None])


def back_kernel(
    dq_ref, dkv_ref, raw_ref, cos_ref, sin_ref, query_gain_ref, key_gain_ref, logit_ref, out_ref, gq_ref, gk_ref, *, heads, pairs, size, factor_q, factor_k
):
    cosine = cos_ref[...]
    sine = sin_ref[...]
    query_at, key_at, value_at, logit_at = columns(heads, pairs, size)

    @pl.when(pl.program_id(0) == 0)
    def _():
        gq_ref[...] = jnp.zeros_like(gq_ref)
        gk_ref[...] = jnp.zeros_like(gk_ref)

    def back(up, value, gain, total_ref):
        up = up * cosine - pltpu.roll(up, size // 2, 1) * sine
        inverse = lax.rsqrt(jnp.mean(value * value, axis=-1, keepdims=True) + EPS)
        hat = value * inverse
        total_ref[...] += jnp.sum(up * hat, axis=0, keepdims=True)
        scaled = up * gain
        return inverse * (scaled - hat * jnp.mean(scaled * hat, axis=-1, keepdims=True))

    for h, at in enumerate(query_at):
        up = dq_ref[:, h * size : (h + 1) * size] * factor_q
        out_ref[:, at : at + size] = back(up, raw_ref[:, at : at + size], query_gain_ref[...], gq_ref).astype(BF16)
    for p, at in enumerate(key_at):
        up = dkv_ref[:, p * size : (p + 1) * size].astype(F32) * factor_k
        out_ref[:, at : at + size] = back(up, raw_ref[:, at : at + size], key_gain_ref[...], gk_ref).astype(BF16)
    for p, at in enumerate(value_at):
        to = (pairs + p) * size
        out_ref[:, at : at + size] = dkv_ref[:, to : to + size].astype(BF16)
    for i, at in enumerate(logit_at):
        out_ref[:, at : at + LANES] = logit_ref[:, i * LANES : (i + 1) * LANES].astype(BF16)


def project_back(dq, dkv, raw, cosine, sine, query_gain, key_gain, logit_grad, heads, pairs, size, factor_q, factor_k):
    rows, width = raw.shape
    step = 256
    row = lambda cols: pl.BlockSpec((step, cols), lambda i: (i, 0))
    one = pl.BlockSpec((1, size), lambda i: (0, 0))
    return pl.pallas_call(
        functools.partial(back_kernel, heads=heads, pairs=pairs, size=size, factor_q=factor_q, factor_k=factor_k),
        grid=(rows // step,),
        in_specs=[row(heads * size), row(2 * pairs * size), row(width), row(size), row(size), one, one, row(2 * LANES)],
        out_specs=[row(width), one, one],
        out_shape=[
            jax.ShapeDtypeStruct((rows, width), BF16),
            jax.ShapeDtypeStruct((1, size), F32),
            jax.ShapeDtypeStruct((1, size), F32),
        ],
        cost_estimate=pl.CostEstimate(flops=rows * width * 30, bytes_accessed=rows * width * 12, transcendentals=0),
        name="project_back",
    )(dq, dkv, raw, cosine, sine, query_gain[None], key_gain[None], logit_grad)


def places(table_ref, stripe, step, length):
    turn = table_ref[stripe, 3]
    core = table_ref[stripe, 4]
    half = length // 2
    blocks = half // step

    def pair(i):
        at = jnp.bitwise_xor(i, turn) * step
        return pl.ds(pl.multiple_of(at, step), step), pl.ds(pl.multiple_of(at + half // 2, step), step)

    def single(b):
        part = b // blocks
        inner = b - part * blocks
        at = part * half + jnp.bitwise_xor(inner % 2, core) * (half // 2) + jnp.bitwise_xor(inner // 2, turn) * step
        return (pl.ds(pl.multiple_of(at, step), step),)

    return pair, single


def logit_of(head, heads, own_ref, other_ref):
    half = heads // 2
    at = head % half
    return (own_ref if head < half else other_ref)[:, at : at + 1]


def logit_specs(raw, heads, pairs, size, step):
    spec = lambda i: pl.BlockSpec((step, LANES), lambda s, t: (s, i))
    return [spec(at // LANES) for at in columns(heads, pairs, size)[3]]


def forward_kernel(table_ref, q_ref, kv_ref, row_ref, start_ref, own_ref, other_ref, gated_ref, context_ref, inverse_ref, *, pairs, repeat, size, step):
    stripe = pl.program_id(0)
    wide_blocks = table_ref[stripe, 0]
    low = table_ref[stripe, 1]
    high = table_ref[stripe, 2]
    pair, single = places(table_ref, stripe, step, kv_ref.shape[0])
    rows = row_ref[...]
    starts = start_ref[...]
    rows = jnp.concatenate([rows] * repeat, axis=0)
    starts = jnp.concatenate([starts] * repeat, axis=0)
    queries = [
        jnp.concatenate([q_ref[:, h * size : (h + 1) * size] for h in range(k * repeat, (k + 1) * repeat)], axis=0)
        for k in range(pairs)
    ]

    def seen(totals, where, first):
        outs = []
        for k in range(pairs):
            keys = join([kv_ref[at, k * size : (k + 1) * size] for at in where])
            weights = jnp.exp2(dot_trans(queries[k], keys))
            if first is not None:
                index = first + lax.broadcasted_iota(jnp.int32, weights.shape, 1)
                weights = jnp.where((index <= rows) & (index >= starts), weights, 0.0)
            values = join([kv_ref[at, (pairs + k) * size : (pairs + k + 1) * size] for at in where])
            values = jnp.concatenate([values, jnp.ones_like(values)], axis=1)
            outs.append(totals[k] + dot_rows(weights.astype(BF16), values))
        return tuple(outs)

    totals = tuple(jnp.zeros((query.shape[0], 2 * size), F32) for query in queries)
    totals = lax.fori_loop(0, wide_blocks, lambda i, t: seen(t, pair(i), None), totals)
    totals = lax.fori_loop(low, high + 1, lambda i, t: seen(t, single(i), i * step), totals)
    for k, total in enumerate(totals):
        inverse = 1.0 / total[:, size:]
        context = total[:, :size] * inverse
        for r in range(repeat):
            h = k * repeat + r
            part = context[r * step : (r + 1) * step]
            cols = slice(h * size, (h + 1) * size)
            gate = jax.nn.sigmoid(logit_of(h, pairs * repeat, own_ref, other_ref))
            gated_ref[:, cols] = (part * gate).astype(BF16)
            context_ref[:, cols] = part
            inverse_ref[:, cols] = inverse[r * step : (r + 1) * step]


def attend(table, q, kv, rows, starts, raw, pairs, size):
    length, cols = q.shape
    heads = cols // size
    step = length // table.shape[0]
    block = lambda width: pl.BlockSpec((step, width), lambda i, t: (i, 0))
    return pl.pallas_call(
        functools.partial(forward_kernel, pairs=pairs, repeat=heads // pairs, size=size, step=step),
        grid_spec=pltpu.PrefetchScalarGridSpec(
            num_scalar_prefetch=1,
            grid=(length // step,),
            in_specs=[
                block(cols),
                pl.BlockSpec(kv.shape, lambda i, t: (0, 0), pipeline_mode=pl.Buffered(1)),
                block(1),
                block(1),
                *logit_specs(raw, heads, pairs, size, step),
            ],
            out_specs=[block(cols), block(cols), block(cols)],
        ),
        out_shape=[
            jax.ShapeDtypeStruct((length, cols), BF16),
            jax.ShapeDtypeStruct((length, cols), F32),
            jax.ShapeDtypeStruct((length, cols), F32),
        ],
        compiler_params=pltpu.CompilerParams(vmem_limit_bytes=VMEM_LIMIT),
        cost_estimate=pl.CostEstimate(flops=20 * 10**9, bytes_accessed=12 * 10**6, transcendentals=7 * 10**6),
        name="attend",
    )(table, q, kv, rows, starts, raw, raw)


def backward_kernel(
    table_ref, q_ref, kv_ref, row_ref, start_ref, own_ref, other_ref, context_ref, inverse_ref, grad_ref,
    dq_ref, dkv_ref, dlogit_ref, sums_ref, *, pairs, repeat, size, step,
):
    stripe = pl.program_id(0)
    wide_blocks = table_ref[stripe, 0]
    low = table_ref[stripe, 1]
    high = table_ref[stripe, 2]
    pair, single = places(table_ref, stripe, step, kv_ref.shape[0])

    @pl.when(stripe == 0)
    def _():
        sums_ref[...] = jnp.zeros_like(sums_ref)

    dlogit_ref[...] = jnp.zeros_like(dlogit_ref)
    rows = jnp.concatenate([row_ref[0]] * repeat, axis=1)
    starts = jnp.concatenate([start_ref[0]] * repeat, axis=1)
    queries, all_grads, all_inners = [], [], []
    for k in range(pairs):
        heads = [k * repeat + r for r in range(repeat)]
        queries.append(jnp.concatenate([q_ref[:, h * size : (h + 1) * size] for h in heads], axis=0))
        grads, inners = [], []
        for h in heads:
            cols = slice(h * size, (h + 1) * size)
            up = grad_ref[:, cols]
            gate = jax.nn.sigmoid(logit_of(h, pairs * repeat, own_ref, other_ref))
            product = jnp.sum(up * context_ref[:, cols], axis=1, keepdims=True)
            half = pairs * repeat // 2
            at = h // half * LANES + h % half
            dlogit_ref[:, at : at + 1] = product * gate * (1.0 - gate)
            inverse = inverse_ref[:, cols]
            grads.append((up * gate * inverse).astype(BF16))
            inners.append(product * gate * inverse)
        all_grads.append(jnp.concatenate(grads, axis=0))
        all_inners.append(jnp.transpose(jnp.concatenate(inners, axis=0))[0:1])

    def seen(totals, where, first):
        outs = []
        for k in range(pairs):
            key_cols = slice(k * size, (k + 1) * size)
            value_cols = slice((pairs + k) * size, (pairs + k + 1) * size)
            keys = join([kv_ref[at, key_cols] for at in where])
            weights = jnp.exp2(dot_trans(keys, queries[k]))
            if first is not None:
                index = first + lax.broadcasted_iota(jnp.int32, weights.shape, 0)
                weights = jnp.where((index <= rows) & (index >= starts), weights, 0.0)
            changes = dot_trans(join([kv_ref[at, value_cols] for at in where]), all_grads[k])
            changes = (weights * (changes - all_inners[k])).astype(BF16)
            value_sums = dot_rows(weights.astype(BF16), all_grads[k])
            key_sums = dot_rows(changes, queries[k])
            for i, at in enumerate(where):
                sums_ref[at, value_cols] += value_sums[i * step : (i + 1) * step]
                sums_ref[at, key_cols] += key_sums[i * step : (i + 1) * step]
            outs.append(totals[k] + dot_inner(changes, keys))
        return tuple(outs)

    totals = tuple(jnp.zeros((query.shape[0], size), F32) for query in queries)
    totals = lax.fori_loop(0, wide_blocks, lambda i, t: seen(t, pair(i), None), totals)
    totals = lax.fori_loop(low, high + 1, lambda i, t: seen(t, single(i), i * step), totals)
    for k, total in enumerate(totals):
        for r in range(repeat):
            h = k * repeat + r
            dq_ref[:, h * size : (h + 1) * size] = total[r * step : (r + 1) * step]

    @pl.when(stripe == pl.num_programs(0) - 1)
    def _():
        dkv_ref[...] = sums_ref[...].astype(BF16)


def attend_back(table, q, kv, rows, starts, raw, context, inverse, grad, pairs, size):
    length, cols = q.shape
    heads = cols // size
    step = length // table.shape[0]
    block = lambda width: pl.BlockSpec((step, width), lambda i, t: (i, 0))
    whole = pl.BlockSpec(kv.shape, lambda i, t: (0, 0), pipeline_mode=pl.Buffered(1))
    lane = pl.BlockSpec((1, 1, step), lambda i, t: (i, 0, 0))
    logits = logit_specs(raw, heads, pairs, size, step)
    return pl.pallas_call(
        functools.partial(backward_kernel, pairs=pairs, repeat=heads // pairs, size=size, step=step),
        grid_spec=pltpu.PrefetchScalarGridSpec(
            num_scalar_prefetch=1,
            grid=(length // step,),
            in_specs=[block(cols), whole, lane, lane, *logits, block(cols), block(cols), block(cols)],
            out_specs=[block(cols), whole, block(2 * LANES)],
            scratch_shapes=[pltpu.VMEM(kv.shape, F32)],
        ),
        out_shape=[
            jax.ShapeDtypeStruct((length, cols), F32),
            jax.ShapeDtypeStruct(kv.shape, BF16),
            jax.ShapeDtypeStruct((length, 2 * LANES), F32),
        ],
        compiler_params=pltpu.CompilerParams(vmem_limit_bytes=VMEM_LIMIT),
        cost_estimate=pl.CostEstimate(flops=50 * 10**9, bytes_accessed=20 * 10**6, transcendentals=7 * 10**6),
        name="attend_back",
    )(table, q, kv, rows.reshape(-1, 1, step), starts.reshape(-1, 1, step), raw, raw, context, inverse, grad)


class Wires:
    def __init__(self, send_sems, recv_sems, local_sems, sizes):
        self.send_sems, self.recv_sems, self.local_sems = send_sems, recv_sems, local_sems
        self.sizes = sizes
        self.sent, self.local, self.open = [], [], []
        self.locals_used, self.sends_used = 0, 0
        self.dp, self.wide, self.narrow = (lax.axis_index(a) for a in ("dp", "wide", "narrow"))
        self.y, self.core = self.narrow // 2, self.narrow % 2
        self.x, self.far = self.dp % 2, self.wide // 2

    def peer(self, *to):
        if isinstance(to[0], tuple):
            return {axis: at for part in to for axis, at in self.peer(*part).items()}
        axis, distance = to
        at = {"dp": self.dp, "wide": self.wide, "narrow": self.narrow}[axis]
        bit = at // distance % 2
        return {axis: at + distance * (1 - 2 * bit) if distance < 3 else 3 - at}

    def greet(self, peers):
        barrier = pltpu.get_barrier_semaphore()
        for to in peers:
            pl.semaphore_signal(barrier, inc=1, device_id=self.peer(*to), device_id_type=pl.DeviceIdType.MESH)
        pl.semaphore_wait(barrier, len(peers))

    def make(self, source, target, to):
        i = self.sends_used
        self.sends_used += 1
        copy = pltpu.make_async_remote_copy(
            src_ref=source, dst_ref=target, send_sem=self.send_sems.at[i], recv_sem=self.recv_sems.at[i],
            device_id=self.peer(*to), device_id_type=pl.DeviceIdType.MESH,
        )
        self.sent.append(copy)
        return copy

    def send(self, source, target, to):
        copy = self.make(source, target, to)
        copy.start()
        self.open.append(copy)
        return copy

    def arrived(self, copy):
        copy.wait_recv()
        self.open = [other for other in self.open if other is not copy]

    def copy(self, source, target):
        copy = pltpu.make_async_copy(source, target, self.local_sems.at[self.locals_used])
        self.locals_used += 1
        copy.start()
        self.local.append(copy)
        return copy

    def finish(self):
        for copy in list(self.open):
            self.arrived(copy)
        for copy in self.sent:
            copy.wait_send()
        for copy in self.local:
            copy.wait()


Y, CORE, CORNER, NEAR, FAR, X = ("narrow", 2), ("narrow", 1), ("narrow", 3), ("wide", 1), ("wide", 2), ("dp", 1)


def local_flow(net, values_ref, rows_ref):
    rows, width = rows_ref.shape[0], values_ref.shape[1]
    half = width // 2
    out = []
    for distance, to in ((0, None), (1, CORE), (2, Y), (3, CORNER)):
        target = net.narrow if to is None else net.peer(*to)["narrow"]
        at = (2 * (distance % 2) + net.y) * width
        for j in range(2):
            sub = net.x if j == 0 else 1 - net.x
            source = values_ref.at[pl.ds(pl.multiple_of(target * rows, rows), rows), pl.ds(pl.multiple_of(sub * half, half), half)]
            goal = rows_ref.at[:, pl.ds(pl.multiple_of(at + j * half, half), half)]
            out.append(net.copy(source, goal) if to is None else net.send(source, goal, to))
    return out


def gather_flow(net, values_ref, all_ref):
    rows = values_ref.shape[0]
    half = rows // 2
    part = lambda i: all_ref.at[pl.ds(i * half, half), :]
    first, second = values_ref.at[pl.ds(0, half), :], values_ref.at[pl.ds(half, half), :]
    first_y = net.send(first, part(2), Y)
    second_z = net.send(second, part(5), NEAR)
    net.send(first, part(4), NEAR)
    net.send(second, part(3), Y)
    net.copy(values_ref, all_ref.at[pl.ds(0, rows), :])
    yield
    net.arrived(first_y)
    net.send(part(2), part(6), NEAR)
    yield
    net.arrived(second_z)
    net.send(part(5), part(7), Y)
    yield


def weight_flow(net, source_ref, out_ref, axis, own, other, across, from_y=None, from_far=None, from_both=None, their_y=None, their_far=None):
    step = source_ref.shape[axis] // 2
    count = source_ref.shape[axis]

    def window(ref, at, start):
        long, wide = pl.ds(pl.multiple_of(at, step), step), pl.ds(start, across)
        return ref.at[long, wide] if axis == 0 else ref.at[wide, long]

    y, x = net.y, net.x
    piece = lambda sub, half: window(source_ref, sub * step, pl.multiple_of(half * across, across))
    place = lambda slot, j, start: window(out_ref, slot * count + j * step, start)
    mine, rest = piece(x, y), piece(1 - x, y)
    net.copy(mine, place(y, 0, own))
    net.copy(rest, place(y, 1, own))
    if from_y is None:
        come_y = net.send(piece(x, 1 - y), place(y, 0, own), Y)
    else:
        net.copy(from_y, place(1 - y, 0, own))
    if from_far is None:
        come_far = net.send(mine, place(y, 0, other), FAR)
    else:
        net.copy(from_far, place(y, 0, other))
    net.send(mine, place(2 + y, 0, own), CORE)
    net.send(rest, place(2 + y, 1, own), CORE)
    if from_y is None:
        yield
        net.arrived(come_y)
        from_y = place(1 - y, 0, own)
    if from_both is None:
        come_both = net.send(from_y, place(1 - y, 0, other), FAR)
    else:
        net.copy(from_both, place(1 - y, 0, other))
    given = their_y is not None
    if given:
        for ref, slot, start in ((their_y, 1 - y, own), (their_far, y, other)):
            net.copy(ref, place(slot, 1, start))
            net.send(ref, place(slot + 2, 1, start), CORE)
    else:
        their_y = net.send(from_y, place(1 - y, 1, own), X)
    net.send(from_y, place(3 - y, 0, own), CORE)
    if from_far is None:
        yield
        net.arrived(come_far)
        from_far = place(y, 0, other)
    if not given:
        their_far = net.send(from_far, place(y, 1, other), X)
    net.send(from_far, place(2 + y, 0, other), CORE)
    if from_both is None:
        yield
        net.arrived(come_both)
        from_both = place(1 - y, 0, other)
    their_both = net.send(from_both, place(1 - y, 1, other), X)
    net.send(from_both, place(3 - y, 0, other), CORE)
    yield
    waiting = ((their_y, 1 - y, own), (their_far, y, other), (their_both, 1 - y, other))
    for copy, slot, start in waiting[2 * given :]:
        net.arrived(copy)
        net.send(place(slot, 1, start), place(slot + 2, 1, start), CORE)
    yield


def run(flow):
    return next(flow, None)


def by_rows(count, body):
    step = 16
    lax.fori_loop(0, count // step, lambda i, _: (body(pl.ds(pl.multiple_of(i * step, step), step)), 0)[1], 0)


def begin_kernel(
    tokens_ref, cotangent_ref, gain_ref, qkv_ref, out_ref, x_ref, rows_ref, all_ref, joined_ref, output_ref,
    here, normed, there, send, recv, local, *, sizes,
):
    net = Wires(send, recv, local, sizes)
    net.greet([Y, CORE, CORNER, NEAR, FAR, X])
    rows = local_flow(net, tokens_ref, here)
    across = qkv_ref.shape[1] // 2
    joined = weight_flow(net, qkv_ref, joined_ref, 0, 0, across, across)
    run(joined)
    rows[0].wait()
    rows[1].wait()
    net.local = net.local[2:]
    for copy in rows[2:]:
        net.arrived(copy)

    def norm(at):
        values = here[at, :].astype(F32)
        inverse = lax.rsqrt(jnp.mean(values * values, axis=1, keepdims=True) + EPS)
        normed[at, :] = (values * inverse * gain_ref[...]).astype(BF16)
        x_ref[at, :] = here[at, :]

    by_rows(here.shape[0], norm)
    gather = gather_flow(net, normed, all_ref)
    run(gather)
    across = out_ref.shape[0] // 2
    output = weight_flow(net, out_ref, output_ref, 1, 0, across, across)
    for flow in (joined, gather, output, joined, gather):
        run(flow)
    rows = local_flow(net, cotangent_ref, there)
    for flow in (joined, output, joined, output, output, output):
        run(flow)
    for copy in rows[:2]:
        copy.wait()
    net.local = [copy for copy in net.local if all(copy is not other for other in rows[:2])]
    for copy in rows[2:]:
        net.arrived(copy)
    net.copy(there, rows_ref)
    net.finish()


ANY = pl.BlockSpec(memory_space=pl.ANY)
VMEM = pl.BlockSpec(memory_space=pltpu.VMEM)


def sems(sends, locals_):
    return [pltpu.SemaphoreType.DMA((sends,)), pltpu.SemaphoreType.DMA((sends,)), pltpu.SemaphoreType.DMA((locals_,))]


def wire_call(kernel, name, number, specs, out_specs, shapes, scratch, sizes, cost, *args):
    return pl.pallas_call(
        functools.partial(kernel, sizes=sizes),
        in_specs=specs,
        out_specs=out_specs,
        out_shape=[jax.ShapeDtypeStruct(*shape) for shape in shapes],
        scratch_shapes=scratch,
        compiler_params=pltpu.CompilerParams(collective_id=number, has_side_effects=True, vmem_limit_bytes=VMEM_LIMIT),
        cost_estimate=pl.CostEstimate(flops=0, bytes_accessed=cost * 3 * 10**6, transcendentals=0),
        name=name,
    )(*args)


def begin(tokens, cotangent, gain, qkv, out, sizes):
    rows, width = tokens.shape[0] // sizes["narrow"], gain.shape[0]
    row = pltpu.VMEM((rows, width), BF16)
    return wire_call(
        begin_kernel, "begin", 1, [ANY, ANY, VMEM, VMEM, VMEM], [VMEM, ANY, ANY, ANY, ANY],
        [
            ((rows, width), BF16), ((rows, width), BF16), ((4 * rows, width), BF16), ((width, qkv.shape[1]), BF16),
            ((out.shape[0], width), BF16),
        ],
        [row, row, row, *sems(48, 16)], sizes, 55, tokens, cotangent, gain[None], qkv, out,
    )


def keys_kernel(kv_ref, keys_ref, done, send, recv, local, *, sizes):
    net = Wires(send, recv, local, sizes)
    across = [FAR, ("wide", 3), (FAR, CORE), (("wide", 3), CORE)]
    net.greet([CORE] + across)
    count, width = kv_ref.shape
    size = width // 4
    part = lambda i, j: keys_ref.at[pl.ds(i, count), pl.ds(j * size, size)]
    base = pl.multiple_of(net.far * 2 * count, count)
    far = [net.make(kv_ref.at[:, pl.ds(j * size, size)], part(0, j ^ 1), FAR) for j in range(4)]
    on = [net.make(part(0, j ^ 1), part(count, j ^ 1), CORE) for j in range(4)]

    @pl.when(net.far == 0)
    def _():
        for copy in far:
            copy.start()

    net.copy(kv_ref, keys_ref.at[pl.ds(base, count), :])
    net.send(kv_ref, keys_ref.at[pl.ds(base + count, count), :], CORE)

    @pl.when(net.far == 1)
    def _():
        for copy, forward in zip(far, on):
            copy.wait_recv()
            forward.start()
        for to in across:
            pl.semaphore_signal(done, inc=1, device_id=net.peer(*to), device_id_type=pl.DeviceIdType.MESH)
        for forward in on:
            forward.wait()

    @pl.when(net.far == 0)
    def _():
        for copy in far:
            copy.wait_send()
        pl.semaphore_wait(done, len(across))

    net.sent = [copy for copy in net.sent if all(copy is not other for other in far + on)]
    net.finish()


def exchange_keys(kv, sizes):
    return wire_call(
        keys_kernel, "keys", 2, [VMEM], [ANY], [((4 * kv.shape[0], kv.shape[1]), BF16)],
        [pltpu.SemaphoreType.REGULAR, *sems(16, 4)], sizes, 45, kv,
    )[0]


def scatter_flow(net, partial_ref, first_ref, second_ref, send_ref, last_ref, total_ref):
    half = partial_ref.shape[0] // 8
    part = lambda i: partial_ref.at[pl.ds(i * half, half), :]
    slot = lambda ref, i: ref.at[pl.ds(i * half, half), :]
    to_z = [net.send(part(6), slot(first_ref, 1), NEAR), net.send(part(4), slot(first_ref, 0), NEAR)]
    to_y = [net.send(part(7), slot(second_ref, 1), Y), net.send(part(3), slot(second_ref, 0), Y)]
    yield

    def add(out_ref, to, i, ref, j):
        def body(at):
            move = lambda start: pl.ds(pl.multiple_of(at.start + start, 16), at.size)
            value = partial_ref[move(i * half), :].astype(F32) + ref[move(j * half), :].astype(F32)
            out_ref[move(to), :] = value.astype(out_ref.dtype)

        by_rows(half, body)

    net.arrived(to_z[0])
    add(send_ref, 0, 2, first_ref, 1)
    last_y = net.send(slot(send_ref, 0), slot(last_ref, 0), Y)
    net.arrived(to_y[0])
    add(send_ref, half, 5, second_ref, 1)
    last_z = net.send(slot(send_ref, 1), slot(last_ref, 1), NEAR)
    yield
    net.arrived(to_z[1])
    add(total_ref, 0, 0, first_ref, 0)
    net.arrived(to_y[1])
    add(total_ref, half, 1, second_ref, 0)
    yield
    net.arrived(last_y)
    net.arrived(last_z)
    yield


def middle_kernel(
    partial_ref, x_ref, gain_ref, gate_ref, up_ref, down_ref, gate_y_ref, up_y_ref, down_y_ref, gate_far_ref, up_far_ref, down_far_ref,
    gate_both_ref, up_both_ref, down_both_ref, middle_ref, all_ref, both_ref, last_ref,
    first, second, sums, last, total, normed, send, recv, local, *, sizes,
):
    net = Wires(send, recv, local, sizes)
    net.greet([Y, CORE, NEAR, FAR, X])
    scatter = scatter_flow(net, partial_ref, first, second, sums, last, total)
    run(scatter)
    across = gate_ref.shape[1] // 2
    flows = [
        weight_flow(net, gate_ref, both_ref, 0, 0, across, across, gate_y_ref, gate_far_ref, gate_both_ref),
        weight_flow(net, up_ref, both_ref, 0, 2 * across, 3 * across, across, up_y_ref, up_far_ref, up_both_ref),
        weight_flow(net, down_ref, last_ref, 1, 0, across, across, down_y_ref, down_far_ref, down_both_ref),
    ]
    for flow in flows:
        run(flow)
    run(scatter)
    run(scatter)
    run(scatter)

    def norm(at):
        values = x_ref[at, :].astype(F32) + total[at, :] + last[at, :].astype(F32)
        middle_ref[at, :] = values
        inverse = lax.rsqrt(jnp.mean(values * values, axis=1, keepdims=True) + EPS)
        normed[at, :] = (values * inverse * gain_ref[...]).astype(BF16)

    by_rows(normed.shape[0], norm)
    gather = gather_flow(net, normed, all_ref)
    run(gather)
    run(flows[0])
    run(gather)
    run(gather)
    run(flows[1])
    run(flows[2])
    net.finish()


def to_middle(partial, x, gain, gate, up, down, pieces, sizes):
    rows, width = x.shape
    buffer = lambda n, kind: pltpu.VMEM((n, width), kind)
    return wire_call(
        middle_kernel, "middle", 3, [VMEM] * 15, [VMEM, ANY, ANY, ANY],
        [((rows, width), F32), ((4 * rows, width), BF16), ((width, 2 * gate.shape[1]), BF16), ((down.shape[0], width), BF16)],
        [
            buffer(rows, BF16), buffer(rows, BF16), buffer(rows, BF16), buffer(rows, BF16), buffer(rows, F32), buffer(rows, BF16),
            *sems(64, 32),
        ],
        sizes, 80, partial, x, gain[None], gate, up, down, *pieces,
    )


def spread_flow(net, rows_ref, out_ref):
    rows, width = rows_ref.shape[0], out_ref.shape[1]
    half = width // 2
    base = pl.multiple_of(net.narrow * rows, rows)
    for distance, to in ((3, CORNER), (2, Y), (1, CORE), (0, None)):
        target = net.narrow if to is None else net.peer(*to)["narrow"]
        at = (2 * (distance % 2) + target // 2) * width
        for j in range(2):
            sub = net.x if j == 0 else 1 - net.x
            source = rows_ref.at[:, pl.ds(pl.multiple_of(at + j * half, half), half)]
            goal = out_ref.at[pl.ds(base, rows), pl.ds(pl.multiple_of(sub * half, half), half)]
            if to is None:
                net.copy(source, goal)
            else:
                net.send(source, goal, to)


def add_rows(target, terms):
    ref, (rows, cols) = target

    def body(at):
        move = lambda r: pl.ds(pl.multiple_of(at.start + r.start, 16), at.size)
        value = sum(term[move(r), c].astype(F32) for term, (r, c) in terms)
        ref[move(rows), cols] = value.astype(BF16)

    by_rows(rows.size, body)


class Gradient:
    def __init__(self, net, axis, step, across):
        self.net, self.axis, self.step, self.across = net, axis, step, across
        self.order = (1 - net.y, net.y)
        self.x, self.far = [], []

    def window(self, at, start, count, length=None):
        step = self.step if length is None else length
        hint = lambda v, unit: v if isinstance(v, int) else pl.multiple_of(v, unit)
        along, wide = pl.ds(hint(at, self.step), step), pl.ds(hint(start, self.across), count)
        return (along, wide) if self.axis == 0 else (wide, along)

    def start(self, g_ref, acc, from_core, given=False):
        self.acc, self.from_core = acc, from_core
        count = 4 * self.step
        own, other = (self.window(i * count, 0, 2 * self.across, count) for i in range(2))
        self.loaded = self.net.copy(g_ref.at[own], acc)
        self.core = None if given else self.net.send(g_ref.at[other], from_core, CORE)

    def wait_core(self):
        self.loaded.wait()
        self.net.local = [copy for copy in self.net.local if copy is not self.loaded]
        if self.core is not None:
            self.net.arrived(self.core)

    def core_to_x(self, from_x):
        self.wait_core()
        self.from_x = from_x
        for slot in self.order:
            place = self.window((2 * slot + 1) * self.step, 0, 2 * self.across)
            add_rows((self.acc, place), [(self.acc, place), (self.from_core, place)])
            goal = from_x.at[self.window(slot * self.step, 0, 2 * self.across)]
            self.x.append(self.net.send(self.acc.at[place], goal, X))

    def x_end(self, k, from_far=None):
        slot = self.order[k]
        self.net.arrived(self.x[k])
        for start in (self.across, 0):
            place = self.window(2 * slot * self.step, start, self.across)
            come = self.window(slot * self.step, start, self.across)
            add_rows((self.acc, place), [(self.acc, place), (self.from_core, place), (self.from_x, come)])
            if start and from_far is not None:
                self.from_far = from_far
                goal = from_far.at[self.window(slot * self.step, 0, self.across)]
                self.far.append(self.net.send(self.acc.at[place], goal, FAR))

    def far_end(self, k, result=None):
        slot = self.order[k]
        self.net.arrived(self.far[k])
        place = self.window(2 * slot * self.step, 0, self.across)
        come = self.window(slot * self.step, 0, self.across)
        add_rows((self.acc, place), [(self.acc, place), (self.from_far, come)])

    def to_owner(self, k, source, out):
        net, across = self.net, self.across
        goal = out.at[self.window(net.x * self.step, net.y * across, across)]
        if k == 0:
            self.out = out
            self.y = net.send(source, goal, Y)
        else:
            net.copy(source, goal)
            net.send(source, goal, X)

    def after_y(self):
        net, across = self.net, self.across
        net.arrived(self.y)
        place = self.out.at[self.window(net.x * self.step, (1 - net.y) * across, across)]
        net.send(place, place, X)

    def slot(self, k, stride, start, count):
        return self.window(stride * self.order[k] * self.step, start, count)


def row_back(grad, values, gain):
    inverse = lax.rsqrt(jnp.mean(values * values, axis=1, keepdims=True) + EPS)
    hat = values * inverse
    scaled = grad * gain
    inner = jnp.mean(scaled * hat, axis=1, keepdims=True)
    return jnp.sum(grad * hat, axis=0, keepdims=True), inverse * (scaled - hat * inner)


def turn_kernel(
    partial_ref, middle_ref, upstream_ref, gain_ref, down_ref, gate_ref, up_ref,
    grad_ref, all_ref, term_ref, down_out, gate_out, up_keep, up_send,
    first, second, sums, last, total, low, *rest, sizes,
):
    buffers, (send, recv, local) = rest[:-3], rest[-3:]
    net = Wires(send, recv, local, sizes)
    net.greet([Y, CORE, NEAR, FAR, X])
    scatter = scatter_flow(net, partial_ref, first, second, sums, last, total)
    run(scatter)
    step, across = low.shape[1] // sizes["narrow"] // 2, gate_ref.shape[1] // 2
    down, gate, up = (Gradient(net, axis, step, across) for axis in (1, 0, 0))
    down.start(down_ref, *buffers[0:2])
    gate.start(gate_ref, *buffers[3:5])
    up.start(up_ref, *buffers[6:8])
    down.core_to_x(buffers[2])
    gate.core_to_x(buffers[5])
    run(scatter)
    run(scatter)
    run(scatter)
    term_ref[...] = jnp.zeros_like(term_ref)

    def rows(at):
        grad = total[at, :] + last[at, :].astype(F32)
        term, change = row_back(grad, middle_ref[at, :], gain_ref[...])
        term_ref[...] += term
        value = upstream_ref[at, :].astype(F32) + change
        grad_ref[at, :] = value
        low[at, :] = value.astype(BF16)

    by_rows(low.shape[0], rows)
    gather = gather_flow(net, low, all_ref)
    run(gather)
    for k in range(2):
        down.x_end(k)
        net.copy(down.acc.at[down.slot(k, 2, 0, 2 * across)], down_out.at[down.slot(k, 1, 0, 2 * across)])
    run(gather)
    run(gather)
    up.wait_core()
    for slot in range(2):
        for j, ref in ((1, up_send), (0, up_keep)):
            place = up.window((2 * slot + j) * step, 0, 2 * across)
            add_rows((up.acc, place), [(up.acc, place), (up.from_core, place)])
            net.copy(up.acc.at[place], ref.at[up.window(slot * step, 0, 2 * across)])
    for k in range(2):
        gate.x_end(k)
        net.copy(gate.acc.at[gate.slot(k, 2, 0, 2 * across)], gate_out.at[gate.slot(k, 1, 0, 2 * across)])
    net.finish()


def gradient_buffers(size, across, axis, count=4):
    shape = lambda a, b: pltpu.VMEM((a, b) if axis == 0 else (b, a), BF16)
    every = [shape(2 * size, 2 * across), shape(2 * size, 2 * across), shape(size, 2 * across), shape(size, across)]
    return every[:count]


def scatter_buffers(rows, width):
    buffer = lambda kind: pltpu.VMEM((rows, width), kind)
    return [buffer(BF16), buffer(BF16), buffer(BF16), buffer(BF16), buffer(F32)]


def turn(partial, middle, upstream, gain, down, gate, up, sizes):
    rows, width = middle.shape
    size, across = width // sizes["narrow"], down.shape[0] // 2
    return wire_call(
        turn_kernel, "turn", 4, [VMEM] * 4 + [ANY] * 3, [VMEM, ANY, VMEM, ANY, ANY, ANY, ANY],
        [
            ((rows, width), F32), ((4 * rows, width), BF16), ((1, width), F32),
            ((2 * across, size), BF16), ((size, 2 * across), BF16), ((size, 2 * across), BF16), ((size, 2 * across), BF16),
        ],
        [
            *scatter_buffers(rows, width), pltpu.VMEM((rows, width), BF16),
            *gradient_buffers(size, across, 1, 3), *gradient_buffers(size, across, 0, 3), *gradient_buffers(size, across, 0, 2), *sems(40, 16),
        ],
        sizes, 80, partial, middle, upstream, gain[None], down, gate, up,
    )


def owner_kernel(
    dkv_ref, partial_ref, middle_ref, down_ref, down_far_ref, gate_ref, gate_far_ref,
    mine_ref, layer_ref, down_out, gate_out,
    prompt_core, rest_core, prompt, prompt_far, first, second, sums, last, total, rows_low, down_sums, gate_sums,
    send, recv, local, *, sizes,
):
    net = Wires(send, recv, local, sizes)
    net.greet([Y, CORE, CORNER, NEAR, FAR, X])
    count, width = prompt.shape
    size = width // 4
    region = lambda i: dkv_ref.at[pl.ds(i * count, count), :]
    come = net.send(region(1), prompt_core, CORE)
    rest = net.send(region(3), rest_core, CORE)
    scatter = scatter_flow(net, partial_ref, first, second, sums, last, total)
    run(scatter)
    step, across = down_far_ref.shape[1] // 2, down_far_ref.shape[0]
    down, gate = (Gradient(net, axis, step, across) for axis in (1, 0))
    net.arrived(come)

    def add(at):
        prompt[at, :] = (dkv_ref[at, :].astype(F32) + prompt_core[at, :].astype(F32)).astype(BF16)

    by_rows(count, add)
    cols = lambda ref, j: ref.at[:, pl.ds(j * size, size)]
    far = [net.make(cols(prompt, j), cols(prompt_far, j ^ 1), FAR) for j in range(4)]

    @pl.when(net.far == 1)
    def _():
        for copy in far:
            copy.start()

    parts = ((down, down_sums, down_ref, down_far_ref, down_out), (gate, gate_sums, gate_ref, gate_far_ref, gate_out))
    for flow, total_ref, ref, far_ref, goal in parts:
        for k in range(2):
            place = flow.slot(k, 1, 0, across)
            add_rows((total_ref, place), [(ref, place), (far_ref, place)])
            flow.to_owner(k, total_ref.at[place], goal)
    run(scatter)
    run(scatter)
    run(scatter)

    def rows(at):
        rows_low[at, :] = (middle_ref[at, :] + total[at, :] + last[at, :].astype(F32)).astype(BF16)

    by_rows(rows_low.shape[0], rows)
    spread_flow(net, rows_low, layer_ref)
    down.after_y()
    gate.after_y()
    net.arrived(rest)

    @pl.when(net.far == 1)
    def _():
        def add(at):
            move = pl.ds(pl.multiple_of(at.start + 2 * count, 16), at.size)
            mine_ref[at, :] = dkv_ref[move, :].astype(F32) + rest_core[at, :].astype(F32)

        by_rows(count, add)
        for copy in far:
            copy.wait_send()

    @pl.when(net.far == 0)
    def _():
        for copy in far:
            copy.wait_recv()

        def add(at):
            mine_ref[at, :] = dkv_ref[at, :].astype(F32) + prompt_core[at, :].astype(F32) + prompt_far[at, :].astype(F32)

        by_rows(count, add)

    net.sent = [copy for copy in net.sent if all(copy is not other for other in far)]
    net.finish()


def to_owner(dkv, partial, middle, down, down_far, gate, gate_far, sizes):
    rows, width = middle.shape
    size, across = width // sizes["narrow"], gate_far.shape[1]
    count = dkv.shape[0] // 4
    block = lambda: pltpu.VMEM((count, dkv.shape[1]), BF16)
    return wire_call(
        owner_kernel, "owner", 5, [VMEM] * 7, [VMEM, ANY, ANY, ANY],
        [
            ((count, dkv.shape[1]), F32), ((sizes["narrow"] * rows, size), BF16), ((2 * across, size), BF16),
            ((size, 2 * across), BF16),
        ],
        [
            block(), block(), block(), block(), *scatter_buffers(rows, width), pltpu.VMEM((rows, width), BF16),
            pltpu.VMEM((across, size), BF16), pltpu.VMEM((size, across), BF16), *sems(40, 16),
        ],
        sizes, 80, dkv, partial, middle, down, down_far, gate, gate_far,
    )


SUMS = [CORE, Y, NEAR, X, FAR]


def end_kernel(
    partial_ref, x_ref, gain_ref, grad_ref, two_ref, query_ref, key_ref, up_ref, up_x_ref, qkv_core_ref, qkv_ref, out_ref,
    tokens_ref, gains_ref, qkv_out, out_out, up_out,
    first, second, sums, last, total, rows_low, vectors, up_sums, up_far, *rest, sizes,
):
    buffers, (send, recv, local) = rest[:-3], rest[-3:]
    net = Wires(send, recv, local, sizes)
    net.greet([Y, CORE, CORNER, NEAR, FAR, X])
    step = x_ref.shape[1] // sizes["narrow"] // 2
    qkv = Gradient(net, 0, step, qkv_ref.shape[1] // 2)
    out = Gradient(net, 1, step, out_ref.shape[0] // 2)
    qkv.start(qkv_ref, buffers[0], qkv_core_ref, True)
    out.start(out_ref, *buffers[3:5])
    scatter = scatter_flow(net, partial_ref, first, second, sums, last, total)
    run(scatter)
    up = Gradient(net, 0, step, up_ref.shape[1] // 2)
    qkv.core_to_x(buffers[1])
    out.core_to_x(buffers[5])

    def up_to_far(k):
        for start in (up.across, 0):
            place = up.slot(k, 1, start, up.across)
            add_rows((up_sums, place), [(up_ref, place), (up_x_ref, place)])
            if start:
                up.far.append(net.send(up_sums.at[place], up_far.at[up.slot(k, 1, 0, up.across)], FAR))

    run(scatter)
    qkv.x_end(0, buffers[2])
    up_to_far(0)
    run(scatter)
    qkv.x_end(1, buffers[2])
    up_to_far(1)
    run(scatter)
    width = x_ref.shape[1]
    size = query_ref.shape[1]
    block = width // sizes["narrow"]
    half = block // 2
    gains_ref[...] = jnp.zeros_like(gains_ref)

    def rows(at):
        grad = total[at, :] + last[at, :].astype(F32)
        term, change = row_back(grad, x_ref[at, :].astype(F32), gain_ref[...])
        gains_ref[:, :width] += term
        rows_low[at, :] = (grad_ref[at, :] + change).astype(BF16)

    by_rows(rows_low.shape[0], rows)
    for i, ref in enumerate((gains_ref, two_ref)):
        for slot in range(4):
            to = (2 * (slot % 2) + jnp.bitwise_xor(net.core, slot // 2)) * block + i * width
            for j in range(2):
                sub = net.x if j == 0 else 1 - net.x
                at = slot * block + j * half
                vectors[0, :, pl.ds(pl.multiple_of(to + sub * half, half), half)] = ref[:, at : at + half]
    vectors[0, :, 2 * width : 2 * width + size] = query_ref[...]
    vectors[0, :, 2 * width + size :] = key_ref[...]

    def add_gains():
        for i, to in enumerate(SUMS):
            copy = net.send(vectors.at[i], vectors.at[len(SUMS) + 1 + i], to)
            yield
            net.arrived(copy)
            vectors[i + 1] = vectors[i] + vectors[len(SUMS) + 1 + i]
        gains_ref[...] = vectors[len(SUMS)]
        yield

    def own(flow, k, ref):
        flow.far_end(k)
        flow.to_owner(k, flow.acc.at[flow.slot(k, 2, 0, flow.across)], ref)

    def own_up(k):
        net.arrived(up.far[k])
        place = up.slot(k, 1, 0, up.across)
        add_rows((up_sums, place), [(up_sums, place), (up_far, place)])
        up.to_owner(k, up_sums.at[place], up_out)

    gains = add_gains()
    run(gains)
    out.x_end(0, buffers[6])
    out.x_end(1, buffers[6])
    run(gains)
    own(qkv, 0, qkv_out)
    own_up(0)
    run(gains)
    spread_flow(net, rows_low, tokens_ref)
    run(gains)
    own(qkv, 1, qkv_out)
    own_up(1)
    run(gains)
    own(out, 0, out_out)
    own(out, 1, out_out)
    up.after_y()
    qkv.after_y()
    out.after_y()
    run(gains)
    net.finish()


def end(partial, x, gain, grad, two, query, key, up, up_x, qkv_core, qkv, out, sizes):
    rows, width = x.shape
    size = width // sizes["narrow"]
    wide, deep = qkv.shape[1], out.shape[0]
    length = 2 * width + 2 * query.shape[1]
    return wire_call(
        end_kernel, "end", 6, [VMEM] * 10 + [ANY] * 2, [ANY, VMEM, ANY, ANY, ANY],
        [((sizes["narrow"] * rows, size), BF16), ((1, length), F32), ((size, wide), BF16), ((deep, size), BF16),
         (up.shape, BF16)],
        [
            *scatter_buffers(rows, width), pltpu.VMEM((rows, width), BF16), pltpu.VMEM((2 * len(SUMS) + 1, 1, length), F32),
            pltpu.VMEM(up.shape, BF16), pltpu.VMEM((size, up.shape[1] // 2), BF16),
            *(v for i, v in enumerate(gradient_buffers(size, wide // 2, 0)) if i != 1), *gradient_buffers(size, deep // 2, 1),
            *sems(40, 16),
        ],
        sizes, 90, partial, x, gain[None], grad, two, query, key, up, up_x, qkv_core, qkv, out,
    )


def layout(lengths, index):
    order = jnp.arange(lengths.shape[0])
    ends = jnp.sum(jnp.where(order[None, :] <= order[:, None], lengths[None, :], 0), axis=1)[None, :]
    begins = ends - lengths[None, :]
    offset = index - PROMPT
    shift = jnp.sum(jnp.where((offset >= begins) & (offset < ends), begins, 0), axis=1, keepdims=True)
    return jnp.where(offset >= 0, PROMPT + shift, 0), index - shift


def make(sizes):
    n_dp, n_wide, n_narrow = sizes["dp"], sizes["wide"], sizes["narrow"]

    def over_y(values):
        return exchange(values, "narrow", 2, n_narrow)

    def over_z(values):
        return exchange(values, "wide", 1, n_wide)

    def over_x(values):
        return exchange(values, "dp", 1, n_dp)

    def over_core(values):
        return exchange(values, "narrow", 1, n_narrow)

    def over_far(values):
        return exchange(values, "wide", 2, n_wide)

    def over_groups(values, kind):
        distance = 2
        while distance < n_dp:
            values = values.astype(F32) + exchange(values.astype(kind), "dp", distance, n_dp).astype(F32)
            distance *= 2
        return values.astype(F32)

    def on_device(
        tokens, continuation_lengths, attention_gain, query_weight, key_weight, value_weight, head_gate, query_gain, key_gain,
        output_weight, feedforward_gain, gate_weight, up_weight, down_weight, cotangent,
    ):
        rows_wide, width_local = tokens.shape
        width = attention_gain.shape[0]
        size = query_gain.shape[0]
        heads = head_gate.shape[1]
        pairs = key_weight.shape[1] // size
        group_rows = rows_wide * n_wide
        rows_local = rows_wide // n_narrow
        x = lax.axis_index("dp") % 2
        z = lax.axis_index("wide")
        narrow = lax.axis_index("narrow")
        y, core = narrow // 2, narrow % 2
        z_near, z_far = z % 2, z // 2
        quarter = width_local // 2
        scale = size ** (-0.5)
        factor = scale * math.log2(math.e)
        log_two = math.log(2.0)

        def relative_vector(vector):
            values = jnp.transpose(vector.reshape(2, 2, 2, quarter), (1, 0, 2, 3))
            values = jnp.where(core == 0, values, values[::-1])
            return jnp.where(x == 0, values, values[:, :, ::-1]).reshape(width)

        def piece_of(weight, i, axis):
            half = weight.shape[1 - axis] // 2
            return cut(cut(weight, x * quarter, quarter, axis), i * half, half, 1 - axis)

        gain_one, gain_two = relative_vector(attention_gain), relative_vector(feedforward_gain)
        lane_pad = ((0, 0), (0, LANES - heads // 2))
        halves = lambda w, i: w[:, i * (w.shape[1] // 2) : (i + 1) * (w.shape[1] // 2)]
        packed = join(
            [v for i in range(2) for v in (
                halves(query_weight, i), halves(key_weight, i), halves(value_weight, i), jnp.pad(halves(head_gate, i), lane_pad)
            )], 1
        )
        inputs, upstream, normed_all, joined_weight, out_weight = begin(tokens, cotangent, gain_one, packed, output_weight, sizes)

        def indices(row):
            part, at = row // rows_local, row % rows_local
            return ((z ^ (part // 2)) * n_narrow + (narrow ^ (2 * (part % 2)))) * rows_local + at

        my_index = indices(lax.broadcasted_iota(jnp.int32, (4 * rows_local, 1), 0))
        my_start, my_position = layout(continuation_lengths[0], my_index)
        frequency = THETA ** (-2.0 * jnp.arange(size // 2, dtype=F32) / size)
        angle = my_position.astype(F32) * frequency[None, :]
        cosine, sine = jnp.cos(angle), jnp.sin(angle)
        cosine = jnp.concatenate([cosine, cosine], axis=1)
        sine = jnp.concatenate([-sine, sine], axis=1)
        heads_index = indices(lax.broadcasted_iota(jnp.int32, (4, 1), 0) * rows_local)
        block = heads_index // rows_local
        first = layout(continuation_lengths[0], heads_index)[0] // rows_local
        prompt_blocks = PROMPT // rows_local
        in_prompt = block < prompt_blocks
        column = lax.broadcasted_iota(jnp.int32, (4, 5), 1)
        pick = lambda values: functools.reduce(lambda acc, item: jnp.where(column == item[0], item[1], acc), enumerate(values), 0)
        table = pick(
            [
                jnp.where(in_prompt, block // 2, prompt_blocks // 2),
                jnp.where(in_prompt, block // 2 * 2, first),
                block,
                2 * z_near + y,
                core,
            ]
        ).astype(jnp.int32)

        raw = dot_rows(normed_all, joined_weight)
        q, kv = post(raw, cosine, sine, query_gain, key_gain, heads, pairs, size, factor)
        send = after((gate_weight, up_weight, down_weight), normed_all)
        axes = (0, 0, 1)
        from_y = [over_y(piece_of(w, 1 - y, axis)) for w, axis in zip(send, axes)]
        from_far = [over_far(piece_of(w, y, axis)) for w, axis in zip(send, axes)]
        part = rows_local // 2
        kv_all = exchange_keys(after(kv, *from_y, *from_far), sizes)
        upstream_y, upstream_z = over_y(after(upstream[:part], kv_all)), over_z(after(upstream[part:], kv_all))
        from_both = [over_far(after(v, kv_all)) for v in from_y]

        gated, context, inverse_total = attend(
            table, q, kv_all, my_index, my_start, raw, pairs, size
        )
        partial = dot_rows(after(gated, upstream_y, upstream_z), out_weight).astype(BF16)
        middle, normed_two_all, gate_up, down = to_middle(
            partial, inputs, gain_two, gate_weight, up_weight, down_weight, from_y + from_far + from_both, sizes
        )
        come_z = over_z(join([upstream[:part], after(upstream_y, normed_two_all)]))
        come_y = over_y(join([upstream[part:], after(upstream_z, normed_two_all)]))
        upstream_all = join(
            [upstream, upstream_y, come_y[:part], come_z[:part], upstream_z, come_z[part:], come_y[part:]]
        )
        both = dot_rows(normed_two_all, gate_up)
        hidden_cols = gate_weight.shape[1]
        gate_pre, up_pre = both[:, :hidden_cols], both[:, hidden_cols:]
        gate_sigmoid = jax.nn.sigmoid(gate_pre)
        silu = gate_pre * gate_sigmoid
        hidden = (silu * up_pre).astype(BF16)
        hidden_grad = dot_trans(upstream_all, down)
        gate_grad = hidden_grad * up_pre * gate_sigmoid * (1.0 + gate_pre * (1.0 - gate_sigmoid))
        up_grad = hidden_grad * silu
        gate_up_low = join([gate_grad, up_grad], 1).astype(BF16)
        partial = dot_trans(gate_up_low, gate_up).astype(BF16)
        gate_low, up_low = gate_up_low[:, :hidden_cols], gate_up_low[:, hidden_cols:]
        down_sums = dot_inner(hidden, upstream_all).astype(BF16)
        gate_sums = dot_inner(normed_two_all, gate_low).astype(BF16)
        up_sums = dot_inner(normed_two_all, up_low).astype(BF16)
        mlp_partial = dot_rows(hidden, down).astype(BF16)
        partial = after(partial, mlp_partial)
        middle_grad, middle_all, two_term, down_part, gate_part, up_keep, up_send = turn(
            partial, middle, upstream, gain_two, down_sums, gate_sums, up_sums, sizes
        )
        down_far = over_far(down_part[hidden_cols // 2 :])
        gate_far = over_far(gate_part[:, hidden_cols // 2 :])
        up_come = over_x(up_send)
        gated_grad = dot_trans(middle_all, out_weight)
        dq, dkv, logit_grad = attend_back(
            table, q, kv_all, my_index, my_start, raw, context, inverse_total, gated_grad, pairs, size
        )
        out_sums = dot_inner(gated, middle_all).astype(BF16)
        dkv_mine, layer_output, down_gradient, gate_gradient = to_owner(
            after(dkv, up_come, out_sums), mlp_partial, middle, down_part, down_far, gate_part, gate_far, sizes
        )
        low, query_term, key_term = project_back(
            dq, dkv_mine, raw, cosine, sine, query_gain, key_gain, logit_grad, heads, pairs, size, scale, log_two
        )
        half = width // 2
        qkv_sums = dot_inner(normed_all, low).astype(BF16)
        qkv_core = over_core(qkv_sums[half:])
        partial = dot_trans(after(low, qkv_sums), joined_weight).astype(BF16)
        tokens_gradient, gains, qkv_gradient, output_gradient, up_gradient = end(
            partial, inputs, gain_one, middle_grad, two_term, query_term, key_term, up_keep, up_come,
            qkv_core, qkv_sums, out_sums, sizes
        )
        tokens_gradient = tokens_gradient.astype(F32)
        gains = over_groups(gains[0], F32)
        qkv_gradient = over_groups(qkv_gradient, BF16)
        down_gradient, gate_gradient, up_gradient, output_gradient = (
            over_groups(v, BF16) for v in (down_gradient, gate_gradient, up_gradient, output_gradient)
        )
        block = qkv_gradient.shape[1] // 2
        query_cols, key_cols = heads // 2 * size, pairs // 2 * size
        take = lambda at, count: join([qkv_gradient[:, at + i * block : at + i * block + count] for i in range(2)], 1)
        query_gradient = take(0, query_cols)
        key_gradient = take(query_cols, key_cols)
        value_gradient = take(query_cols + key_cols, key_cols)
        head_gate_gradient = take(query_cols + 2 * key_cols, heads // 2)
        return (
            layer_output,
            tokens_gradient,
            gains[:width],
            query_gradient,
            key_gradient,
            value_gradient,
            head_gate_gradient,
            gains[2 * width : 2 * width + size],
            gains[2 * width + size :],
            output_gradient,
            gains[width : 2 * width],
            gate_gradient,
            up_gradient,
            down_gradient,
        )

    return on_device


def solution(mesh):
    rows, up, down = P(("dp", "wide"), "narrow"), P("narrow", "wide"), P("wide", "narrow")
    return jax.shard_map(
        make(dict(mesh.shape)),
        mesh=mesh,
        in_specs=(rows, P("dp", None), P(), up, up, up, up, P(), P(), down, P(), up, up, down, rows),
        out_specs=(rows, rows, P(), up, up, up, up, P(), P(), down, P(), up, up, down),
        check_vma=False,
    )
```

```python
import functools
import math

import jax
import jax.numpy as jnp
from jax import lax
from jax.experimental import pallas as pl
from jax.experimental.pallas import tpu as pltpu
from jax.sharding import PartitionSpec as P

PROMPT = 2048
EPS = 1e-06
THETA = 1000000.0
RELATIVE = (0, 2, 1, 3)
BF16 = jnp.bfloat16
F32 = jnp.float32
VMEM_LIMIT = 56 * 1024 * 1024
LANES = 128


def dot_rows(left, right):
    return jnp.dot(left, right, preferred_element_type=F32)


def dot_trans(left, right):
    return lax.dot_general(left, right, (((1,), (1,)), ((), ())), preferred_element_type=F32)


def dot_inner(left, right):
    return lax.dot_general(left, right, (((0,), (0,)), ((), ())), preferred_element_type=F32)


def exchange(values, axis, distance, size):
    return lax.ppermute(values, axis, [(i, i ^ distance) for i in range(size)])


def join(parts, axis=0):
    return jnp.concatenate(parts, axis=axis)


def cut(values, at, length, axis):
    return lax.dynamic_slice_in_dim(values, at, length, axis=axis)


def turn_pairs(values):
    step = values.shape[1] // 4
    return join([values[:, i * step : (i + 1) * step] for i in (1, 0, 3, 2)], 1)


def after(values, *others):
    return lax.optimization_barrier((values,) + others)[0]


def columns(heads, pairs, size):
    query, pair = heads // 2, pairs // 2
    block = (query + 2 * pair) * size + LANES
    of = lambda i, count, before: (i // count) * block + (before + i % count) * size
    return (
        [of(h, query, 0) for h in range(heads)],
        [of(p, pair, query) for p in range(pairs)],
        [of(p, pair, query + pair) for p in range(pairs)],
        [block - LANES, 2 * block - LANES],
    )


def post_kernel(raw_ref, cos_ref, sin_ref, query_gain_ref, key_gain_ref, q_ref, kv_ref, *, heads, pairs, size, factor):
    cosine = cos_ref[...]
    sine = sin_ref[...]
    query_at, key_at, value_at, _ = columns(heads, pairs, size)

    def turned(value, gain):
        inverse = lax.rsqrt(jnp.mean(value * value, axis=-1, keepdims=True) + EPS)
        normal = value * inverse * gain
        return normal * cosine + pltpu.roll(normal, size // 2, 1) * sine

    for h, at in enumerate(query_at):
        value = raw_ref[:, at : at + size]
        q_ref[:, h * size : (h + 1) * size] = (turned(value, query_gain_ref[...]) * factor).astype(BF16)
    for p, at in enumerate(key_at):
        kv_ref[:, p * size : (p + 1) * size] = turned(raw_ref[:, at : at + size], key_gain_ref[...]).astype(BF16)
    for p, at in enumerate(value_at):
        to = (pairs + p) * size
        kv_ref[:, to : to + size] = raw_ref[:, at : at + size].astype(BF16)


def post(raw, cosine, sine, query_gain, key_gain, heads, pairs, size, factor):
    rows, width = raw.shape
    step = 256
    return pl.pallas_call(
        functools.partial(post_kernel, heads=heads, pairs=pairs, size=size, factor=factor),
        grid=(rows // step,),
        in_specs=[
            pl.BlockSpec((step, width), lambda i: (i, 0)),
            pl.BlockSpec((step, size), lambda i: (i, 0)),
            pl.BlockSpec((step, size), lambda i: (i, 0)),
            pl.BlockSpec((1, size), lambda i: (0, 0)),
            pl.BlockSpec((1, size), lambda i: (0, 0)),
        ],
        out_specs=[
            pl.BlockSpec((step, heads * size), lambda i: (i, 0)),
            pl.BlockSpec((step, 2 * pairs * size), lambda i: (i, 0)),
        ],
        out_shape=[
            jax.ShapeDtypeStruct((rows, heads * size), BF16),
            jax.ShapeDtypeStruct((rows, 2 * pairs * size), BF16),
        ],
        cost_estimate=pl.CostEstimate(flops=rows * width * 20, bytes_accessed=rows * width * 8, transcendentals=0),
        name="post",
    )(raw, cosine, sine, query_gain[None], key_gain[None])


def back_kernel(
    dq_ref, dkv_ref, raw_ref, cos_ref, sin_ref, query_gain_ref, key_gain_ref, logit_ref, out_ref, gq_ref, gk_ref, *, heads, pairs, size, factor_q, factor_k
):
    cosine = cos_ref[...]
    sine = sin_ref[...]
    query_at, key_at, value_at, logit_at = columns(heads, pairs, size)

    @pl.when(pl.program_id(0) == 0)
    def _():
        gq_ref[...] = jnp.zeros_like(gq_ref)
        gk_ref[...] = jnp.zeros_like(gk_ref)

    def back(up, value, gain, total_ref):
        up = up * cosine - pltpu.roll(up, size // 2, 1) * sine
        inverse = lax.rsqrt(jnp.mean(value * value, axis=-1, keepdims=True) + EPS)
        hat = value * inverse
        total_ref[...] += jnp.sum(up * hat, axis=0, keepdims=True)
        scaled = up * gain
        return inverse * (scaled - hat * jnp.mean(scaled * hat, axis=-1, keepdims=True))

    for h, at in enumerate(query_at):
        up = dq_ref[:, h * size : (h + 1) * size] * factor_q
        out_ref[:, at : at + size] = back(up, raw_ref[:, at : at + size], query_gain_ref[...], gq_ref).astype(BF16)
    for p, at in enumerate(key_at):
        up = dkv_ref[:, p * size : (p + 1) * size].astype(F32) * factor_k
        out_ref[:, at : at + size] = back(up, raw_ref[:, at : at + size], key_gain_ref[...], gk_ref).astype(BF16)
    for p, at in enumerate(value_at):
        to = (pairs + p) * size
        out_ref[:, at : at + size] = dkv_ref[:, to : to + size].astype(BF16)
    for i, at in enumerate(logit_at):
        out_ref[:, at : at + LANES] = logit_ref[:, i * LANES : (i + 1) * LANES].astype(BF16)


def project_back(dq, dkv, raw, cosine, sine, query_gain, key_gain, logit_grad, heads, pairs, size, factor_q, factor_k):
    rows, width = raw.shape
    step = 256
    row = lambda cols: pl.BlockSpec((step, cols), lambda i: (i, 0))
    one = pl.BlockSpec((1, size), lambda i: (0, 0))
    return pl.pallas_call(
        functools.partial(back_kernel, heads=heads, pairs=pairs, size=size, factor_q=factor_q, factor_k=factor_k),
        grid=(rows // step,),
        in_specs=[row(heads * size), row(2 * pairs * size), row(width), row(size), row(size), one, one, row(2 * LANES)],
        out_specs=[row(width), one, one],
        out_shape=[
            jax.ShapeDtypeStruct((rows, width), BF16),
            jax.ShapeDtypeStruct((1, size), F32),
            jax.ShapeDtypeStruct((1, size), F32),
        ],
        cost_estimate=pl.CostEstimate(flops=rows * width * 30, bytes_accessed=rows * width * 12, transcendentals=0),
        name="project_back",
    )(dq, dkv, raw, cosine, sine, query_gain[None], key_gain[None], logit_grad)


def places(table_ref, stripe, step, length):
    turn = table_ref[stripe, 3]
    core = table_ref[stripe, 4]
    half = length // 2
    blocks = half // step

    def pair(i):
        at = jnp.bitwise_xor(i, turn) * step
        return pl.ds(pl.multiple_of(at, step), step), pl.ds(pl.multiple_of(at + half // 2, step), step)

    def single(b):
        part = b // blocks
        inner = b - part * blocks
        at = part * half + jnp.bitwise_xor(inner % 2, core) * (half // 2) + jnp.bitwise_xor(inner // 2, turn) * step
        return (pl.ds(pl.multiple_of(at, step), step),)

    return pair, single


def logit_of(head, heads, own_ref, other_ref):
    half = heads // 2
    at = head % half
    return (own_ref if head < half else other_ref)[:, at : at + 1]


def logit_specs(raw, heads, pairs, size, step):
    spec = lambda i: pl.BlockSpec((step, LANES), lambda s, t: (s, i))
    return [spec(at // LANES) for at in columns(heads, pairs, size)[3]]


def forward_kernel(table_ref, q_ref, kv_ref, row_ref, start_ref, own_ref, other_ref, gated_ref, context_ref, inverse_ref, *, pairs, repeat, size, step):
    stripe = pl.program_id(0)
    wide_blocks = table_ref[stripe, 0]
    low = table_ref[stripe, 1]
    high = table_ref[stripe, 2]
    pair, single = places(table_ref, stripe, step, kv_ref.shape[0])
    rows = row_ref[...]
    starts = start_ref[...]
    rows = jnp.concatenate([rows] * repeat, axis=0)
    starts = jnp.concatenate([starts] * repeat, axis=0)
    queries = [
        jnp.concatenate([q_ref[:, h * size : (h + 1) * size] for h in range(k * repeat, (k + 1) * repeat)], axis=0)
        for k in range(pairs)
    ]

    def seen(totals, where, first):
        outs = []
        for k in range(pairs):
            keys = join([kv_ref[at, k * size : (k + 1) * size] for at in where])
            weights = jnp.exp2(dot_trans(queries[k], keys))
            if first is not None:
                index = first + lax.broadcasted_iota(jnp.int32, weights.shape, 1)
                weights = jnp.where((index <= rows) & (index >= starts), weights, 0.0)
            values = join([kv_ref[at, (pairs + k) * size : (pairs + k + 1) * size] for at in where])
            values = jnp.concatenate([values, jnp.ones_like(values)], axis=1)
            outs.append(totals[k] + dot_rows(weights.astype(BF16), values))
        return tuple(outs)

    totals = tuple(jnp.zeros((query.shape[0], 2 * size), F32) for query in queries)
    totals = lax.fori_loop(0, wide_blocks, lambda i, t: seen(t, pair(i), None), totals)
    totals = lax.fori_loop(low, high + 1, lambda i, t: seen(t, single(i), i * step), totals)
    for k, total in enumerate(totals):
        inverse = 1.0 / total[:, size:]
        context = total[:, :size] * inverse
        for r in range(repeat):
            h = k * repeat + r
            part = context[r * step : (r + 1) * step]
            cols = slice(h * size, (h + 1) * size)
            gate = jax.nn.sigmoid(logit_of(h, pairs * repeat, own_ref, other_ref))
            gated_ref[:, cols] = (part * gate).astype(BF16)
            context_ref[:, cols] = part
            inverse_ref[:, cols] = inverse[r * step : (r + 1) * step]


def attend(table, q, kv, rows, starts, raw, pairs, size):
    length, cols = q.shape
    heads = cols // size
    step = length // table.shape[0]
    block = lambda width: pl.BlockSpec((step, width), lambda i, t: (i, 0))
    return pl.pallas_call(
        functools.partial(forward_kernel, pairs=pairs, repeat=heads // pairs, size=size, step=step),
        grid_spec=pltpu.PrefetchScalarGridSpec(
            num_scalar_prefetch=1,
            grid=(length // step,),
            in_specs=[
                block(cols),
                pl.BlockSpec(kv.shape, lambda i, t: (0, 0), pipeline_mode=pl.Buffered(1)),
                block(1),
                block(1),
                *logit_specs(raw, heads, pairs, size, step),
            ],
            out_specs=[block(cols), block(cols), block(cols)],
        ),
        out_shape=[
            jax.ShapeDtypeStruct((length, cols), BF16),
            jax.ShapeDtypeStruct((length, cols), F32),
            jax.ShapeDtypeStruct((length, cols), F32),
        ],
        compiler_params=pltpu.CompilerParams(vmem_limit_bytes=VMEM_LIMIT),
        cost_estimate=pl.CostEstimate(flops=20 * 10**9, bytes_accessed=12 * 10**6, transcendentals=7 * 10**6),
        name="attend",
    )(table, q, kv, rows, starts, raw, raw)


def backward_kernel(
    table_ref, q_ref, kv_ref, row_ref, start_ref, own_ref, other_ref, context_ref, inverse_ref, grad_ref,
    dq_ref, dkv_ref, dlogit_ref, sums_ref, *, pairs, repeat, size, step,
):
    stripe = pl.program_id(0)
    wide_blocks = table_ref[stripe, 0]
    low = table_ref[stripe, 1]
    high = table_ref[stripe, 2]
    pair, single = places(table_ref, stripe, step, kv_ref.shape[0])

    @pl.when(stripe == 0)
    def _():
        sums_ref[...] = jnp.zeros_like(sums_ref)

    dlogit_ref[...] = jnp.zeros_like(dlogit_ref)
    rows = jnp.concatenate([row_ref[0]] * repeat, axis=1)
    starts = jnp.concatenate([start_ref[0]] * repeat, axis=1)
    queries, all_grads, all_inners = [], [], []
    for k in range(pairs):
        heads = [k * repeat + r for r in range(repeat)]
        queries.append(jnp.concatenate([q_ref[:, h * size : (h + 1) * size] for h in heads], axis=0))
        grads, inners = [], []
        for h in heads:
            cols = slice(h * size, (h + 1) * size)
            up = grad_ref[:, cols]
            gate = jax.nn.sigmoid(logit_of(h, pairs * repeat, own_ref, other_ref))
            product = jnp.sum(up * context_ref[:, cols], axis=1, keepdims=True)
            half = pairs * repeat // 2
            at = h // half * LANES + h % half
            dlogit_ref[:, at : at + 1] = product * gate * (1.0 - gate)
            inverse = inverse_ref[:, cols]
            grads.append((up * gate * inverse).astype(BF16))
            inners.append(product * gate * inverse)
        all_grads.append(jnp.concatenate(grads, axis=0))
        all_inners.append(jnp.transpose(jnp.concatenate(inners, axis=0))[0:1])

    def seen(totals, where, first):
        outs = []
        for k in range(pairs):
            key_cols = slice(k * size, (k + 1) * size)
            value_cols = slice((pairs + k) * size, (pairs + k + 1) * size)
            keys = join([kv_ref[at, key_cols] for at in where])
            weights = jnp.exp2(dot_trans(keys, queries[k]))
            if first is not None:
                index = first + lax.broadcasted_iota(jnp.int32, weights.shape, 0)
                weights = jnp.where((index <= rows) & (index >= starts), weights, 0.0)
            changes = dot_trans(join([kv_ref[at, value_cols] for at in where]), all_grads[k])
            changes = (weights * (changes - all_inners[k])).astype(BF16)
            value_sums = dot_rows(weights.astype(BF16), all_grads[k])
            key_sums = dot_rows(changes, queries[k])
            for i, at in enumerate(where):
                sums_ref[at, value_cols] += value_sums[i * step : (i + 1) * step]
                sums_ref[at, key_cols] += key_sums[i * step : (i + 1) * step]
            outs.append(totals[k] + dot_inner(changes, keys))
        return tuple(outs)

    totals = tuple(jnp.zeros((query.shape[0], size), F32) for query in queries)
    totals = lax.fori_loop(0, wide_blocks, lambda i, t: seen(t, pair(i), None), totals)
    totals = lax.fori_loop(low, high + 1, lambda i, t: seen(t, single(i), i * step), totals)
    for k, total in enumerate(totals):
        for r in range(repeat):
            h = k * repeat + r
            dq_ref[:, h * size : (h + 1) * size] = total[r * step : (r + 1) * step]

    @pl.when(stripe == pl.num_programs(0) - 1)
    def _():
        dkv_ref[...] = sums_ref[...].astype(BF16)


def attend_back(table, q, kv, rows, starts, raw, context, inverse, grad, pairs, size):
    length, cols = q.shape
    heads = cols // size
    step = length // table.shape[0]
    block = lambda width: pl.BlockSpec((step, width), lambda i, t: (i, 0))
    whole = pl.BlockSpec(kv.shape, lambda i, t: (0, 0), pipeline_mode=pl.Buffered(1))
    lane = pl.BlockSpec((1, 1, step), lambda i, t: (i, 0, 0))
    logits = logit_specs(raw, heads, pairs, size, step)
    return pl.pallas_call(
        functools.partial(backward_kernel, pairs=pairs, repeat=heads // pairs, size=size, step=step),
        grid_spec=pltpu.PrefetchScalarGridSpec(
            num_scalar_prefetch=1,
            grid=(length // step,),
            in_specs=[block(cols), whole, lane, lane, *logits, block(cols), block(cols), block(cols)],
            out_specs=[block(cols), whole, block(2 * LANES)],
            scratch_shapes=[pltpu.VMEM(kv.shape, F32)],
        ),
        out_shape=[
            jax.ShapeDtypeStruct((length, cols), F32),
            jax.ShapeDtypeStruct(kv.shape, BF16),
            jax.ShapeDtypeStruct((length, 2 * LANES), F32),
        ],
        compiler_params=pltpu.CompilerParams(vmem_limit_bytes=VMEM_LIMIT),
        cost_estimate=pl.CostEstimate(flops=50 * 10**9, bytes_accessed=20 * 10**6, transcendentals=7 * 10**6),
        name="attend_back",
    )(table, q, kv, rows.reshape(-1, 1, step), starts.reshape(-1, 1, step), raw, raw, context, inverse, grad)


class Wires:
    def __init__(self, send_sems, recv_sems, local_sems, sizes):
        self.send_sems, self.recv_sems, self.local_sems = send_sems, recv_sems, local_sems
        self.sizes = sizes
        self.sent, self.local, self.open = [], [], []
        self.locals_used, self.sends_used = 0, 0
        self.dp, self.wide, self.narrow = (lax.axis_index(a) for a in ("dp", "wide", "narrow"))
        self.y, self.core = self.narrow // 2, self.narrow % 2
        self.x, self.far = self.dp % 2, self.wide // 2

    def peer(self, *to):
        if isinstance(to[0], tuple):
            return {axis: at for part in to for axis, at in self.peer(*part).items()}
        axis, distance = to
        at = {"dp": self.dp, "wide": self.wide, "narrow": self.narrow}[axis]
        bit = at // distance % 2
        return {axis: at + distance * (1 - 2 * bit) if distance < 3 else 3 - at}

    def greet(self, peers):
        barrier = pltpu.get_barrier_semaphore()
        for to in peers:
            pl.semaphore_signal(barrier, inc=1, device_id=self.peer(*to), device_id_type=pl.DeviceIdType.MESH)
        pl.semaphore_wait(barrier, len(peers))

    def make(self, source, target, to):
        i = self.sends_used
        self.sends_used += 1
        copy = pltpu.make_async_remote_copy(
            src_ref=source, dst_ref=target, send_sem=self.send_sems.at[i], recv_sem=self.recv_sems.at[i],
            device_id=self.peer(*to), device_id_type=pl.DeviceIdType.MESH,
        )
        self.sent.append(copy)
        return copy

    def send(self, source, target, to):
        copy = self.make(source, target, to)
        copy.start()
        self.open.append(copy)
        return copy

    def arrived(self, copy):
        copy.wait_recv()
        self.open = [other for other in self.open if other is not copy]

    def copy(self, source, target):
        copy = pltpu.make_async_copy(source, target, self.local_sems.at[self.locals_used])
        self.locals_used += 1
        copy.start()
        self.local.append(copy)
        return copy

    def finish(self):
        for copy in list(self.open):
            self.arrived(copy)
        for copy in self.sent:
            copy.wait_send()
        for copy in self.local:
            copy.wait()


Y, CORE, CORNER, NEAR, FAR, X = ("narrow", 2), ("narrow", 1), ("narrow", 3), ("wide", 1), ("wide", 2), ("dp", 1)


def local_flow(net, values_ref, rows_ref):
    rows, width = rows_ref.shape[0], values_ref.shape[1]
    half = width // 2
    out = []
    for distance, to in ((0, None), (1, CORE), (2, Y), (3, CORNER)):
        target = net.narrow if to is None else net.peer(*to)["narrow"]
        at = (2 * (distance % 2) + net.y) * width
        for j in range(2):
            sub = net.x if j == 0 else 1 - net.x
            source = values_ref.at[pl.ds(pl.multiple_of(target * rows, rows), rows), pl.ds(pl.multiple_of(sub * half, half), half)]
            goal = rows_ref.at[:, pl.ds(pl.multiple_of(at + j * half, half), half)]
            out.append(net.copy(source, goal) if to is None else net.send(source, goal, to))
    return out


def gather_flow(net, values_ref, all_ref):
    rows = values_ref.shape[0]
    half = rows // 2
    part = lambda i: all_ref.at[pl.ds(i * half, half), :]
    first, second = values_ref.at[pl.ds(0, half), :], values_ref.at[pl.ds(half, half), :]
    first_y = net.send(first, part(2), Y)
    second_z = net.send(second, part(5), NEAR)
    net.send(first, part(4), NEAR)
    net.send(second, part(3), Y)
    net.copy(values_ref, all_ref.at[pl.ds(0, rows), :])
    yield
    net.arrived(first_y)
    net.send(part(2), part(6), NEAR)
    yield
    net.arrived(second_z)
    net.send(part(5), part(7), Y)
    yield


def weight_flow(net, source_ref, out_ref, axis, own, other, across, from_y=None, from_far=None, from_both=None, their_y=None, their_far=None):
    step = source_ref.shape[axis] // 2
    count = source_ref.shape[axis]

    def window(ref, at, start):
        long, wide = pl.ds(pl.multiple_of(at, step), step), pl.ds(start, across)
        return ref.at[long, wide] if axis == 0 else ref.at[wide, long]

    y, x = net.y, net.x
    piece = lambda sub, half: window(source_ref, sub * step, pl.multiple_of(half * across, across))
    place = lambda slot, j, start: window(out_ref, slot * count + j * step, start)
    mine, rest = piece(x, y), piece(1 - x, y)
    net.copy(mine, place(y, 0, own))
    net.copy(rest, place(y, 1, own))
    if from_y is None:
        come_y = net.send(piece(x, 1 - y), place(y, 0, own), Y)
    else:
        net.copy(from_y, place(1 - y, 0, own))
    if from_far is None:
        come_far = net.send(mine, place(y, 0, other), FAR)
    else:
        net.copy(from_far, place(y, 0, other))
    net.send(mine, place(2 + y, 0, own), CORE)
    net.send(rest, place(2 + y, 1, own), CORE)
    if from_y is None:
        yield
        net.arrived(come_y)
        from_y = place(1 - y, 0, own)
    if from_both is None:
        come_both = net.send(from_y, place(1 - y, 0, other), FAR)
    else:
        net.copy(from_both, place(1 - y, 0, other))
    given = their_y is not None
    if given:
        for ref, slot, start in ((their_y, 1 - y, own), (their_far, y, other)):
            net.copy(ref, place(slot, 1, start))
            net.send(ref, place(slot + 2, 1, start), CORE)
    else:
        their_y = net.send(from_y, place(1 - y, 1, own), X)
    net.send(from_y, place(3 - y, 0, own), CORE)
    if from_far is None:
        yield
        net.arrived(come_far)
        from_far = place(y, 0, other)
    if not given:
        their_far = net.send(from_far, place(y, 1, other), X)
    net.send(from_far, place(2 + y, 0, other), CORE)
    if from_both is None:
        yield
        net.arrived(come_both)
        from_both = place(1 - y, 0, other)
    their_both = net.send(from_both, place(1 - y, 1, other), X)
    net.send(from_both, place(3 - y, 0, other), CORE)
    yield
    waiting = ((their_y, 1 - y, own), (their_far, y, other), (their_both, 1 - y, other))
    for copy, slot, start in waiting[2 * given :]:
        net.arrived(copy)
        net.send(place(slot, 1, start), place(slot + 2, 1, start), CORE)
    yield


def run(flow):
    return next(flow, None)


def by_rows(count, body):
    step = 16
    lax.fori_loop(0, count // step, lambda i, _: (body(pl.ds(pl.multiple_of(i * step, step), step)), 0)[1], 0)


def begin_kernel(
    tokens_ref, cotangent_ref, gain_ref, query_ref, key_ref, value_ref, gates_ref, out_ref,
    x_ref, rows_ref, all_ref, joined_ref, output_ref, here, normed, there, qkv_ref, send, recv, local, *, sizes,
):
    net = Wires(send, recv, local, sizes)
    net.greet([Y, CORE, CORNER, NEAR, FAR, X])
    rows = local_flow(net, tokens_ref, here)
    across = qkv_ref.shape[1] // 2
    packed, at = [], 0
    for ref in (query_ref, key_ref, value_ref, gates_ref):
        wide = ref.shape[1] // 2
        for i in range(2):
            packed.append(net.copy(ref.at[:, pl.ds(i * wide, wide)], qkv_ref.at[:, pl.ds(i * across + at, wide)]))
        at += wide
    for copy in packed:
        copy.wait()
    net.local = [copy for copy in net.local if all(copy is not other for other in packed)]
    joined = weight_flow(net, qkv_ref, joined_ref, 0, 0, across, across)
    run(joined)
    rows[0].wait()
    rows[1].wait()
    net.local = net.local[2:]
    for copy in rows[2:]:
        net.arrived(copy)

    def norm(at):
        values = here[at, :].astype(F32)
        inverse = lax.rsqrt(jnp.mean(values * values, axis=1, keepdims=True) + EPS)
        normed[at, :] = (values * inverse * gain_ref[...]).astype(BF16)
        x_ref[at, :] = here[at, :]

    by_rows(here.shape[0], norm)
    gather = gather_flow(net, normed, all_ref)
    run(gather)
    across = out_ref.shape[0] // 2
    output = weight_flow(net, out_ref, output_ref, 1, 0, across, across)
    for flow in (joined, gather, output, joined, gather):
        run(flow)
    rows = local_flow(net, cotangent_ref, there)
    for flow in (joined, output, joined, output, output, output):
        run(flow)
    for copy in rows[:2]:
        copy.wait()
    net.local = [copy for copy in net.local if all(copy is not other for other in rows[:2])]
    for copy in rows[2:]:
        net.arrived(copy)
    net.copy(there, rows_ref)
    net.finish()


ANY = pl.BlockSpec(memory_space=pl.ANY)
VMEM = pl.BlockSpec(memory_space=pltpu.VMEM)


def sems(sends, locals_):
    return [pltpu.SemaphoreType.DMA((sends,)), pltpu.SemaphoreType.DMA((sends,)), pltpu.SemaphoreType.DMA((locals_,))]


def wire_call(kernel, name, number, specs, out_specs, shapes, scratch, sizes, cost, *args):
    return pl.pallas_call(
        functools.partial(kernel, sizes=sizes),
        in_specs=specs,
        out_specs=out_specs,
        out_shape=[jax.ShapeDtypeStruct(*shape) for shape in shapes],
        scratch_shapes=scratch,
        compiler_params=pltpu.CompilerParams(collective_id=number, has_side_effects=True, vmem_limit_bytes=VMEM_LIMIT),
        cost_estimate=pl.CostEstimate(flops=0, bytes_accessed=cost * 3 * 10**6, transcendentals=0),
        name=name,
    )(*args)


def begin(tokens, cotangent, gain, weights, out, sizes):
    rows, width = tokens.shape[0] // sizes["narrow"], gain.shape[0]
    wide = sum(w.shape[1] for w in weights)
    row = pltpu.VMEM((rows, width), BF16)
    return wire_call(
        begin_kernel, "begin", 1, [ANY, ANY, VMEM] + [ANY] * 4 + [VMEM], [VMEM, ANY, ANY, ANY, ANY],
        [
            ((rows, width), BF16), ((rows, width), BF16), ((4 * rows, width), BF16), ((width, wide), BF16),
            ((out.shape[0], width), BF16),
        ],
        [row, row, row, pltpu.VMEM((weights[0].shape[0], wide), BF16), *sems(48, 24)],
        sizes, 55, tokens, cotangent, gain[None], *weights, out,
    )


def keys_kernel(kv_ref, keys_ref, done, send, recv, local, *, sizes):
    net = Wires(send, recv, local, sizes)
    across = [FAR, ("wide", 3), (FAR, CORE), (("wide", 3), CORE)]
    net.greet([CORE] + across)
    count, width = kv_ref.shape
    size = width // 4
    part = lambda i, j: keys_ref.at[pl.ds(i, count), pl.ds(j * size, size)]
    base = pl.multiple_of(net.far * 2 * count, count)
    far = [net.make(kv_ref.at[:, pl.ds(j * size, size)], part(0, j ^ 1), FAR) for j in range(4)]
    on = [net.make(part(0, j ^ 1), part(count, j ^ 1), CORE) for j in range(4)]

    @pl.when(net.far == 0)
    def _():
        for copy in far:
            copy.start()

    net.copy(kv_ref, keys_ref.at[pl.ds(base, count), :])
    net.send(kv_ref, keys_ref.at[pl.ds(base + count, count), :], CORE)

    @pl.when(net.far == 1)
    def _():
        for copy, forward in zip(far, on):
            copy.wait_recv()
            forward.start()
        for to in across:
            pl.semaphore_signal(done, inc=1, device_id=net.peer(*to), device_id_type=pl.DeviceIdType.MESH)
        for forward in on:
            forward.wait()

    @pl.when(net.far == 0)
    def _():
        for copy in far:
            copy.wait_send()
        pl.semaphore_wait(done, len(across))

    net.sent = [copy for copy in net.sent if all(copy is not other for other in far + on)]
    net.finish()


def exchange_keys(kv, sizes):
    return wire_call(
        keys_kernel, "keys", 2, [VMEM], [ANY], [((4 * kv.shape[0], kv.shape[1]), BF16)],
        [pltpu.SemaphoreType.REGULAR, *sems(16, 4)], sizes, 45, kv,
    )[0]


def scatter_flow(net, partial_ref, first_ref, second_ref, send_ref, last_ref, total_ref):
    half = partial_ref.shape[0] // 8
    part = lambda i: partial_ref.at[pl.ds(i * half, half), :]
    slot = lambda ref, i: ref.at[pl.ds(i * half, half), :]
    to_z = [net.send(part(6), slot(first_ref, 1), NEAR), net.send(part(4), slot(first_ref, 0), NEAR)]
    to_y = [net.send(part(7), slot(second_ref, 1), Y), net.send(part(3), slot(second_ref, 0), Y)]
    yield

    def add(out_ref, to, i, ref, j):
        def body(at):
            move = lambda start: pl.ds(pl.multiple_of(at.start + start, 16), at.size)
            value = partial_ref[move(i * half), :].astype(F32) + ref[move(j * half), :].astype(F32)
            out_ref[move(to), :] = value.astype(out_ref.dtype)

        by_rows(half, body)

    net.arrived(to_z[0])
    add(send_ref, 0, 2, first_ref, 1)
    last_y = net.send(slot(send_ref, 0), slot(last_ref, 0), Y)
    net.arrived(to_y[0])
    add(send_ref, half, 5, second_ref, 1)
    last_z = net.send(slot(send_ref, 1), slot(last_ref, 1), NEAR)
    yield
    net.arrived(to_z[1])
    add(total_ref, 0, 0, first_ref, 0)
    net.arrived(to_y[1])
    add(total_ref, half, 1, second_ref, 0)
    yield
    net.arrived(last_y)
    net.arrived(last_z)
    yield


def middle_kernel(
    partial_ref, x_ref, gain_ref, gate_ref, up_ref, down_ref, gate_y_ref, up_y_ref, down_y_ref, gate_far_ref, up_far_ref, down_far_ref,
    gate_both_ref, up_both_ref, down_both_ref, middle_ref, all_ref, both_ref, last_ref,
    first, second, sums, last, total, normed, send, recv, local, *, sizes,
):
    net = Wires(send, recv, local, sizes)
    net.greet([Y, CORE, NEAR, FAR, X])
    scatter = scatter_flow(net, partial_ref, first, second, sums, last, total)
    run(scatter)
    across = gate_ref.shape[1] // 2
    flows = [
        weight_flow(net, gate_ref, both_ref, 0, 0, across, across, gate_y_ref, gate_far_ref, gate_both_ref),
        weight_flow(net, up_ref, both_ref, 0, 2 * across, 3 * across, across, up_y_ref, up_far_ref, up_both_ref),
        weight_flow(net, down_ref, last_ref, 1, 0, across, across, down_y_ref, down_far_ref, down_both_ref),
    ]
    for flow in flows:
        run(flow)
    run(scatter)
    run(scatter)
    run(scatter)

    def norm(at):
        values = x_ref[at, :].astype(F32) + total[at, :] + last[at, :].astype(F32)
        middle_ref[at, :] = values
        inverse = lax.rsqrt(jnp.mean(values * values, axis=1, keepdims=True) + EPS)
        normed[at, :] = (values * inverse * gain_ref[...]).astype(BF16)

    by_rows(normed.shape[0], norm)
    gather = gather_flow(net, normed, all_ref)
    run(gather)
    run(flows[0])
    run(gather)
    run(gather)
    run(flows[1])
    run(flows[2])
    net.finish()


def to_middle(partial, x, gain, gate, up, down, pieces, sizes):
    rows, width = x.shape
    buffer = lambda n, kind: pltpu.VMEM((n, width), kind)
    return wire_call(
        middle_kernel, "middle", 3, [VMEM] * 15, [VMEM, ANY, ANY, ANY],
        [((rows, width), F32), ((4 * rows, width), BF16), ((width, 2 * gate.shape[1]), BF16), ((down.shape[0], width), BF16)],
        [
            buffer(rows, BF16), buffer(rows, BF16), buffer(rows, BF16), buffer(rows, BF16), buffer(rows, F32), buffer(rows, BF16),
            *sems(64, 32),
        ],
        sizes, 80, partial, x, gain[None], gate, up, down, *pieces,
    )


def spread_flow(net, rows_ref, out_ref):
    rows, width = rows_ref.shape[0], out_ref.shape[1]
    half = width // 2
    base = pl.multiple_of(net.narrow * rows, rows)
    for distance, to in ((3, CORNER), (2, Y), (1, CORE), (0, None)):
        target = net.narrow if to is None else net.peer(*to)["narrow"]
        at = (2 * (distance % 2) + target // 2) * width
        for j in range(2):
            sub = net.x if j == 0 else 1 - net.x
            source = rows_ref.at[:, pl.ds(pl.multiple_of(at + j * half, half), half)]
            goal = out_ref.at[pl.ds(base, rows), pl.ds(pl.multiple_of(sub * half, half), half)]
            if to is None:
                net.copy(source, goal)
            else:
                net.send(source, goal, to)


def add_rows(target, terms):
    ref, (rows, cols) = target

    def body(at):
        move = lambda r: pl.ds(pl.multiple_of(at.start + r.start, 16), at.size)
        value = sum(term[move(r), c].astype(F32) for term, (r, c) in terms)
        ref[move(rows), cols] = value.astype(BF16)

    by_rows(rows.size, body)


class Gradient:
    def __init__(self, net, axis, step, across):
        self.net, self.axis, self.step, self.across = net, axis, step, across
        self.order = (1 - net.y, net.y)
        self.x, self.far = [], []

    def window(self, at, start, count, length=None):
        step = self.step if length is None else length
        hint = lambda v, unit: v if isinstance(v, int) else pl.multiple_of(v, unit)
        along, wide = pl.ds(hint(at, self.step), step), pl.ds(hint(start, self.across), count)
        return (along, wide) if self.axis == 0 else (wide, along)

    def start(self, g_ref, acc, from_core, given=False):
        self.acc, self.from_core = acc, from_core
        count = 4 * self.step
        own, other = (self.window(i * count, 0, 2 * self.across, count) for i in range(2))
        self.loaded = self.net.copy(g_ref.at[own], acc)
        self.core = None if given else self.net.send(g_ref.at[other], from_core, CORE)

    def wait_core(self):
        if self.loaded is not None:
            self.loaded.wait()
            self.net.local = [copy for copy in self.net.local if copy is not self.loaded]
        if self.core is not None:
            self.net.arrived(self.core)

    def core_to_x(self, from_x):
        self.wait_core()
        self.from_x = from_x
        for slot in self.order:
            place = self.window((2 * slot + 1) * self.step, 0, 2 * self.across)
            add_rows((self.acc, place), [(self.acc, place), (self.from_core, place)])
            goal = from_x.at[self.window(slot * self.step, 0, 2 * self.across)]
            self.x.append(self.net.send(self.acc.at[place], goal, X))

    def x_end(self, k, from_far=None):
        slot = self.order[k]
        self.net.arrived(self.x[k])
        for start in (self.across, 0):
            place = self.window(2 * slot * self.step, start, self.across)
            come = self.window(slot * self.step, start, self.across)
            add_rows((self.acc, place), [(self.acc, place), (self.from_core, place), (self.from_x, come)])
            if start and from_far is not None:
                self.from_far = from_far
                goal = from_far.at[self.window(slot * self.step, 0, self.across)]
                self.far.append(self.net.send(self.acc.at[place], goal, FAR))

    def far_end(self, k, result=None):
        slot = self.order[k]
        self.net.arrived(self.far[k])
        place = self.window(2 * slot * self.step, 0, self.across)
        come = self.window(slot * self.step, 0, self.across)
        add_rows((self.acc, place), [(self.acc, place), (self.from_far, come)])

    def to_owner(self, k, source, out):
        net, across = self.net, self.across
        goal = out.at[self.window(net.x * self.step, net.y * across, across)]
        if k == 0:
            self.out = out
            self.y = net.send(source, goal, Y)
        else:
            net.copy(source, goal)
            net.send(source, goal, X)

    def after_y(self):
        net, across = self.net, self.across
        net.arrived(self.y)
        place = self.out.at[self.window(net.x * self.step, (1 - net.y) * across, across)]
        net.send(place, place, X)

    def slot(self, k, stride, start, count):
        return self.window(stride * self.order[k] * self.step, start, count)


def row_back(grad, values, gain):
    inverse = lax.rsqrt(jnp.mean(values * values, axis=1, keepdims=True) + EPS)
    hat = values * inverse
    scaled = grad * gain
    inner = jnp.mean(scaled * hat, axis=1, keepdims=True)
    return jnp.sum(grad * hat, axis=0, keepdims=True), inverse * (scaled - hat * inner)


def turn_kernel(
    partial_ref, middle_ref, upstream_ref, gain_ref, down_ref, gate_ref, inputs_ref, grads_ref,
    grad_ref, all_ref, term_ref, down_out, gate_out, up_keep, up_send,
    first, second, sums, last, total, low, *rest, sizes,
):
    buffers, (rows_two, up_grads, up_other), (send, recv, local) = rest[:-6], rest[-6:-3], rest[-3:]
    net = Wires(send, recv, local, sizes)
    net.greet([Y, CORE, NEAR, FAR, X])
    scatter = scatter_flow(net, partial_ref, first, second, sums, last, total)
    run(scatter)
    step, across = low.shape[1] // sizes["narrow"] // 2, gate_ref.shape[1] // 2
    down, gate, up = (Gradient(net, axis, step, across) for axis in (1, 0, 0))
    down.start(down_ref, *buffers[0:2])
    gate.start(gate_ref, *buffers[3:5])
    up.acc, up.from_core = buffers[6:8]
    loads = [net.copy(inputs_ref, rows_two), net.copy(grads_ref.at[:, pl.ds(2 * across, 2 * across)], up_grads)]
    down.core_to_x(buffers[2])
    gate.core_to_x(buffers[5])
    run(scatter)
    run(scatter)
    run(scatter)
    term_ref[...] = jnp.zeros_like(term_ref)

    def rows(at):
        grad = total[at, :] + last[at, :].astype(F32)
        term, change = row_back(grad, middle_ref[at, :], gain_ref[...])
        term_ref[...] += term
        value = upstream_ref[at, :].astype(F32) + change
        grad_ref[at, :] = value
        low[at, :] = value.astype(BF16)

    by_rows(low.shape[0], rows)
    gather = gather_flow(net, low, all_ref)
    run(gather)
    for copy in loads:
        copy.wait()
    net.local = [copy for copy in net.local if all(copy is not other for other in loads)]
    half = rows_two.shape[1] // 2

    def up_dots(base, target):
        def body(i, _):
            at = pl.multiple_of(i * step, step)
            part = dot_inner(rows_two[:, pl.ds(pl.multiple_of(base + at, step), step)], up_grads[...])
            target[pl.ds(at, step), :] = part.astype(BF16)
            return 0

        lax.fori_loop(0, half // step, body, 0)

    up_dots(half, up_other)
    up.loaded, up.core = None, net.send(up_other, up.from_core, CORE)
    for k in range(2):
        down.x_end(k)
        net.copy(down.acc.at[down.slot(k, 2, 0, 2 * across)], down_out.at[down.slot(k, 1, 0, 2 * across)])
    run(gather)
    run(gather)
    up_dots(0, up.acc)
    up.wait_core()
    for slot in range(2):
        for j, ref in ((1, up_send), (0, up_keep)):
            place = up.window((2 * slot + j) * step, 0, 2 * across)
            add_rows((up.acc, place), [(up.acc, place), (up.from_core, place)])
            net.copy(up.acc.at[place], ref.at[up.window(slot * step, 0, 2 * across)])
    for k in range(2):
        gate.x_end(k)
        net.copy(gate.acc.at[gate.slot(k, 2, 0, 2 * across)], gate_out.at[gate.slot(k, 1, 0, 2 * across)])
    net.finish()


def gradient_buffers(size, across, axis, count=4):
    shape = lambda a, b: pltpu.VMEM((a, b) if axis == 0 else (b, a), BF16)
    every = [shape(2 * size, 2 * across), shape(2 * size, 2 * across), shape(size, 2 * across), shape(size, across)]
    return every[:count]


def scatter_buffers(rows, width):
    buffer = lambda kind: pltpu.VMEM((rows, width), kind)
    return [buffer(BF16), buffer(BF16), buffer(BF16), buffer(BF16), buffer(F32)]


def turn(partial, middle, upstream, gain, down, gate, inputs, grads, sizes):
    rows, width = middle.shape
    size, across = width // sizes["narrow"], down.shape[0] // 2
    return wire_call(
        turn_kernel, "turn", 4, [VMEM] * 4 + [ANY] * 4, [VMEM, ANY, VMEM, ANY, ANY, ANY, ANY],
        [
            ((rows, width), F32), ((4 * rows, width), BF16), ((1, width), F32),
            ((2 * across, size), BF16), ((size, 2 * across), BF16), ((size, 2 * across), BF16), ((size, 2 * across), BF16),
        ],
        [
            *scatter_buffers(rows, width), pltpu.VMEM((rows, width), BF16),
            *gradient_buffers(size, across, 1, 3), *gradient_buffers(size, across, 0, 3), *gradient_buffers(size, across, 0, 2),
            pltpu.VMEM(inputs.shape, BF16), pltpu.VMEM((inputs.shape[0], 2 * across), BF16), pltpu.VMEM((2 * size, 2 * across), BF16),
            *sems(40, 24),
        ],
        sizes, 80, partial, middle, upstream, gain[None], down, gate, inputs, grads,
    )


def owner_kernel(
    dkv_ref, partial_ref, middle_ref, down_ref, down_far_ref, gate_ref, gate_far_ref,
    mine_ref, layer_ref, down_out, gate_out,
    prompt_core, rest_core, prompt, prompt_far, first, second, sums, last, total, rows_low, down_sums, gate_sums,
    send, recv, local, *, sizes,
):
    net = Wires(send, recv, local, sizes)
    net.greet([Y, CORE, CORNER, NEAR, FAR, X])
    count, width = prompt.shape
    size = width // 4
    region = lambda i: dkv_ref.at[pl.ds(i * count, count), :]
    come = net.send(region(1), prompt_core, CORE)
    rest = net.send(region(3), rest_core, CORE)
    scatter = scatter_flow(net, partial_ref, first, second, sums, last, total)
    run(scatter)
    step, across = down_far_ref.shape[1] // 2, down_far_ref.shape[0]
    down, gate = (Gradient(net, axis, step, across) for axis in (1, 0))
    net.arrived(come)

    def add(at):
        prompt[at, :] = (dkv_ref[at, :].astype(F32) + prompt_core[at, :].astype(F32)).astype(BF16)

    by_rows(count, add)
    cols = lambda ref, j: ref.at[:, pl.ds(j * size, size)]
    far = [net.make(cols(prompt, j), cols(prompt_far, j ^ 1), FAR) for j in range(4)]

    @pl.when(net.far == 1)
    def _():
        for copy in far:
            copy.start()

    parts = ((down, down_sums, down_ref, down_far_ref, down_out), (gate, gate_sums, gate_ref, gate_far_ref, gate_out))
    for flow, total_ref, ref, far_ref, goal in parts:
        for k in range(2):
            place = flow.slot(k, 1, 0, across)
            add_rows((total_ref, place), [(ref, place), (far_ref, place)])
            flow.to_owner(k, total_ref.at[place], goal)
    run(scatter)
    run(scatter)
    run(scatter)

    def rows(at):
        rows_low[at, :] = (middle_ref[at, :] + total[at, :] + last[at, :].astype(F32)).astype(BF16)

    by_rows(rows_low.shape[0], rows)
    spread_flow(net, rows_low, layer_ref)
    down.after_y()
    gate.after_y()
    net.arrived(rest)

    @pl.when(net.far == 1)
    def _():
        def add(at):
            move = pl.ds(pl.multiple_of(at.start + 2 * count, 16), at.size)
            mine_ref[at, :] = dkv_ref[move, :].astype(F32) + rest_core[at, :].astype(F32)

        by_rows(count, add)
        for copy in far:
            copy.wait_send()

    @pl.when(net.far == 0)
    def _():
        for copy in far:
            copy.wait_recv()

        def add(at):
            mine_ref[at, :] = dkv_ref[at, :].astype(F32) + prompt_core[at, :].astype(F32) + prompt_far[at, :].astype(F32)

        by_rows(count, add)

    net.sent = [copy for copy in net.sent if all(copy is not other for other in far)]
    net.finish()


def to_owner(dkv, partial, middle, down, down_far, gate, gate_far, sizes):
    rows, width = middle.shape
    size, across = width // sizes["narrow"], gate_far.shape[1]
    count = dkv.shape[0] // 4
    block = lambda: pltpu.VMEM((count, dkv.shape[1]), BF16)
    return wire_call(
        owner_kernel, "owner", 5, [VMEM] * 7, [VMEM, ANY, ANY, ANY],
        [
            ((count, dkv.shape[1]), F32), ((sizes["narrow"] * rows, size), BF16), ((2 * across, size), BF16),
            ((size, 2 * across), BF16),
        ],
        [
            block(), block(), block(), block(), *scatter_buffers(rows, width), pltpu.VMEM((rows, width), BF16),
            pltpu.VMEM((across, size), BF16), pltpu.VMEM((size, across), BF16), *sems(40, 16),
        ],
        sizes, 80, dkv, partial, middle, down, down_far, gate, gate_far,
    )


SUMS = [CORE, Y, NEAR, X, FAR]


def end_kernel(
    partial_ref, x_ref, gain_ref, grad_ref, two_ref, query_ref, key_ref, up_ref, up_x_ref, qkv_core_ref, qkv_ref, out_ref,
    tokens_ref, gains_ref, qkv_out, out_out, up_out,
    first, second, sums, last, total, rows_low, vectors, up_sums, up_far, *rest, sizes,
):
    buffers, (send, recv, local) = rest[:-3], rest[-3:]
    net = Wires(send, recv, local, sizes)
    net.greet([Y, CORE, CORNER, NEAR, FAR, X])
    step = x_ref.shape[1] // sizes["narrow"] // 2
    qkv = Gradient(net, 0, step, qkv_ref.shape[1] // 2)
    out = Gradient(net, 1, step, out_ref.shape[0] // 2)
    qkv.start(qkv_ref, buffers[0], qkv_core_ref, True)
    out.start(out_ref, *buffers[3:5])
    scatter = scatter_flow(net, partial_ref, first, second, sums, last, total)
    run(scatter)
    up = Gradient(net, 0, step, up_ref.shape[1] // 2)
    qkv.core_to_x(buffers[1])
    out.core_to_x(buffers[5])

    def up_to_far(k):
        for start in (up.across, 0):
            place = up.slot(k, 1, start, up.across)
            add_rows((up_sums, place), [(up_ref, place), (up_x_ref, place)])
            if start:
                up.far.append(net.send(up_sums.at[place], up_far.at[up.slot(k, 1, 0, up.across)], FAR))

    run(scatter)
    qkv.x_end(0, buffers[2])
    up_to_far(0)
    run(scatter)
    qkv.x_end(1, buffers[2])
    up_to_far(1)
    run(scatter)
    width = x_ref.shape[1]
    size = query_ref.shape[1]
    block = width // sizes["narrow"]
    half = block // 2
    gains_ref[...] = jnp.zeros_like(gains_ref)

    def rows(at):
        grad = total[at, :] + last[at, :].astype(F32)
        term, change = row_back(grad, x_ref[at, :].astype(F32), gain_ref[...])
        gains_ref[:, :width] += term
        rows_low[at, :] = (grad_ref[at, :] + change).astype(BF16)

    by_rows(rows_low.shape[0], rows)
    for i, ref in enumerate((gains_ref, two_ref)):
        for slot in range(4):
            to = (2 * (slot % 2) + jnp.bitwise_xor(net.core, slot // 2)) * block + i * width
            for j in range(2):
                sub = net.x if j == 0 else 1 - net.x
                at = slot * block + j * half
                vectors[0, :, pl.ds(pl.multiple_of(to + sub * half, half), half)] = ref[:, at : at + half]
    vectors[0, :, 2 * width : 2 * width + size] = query_ref[...]
    vectors[0, :, 2 * width + size :] = key_ref[...]

    def add_gains():
        for i, to in enumerate(SUMS):
            copy = net.send(vectors.at[i], vectors.at[len(SUMS) + 1 + i], to)
            yield
            net.arrived(copy)
            vectors[i + 1] = vectors[i] + vectors[len(SUMS) + 1 + i]
        gains_ref[...] = vectors[len(SUMS)]
        yield

    def own(flow, k, ref):
        flow.far_end(k)
        flow.to_owner(k, flow.acc.at[flow.slot(k, 2, 0, flow.across)], ref)

    def own_up(k):
        net.arrived(up.far[k])
        place = up.slot(k, 1, 0, up.across)
        add_rows((up_sums, place), [(up_sums, place), (up_far, place)])
        up.to_owner(k, up_sums.at[place], up_out)

    gains = add_gains()
    run(gains)
    out.x_end(0, buffers[6])
    out.x_end(1, buffers[6])
    run(gains)
    own(qkv, 0, qkv_out)
    own_up(0)
    run(gains)
    spread_flow(net, rows_low, tokens_ref)
    run(gains)
    own(qkv, 1, qkv_out)
    own_up(1)
    run(gains)
    own(out, 0, out_out)
    own(out, 1, out_out)
    up.after_y()
    qkv.after_y()
    out.after_y()
    run(gains)
    net.finish()


def end(partial, x, gain, grad, two, query, key, up, up_x, qkv_core, qkv, out, sizes):
    rows, width = x.shape
    size = width // sizes["narrow"]
    wide, deep = qkv.shape[1], out.shape[0]
    length = 2 * width + 2 * query.shape[1]
    return wire_call(
        end_kernel, "end", 6, [VMEM] * 10 + [ANY] * 2, [ANY, VMEM, ANY, ANY, ANY],
        [((sizes["narrow"] * rows, size), BF16), ((1, length), F32), ((size, wide), BF16), ((deep, size), BF16),
         (up.shape, BF16)],
        [
            *scatter_buffers(rows, width), pltpu.VMEM((rows, width), BF16), pltpu.VMEM((2 * len(SUMS) + 1, 1, length), F32),
            pltpu.VMEM(up.shape, BF16), pltpu.VMEM((size, up.shape[1] // 2), BF16),
            *(v for i, v in enumerate(gradient_buffers(size, wide // 2, 0)) if i != 1), *gradient_buffers(size, deep // 2, 1),
            *sems(40, 16),
        ],
        sizes, 90, partial, x, gain[None], grad, two, query, key, up, up_x, qkv_core, qkv, out,
    )


def layout(lengths, index):
    order = jnp.arange(lengths.shape[0])
    ends = jnp.sum(jnp.where(order[None, :] <= order[:, None], lengths[None, :], 0), axis=1)[None, :]
    begins = ends - lengths[None, :]
    offset = index - PROMPT
    shift = jnp.sum(jnp.where((offset >= begins) & (offset < ends), begins, 0), axis=1, keepdims=True)
    return jnp.where(offset >= 0, PROMPT + shift, 0), index - shift


def make(sizes):
    n_dp, n_wide, n_narrow = sizes["dp"], sizes["wide"], sizes["narrow"]

    def over_y(values):
        return exchange(values, "narrow", 2, n_narrow)

    def over_z(values):
        return exchange(values, "wide", 1, n_wide)

    def over_x(values):
        return exchange(values, "dp", 1, n_dp)

    def over_core(values):
        return exchange(values, "narrow", 1, n_narrow)

    def over_far(values):
        return exchange(values, "wide", 2, n_wide)

    def over_groups(values, kind):
        distance = 2
        while distance < n_dp:
            values = values.astype(F32) + exchange(values.astype(kind), "dp", distance, n_dp).astype(F32)
            distance *= 2
        return values.astype(F32)

    def on_device(
        tokens, continuation_lengths, attention_gain, query_weight, key_weight, value_weight, head_gate, query_gain, key_gain,
        output_weight, feedforward_gain, gate_weight, up_weight, down_weight, cotangent,
    ):
        rows_wide, width_local = tokens.shape
        width = attention_gain.shape[0]
        size = query_gain.shape[0]
        heads = head_gate.shape[1]
        pairs = key_weight.shape[1] // size
        group_rows = rows_wide * n_wide
        rows_local = rows_wide // n_narrow
        x = lax.axis_index("dp") % 2
        z = lax.axis_index("wide")
        narrow = lax.axis_index("narrow")
        y, core = narrow // 2, narrow % 2
        z_near, z_far = z % 2, z // 2
        quarter = width_local // 2
        scale = size ** (-0.5)
        factor = scale * math.log2(math.e)
        log_two = math.log(2.0)

        def relative_vector(vector):
            values = jnp.transpose(vector.reshape(2, 2, 2, quarter), (1, 0, 2, 3))
            values = jnp.where(core == 0, values, values[::-1])
            return jnp.where(x == 0, values, values[:, :, ::-1]).reshape(width)

        def piece_of(weight, i, axis):
            half = weight.shape[1 - axis] // 2
            return cut(cut(weight, x * quarter, quarter, axis), i * half, half, 1 - axis)

        gain_one, gain_two = relative_vector(attention_gain), relative_vector(feedforward_gain)
        lane_pad = ((0, 0), (0, LANES - heads // 2))
        halves = lambda w, i: w[:, i * (w.shape[1] // 2) : (i + 1) * (w.shape[1] // 2)]
        gates = join([jnp.pad(halves(head_gate, i), lane_pad) for i in range(2)], 1)
        packed = (query_weight, key_weight, value_weight, gates)
        inputs, upstream, normed_all, joined_weight, out_weight = begin(tokens, cotangent, gain_one, packed, output_weight, sizes)

        def indices(row):
            part, at = row // rows_local, row % rows_local
            return ((z ^ (part // 2)) * n_narrow + (narrow ^ (2 * (part % 2)))) * rows_local + at

        my_index = indices(lax.broadcasted_iota(jnp.int32, (4 * rows_local, 1), 0))
        my_start, my_position = layout(continuation_lengths[0], my_index)
        frequency = THETA ** (-2.0 * jnp.arange(size // 2, dtype=F32) / size)
        angle = my_position.astype(F32) * frequency[None, :]
        cosine, sine = jnp.cos(angle), jnp.sin(angle)
        cosine = jnp.concatenate([cosine, cosine], axis=1)
        sine = jnp.concatenate([-sine, sine], axis=1)
        heads_index = indices(lax.broadcasted_iota(jnp.int32, (4, 1), 0) * rows_local)
        block = heads_index // rows_local
        first = layout(continuation_lengths[0], heads_index)[0] // rows_local
        prompt_blocks = PROMPT // rows_local
        in_prompt = block < prompt_blocks
        column = lax.broadcasted_iota(jnp.int32, (4, 5), 1)
        pick = lambda values: functools.reduce(lambda acc, item: jnp.where(column == item[0], item[1], acc), enumerate(values), 0)
        table = pick(
            [
                jnp.where(in_prompt, block // 2, prompt_blocks // 2),
                jnp.where(in_prompt, block // 2 * 2, first),
                block,
                2 * z_near + y,
                core,
            ]
        ).astype(jnp.int32)

        raw = dot_rows(normed_all, joined_weight)
        q, kv = post(raw, cosine, sine, query_gain, key_gain, heads, pairs, size, factor)
        send = after((gate_weight, up_weight, down_weight), normed_all)
        axes = (0, 0, 1)
        from_y = [over_y(piece_of(w, 1 - y, axis)) for w, axis in zip(send, axes)]
        from_far = [over_far(piece_of(w, y, axis)) for w, axis in zip(send, axes)]
        part = rows_local // 2
        upstream_y, upstream_z = over_y(upstream[:part]), over_z(upstream[part:])
        kv_all = exchange_keys(after(kv, *from_y, *from_far, upstream_y, upstream_z), sizes)
        from_both = [over_far(after(v, kv_all)) for v in from_y]

        come_z = over_z(join([upstream[:part], after(upstream_y, kv_all)]))
        come_y = over_y(join([upstream[part:], after(upstream_z, kv_all)]))
        upstream_all = join(
            [upstream, upstream_y, come_y[:part], come_z[:part], upstream_z, come_z[part:], come_y[part:]]
        )

        gated, context, inverse_total = attend(
            table, q, kv_all, my_index, my_start, raw, pairs, size
        )
        partial = dot_rows(gated, out_weight).astype(BF16)
        middle, normed_two_all, gate_up, down = to_middle(
            partial, inputs, gain_two, gate_weight, up_weight, down_weight, from_y + from_far + from_both, sizes
        )
        both = dot_rows(normed_two_all, gate_up)
        hidden_cols = gate_weight.shape[1]
        gate_pre, up_pre = both[:, :hidden_cols], both[:, hidden_cols:]
        gate_sigmoid = jax.nn.sigmoid(gate_pre)
        silu = gate_pre * gate_sigmoid
        hidden = (silu * up_pre).astype(BF16)
        hidden_grad = dot_trans(upstream_all, down)
        gate_grad = hidden_grad * up_pre * gate_sigmoid * (1.0 + gate_pre * (1.0 - gate_sigmoid))
        up_grad = hidden_grad * silu
        gate_up_low = join([gate_grad, up_grad], 1).astype(BF16)
        partial = dot_trans(gate_up_low, gate_up).astype(BF16)
        down_sums = dot_inner(hidden, upstream_all).astype(BF16)
        gate_sums = dot_inner(normed_two_all, gate_up_low[:, :hidden_cols]).astype(BF16)
        mlp_partial = dot_rows(hidden, down).astype(BF16)
        partial = after(partial, mlp_partial)
        middle_grad, middle_all, two_term, down_part, gate_part, up_keep, up_send = turn(
            partial, middle, upstream, gain_two, down_sums, gate_sums, normed_two_all, gate_up_low, sizes
        )
        down_far = over_far(down_part[hidden_cols // 2 :])
        gate_far = over_far(gate_part[:, hidden_cols // 2 :])
        up_come = over_x(up_send)
        gated_grad = dot_trans(middle_all, out_weight)
        dq, dkv, logit_grad = attend_back(
            table, q, kv_all, my_index, my_start, raw, context, inverse_total, gated_grad, pairs, size
        )
        out_sums = dot_inner(gated, middle_all).astype(BF16)
        dkv_mine, layer_output, down_gradient, gate_gradient = to_owner(
            after(dkv, up_come, out_sums), mlp_partial, middle, down_part, down_far, gate_part, gate_far, sizes
        )
        low, query_term, key_term = project_back(
            dq, dkv_mine, raw, cosine, sine, query_gain, key_gain, logit_grad, heads, pairs, size, scale, log_two
        )
        half = width // 2
        qkv_sums = dot_inner(normed_all, low).astype(BF16)
        qkv_core = over_core(qkv_sums[half:])
        partial = dot_trans(after(low, qkv_sums), joined_weight).astype(BF16)
        tokens_gradient, gains, qkv_gradient, output_gradient, up_gradient = end(
            partial, inputs, gain_one, middle_grad, two_term, query_term, key_term, up_keep, up_come,
            qkv_core, qkv_sums, out_sums, sizes
        )
        tokens_gradient = tokens_gradient.astype(F32)
        gains = over_groups(gains[0], F32)
        qkv_gradient = over_groups(qkv_gradient, BF16)
        down_gradient, gate_gradient, up_gradient, output_gradient = (
            over_groups(v, BF16) for v in (down_gradient, gate_gradient, up_gradient, output_gradient)
        )
        block = qkv_gradient.shape[1] // 2
        query_cols, key_cols = heads // 2 * size, pairs // 2 * size
        take = lambda at, count: join([qkv_gradient[:, at + i * block : at + i * block + count] for i in range(2)], 1)
        query_gradient = take(0, query_cols)
        key_gradient = take(query_cols, key_cols)
        value_gradient = take(query_cols + key_cols, key_cols)
        head_gate_gradient = take(query_cols + 2 * key_cols, heads // 2)
        return (
            layer_output,
            tokens_gradient,
            gains[:width],
            query_gradient,
            key_gradient,
            value_gradient,
            head_gate_gradient,
            gains[2 * width : 2 * width + size],
            gains[2 * width + size :],
            output_gradient,
            gains[width : 2 * width],
            gate_gradient,
            up_gradient,
            down_gradient,
        )

    return on_device


def solution(mesh):
    rows, up, down = P(("dp", "wide"), "narrow"), P("narrow", "wide"), P("wide", "narrow")
    return jax.shard_map(
        make(dict(mesh.shape)),
        mesh=mesh,
        in_specs=(rows, P("dp", None), P(), up, up, up, up, P(), P(), down, P(), up, up, down, rows),
        out_specs=(rows, rows, P(), up, up, up, up, P(), P(), down, P(), up, up, down),
        check_vma=False,
    )
```

```python
import functools
import math

import jax
import jax.numpy as jnp
from jax import lax
from jax.experimental import pallas as pl
from jax.experimental.pallas import tpu as pltpu
from jax.sharding import PartitionSpec as P

PROMPT = 2048
EPS = 1e-06
THETA = 1000000.0
RELATIVE = (0, 2, 1, 3)
BF16 = jnp.bfloat16
F32 = jnp.float32
VMEM_LIMIT = 56 * 1024 * 1024
LANES = 128


def dot_rows(left, right):
    return jnp.dot(left, right, preferred_element_type=F32)


def dot_trans(left, right):
    return lax.dot_general(left, right, (((1,), (1,)), ((), ())), preferred_element_type=F32)


def dot_inner(left, right):
    return lax.dot_general(left, right, (((0,), (0,)), ((), ())), preferred_element_type=F32)


def exchange(values, axis, distance, size):
    return lax.ppermute(values, axis, [(i, i ^ distance) for i in range(size)])


def join(parts, axis=0):
    return jnp.concatenate(parts, axis=axis)


def cut(values, at, length, axis):
    return lax.dynamic_slice_in_dim(values, at, length, axis=axis)


def turn_pairs(values):
    step = values.shape[1] // 4
    return join([values[:, i * step : (i + 1) * step] for i in (1, 0, 3, 2)], 1)


def after(values, *others):
    return lax.optimization_barrier((values,) + others)[0]


def columns(heads, pairs, size):
    query, pair = heads // 2, pairs // 2
    block = (query + 2 * pair) * size + LANES
    of = lambda i, count, before: (i // count) * block + (before + i % count) * size
    return (
        [of(h, query, 0) for h in range(heads)],
        [of(p, pair, query) for p in range(pairs)],
        [of(p, pair, query + pair) for p in range(pairs)],
        [block - LANES, 2 * block - LANES],
    )


def post_kernel(raw_ref, cos_ref, sin_ref, query_gain_ref, key_gain_ref, q_ref, kv_ref, *, heads, pairs, size, factor):
    cosine = cos_ref[...]
    sine = sin_ref[...]
    query_at, key_at, value_at, _ = columns(heads, pairs, size)

    def turned(value, gain):
        inverse = lax.rsqrt(jnp.mean(value * value, axis=-1, keepdims=True) + EPS)
        normal = value * inverse * gain
        return normal * cosine + pltpu.roll(normal, size // 2, 1) * sine

    for h, at in enumerate(query_at):
        value = raw_ref[:, at : at + size]
        q_ref[:, h * size : (h + 1) * size] = (turned(value, query_gain_ref[...]) * factor).astype(BF16)
    for p, at in enumerate(key_at):
        kv_ref[:, p * size : (p + 1) * size] = turned(raw_ref[:, at : at + size], key_gain_ref[...]).astype(BF16)
    for p, at in enumerate(value_at):
        to = (pairs + p) * size
        kv_ref[:, to : to + size] = raw_ref[:, at : at + size].astype(BF16)


def post(raw, cosine, sine, query_gain, key_gain, heads, pairs, size, factor):
    rows, width = raw.shape
    step = 256
    return pl.pallas_call(
        functools.partial(post_kernel, heads=heads, pairs=pairs, size=size, factor=factor),
        grid=(rows // step,),
        in_specs=[
            pl.BlockSpec((step, width), lambda i: (i, 0)),
            pl.BlockSpec((step, size), lambda i: (i, 0)),
            pl.BlockSpec((step, size), lambda i: (i, 0)),
            pl.BlockSpec((1, size), lambda i: (0, 0)),
            pl.BlockSpec((1, size), lambda i: (0, 0)),
        ],
        out_specs=[
            pl.BlockSpec((step, heads * size), lambda i: (i, 0)),
            pl.BlockSpec((step, 2 * pairs * size), lambda i: (i, 0)),
        ],
        out_shape=[
            jax.ShapeDtypeStruct((rows, heads * size), BF16),
            jax.ShapeDtypeStruct((rows, 2 * pairs * size), BF16),
        ],
        cost_estimate=pl.CostEstimate(flops=rows * width * 20, bytes_accessed=rows * width * 8, transcendentals=0),
        name="post",
    )(raw, cosine, sine, query_gain[None], key_gain[None])


def back_kernel(
    dq_ref, dkv_ref, raw_ref, cos_ref, sin_ref, query_gain_ref, key_gain_ref, logit_ref, out_ref, gq_ref, gk_ref, *, heads, pairs, size, factor_q, factor_k
):
    cosine = cos_ref[...]
    sine = sin_ref[...]
    query_at, key_at, value_at, logit_at = columns(heads, pairs, size)

    @pl.when(pl.program_id(0) == 0)
    def _():
        gq_ref[...] = jnp.zeros_like(gq_ref)
        gk_ref[...] = jnp.zeros_like(gk_ref)

    def back(up, value, gain, total_ref):
        up = up * cosine - pltpu.roll(up, size // 2, 1) * sine
        inverse = lax.rsqrt(jnp.mean(value * value, axis=-1, keepdims=True) + EPS)
        hat = value * inverse
        total_ref[...] += jnp.sum(up * hat, axis=0, keepdims=True)
        scaled = up * gain
        return inverse * (scaled - hat * jnp.mean(scaled * hat, axis=-1, keepdims=True))

    for h, at in enumerate(query_at):
        up = dq_ref[:, h * size : (h + 1) * size] * factor_q
        out_ref[:, at : at + size] = back(up, raw_ref[:, at : at + size], query_gain_ref[...], gq_ref).astype(BF16)
    for p, at in enumerate(key_at):
        up = dkv_ref[:, p * size : (p + 1) * size].astype(F32) * factor_k
        out_ref[:, at : at + size] = back(up, raw_ref[:, at : at + size], key_gain_ref[...], gk_ref).astype(BF16)
    for p, at in enumerate(value_at):
        to = (pairs + p) * size
        out_ref[:, at : at + size] = dkv_ref[:, to : to + size].astype(BF16)
    for i, at in enumerate(logit_at):
        out_ref[:, at : at + LANES] = logit_ref[:, i * LANES : (i + 1) * LANES].astype(BF16)


def project_back(dq, dkv, raw, cosine, sine, query_gain, key_gain, logit_grad, heads, pairs, size, factor_q, factor_k):
    rows, width = raw.shape
    step = 256
    row = lambda cols: pl.BlockSpec((step, cols), lambda i: (i, 0))
    one = pl.BlockSpec((1, size), lambda i: (0, 0))
    return pl.pallas_call(
        functools.partial(back_kernel, heads=heads, pairs=pairs, size=size, factor_q=factor_q, factor_k=factor_k),
        grid=(rows // step,),
        in_specs=[row(heads * size), row(2 * pairs * size), row(width), row(size), row(size), one, one, row(2 * LANES)],
        out_specs=[row(width), one, one],
        out_shape=[
            jax.ShapeDtypeStruct((rows, width), BF16),
            jax.ShapeDtypeStruct((1, size), F32),
            jax.ShapeDtypeStruct((1, size), F32),
        ],
        cost_estimate=pl.CostEstimate(flops=rows * width * 30, bytes_accessed=rows * width * 12, transcendentals=0),
        name="project_back",
    )(dq, dkv, raw, cosine, sine, query_gain[None], key_gain[None], logit_grad)


def places(table_ref, stripe, step, length):
    turn = table_ref[stripe, 3]
    core = table_ref[stripe, 4]
    half = length // 2
    blocks = half // step

    def pair(i):
        at = jnp.bitwise_xor(i, turn) * step
        return pl.ds(pl.multiple_of(at, step), step), pl.ds(pl.multiple_of(at + half // 2, step), step)

    def single(b):
        part = b // blocks
        inner = b - part * blocks
        at = part * half + jnp.bitwise_xor(inner % 2, core) * (half // 2) + jnp.bitwise_xor(inner // 2, turn) * step
        return (pl.ds(pl.multiple_of(at, step), step),)

    return pair, single


def logit_of(head, heads, own_ref, other_ref):
    half = heads // 2
    at = head % half
    return (own_ref if head < half else other_ref)[:, at : at + 1]


def logit_specs(raw, heads, pairs, size, step):
    spec = lambda i: pl.BlockSpec((step, LANES), lambda s, t: (s, i))
    return [spec(at // LANES) for at in columns(heads, pairs, size)[3]]


def forward_kernel(table_ref, q_ref, kv_ref, row_ref, start_ref, own_ref, other_ref, gated_ref, context_ref, inverse_ref, *, pairs, repeat, size, step):
    stripe = pl.program_id(0)
    wide_blocks = table_ref[stripe, 0]
    low = table_ref[stripe, 1]
    high = table_ref[stripe, 2]
    pair, single = places(table_ref, stripe, step, kv_ref.shape[0])
    rows = row_ref[...]
    starts = start_ref[...]
    rows = jnp.concatenate([rows] * repeat, axis=0)
    starts = jnp.concatenate([starts] * repeat, axis=0)
    queries = [
        jnp.concatenate([q_ref[:, h * size : (h + 1) * size] for h in range(k * repeat, (k + 1) * repeat)], axis=0)
        for k in range(pairs)
    ]

    def seen(totals, where, first):
        outs = []
        for k in range(pairs):
            keys = join([kv_ref[at, k * size : (k + 1) * size] for at in where])
            weights = jnp.exp2(dot_trans(queries[k], keys))
            if first is not None:
                index = first + lax.broadcasted_iota(jnp.int32, weights.shape, 1)
                weights = jnp.where((index <= rows) & (index >= starts), weights, 0.0)
            values = join([kv_ref[at, (pairs + k) * size : (pairs + k + 1) * size] for at in where])
            values = jnp.concatenate([values, jnp.ones_like(values)], axis=1)
            outs.append(totals[k] + dot_rows(weights.astype(BF16), values))
        return tuple(outs)

    totals = tuple(jnp.zeros((query.shape[0], 2 * size), F32) for query in queries)
    totals = lax.fori_loop(0, wide_blocks, lambda i, t: seen(t, pair(i), None), totals)
    totals = lax.fori_loop(low, high + 1, lambda i, t: seen(t, single(i), i * step), totals)
    for k, total in enumerate(totals):
        inverse = 1.0 / total[:, size:]
        context = total[:, :size] * inverse
        for r in range(repeat):
            h = k * repeat + r
            part = context[r * step : (r + 1) * step]
            cols = slice(h * size, (h + 1) * size)
            gate = jax.nn.sigmoid(logit_of(h, pairs * repeat, own_ref, other_ref))
            gated_ref[:, cols] = (part * gate).astype(BF16)
            context_ref[:, cols] = part
            inverse_ref[:, cols] = inverse[r * step : (r + 1) * step]


def attend(table, q, kv, rows, starts, raw, pairs, size):
    length, cols = q.shape
    heads = cols // size
    step = length // table.shape[0]
    block = lambda width: pl.BlockSpec((step, width), lambda i, t: (i, 0))
    return pl.pallas_call(
        functools.partial(forward_kernel, pairs=pairs, repeat=heads // pairs, size=size, step=step),
        grid_spec=pltpu.PrefetchScalarGridSpec(
            num_scalar_prefetch=1,
            grid=(length // step,),
            in_specs=[
                block(cols),
                pl.BlockSpec(kv.shape, lambda i, t: (0, 0), pipeline_mode=pl.Buffered(1)),
                block(1),
                block(1),
                *logit_specs(raw, heads, pairs, size, step),
            ],
            out_specs=[block(cols), block(cols), block(cols)],
        ),
        out_shape=[
            jax.ShapeDtypeStruct((length, cols), BF16),
            jax.ShapeDtypeStruct((length, cols), F32),
            jax.ShapeDtypeStruct((length, cols), F32),
        ],
        compiler_params=pltpu.CompilerParams(vmem_limit_bytes=VMEM_LIMIT),
        cost_estimate=pl.CostEstimate(flops=20 * 10**9, bytes_accessed=12 * 10**6, transcendentals=7 * 10**6),
        name="attend",
    )(table, q, kv, rows, starts, raw, raw)


def backward_kernel(
    table_ref, q_ref, kv_ref, row_ref, start_ref, own_ref, other_ref, context_ref, inverse_ref, grad_ref,
    dq_ref, dkv_ref, dlogit_ref, sums_ref, *, pairs, repeat, size, step,
):
    stripe = pl.program_id(0)
    wide_blocks = table_ref[stripe, 0]
    low = table_ref[stripe, 1]
    high = table_ref[stripe, 2]
    pair, single = places(table_ref, stripe, step, kv_ref.shape[0])

    @pl.when(stripe == 0)
    def _():
        sums_ref[...] = jnp.zeros_like(sums_ref)

    dlogit_ref[...] = jnp.zeros_like(dlogit_ref)
    rows = jnp.concatenate([row_ref[0]] * repeat, axis=1)
    starts = jnp.concatenate([start_ref[0]] * repeat, axis=1)
    queries, all_grads, all_inners = [], [], []
    for k in range(pairs):
        heads = [k * repeat + r for r in range(repeat)]
        queries.append(jnp.concatenate([q_ref[:, h * size : (h + 1) * size] for h in heads], axis=0))
        grads, inners = [], []
        for h in heads:
            cols = slice(h * size, (h + 1) * size)
            up = grad_ref[:, cols]
            gate = jax.nn.sigmoid(logit_of(h, pairs * repeat, own_ref, other_ref))
            product = jnp.sum(up * context_ref[:, cols], axis=1, keepdims=True)
            half = pairs * repeat // 2
            at = h // half * LANES + h % half
            dlogit_ref[:, at : at + 1] = product * gate * (1.0 - gate)
            inverse = inverse_ref[:, cols]
            grads.append((up * gate * inverse).astype(BF16))
            inners.append(product * gate * inverse)
        all_grads.append(jnp.concatenate(grads, axis=0))
        all_inners.append(jnp.transpose(jnp.concatenate(inners, axis=0))[0:1])

    def seen(totals, where, first):
        outs = []
        for k in range(pairs):
            key_cols = slice(k * size, (k + 1) * size)
            value_cols = slice((pairs + k) * size, (pairs + k + 1) * size)
            keys = join([kv_ref[at, key_cols] for at in where])
            weights = jnp.exp2(dot_trans(keys, queries[k]))
            if first is not None:
                index = first + lax.broadcasted_iota(jnp.int32, weights.shape, 0)
                weights = jnp.where((index <= rows) & (index >= starts), weights, 0.0)
            changes = dot_trans(join([kv_ref[at, value_cols] for at in where]), all_grads[k])
            changes = (weights * (changes - all_inners[k])).astype(BF16)
            value_sums = dot_rows(weights.astype(BF16), all_grads[k])
            key_sums = dot_rows(changes, queries[k])
            for i, at in enumerate(where):
                sums_ref[at, value_cols] += value_sums[i * step : (i + 1) * step]
                sums_ref[at, key_cols] += key_sums[i * step : (i + 1) * step]
            outs.append(totals[k] + dot_inner(changes, keys))
        return tuple(outs)

    totals = tuple(jnp.zeros((query.shape[0], size), F32) for query in queries)
    totals = lax.fori_loop(0, wide_blocks, lambda i, t: seen(t, pair(i), None), totals)
    totals = lax.fori_loop(low, high + 1, lambda i, t: seen(t, single(i), i * step), totals)
    for k, total in enumerate(totals):
        for r in range(repeat):
            h = k * repeat + r
            dq_ref[:, h * size : (h + 1) * size] = total[r * step : (r + 1) * step]

    @pl.when(stripe == pl.num_programs(0) - 1)
    def _():
        dkv_ref[...] = sums_ref[...].astype(BF16)


def attend_back(table, q, kv, rows, starts, raw, context, inverse, grad, pairs, size):
    length, cols = q.shape
    heads = cols // size
    step = length // table.shape[0]
    block = lambda width: pl.BlockSpec((step, width), lambda i, t: (i, 0))
    whole = pl.BlockSpec(kv.shape, lambda i, t: (0, 0), pipeline_mode=pl.Buffered(1))
    lane = pl.BlockSpec((1, 1, step), lambda i, t: (i, 0, 0))
    logits = logit_specs(raw, heads, pairs, size, step)
    return pl.pallas_call(
        functools.partial(backward_kernel, pairs=pairs, repeat=heads // pairs, size=size, step=step),
        grid_spec=pltpu.PrefetchScalarGridSpec(
            num_scalar_prefetch=1,
            grid=(length // step,),
            in_specs=[block(cols), whole, lane, lane, *logits, block(cols), block(cols), block(cols)],
            out_specs=[block(cols), whole, block(2 * LANES)],
            scratch_shapes=[pltpu.VMEM(kv.shape, F32)],
        ),
        out_shape=[
            jax.ShapeDtypeStruct((length, cols), F32),
            jax.ShapeDtypeStruct(kv.shape, BF16),
            jax.ShapeDtypeStruct((length, 2 * LANES), F32),
        ],
        compiler_params=pltpu.CompilerParams(vmem_limit_bytes=VMEM_LIMIT),
        cost_estimate=pl.CostEstimate(flops=50 * 10**9, bytes_accessed=20 * 10**6, transcendentals=7 * 10**6),
        name="attend_back",
    )(table, q, kv, rows.reshape(-1, 1, step), starts.reshape(-1, 1, step), raw, raw, context, inverse, grad)


class Wires:
    def __init__(self, send_sems, recv_sems, local_sems, sizes):
        self.send_sems, self.recv_sems, self.local_sems = send_sems, recv_sems, local_sems
        self.sizes = sizes
        self.sent, self.local, self.open = [], [], []
        self.locals_used, self.sends_used = 0, 0
        self.dp, self.wide, self.narrow = (lax.axis_index(a) for a in ("dp", "wide", "narrow"))
        self.y, self.core = self.narrow // 2, self.narrow % 2
        self.x, self.far = self.dp % 2, self.wide // 2

    def peer(self, *to):
        if isinstance(to[0], tuple):
            return {axis: at for part in to for axis, at in self.peer(*part).items()}
        axis, distance = to
        at = {"dp": self.dp, "wide": self.wide, "narrow": self.narrow}[axis]
        bit = at // distance % 2
        return {axis: at + distance * (1 - 2 * bit) if distance < 3 else 3 - at}

    def greet(self, peers):
        barrier = pltpu.get_barrier_semaphore()
        for to in peers:
            pl.semaphore_signal(barrier, inc=1, device_id=self.peer(*to), device_id_type=pl.DeviceIdType.MESH)
        pl.semaphore_wait(barrier, len(peers))

    def make(self, source, target, to):
        i = self.sends_used
        self.sends_used += 1
        copy = pltpu.make_async_remote_copy(
            src_ref=source, dst_ref=target, send_sem=self.send_sems.at[i], recv_sem=self.recv_sems.at[i],
            device_id=self.peer(*to), device_id_type=pl.DeviceIdType.MESH,
        )
        self.sent.append(copy)
        return copy

    def send(self, source, target, to):
        copy = self.make(source, target, to)
        copy.start()
        self.open.append(copy)
        return copy

    def arrived(self, copy):
        copy.wait_recv()
        self.open = [other for other in self.open if other is not copy]

    def copy(self, source, target):
        copy = pltpu.make_async_copy(source, target, self.local_sems.at[self.locals_used])
        self.locals_used += 1
        copy.start()
        self.local.append(copy)
        return copy

    def finish(self):
        for copy in list(self.open):
            self.arrived(copy)
        for copy in self.sent:
            copy.wait_send()
        for copy in self.local:
            copy.wait()


Y, CORE, CORNER, NEAR, FAR, X = ("narrow", 2), ("narrow", 1), ("narrow", 3), ("wide", 1), ("wide", 2), ("dp", 1)


def local_flow(net, values_ref, rows_ref):
    rows, width = rows_ref.shape[0], values_ref.shape[1]
    half = width // 2
    out = []
    for distance, to in ((0, None), (1, CORE), (2, Y), (3, CORNER)):
        target = net.narrow if to is None else net.peer(*to)["narrow"]
        at = (2 * (distance % 2) + net.y) * width
        for j in range(2):
            sub = net.x if j == 0 else 1 - net.x
            source = values_ref.at[pl.ds(pl.multiple_of(target * rows, rows), rows), pl.ds(pl.multiple_of(sub * half, half), half)]
            goal = rows_ref.at[:, pl.ds(pl.multiple_of(at + j * half, half), half)]
            out.append(net.copy(source, goal) if to is None else net.send(source, goal, to))
    return out


def gather_flow(net, values_ref, all_ref):
    rows = values_ref.shape[0]
    half = rows // 2
    part = lambda i: all_ref.at[pl.ds(i * half, half), :]
    first, second = values_ref.at[pl.ds(0, half), :], values_ref.at[pl.ds(half, half), :]
    first_y = net.send(first, part(2), Y)
    second_z = net.send(second, part(5), NEAR)
    net.send(first, part(4), NEAR)
    net.send(second, part(3), Y)
    net.copy(values_ref, all_ref.at[pl.ds(0, rows), :])
    yield
    net.arrived(first_y)
    net.send(part(2), part(6), NEAR)
    yield
    net.arrived(second_z)
    net.send(part(5), part(7), Y)
    yield


def weight_flow(net, source_ref, out_ref, axis, own, other, across, from_y=None, from_far=None, from_both=None, their_y=None, their_far=None):
    step = source_ref.shape[axis] // 2
    count = source_ref.shape[axis]

    def window(ref, at, start):
        long, wide = pl.ds(pl.multiple_of(at, step), step), pl.ds(start, across)
        return ref.at[long, wide] if axis == 0 else ref.at[wide, long]

    y, x = net.y, net.x
    piece = lambda sub, half: window(source_ref, sub * step, pl.multiple_of(half * across, across))
    place = lambda slot, j, start: window(out_ref, slot * count + j * step, start)
    mine, rest = piece(x, y), piece(1 - x, y)
    net.copy(mine, place(y, 0, own))
    net.copy(rest, place(y, 1, own))
    if from_y is None:
        come_y = net.send(piece(x, 1 - y), place(y, 0, own), Y)
    else:
        net.copy(from_y, place(1 - y, 0, own))
    if from_far is None:
        come_far = net.send(mine, place(y, 0, other), FAR)
    else:
        net.copy(from_far, place(y, 0, other))
    net.send(mine, place(2 + y, 0, own), CORE)
    net.send(rest, place(2 + y, 1, own), CORE)
    if from_y is None:
        yield
        net.arrived(come_y)
        from_y = place(1 - y, 0, own)
    if from_both is None:
        come_both = net.send(from_y, place(1 - y, 0, other), FAR)
    else:
        net.copy(from_both, place(1 - y, 0, other))
    given = their_y is not None
    if given:
        for ref, slot, start in ((their_y, 1 - y, own), (their_far, y, other)):
            net.copy(ref, place(slot, 1, start))
            net.send(ref, place(slot + 2, 1, start), CORE)
    else:
        their_y = net.send(from_y, place(1 - y, 1, own), X)
    net.send(from_y, place(3 - y, 0, own), CORE)
    if from_far is None:
        yield
        net.arrived(come_far)
        from_far = place(y, 0, other)
    if not given:
        their_far = net.send(from_far, place(y, 1, other), X)
    net.send(from_far, place(2 + y, 0, other), CORE)
    if from_both is None:
        yield
        net.arrived(come_both)
        from_both = place(1 - y, 0, other)
    their_both = net.send(from_both, place(1 - y, 1, other), X)
    net.send(from_both, place(3 - y, 0, other), CORE)
    yield
    waiting = ((their_y, 1 - y, own), (their_far, y, other), (their_both, 1 - y, other))
    for copy, slot, start in waiting[2 * given :]:
        net.arrived(copy)
        net.send(place(slot, 1, start), place(slot + 2, 1, start), CORE)
    yield


def run(flow):
    return next(flow, None)


def by_rows(count, body):
    step = 16
    lax.fori_loop(0, count // step, lambda i, _: (body(pl.ds(pl.multiple_of(i * step, step), step)), 0)[1], 0)


def begin_kernel(
    tokens_ref, cotangent_ref, gain_ref, query_ref, key_ref, value_ref, gates_ref, out_ref,
    x_ref, rows_ref, all_ref, joined_ref, output_ref, here, normed, there, qkv_ref, send, recv, local, *, sizes,
):
    net = Wires(send, recv, local, sizes)
    net.greet([Y, CORE, CORNER, NEAR, FAR, X])
    rows = local_flow(net, tokens_ref, here)
    across = qkv_ref.shape[1] // 2
    packed, at = [], 0
    for ref in (query_ref, key_ref, value_ref, gates_ref):
        wide = ref.shape[1] // 2
        for i in range(2):
            packed.append(net.copy(ref.at[:, pl.ds(i * wide, wide)], qkv_ref.at[:, pl.ds(i * across + at, wide)]))
        at += wide
    for copy in packed:
        copy.wait()
    net.local = [copy for copy in net.local if all(copy is not other for other in packed)]
    joined = weight_flow(net, qkv_ref, joined_ref, 0, 0, across, across)
    run(joined)
    rows[0].wait()
    rows[1].wait()
    net.local = net.local[2:]
    for copy in rows[2:]:
        net.arrived(copy)

    def norm(at):
        values = here[at, :].astype(F32)
        inverse = lax.rsqrt(jnp.mean(values * values, axis=1, keepdims=True) + EPS)
        normed[at, :] = (values * inverse * gain_ref[...]).astype(BF16)
        x_ref[at, :] = here[at, :]

    by_rows(here.shape[0], norm)
    gather = gather_flow(net, normed, all_ref)
    run(gather)
    across = out_ref.shape[0] // 2
    output = weight_flow(net, out_ref, output_ref, 1, 0, across, across)
    for flow in (joined, gather, output, joined, gather):
        run(flow)
    rows = local_flow(net, cotangent_ref, there)
    for flow in (joined, output, joined, output, output, output):
        run(flow)
    for copy in rows[:2]:
        copy.wait()
    net.local = [copy for copy in net.local if all(copy is not other for other in rows[:2])]
    for copy in rows[2:]:
        net.arrived(copy)
    net.copy(there, rows_ref)
    net.finish()


ANY = pl.BlockSpec(memory_space=pl.ANY)
VMEM = pl.BlockSpec(memory_space=pltpu.VMEM)


def sems(sends, locals_):
    return [pltpu.SemaphoreType.DMA((sends,)), pltpu.SemaphoreType.DMA((sends,)), pltpu.SemaphoreType.DMA((locals_,))]


def wire_call(kernel, name, number, specs, out_specs, shapes, scratch, sizes, cost, *args):
    return pl.pallas_call(
        functools.partial(kernel, sizes=sizes),
        in_specs=specs,
        out_specs=out_specs,
        out_shape=[jax.ShapeDtypeStruct(*shape) for shape in shapes],
        scratch_shapes=scratch,
        compiler_params=pltpu.CompilerParams(collective_id=number, has_side_effects=True, vmem_limit_bytes=VMEM_LIMIT),
        cost_estimate=pl.CostEstimate(flops=0, bytes_accessed=cost * 3 * 10**6, transcendentals=0),
        name=name,
    )(*args)


def begin(tokens, cotangent, gain, weights, out, sizes):
    rows, width = tokens.shape[0] // sizes["narrow"], gain.shape[0]
    wide = sum(w.shape[1] for w in weights)
    row = pltpu.VMEM((rows, width), BF16)
    return wire_call(
        begin_kernel, "begin", 1, [ANY, ANY, VMEM] + [ANY] * 4 + [VMEM], [VMEM, ANY, ANY, ANY, ANY],
        [
            ((rows, width), BF16), ((rows, width), BF16), ((4 * rows, width), BF16), ((width, wide), BF16),
            ((out.shape[0], width), BF16),
        ],
        [row, row, row, pltpu.VMEM((weights[0].shape[0], wide), BF16), *sems(48, 24)],
        sizes, 55, tokens, cotangent, gain[None], *weights, out,
    )


def keys_kernel(kv_ref, keys_ref, done, send, recv, local, *, sizes):
    net = Wires(send, recv, local, sizes)
    across = [FAR, ("wide", 3), (FAR, CORE), (("wide", 3), CORE)]
    net.greet([CORE] + across)
    count, width = kv_ref.shape
    size = width // 4
    part = lambda i, j: keys_ref.at[pl.ds(i, count), pl.ds(j * size, size)]
    base = pl.multiple_of(net.far * 2 * count, count)
    far = [net.make(kv_ref.at[:, pl.ds(j * size, size)], part(0, j ^ 1), FAR) for j in range(4)]
    on = [net.make(part(0, j ^ 1), part(count, j ^ 1), CORE) for j in range(4)]

    @pl.when(net.far == 0)
    def _():
        for copy in far:
            copy.start()

    net.copy(kv_ref, keys_ref.at[pl.ds(base, count), :])
    net.send(kv_ref, keys_ref.at[pl.ds(base + count, count), :], CORE)

    @pl.when(net.far == 1)
    def _():
        for copy, forward in zip(far, on):
            copy.wait_recv()
            forward.start()
        for to in across:
            pl.semaphore_signal(done, inc=1, device_id=net.peer(*to), device_id_type=pl.DeviceIdType.MESH)
        for forward in on:
            forward.wait()

    @pl.when(net.far == 0)
    def _():
        for copy in far:
            copy.wait_send()
        pl.semaphore_wait(done, len(across))

    net.sent = [copy for copy in net.sent if all(copy is not other for other in far + on)]
    net.finish()


def exchange_keys(kv, sizes):
    return wire_call(
        keys_kernel, "keys", 2, [VMEM], [ANY], [((4 * kv.shape[0], kv.shape[1]), BF16)],
        [pltpu.SemaphoreType.REGULAR, *sems(16, 4)], sizes, 45, kv,
    )[0]


def scatter_flow(net, partial_ref, first_ref, second_ref, send_ref, last_ref, total_ref):
    half = partial_ref.shape[0] // 8
    part = lambda i: partial_ref.at[pl.ds(i * half, half), :]
    slot = lambda ref, i: ref.at[pl.ds(i * half, half), :]
    to_z = [net.send(part(6), slot(first_ref, 1), NEAR), net.send(part(4), slot(first_ref, 0), NEAR)]
    to_y = [net.send(part(7), slot(second_ref, 1), Y), net.send(part(3), slot(second_ref, 0), Y)]
    yield

    def add(out_ref, to, i, ref, j):
        def body(at):
            move = lambda start: pl.ds(pl.multiple_of(at.start + start, 16), at.size)
            value = partial_ref[move(i * half), :].astype(F32) + ref[move(j * half), :].astype(F32)
            out_ref[move(to), :] = value.astype(out_ref.dtype)

        by_rows(half, body)

    net.arrived(to_z[0])
    add(send_ref, 0, 2, first_ref, 1)
    last_y = net.send(slot(send_ref, 0), slot(last_ref, 0), Y)
    net.arrived(to_y[0])
    add(send_ref, half, 5, second_ref, 1)
    last_z = net.send(slot(send_ref, 1), slot(last_ref, 1), NEAR)
    yield
    net.arrived(to_z[1])
    add(total_ref, 0, 0, first_ref, 0)
    net.arrived(to_y[1])
    add(total_ref, half, 1, second_ref, 0)
    yield
    net.arrived(last_y)
    net.arrived(last_z)
    yield


def middle_kernel(
    partial_ref, x_ref, gain_ref, gate_ref, up_ref, down_ref, gate_y_ref, up_y_ref, down_y_ref, gate_far_ref, up_far_ref, down_far_ref,
    gate_both_ref, up_both_ref, down_both_ref, middle_ref, all_ref, both_ref, last_ref,
    first, second, sums, last, total, normed, send, recv, local, *, sizes,
):
    net = Wires(send, recv, local, sizes)
    net.greet([Y, CORE, NEAR, FAR, X])
    scatter = scatter_flow(net, partial_ref, first, second, sums, last, total)
    run(scatter)
    across = gate_ref.shape[1] // 2
    flows = [
        weight_flow(net, gate_ref, both_ref, 0, 0, across, across, gate_y_ref, gate_far_ref, gate_both_ref),
        weight_flow(net, up_ref, both_ref, 0, 2 * across, 3 * across, across, up_y_ref, up_far_ref, up_both_ref),
        weight_flow(net, down_ref, last_ref, 1, 0, across, across, down_y_ref, down_far_ref, down_both_ref),
    ]
    for flow in flows:
        run(flow)
    run(scatter)
    run(scatter)
    run(scatter)

    def norm(at):
        values = x_ref[at, :].astype(F32) + total[at, :] + last[at, :].astype(F32)
        middle_ref[at, :] = values
        inverse = lax.rsqrt(jnp.mean(values * values, axis=1, keepdims=True) + EPS)
        normed[at, :] = (values * inverse * gain_ref[...]).astype(BF16)

    by_rows(normed.shape[0], norm)
    gather = gather_flow(net, normed, all_ref)
    run(gather)
    run(flows[0])
    run(gather)
    run(gather)
    run(flows[1])
    run(flows[2])
    net.finish()


def to_middle(partial, x, gain, gate, up, down, pieces, sizes):
    rows, width = x.shape
    buffer = lambda n, kind: pltpu.VMEM((n, width), kind)
    return wire_call(
        middle_kernel, "middle", 3, [VMEM] * 15, [VMEM, ANY, ANY, ANY],
        [((rows, width), F32), ((4 * rows, width), BF16), ((width, 2 * gate.shape[1]), BF16), ((down.shape[0], width), BF16)],
        [
            buffer(rows, BF16), buffer(rows, BF16), buffer(rows, BF16), buffer(rows, BF16), buffer(rows, F32), buffer(rows, BF16),
            *sems(64, 32),
        ],
        sizes, 80, partial, x, gain[None], gate, up, down, *pieces,
    )


def spread_flow(net, rows_ref, out_ref):
    rows, width = rows_ref.shape[0], out_ref.shape[1]
    half = width // 2
    base = pl.multiple_of(net.narrow * rows, rows)
    for distance, to in ((3, CORNER), (2, Y), (1, CORE), (0, None)):
        target = net.narrow if to is None else net.peer(*to)["narrow"]
        at = (2 * (distance % 2) + target // 2) * width
        for j in range(2):
            sub = net.x if j == 0 else 1 - net.x
            source = rows_ref.at[:, pl.ds(pl.multiple_of(at + j * half, half), half)]
            goal = out_ref.at[pl.ds(base, rows), pl.ds(pl.multiple_of(sub * half, half), half)]
            if to is None:
                net.copy(source, goal)
            else:
                net.send(source, goal, to)


def add_rows(target, terms):
    ref, (rows, cols) = target

    def body(at):
        move = lambda r: pl.ds(pl.multiple_of(at.start + r.start, 16), at.size)
        value = sum(term[move(r), c].astype(F32) for term, (r, c) in terms)
        ref[move(rows), cols] = value.astype(BF16)

    by_rows(rows.size, body)


class Gradient:
    def __init__(self, net, axis, step, across):
        self.net, self.axis, self.step, self.across = net, axis, step, across
        self.order = (1 - net.y, net.y)
        self.x, self.far = [], []

    def window(self, at, start, count, length=None):
        step = self.step if length is None else length
        hint = lambda v, unit: v if isinstance(v, int) else pl.multiple_of(v, unit)
        along, wide = pl.ds(hint(at, self.step), step), pl.ds(hint(start, self.across), count)
        return (along, wide) if self.axis == 0 else (wide, along)

    def start(self, g_ref, acc, from_core, given=False):
        self.acc, self.from_core = acc, from_core
        count = 4 * self.step
        own, other = (self.window(i * count, 0, 2 * self.across, count) for i in range(2))
        self.loaded = self.net.copy(g_ref.at[own], acc)
        self.core = None if given else self.net.send(g_ref.at[other], from_core, CORE)

    def wait_core(self):
        if self.loaded is not None:
            self.loaded.wait()
            self.net.local = [copy for copy in self.net.local if copy is not self.loaded]
        if self.core is not None:
            self.net.arrived(self.core)

    def core_to_x(self, from_x):
        self.wait_core()
        self.from_x = from_x
        for slot in self.order:
            place = self.window((2 * slot + 1) * self.step, 0, 2 * self.across)
            add_rows((self.acc, place), [(self.acc, place), (self.from_core, place)])
            goal = from_x.at[self.window(slot * self.step, 0, 2 * self.across)]
            self.x.append(self.net.send(self.acc.at[place], goal, X))

    def x_end(self, k, from_far=None):
        slot = self.order[k]
        self.net.arrived(self.x[k])
        for start in (self.across, 0):
            place = self.window(2 * slot * self.step, start, self.across)
            come = self.window(slot * self.step, start, self.across)
            add_rows((self.acc, place), [(self.acc, place), (self.from_core, place), (self.from_x, come)])
            if start and from_far is not None:
                self.from_far = from_far
                goal = from_far.at[self.window(slot * self.step, 0, self.across)]
                self.far.append(self.net.send(self.acc.at[place], goal, FAR))

    def far_end(self, k, result=None):
        slot = self.order[k]
        self.net.arrived(self.far[k])
        place = self.window(2 * slot * self.step, 0, self.across)
        come = self.window(slot * self.step, 0, self.across)
        add_rows((self.acc, place), [(self.acc, place), (self.from_far, come)])

    def to_owner(self, k, source, out):
        net, across = self.net, self.across
        goal = out.at[self.window(net.x * self.step, net.y * across, across)]
        if k == 0:
            self.out = out
            self.y = net.send(source, goal, Y)
        else:
            net.copy(source, goal)
            net.send(source, goal, X)

    def after_y(self):
        net, across = self.net, self.across
        net.arrived(self.y)
        place = self.out.at[self.window(net.x * self.step, (1 - net.y) * across, across)]
        net.send(place, place, X)

    def slot(self, k, stride, start, count):
        return self.window(stride * self.order[k] * self.step, start, count)


def row_back(grad, values, gain):
    inverse = lax.rsqrt(jnp.mean(values * values, axis=1, keepdims=True) + EPS)
    hat = values * inverse
    scaled = grad * gain
    inner = jnp.mean(scaled * hat, axis=1, keepdims=True)
    return jnp.sum(grad * hat, axis=0, keepdims=True), inverse * (scaled - hat * inner)


def turn_kernel(
    partial_ref, middle_ref, upstream_ref, gain_ref, down_ref, inputs_ref, gate_ref, up_ref,
    grad_ref, all_ref, term_ref, down_out, gate_out, up_keep, up_send,
    first, second, sums, last, total, low, *rest, sizes,
):
    buffers, (rows_two, gate_grads, up_grads, gate_other, up_other), (send, recv, local) = rest[:-8], rest[-8:-3], rest[-3:]
    net = Wires(send, recv, local, sizes)
    net.greet([Y, CORE, NEAR, FAR, X])
    scatter = scatter_flow(net, partial_ref, first, second, sums, last, total)
    run(scatter)
    step, across = low.shape[1] // sizes["narrow"] // 2, gate_ref.shape[1] // 2
    down, gate, up = (Gradient(net, axis, step, across) for axis in (1, 0, 0))
    down.start(down_ref, *buffers[0:2])
    gate.acc, gate.from_core = buffers[3:5]
    up.acc, up.from_core = buffers[6:8]
    loads = [net.copy(inputs_ref, rows_two), net.copy(gate_ref, gate_grads), net.copy(up_ref, up_grads)]
    for copy in loads:
        copy.wait()
    net.local = [copy for copy in net.local if all(copy is not other for other in loads)]
    half = rows_two.shape[1] // 2

    def dots(base, grads, target):
        def body(i, _):
            at = pl.multiple_of(i * step, step)
            part = dot_inner(rows_two[:, pl.ds(pl.multiple_of(base + at, step), step)], grads[...])
            target[pl.ds(at, step), :] = part.astype(BF16)
            return 0

        lax.fori_loop(0, half // step, body, 0)

    dots(half, gate_grads, gate_other)
    gate.loaded, gate.core = None, net.send(gate_other, gate.from_core, CORE)
    down.core_to_x(buffers[2])
    dots(0, gate_grads, gate.acc)
    gate.core_to_x(buffers[5])
    run(scatter)
    run(scatter)
    run(scatter)
    term_ref[...] = jnp.zeros_like(term_ref)

    def rows(at):
        grad = total[at, :] + last[at, :].astype(F32)
        term, change = row_back(grad, middle_ref[at, :], gain_ref[...])
        term_ref[...] += term
        value = upstream_ref[at, :].astype(F32) + change
        grad_ref[at, :] = value
        low[at, :] = value.astype(BF16)

    by_rows(low.shape[0], rows)
    gather = gather_flow(net, low, all_ref)
    run(gather)
    dots(half, up_grads, up_other)
    up.loaded, up.core = None, net.send(up_other, up.from_core, CORE)
    for k in range(2):
        down.x_end(k)
        net.copy(down.acc.at[down.slot(k, 2, 0, 2 * across)], down_out.at[down.slot(k, 1, 0, 2 * across)])
    run(gather)
    run(gather)
    dots(0, up_grads, up.acc)
    up.wait_core()
    for slot in range(2):
        for j, ref in ((1, up_send), (0, up_keep)):
            place = up.window((2 * slot + j) * step, 0, 2 * across)
            add_rows((up.acc, place), [(up.acc, place), (up.from_core, place)])
            net.copy(up.acc.at[place], ref.at[up.window(slot * step, 0, 2 * across)])
    for k in range(2):
        gate.x_end(k)
        net.copy(gate.acc.at[gate.slot(k, 2, 0, 2 * across)], gate_out.at[gate.slot(k, 1, 0, 2 * across)])
    net.finish()


def gradient_buffers(size, across, axis, count=4):
    shape = lambda a, b: pltpu.VMEM((a, b) if axis == 0 else (b, a), BF16)
    every = [shape(2 * size, 2 * across), shape(2 * size, 2 * across), shape(size, 2 * across), shape(size, across)]
    return every[:count]


def scatter_buffers(rows, width):
    buffer = lambda kind: pltpu.VMEM((rows, width), kind)
    return [buffer(BF16), buffer(BF16), buffer(BF16), buffer(BF16), buffer(F32)]


def turn(partial, middle, upstream, gain, down, inputs, gate, up, sizes):
    rows, width = middle.shape
    size, across = width // sizes["narrow"], down.shape[0] // 2
    return wire_call(
        turn_kernel, "turn", 4, [VMEM] * 4 + [ANY] * 4, [VMEM, ANY, VMEM, ANY, ANY, ANY, ANY],
        [
            ((rows, width), F32), ((4 * rows, width), BF16), ((1, width), F32),
            ((2 * across, size), BF16), ((size, 2 * across), BF16), ((size, 2 * across), BF16), ((size, 2 * across), BF16),
        ],
        [
            *scatter_buffers(rows, width), pltpu.VMEM((rows, width), BF16),
            *gradient_buffers(size, across, 1, 3), *gradient_buffers(size, across, 0, 3), *gradient_buffers(size, across, 0, 2),
            pltpu.VMEM(inputs.shape, BF16), *(pltpu.VMEM((n, 2 * across), BF16) for n in (gate.shape[0],) * 2 + (2 * size,) * 2),
            *sems(40, 24),
        ],
        sizes, 80, partial, middle, upstream, gain[None], down, inputs, gate, up,
    )


def owner_kernel(
    dkv_ref, partial_ref, middle_ref, down_ref, down_far_ref, gate_ref, gate_far_ref,
    mine_ref, layer_ref, down_out, gate_out,
    prompt_core, rest_core, prompt, prompt_far, first, second, sums, last, total, rows_low, down_sums, gate_sums,
    send, recv, local, *, sizes,
):
    net = Wires(send, recv, local, sizes)
    net.greet([Y, CORE, CORNER, NEAR, FAR, X])
    count, width = prompt.shape
    size = width // 4
    region = lambda i: dkv_ref.at[pl.ds(i * count, count), :]
    come = net.send(region(1), prompt_core, CORE)
    rest = net.send(region(3), rest_core, CORE)
    scatter = scatter_flow(net, partial_ref, first, second, sums, last, total)
    run(scatter)
    step, across = down_far_ref.shape[1] // 2, down_far_ref.shape[0]
    down, gate = (Gradient(net, axis, step, across) for axis in (1, 0))
    net.arrived(come)

    def add(at):
        prompt[at, :] = (dkv_ref[at, :].astype(F32) + prompt_core[at, :].astype(F32)).astype(BF16)

    by_rows(count, add)
    cols = lambda ref, j: ref.at[:, pl.ds(j * size, size)]
    far = [net.make(cols(prompt, j), cols(prompt_far, j ^ 1), FAR) for j in range(4)]

    @pl.when(net.far == 1)
    def _():
        for copy in far:
            copy.start()

    parts = ((down, down_sums, down_ref, down_far_ref, down_out), (gate, gate_sums, gate_ref, gate_far_ref, gate_out))
    for flow, total_ref, ref, far_ref, goal in parts:
        for k in range(2):
            place = flow.slot(k, 1, 0, across)
            add_rows((total_ref, place), [(ref, place), (far_ref, place)])
            flow.to_owner(k, total_ref.at[place], goal)
    run(scatter)
    run(scatter)
    run(scatter)

    def rows(at):
        rows_low[at, :] = (middle_ref[at, :] + total[at, :] + last[at, :].astype(F32)).astype(BF16)

    by_rows(rows_low.shape[0], rows)
    spread_flow(net, rows_low, layer_ref)
    down.after_y()
    gate.after_y()
    net.arrived(rest)

    @pl.when(net.far == 1)
    def _():
        def add(at):
            move = pl.ds(pl.multiple_of(at.start + 2 * count, 16), at.size)
            mine_ref[at, :] = dkv_ref[move, :].astype(F32) + rest_core[at, :].astype(F32)

        by_rows(count, add)
        for copy in far:
            copy.wait_send()

    @pl.when(net.far == 0)
    def _():
        for copy in far:
            copy.wait_recv()

        def add(at):
            mine_ref[at, :] = dkv_ref[at, :].astype(F32) + prompt_core[at, :].astype(F32) + prompt_far[at, :].astype(F32)

        by_rows(count, add)

    net.sent = [copy for copy in net.sent if all(copy is not other for other in far)]
    net.finish()


def to_owner(dkv, partial, middle, down, down_far, gate, gate_far, sizes):
    rows, width = middle.shape
    size, across = width // sizes["narrow"], gate_far.shape[1]
    count = dkv.shape[0] // 4
    block = lambda: pltpu.VMEM((count, dkv.shape[1]), BF16)
    return wire_call(
        owner_kernel, "owner", 5, [VMEM] * 7, [VMEM, ANY, ANY, ANY],
        [
            ((count, dkv.shape[1]), F32), ((sizes["narrow"] * rows, size), BF16), ((2 * across, size), BF16),
            ((size, 2 * across), BF16),
        ],
        [
            block(), block(), block(), block(), *scatter_buffers(rows, width), pltpu.VMEM((rows, width), BF16),
            pltpu.VMEM((across, size), BF16), pltpu.VMEM((size, across), BF16), *sems(40, 16),
        ],
        sizes, 80, dkv, partial, middle, down, down_far, gate, gate_far,
    )


SUMS = [CORE, Y, X, NEAR, FAR]


def end_kernel(
    partial_ref, x_ref, gain_ref, grad_ref, two_ref, query_ref, key_ref, up_ref, up_x_ref, qkv_core_ref, qkv_ref, out_ref,
    tokens_ref, gains_ref, qkv_out, out_out, up_out,
    first, second, sums, last, total, rows_low, vectors, up_sums, up_far, *rest, sizes,
):
    buffers, (send, recv, local) = rest[:-3], rest[-3:]
    net = Wires(send, recv, local, sizes)
    net.greet([Y, CORE, CORNER, NEAR, FAR, X])
    step = x_ref.shape[1] // sizes["narrow"] // 2
    qkv = Gradient(net, 0, step, qkv_ref.shape[1] // 2)
    out = Gradient(net, 1, step, out_ref.shape[0] // 2)
    qkv.start(qkv_ref, buffers[0], qkv_core_ref, True)
    out.start(out_ref, *buffers[3:5])
    scatter = scatter_flow(net, partial_ref, first, second, sums, last, total)
    run(scatter)
    up = Gradient(net, 0, step, up_ref.shape[1] // 2)
    qkv.core_to_x(buffers[1])
    out.core_to_x(buffers[5])

    def up_to_far(k):
        for start in (up.across, 0):
            place = up.slot(k, 1, start, up.across)
            add_rows((up_sums, place), [(up_ref, place), (up_x_ref, place)])
            if start:
                up.far.append(net.send(up_sums.at[place], up_far.at[up.slot(k, 1, 0, up.across)], FAR))

    run(scatter)
    qkv.x_end(0, buffers[2])
    up_to_far(0)
    run(scatter)
    qkv.x_end(1, buffers[2])
    up_to_far(1)
    run(scatter)
    width = x_ref.shape[1]
    size = query_ref.shape[1]
    block = width // sizes["narrow"]
    half = block // 2
    gains_ref[...] = jnp.zeros_like(gains_ref)

    def rows(at):
        grad = total[at, :] + last[at, :].astype(F32)
        term, change = row_back(grad, x_ref[at, :].astype(F32), gain_ref[...])
        gains_ref[:, :width] += term
        rows_low[at, :] = (grad_ref[at, :] + change).astype(BF16)

    by_rows(rows_low.shape[0], rows)
    for i, ref in enumerate((gains_ref, two_ref)):
        for slot in range(4):
            to = (2 * (slot % 2) + jnp.bitwise_xor(net.core, slot // 2)) * block + i * width
            for j in range(2):
                sub = net.x if j == 0 else 1 - net.x
                at = slot * block + j * half
                vectors[0, :, pl.ds(pl.multiple_of(to + sub * half, half), half)] = ref[:, at : at + half]
    vectors[0, :, 2 * width : 2 * width + size] = query_ref[...]
    vectors[0, :, 2 * width + size :] = key_ref[...]

    def add_gains():
        for i, to in enumerate(SUMS):
            copy = net.send(vectors.at[i], vectors.at[len(SUMS) + 1 + i], to)
            yield
            net.arrived(copy)
            vectors[i + 1] = vectors[i] + vectors[len(SUMS) + 1 + i]
        gains_ref[...] = vectors[len(SUMS)]
        yield

    def own(flow, k, ref):
        flow.far_end(k)
        flow.to_owner(k, flow.acc.at[flow.slot(k, 2, 0, flow.across)], ref)

    def own_up(k):
        net.arrived(up.far[k])
        place = up.slot(k, 1, 0, up.across)
        add_rows((up_sums, place), [(up_sums, place), (up_far, place)])
        up.to_owner(k, up_sums.at[place], up_out)

    gains = add_gains()
    run(gains)
    out.x_end(0, buffers[6])
    out.x_end(1, buffers[6])
    run(gains)
    spread_flow(net, rows_low, tokens_ref)
    own(qkv, 0, qkv_out)
    own_up(0)
    run(gains)
    own(qkv, 1, qkv_out)
    own_up(1)
    run(gains)
    own(out, 0, out_out)
    own(out, 1, out_out)
    up.after_y()
    qkv.after_y()
    out.after_y()
    run(gains)
    run(gains)
    net.finish()


def end(partial, x, gain, grad, two, query, key, up, up_x, qkv_core, qkv, out, sizes):
    rows, width = x.shape
    size = width // sizes["narrow"]
    wide, deep = qkv.shape[1], out.shape[0]
    length = 2 * width + 2 * query.shape[1]
    return wire_call(
        end_kernel, "end", 6, [VMEM] * 10 + [ANY] * 2, [ANY, VMEM, ANY, ANY, ANY],
        [((sizes["narrow"] * rows, size), BF16), ((1, length), F32), ((size, wide), BF16), ((deep, size), BF16),
         (up.shape, BF16)],
        [
            *scatter_buffers(rows, width), pltpu.VMEM((rows, width), BF16), pltpu.VMEM((2 * len(SUMS) + 1, 1, length), F32),
            pltpu.VMEM(up.shape, BF16), pltpu.VMEM((size, up.shape[1] // 2), BF16),
            *(v for i, v in enumerate(gradient_buffers(size, wide // 2, 0)) if i != 1), *gradient_buffers(size, deep // 2, 1),
            *sems(40, 16),
        ],
        sizes, 90, partial, x, gain[None], grad, two, query, key, up, up_x, qkv_core, qkv, out,
    )


def layout(lengths, index):
    order = jnp.arange(lengths.shape[0])
    ends = jnp.sum(jnp.where(order[None, :] <= order[:, None], lengths[None, :], 0), axis=1)[None, :]
    begins = ends - lengths[None, :]
    offset = index - PROMPT
    shift = jnp.sum(jnp.where((offset >= begins) & (offset < ends), begins, 0), axis=1, keepdims=True)
    return jnp.where(offset >= 0, PROMPT + shift, 0), index - shift


def make(sizes):
    n_dp, n_wide, n_narrow = sizes["dp"], sizes["wide"], sizes["narrow"]

    def over_y(values):
        return exchange(values, "narrow", 2, n_narrow)

    def over_z(values):
        return exchange(values, "wide", 1, n_wide)

    def over_x(values):
        return exchange(values, "dp", 1, n_dp)

    def over_core(values):
        return exchange(values, "narrow", 1, n_narrow)

    def over_far(values):
        return exchange(values, "wide", 2, n_wide)

    def over_groups(values, kind):
        distance = 2
        while distance < n_dp:
            values = values.astype(F32) + exchange(values.astype(kind), "dp", distance, n_dp).astype(F32)
            distance *= 2
        return values.astype(F32)

    def on_device(
        tokens, continuation_lengths, attention_gain, query_weight, key_weight, value_weight, head_gate, query_gain, key_gain,
        output_weight, feedforward_gain, gate_weight, up_weight, down_weight, cotangent,
    ):
        rows_wide, width_local = tokens.shape
        width = attention_gain.shape[0]
        size = query_gain.shape[0]
        heads = head_gate.shape[1]
        pairs = key_weight.shape[1] // size
        group_rows = rows_wide * n_wide
        rows_local = rows_wide // n_narrow
        x = lax.axis_index("dp") % 2
        z = lax.axis_index("wide")
        narrow = lax.axis_index("narrow")
        y, core = narrow // 2, narrow % 2
        z_near, z_far = z % 2, z // 2
        quarter = width_local // 2
        scale = size ** (-0.5)
        factor = scale * math.log2(math.e)
        log_two = math.log(2.0)

        def relative_vector(vector):
            values = jnp.transpose(vector.reshape(2, 2, 2, quarter), (1, 0, 2, 3))
            values = jnp.where(core == 0, values, values[::-1])
            return jnp.where(x == 0, values, values[:, :, ::-1]).reshape(width)

        def piece_of(weight, i, axis):
            half = weight.shape[1 - axis] // 2
            return cut(cut(weight, x * quarter, quarter, axis), i * half, half, 1 - axis)

        gain_one, gain_two = relative_vector(attention_gain), relative_vector(feedforward_gain)
        lane_pad = ((0, 0), (0, LANES - heads // 2))
        halves = lambda w, i: w[:, i * (w.shape[1] // 2) : (i + 1) * (w.shape[1] // 2)]
        gates = join([jnp.pad(halves(head_gate, i), lane_pad) for i in range(2)], 1)
        packed = (query_weight, key_weight, value_weight, gates)
        inputs, upstream, normed_all, joined_weight, out_weight = begin(tokens, cotangent, gain_one, packed, output_weight, sizes)

        def indices(row):
            part, at = row // rows_local, row % rows_local
            return ((z ^ (part // 2)) * n_narrow + (narrow ^ (2 * (part % 2)))) * rows_local + at

        my_index = indices(lax.broadcasted_iota(jnp.int32, (4 * rows_local, 1), 0))
        my_start, my_position = layout(continuation_lengths[0], my_index)
        frequency = THETA ** (-2.0 * jnp.arange(size // 2, dtype=F32) / size)
        angle = my_position.astype(F32) * frequency[None, :]
        cosine, sine = jnp.cos(angle), jnp.sin(angle)
        cosine = jnp.concatenate([cosine, cosine], axis=1)
        sine = jnp.concatenate([-sine, sine], axis=1)
        heads_index = indices(lax.broadcasted_iota(jnp.int32, (4, 1), 0) * rows_local)
        block = heads_index // rows_local
        first = layout(continuation_lengths[0], heads_index)[0] // rows_local
        prompt_blocks = PROMPT // rows_local
        in_prompt = block < prompt_blocks
        column = lax.broadcasted_iota(jnp.int32, (4, 5), 1)
        pick = lambda values: functools.reduce(lambda acc, item: jnp.where(column == item[0], item[1], acc), enumerate(values), 0)
        table = pick(
            [
                jnp.where(in_prompt, block // 2, prompt_blocks // 2),
                jnp.where(in_prompt, block // 2 * 2, first),
                block,
                2 * z_near + y,
                core,
            ]
        ).astype(jnp.int32)

        raw = dot_rows(normed_all, joined_weight)
        q, kv = post(raw, cosine, sine, query_gain, key_gain, heads, pairs, size, factor)
        send = after((gate_weight, up_weight, down_weight), normed_all)
        axes = (0, 0, 1)
        from_y = [over_y(piece_of(w, 1 - y, axis)) for w, axis in zip(send, axes)]
        from_far = [over_far(piece_of(w, y, axis)) for w, axis in zip(send, axes)]
        part = rows_local // 2
        upstream_y, upstream_z = over_y(upstream[:part]), over_z(upstream[part:])
        kv_all = exchange_keys(after(kv, *from_y, *from_far, upstream_y, upstream_z), sizes)
        from_both = [over_far(after(v, kv_all)) for v in from_y]

        come_z = over_z(join([upstream[:part], after(upstream_y, kv_all)]))
        come_y = over_y(join([upstream[part:], after(upstream_z, kv_all)]))
        upstream_all = join(
            [upstream, upstream_y, come_y[:part], come_z[:part], upstream_z, come_z[part:], come_y[part:]]
        )

        gated, context, inverse_total = attend(
            table, q, kv_all, my_index, my_start, raw, pairs, size
        )
        partial = dot_rows(gated, out_weight).astype(BF16)
        middle, normed_two_all, gate_up, down = to_middle(
            partial, inputs, gain_two, gate_weight, up_weight, down_weight, from_y + from_far + from_both, sizes
        )
        both = dot_rows(normed_two_all, gate_up)
        hidden_cols = gate_weight.shape[1]
        gate_pre, up_pre = both[:, :hidden_cols], both[:, hidden_cols:]
        gate_sigmoid = jax.nn.sigmoid(gate_pre)
        silu = gate_pre * gate_sigmoid
        hidden = (silu * up_pre).astype(BF16)
        hidden_grad = dot_trans(upstream_all, down)
        gate_grad = hidden_grad * up_pre * gate_sigmoid * (1.0 + gate_pre * (1.0 - gate_sigmoid))
        up_grad = hidden_grad * silu
        gate_low, up_low = gate_grad.astype(BF16), up_grad.astype(BF16)
        gate_up_low = join([gate_low, up_low], 1)
        partial = dot_trans(gate_up_low, gate_up).astype(BF16)
        down_sums = dot_inner(hidden, upstream_all).astype(BF16)
        mlp_partial = dot_rows(hidden, down).astype(BF16)
        partial = after(partial, mlp_partial)
        middle_grad, middle_all, two_term, down_part, gate_part, up_keep, up_send = turn(
            partial, middle, upstream, gain_two, down_sums, normed_two_all, gate_low, up_low, sizes
        )
        down_far = over_far(down_part[hidden_cols // 2 :])
        gate_far = over_far(gate_part[:, hidden_cols // 2 :])
        up_come = over_x(up_send)
        gated_grad = dot_trans(middle_all, out_weight)
        dq, dkv, logit_grad = attend_back(
            table, q, kv_all, my_index, my_start, raw, context, inverse_total, gated_grad, pairs, size
        )
        out_sums = dot_inner(gated, middle_all).astype(BF16)
        dkv_mine, layer_output, down_gradient, gate_gradient = to_owner(
            after(dkv, up_come, out_sums), mlp_partial, middle, down_part, down_far, gate_part, gate_far, sizes
        )
        low, query_term, key_term = project_back(
            dq, dkv_mine, raw, cosine, sine, query_gain, key_gain, logit_grad, heads, pairs, size, scale, log_two
        )
        half = width // 2
        qkv_sums = dot_inner(normed_all, low).astype(BF16)
        qkv_core = over_core(qkv_sums[half:])
        partial = dot_trans(after(low, qkv_sums), joined_weight).astype(BF16)
        tokens_gradient, gains, qkv_gradient, output_gradient, up_gradient = end(
            partial, inputs, gain_one, middle_grad, two_term, query_term, key_term, up_keep, up_come,
            qkv_core, qkv_sums, out_sums, sizes
        )
        tokens_gradient = tokens_gradient.astype(F32)
        gains = over_groups(gains[0], F32)
        qkv_gradient = over_groups(qkv_gradient, BF16)
        down_gradient, gate_gradient, up_gradient, output_gradient = (
            over_groups(v, BF16) for v in (down_gradient, gate_gradient, up_gradient, output_gradient)
        )
        block = qkv_gradient.shape[1] // 2
        query_cols, key_cols = heads // 2 * size, pairs // 2 * size
        take = lambda at, count: join([qkv_gradient[:, at + i * block : at + i * block + count] for i in range(2)], 1)
        query_gradient = take(0, query_cols)
        key_gradient = take(query_cols, key_cols)
        value_gradient = take(query_cols + key_cols, key_cols)
        head_gate_gradient = take(query_cols + 2 * key_cols, heads // 2)
        return (
            layer_output,
            tokens_gradient,
            gains[:width],
            query_gradient,
            key_gradient,
            value_gradient,
            head_gate_gradient,
            gains[2 * width : 2 * width + size],
            gains[2 * width + size :],
            output_gradient,
            gains[width : 2 * width],
            gate_gradient,
            up_gradient,
            down_gradient,
        )

    return on_device


def solution(mesh):
    rows, up, down = P(("dp", "wide"), "narrow"), P("narrow", "wide"), P("wide", "narrow")
    return jax.shard_map(
        make(dict(mesh.shape)),
        mesh=mesh,
        in_specs=(rows, P("dp", None), P(), up, up, up, up, P(), P(), down, P(), up, up, down, rows),
        out_specs=(rows, rows, P(), up, up, up, up, P(), P(), down, P(), up, up, down),
        check_vma=False,
    )
```

```python
import functools
import math

import jax
import jax.numpy as jnp
from jax import lax
from jax.experimental import pallas as pl
from jax.experimental.pallas import tpu as pltpu
from jax.sharding import PartitionSpec as P

PROMPT = 2048
EPS = 1e-06
THETA = 1000000.0
RELATIVE = (0, 2, 1, 3)
BF16 = jnp.bfloat16
F32 = jnp.float32
VMEM_LIMIT = 56 * 1024 * 1024
LANES = 128


def dot_rows(left, right):
    return jnp.dot(left, right, preferred_element_type=F32)


def dot_trans(left, right):
    return lax.dot_general(left, right, (((1,), (1,)), ((), ())), preferred_element_type=F32)


def dot_inner(left, right):
    return lax.dot_general(left, right, (((0,), (0,)), ((), ())), preferred_element_type=F32)


def exchange(values, axis, distance, size):
    return lax.ppermute(values, axis, [(i, i ^ distance) for i in range(size)])


def join(parts, axis=0):
    return jnp.concatenate(parts, axis=axis)


def cut(values, at, length, axis):
    return lax.dynamic_slice_in_dim(values, at, length, axis=axis)


def turn_pairs(values):
    step = values.shape[1] // 4
    return join([values[:, i * step : (i + 1) * step] for i in (1, 0, 3, 2)], 1)


def after(values, *others):
    return lax.optimization_barrier((values,) + others)[0]


def columns(heads, pairs, size):
    query, pair = heads // 2, pairs // 2
    block = (query + 2 * pair) * size + LANES
    of = lambda i, count, before: (i // count) * block + (before + i % count) * size
    return (
        [of(h, query, 0) for h in range(heads)],
        [of(p, pair, query) for p in range(pairs)],
        [of(p, pair, query + pair) for p in range(pairs)],
        [block - LANES, 2 * block - LANES],
    )


def post_kernel(raw_ref, cos_ref, sin_ref, query_gain_ref, key_gain_ref, q_ref, kv_ref, *, heads, pairs, size, factor):
    cosine = cos_ref[...]
    sine = sin_ref[...]
    query_at, key_at, value_at, _ = columns(heads, pairs, size)

    def turned(value, gain):
        inverse = lax.rsqrt(jnp.mean(value * value, axis=-1, keepdims=True) + EPS)
        normal = value * inverse * gain
        return normal * cosine + pltpu.roll(normal, size // 2, 1) * sine

    for h, at in enumerate(query_at):
        value = raw_ref[:, at : at + size]
        q_ref[:, h * size : (h + 1) * size] = (turned(value, query_gain_ref[...]) * factor).astype(BF16)
    for p, at in enumerate(key_at):
        kv_ref[:, p * size : (p + 1) * size] = turned(raw_ref[:, at : at + size], key_gain_ref[...]).astype(BF16)
    for p, at in enumerate(value_at):
        to = (pairs + p) * size
        kv_ref[:, to : to + size] = raw_ref[:, at : at + size].astype(BF16)


def post(raw, cosine, sine, query_gain, key_gain, heads, pairs, size, factor):
    rows, width = raw.shape
    step = 256
    return pl.pallas_call(
        functools.partial(post_kernel, heads=heads, pairs=pairs, size=size, factor=factor),
        grid=(rows // step,),
        in_specs=[
            pl.BlockSpec((step, width), lambda i: (i, 0)),
            pl.BlockSpec((step, size), lambda i: (i, 0)),
            pl.BlockSpec((step, size), lambda i: (i, 0)),
            pl.BlockSpec((1, size), lambda i: (0, 0)),
            pl.BlockSpec((1, size), lambda i: (0, 0)),
        ],
        out_specs=[
            pl.BlockSpec((step, heads * size), lambda i: (i, 0)),
            pl.BlockSpec((step, 2 * pairs * size), lambda i: (i, 0)),
        ],
        out_shape=[
            jax.ShapeDtypeStruct((rows, heads * size), BF16),
            jax.ShapeDtypeStruct((rows, 2 * pairs * size), BF16),
        ],
        cost_estimate=pl.CostEstimate(flops=rows * width * 20, bytes_accessed=rows * width * 8, transcendentals=0),
        name="post",
    )(raw, cosine, sine, query_gain[None], key_gain[None])


def back_kernel(
    dq_ref, dkv_ref, raw_ref, cos_ref, sin_ref, query_gain_ref, key_gain_ref, logit_ref, out_ref, gq_ref, gk_ref, *, heads, pairs, size, factor_q, factor_k
):
    cosine = cos_ref[...]
    sine = sin_ref[...]
    query_at, key_at, value_at, logit_at = columns(heads, pairs, size)

    @pl.when(pl.program_id(0) == 0)
    def _():
        gq_ref[...] = jnp.zeros_like(gq_ref)
        gk_ref[...] = jnp.zeros_like(gk_ref)

    def back(up, value, gain, total_ref):
        up = up * cosine - pltpu.roll(up, size // 2, 1) * sine
        inverse = lax.rsqrt(jnp.mean(value * value, axis=-1, keepdims=True) + EPS)
        hat = value * inverse
        total_ref[...] += jnp.sum(up * hat, axis=0, keepdims=True)
        scaled = up * gain
        return inverse * (scaled - hat * jnp.mean(scaled * hat, axis=-1, keepdims=True))

    for h, at in enumerate(query_at):
        up = dq_ref[:, h * size : (h + 1) * size] * factor_q
        out_ref[:, at : at + size] = back(up, raw_ref[:, at : at + size], query_gain_ref[...], gq_ref).astype(BF16)
    for p, at in enumerate(key_at):
        up = dkv_ref[:, p * size : (p + 1) * size].astype(F32) * factor_k
        out_ref[:, at : at + size] = back(up, raw_ref[:, at : at + size], key_gain_ref[...], gk_ref).astype(BF16)
    for p, at in enumerate(value_at):
        to = (pairs + p) * size
        out_ref[:, at : at + size] = dkv_ref[:, to : to + size].astype(BF16)
    for i, at in enumerate(logit_at):
        out_ref[:, at : at + LANES] = logit_ref[:, i * LANES : (i + 1) * LANES].astype(BF16)


def project_back(dq, dkv, raw, cosine, sine, query_gain, key_gain, logit_grad, heads, pairs, size, factor_q, factor_k):
    rows, width = raw.shape
    step = 256
    row = lambda cols: pl.BlockSpec((step, cols), lambda i: (i, 0))
    one = pl.BlockSpec((1, size), lambda i: (0, 0))
    return pl.pallas_call(
        functools.partial(back_kernel, heads=heads, pairs=pairs, size=size, factor_q=factor_q, factor_k=factor_k),
        grid=(rows // step,),
        in_specs=[row(heads * size), row(2 * pairs * size), row(width), row(size), row(size), one, one, row(2 * LANES)],
        out_specs=[row(width), one, one],
        out_shape=[
            jax.ShapeDtypeStruct((rows, width), BF16),
            jax.ShapeDtypeStruct((1, size), F32),
            jax.ShapeDtypeStruct((1, size), F32),
        ],
        cost_estimate=pl.CostEstimate(flops=rows * width * 30, bytes_accessed=rows * width * 12, transcendentals=0),
        name="project_back",
    )(dq, dkv, raw, cosine, sine, query_gain[None], key_gain[None], logit_grad)


def places(table_ref, stripe, step, length):
    turn = table_ref[stripe, 3]
    core = table_ref[stripe, 4]
    half = length // 2
    blocks = half // step

    def pair(i):
        at = jnp.bitwise_xor(i, turn) * step
        return pl.ds(pl.multiple_of(at, step), step), pl.ds(pl.multiple_of(at + half // 2, step), step)

    def single(b):
        part = b // blocks
        inner = b - part * blocks
        at = part * half + jnp.bitwise_xor(inner % 2, core) * (half // 2) + jnp.bitwise_xor(inner // 2, turn) * step
        return (pl.ds(pl.multiple_of(at, step), step),)

    return pair, single


def logit_of(head, heads, own_ref, other_ref):
    half = heads // 2
    at = head % half
    return (own_ref if head < half else other_ref)[:, at : at + 1]


def logit_specs(raw, heads, pairs, size, step):
    spec = lambda i: pl.BlockSpec((step, LANES), lambda s, t: (s, i))
    return [spec(at // LANES) for at in columns(heads, pairs, size)[3]]


def forward_kernel(table_ref, q_ref, kv_ref, row_ref, start_ref, own_ref, other_ref, gated_ref, context_ref, inverse_ref, *, pairs, repeat, size, step):
    stripe = pl.program_id(0)
    wide_blocks = table_ref[stripe, 0]
    low = table_ref[stripe, 1]
    high = table_ref[stripe, 2]
    pair, single = places(table_ref, stripe, step, kv_ref.shape[0])
    rows = row_ref[...]
    starts = start_ref[...]
    rows = jnp.concatenate([rows] * repeat, axis=0)
    starts = jnp.concatenate([starts] * repeat, axis=0)
    queries = [
        jnp.concatenate([q_ref[:, h * size : (h + 1) * size] for h in range(k * repeat, (k + 1) * repeat)], axis=0)
        for k in range(pairs)
    ]

    def seen(totals, where, first):
        outs = []
        for k in range(pairs):
            keys = join([kv_ref[at, k * size : (k + 1) * size] for at in where])
            weights = jnp.exp2(dot_trans(queries[k], keys))
            if first is not None:
                index = first + lax.broadcasted_iota(jnp.int32, weights.shape, 1)
                weights = jnp.where((index <= rows) & (index >= starts), weights, 0.0)
            values = join([kv_ref[at, (pairs + k) * size : (pairs + k + 1) * size] for at in where])
            values = jnp.concatenate([values, jnp.ones_like(values)], axis=1)
            outs.append(totals[k] + dot_rows(weights.astype(BF16), values))
        return tuple(outs)

    totals = tuple(jnp.zeros((query.shape[0], 2 * size), F32) for query in queries)
    totals = lax.fori_loop(0, wide_blocks, lambda i, t: seen(t, pair(i), None), totals)
    totals = lax.fori_loop(low, high + 1, lambda i, t: seen(t, single(i), i * step), totals)
    for k, total in enumerate(totals):
        inverse = 1.0 / total[:, size:]
        context = total[:, :size] * inverse
        for r in range(repeat):
            h = k * repeat + r
            part = context[r * step : (r + 1) * step]
            cols = slice(h * size, (h + 1) * size)
            gate = jax.nn.sigmoid(logit_of(h, pairs * repeat, own_ref, other_ref))
            gated_ref[:, cols] = (part * gate).astype(BF16)
            context_ref[:, cols] = part
            inverse_ref[:, cols] = inverse[r * step : (r + 1) * step]


def attend(table, q, kv, rows, starts, raw, pairs, size):
    length, cols = q.shape
    heads = cols // size
    step = length // table.shape[0]
    block = lambda width: pl.BlockSpec((step, width), lambda i, t: (i, 0))
    return pl.pallas_call(
        functools.partial(forward_kernel, pairs=pairs, repeat=heads // pairs, size=size, step=step),
        grid_spec=pltpu.PrefetchScalarGridSpec(
            num_scalar_prefetch=1,
            grid=(length // step,),
            in_specs=[
                block(cols),
                pl.BlockSpec(kv.shape, lambda i, t: (0, 0), pipeline_mode=pl.Buffered(1)),
                block(1),
                block(1),
                *logit_specs(raw, heads, pairs, size, step),
            ],
            out_specs=[block(cols), block(cols), block(cols)],
        ),
        out_shape=[
            jax.ShapeDtypeStruct((length, cols), BF16),
            jax.ShapeDtypeStruct((length, cols), F32),
            jax.ShapeDtypeStruct((length, cols), F32),
        ],
        compiler_params=pltpu.CompilerParams(vmem_limit_bytes=VMEM_LIMIT),
        cost_estimate=pl.CostEstimate(flops=20 * 10**9, bytes_accessed=12 * 10**6, transcendentals=7 * 10**6),
        name="attend",
    )(table, q, kv, rows, starts, raw, raw)


def backward_kernel(
    table_ref, q_ref, kv_ref, row_ref, start_ref, own_ref, other_ref, context_ref, inverse_ref, grad_ref,
    dq_ref, dkv_ref, dlogit_ref, sums_ref, *, pairs, repeat, size, step,
):
    stripe = pl.program_id(0)
    wide_blocks = table_ref[stripe, 0]
    low = table_ref[stripe, 1]
    high = table_ref[stripe, 2]
    pair, single = places(table_ref, stripe, step, kv_ref.shape[0])

    @pl.when(stripe == 0)
    def _():
        sums_ref[...] = jnp.zeros_like(sums_ref)

    dlogit_ref[...] = jnp.zeros_like(dlogit_ref)
    rows = jnp.concatenate([row_ref[0]] * repeat, axis=1)
    starts = jnp.concatenate([start_ref[0]] * repeat, axis=1)
    queries, all_grads, all_inners = [], [], []
    for k in range(pairs):
        heads = [k * repeat + r for r in range(repeat)]
        queries.append(jnp.concatenate([q_ref[:, h * size : (h + 1) * size] for h in heads], axis=0))
        grads, inners = [], []
        for h in heads:
            cols = slice(h * size, (h + 1) * size)
            up = grad_ref[:, cols]
            gate = jax.nn.sigmoid(logit_of(h, pairs * repeat, own_ref, other_ref))
            product = jnp.sum(up * context_ref[:, cols], axis=1, keepdims=True)
            half = pairs * repeat // 2
            at = h // half * LANES + h % half
            dlogit_ref[:, at : at + 1] = product * gate * (1.0 - gate)
            inverse = inverse_ref[:, cols]
            grads.append((up * gate * inverse).astype(BF16))
            inners.append(product * gate * inverse)
        all_grads.append(jnp.concatenate(grads, axis=0))
        all_inners.append(jnp.transpose(jnp.concatenate(inners, axis=0))[0:1])

    def seen(totals, where, first):
        outs = []
        for k in range(pairs):
            key_cols = slice(k * size, (k + 1) * size)
            value_cols = slice((pairs + k) * size, (pairs + k + 1) * size)
            keys = join([kv_ref[at, key_cols] for at in where])
            weights = jnp.exp2(dot_trans(keys, queries[k]))
            if first is not None:
                index = first + lax.broadcasted_iota(jnp.int32, weights.shape, 0)
                weights = jnp.where((index <= rows) & (index >= starts), weights, 0.0)
            changes = dot_trans(join([kv_ref[at, value_cols] for at in where]), all_grads[k])
            changes = (weights * (changes - all_inners[k])).astype(BF16)
            value_sums = dot_rows(weights.astype(BF16), all_grads[k])
            key_sums = dot_rows(changes, queries[k])
            for i, at in enumerate(where):
                sums_ref[at, value_cols] += value_sums[i * step : (i + 1) * step]
                sums_ref[at, key_cols] += key_sums[i * step : (i + 1) * step]
            outs.append(totals[k] + dot_inner(changes, keys))
        return tuple(outs)

    totals = tuple(jnp.zeros((query.shape[0], size), F32) for query in queries)
    totals = lax.fori_loop(0, wide_blocks, lambda i, t: seen(t, pair(i), None), totals)
    totals = lax.fori_loop(low, high + 1, lambda i, t: seen(t, single(i), i * step), totals)
    for k, total in enumerate(totals):
        for r in range(repeat):
            h = k * repeat + r
            dq_ref[:, h * size : (h + 1) * size] = total[r * step : (r + 1) * step]

    @pl.when(stripe == pl.num_programs(0) - 1)
    def _():
        dkv_ref[...] = sums_ref[...].astype(BF16)


def attend_back(table, q, kv, rows, starts, raw, context, inverse, grad, pairs, size):
    length, cols = q.shape
    heads = cols // size
    step = length // table.shape[0]
    block = lambda width: pl.BlockSpec((step, width), lambda i, t: (i, 0))
    whole = pl.BlockSpec(kv.shape, lambda i, t: (0, 0), pipeline_mode=pl.Buffered(1))
    lane = pl.BlockSpec((1, 1, step), lambda i, t: (i, 0, 0))
    logits = logit_specs(raw, heads, pairs, size, step)
    return pl.pallas_call(
        functools.partial(backward_kernel, pairs=pairs, repeat=heads // pairs, size=size, step=step),
        grid_spec=pltpu.PrefetchScalarGridSpec(
            num_scalar_prefetch=1,
            grid=(length // step,),
            in_specs=[block(cols), whole, lane, lane, *logits, block(cols), block(cols), block(cols)],
            out_specs=[block(cols), whole, block(2 * LANES)],
            scratch_shapes=[pltpu.VMEM(kv.shape, F32)],
        ),
        out_shape=[
            jax.ShapeDtypeStruct((length, cols), F32),
            jax.ShapeDtypeStruct(kv.shape, BF16),
            jax.ShapeDtypeStruct((length, 2 * LANES), F32),
        ],
        compiler_params=pltpu.CompilerParams(vmem_limit_bytes=VMEM_LIMIT),
        cost_estimate=pl.CostEstimate(flops=50 * 10**9, bytes_accessed=20 * 10**6, transcendentals=7 * 10**6),
        name="attend_back",
    )(table, q, kv, rows.reshape(-1, 1, step), starts.reshape(-1, 1, step), raw, raw, context, inverse, grad)


class Wires:
    def __init__(self, send_sems, recv_sems, local_sems, sizes):
        self.send_sems, self.recv_sems, self.local_sems = send_sems, recv_sems, local_sems
        self.sizes = sizes
        self.sent, self.local, self.open = [], [], []
        self.locals_used, self.sends_used = 0, 0
        self.dp, self.wide, self.narrow = (lax.axis_index(a) for a in ("dp", "wide", "narrow"))
        self.y, self.core = self.narrow // 2, self.narrow % 2
        self.x, self.far = self.dp % 2, self.wide // 2

    def peer(self, *to):
        if isinstance(to[0], tuple):
            return {axis: at for part in to for axis, at in self.peer(*part).items()}
        axis, distance = to
        at = {"dp": self.dp, "wide": self.wide, "narrow": self.narrow}[axis]
        bit = at // distance % 2
        return {axis: at + distance * (1 - 2 * bit) if distance < 3 else 3 - at}

    def greet(self, peers):
        barrier = pltpu.get_barrier_semaphore()
        for to in peers:
            pl.semaphore_signal(barrier, inc=1, device_id=self.peer(*to), device_id_type=pl.DeviceIdType.MESH)
        pl.semaphore_wait(barrier, len(peers))

    def make(self, source, target, to):
        i = self.sends_used
        self.sends_used += 1
        copy = pltpu.make_async_remote_copy(
            src_ref=source, dst_ref=target, send_sem=self.send_sems.at[i], recv_sem=self.recv_sems.at[i],
            device_id=self.peer(*to), device_id_type=pl.DeviceIdType.MESH,
        )
        self.sent.append(copy)
        return copy

    def send(self, source, target, to):
        copy = self.make(source, target, to)
        copy.start()
        self.open.append(copy)
        return copy

    def arrived(self, copy):
        copy.wait_recv()
        self.open = [other for other in self.open if other is not copy]

    def copy(self, source, target):
        copy = pltpu.make_async_copy(source, target, self.local_sems.at[self.locals_used])
        self.locals_used += 1
        copy.start()
        self.local.append(copy)
        return copy

    def finish(self):
        for copy in list(self.open):
            self.arrived(copy)
        for copy in self.sent:
            copy.wait_send()
        for copy in self.local:
            copy.wait()


Y, CORE, CORNER, NEAR, FAR, X = ("narrow", 2), ("narrow", 1), ("narrow", 3), ("wide", 1), ("wide", 2), ("dp", 1)


def local_flow(net, values_ref, rows_ref):
    rows, width = rows_ref.shape[0], values_ref.shape[1]
    half = width // 2
    out = []
    for distance, to in ((0, None), (1, CORE), (2, Y), (3, CORNER)):
        target = net.narrow if to is None else net.peer(*to)["narrow"]
        at = (2 * (distance % 2) + net.y) * width
        for j in range(2):
            sub = net.x if j == 0 else 1 - net.x
            source = values_ref.at[pl.ds(pl.multiple_of(target * rows, rows), rows), pl.ds(pl.multiple_of(sub * half, half), half)]
            goal = rows_ref.at[:, pl.ds(pl.multiple_of(at + j * half, half), half)]
            out.append(net.copy(source, goal) if to is None else net.send(source, goal, to))
    return out


def gather_flow(net, values_ref, all_ref):
    rows = values_ref.shape[0]
    half = rows // 2
    part = lambda i: all_ref.at[pl.ds(i * half, half), :]
    first, second = values_ref.at[pl.ds(0, half), :], values_ref.at[pl.ds(half, half), :]
    first_y = net.send(first, part(2), Y)
    second_z = net.send(second, part(5), NEAR)
    net.send(first, part(4), NEAR)
    net.send(second, part(3), Y)
    net.copy(values_ref, all_ref.at[pl.ds(0, rows), :])
    yield
    net.arrived(first_y)
    net.send(part(2), part(6), NEAR)
    yield
    net.arrived(second_z)
    net.send(part(5), part(7), Y)
    yield


def weight_flow(net, source_ref, out_ref, axis, own, other, across, from_y=None, from_far=None, from_both=None, their_y=None, their_far=None):
    step = source_ref.shape[axis] // 2
    count = source_ref.shape[axis]

    def window(ref, at, start):
        long, wide = pl.ds(pl.multiple_of(at, step), step), pl.ds(start, across)
        return ref.at[long, wide] if axis == 0 else ref.at[wide, long]

    y, x = net.y, net.x
    piece = lambda sub, half: window(source_ref, sub * step, pl.multiple_of(half * across, across))
    place = lambda slot, j, start: window(out_ref, slot * count + j * step, start)
    mine, rest = piece(x, y), piece(1 - x, y)
    net.copy(mine, place(y, 0, own))
    net.copy(rest, place(y, 1, own))
    if from_y is None:
        come_y = net.send(piece(x, 1 - y), place(y, 0, own), Y)
    else:
        net.copy(from_y, place(1 - y, 0, own))
    if from_far is None:
        come_far = net.send(mine, place(y, 0, other), FAR)
    else:
        net.copy(from_far, place(y, 0, other))
    net.send(mine, place(2 + y, 0, own), CORE)
    net.send(rest, place(2 + y, 1, own), CORE)
    if from_y is None:
        yield
        net.arrived(come_y)
        from_y = place(1 - y, 0, own)
    if from_both is None:
        come_both = net.send(from_y, place(1 - y, 0, other), FAR)
    else:
        net.copy(from_both, place(1 - y, 0, other))
    given = their_y is not None
    if given:
        for ref, slot, start in ((their_y, 1 - y, own), (their_far, y, other)):
            net.copy(ref, place(slot, 1, start))
            net.send(ref, place(slot + 2, 1, start), CORE)
    else:
        their_y = net.send(from_y, place(1 - y, 1, own), X)
    net.send(from_y, place(3 - y, 0, own), CORE)
    if from_far is None:
        yield
        net.arrived(come_far)
        from_far = place(y, 0, other)
    if not given:
        their_far = net.send(from_far, place(y, 1, other), X)
    net.send(from_far, place(2 + y, 0, other), CORE)
    if from_both is None:
        yield
        net.arrived(come_both)
        from_both = place(1 - y, 0, other)
    their_both = net.send(from_both, place(1 - y, 1, other), X)
    net.send(from_both, place(3 - y, 0, other), CORE)
    yield
    waiting = ((their_y, 1 - y, own), (their_far, y, other), (their_both, 1 - y, other))
    for copy, slot, start in waiting[2 * given :]:
        net.arrived(copy)
        net.send(place(slot, 1, start), place(slot + 2, 1, start), CORE)
    yield


def run(flow):
    return next(flow, None)


def by_rows(count, body):
    step = 16
    lax.fori_loop(0, count // step, lambda i, _: (body(pl.ds(pl.multiple_of(i * step, step), step)), 0)[1], 0)


def begin_kernel(
    tokens_ref, cotangent_ref, gain_ref, query_ref, key_ref, value_ref, gates_ref, out_ref,
    x_ref, rows_ref, all_ref, joined_ref, output_ref, here, normed, there, qkv_ref, send, recv, local, *, sizes,
):
    net = Wires(send, recv, local, sizes)
    net.greet([Y, CORE, CORNER, NEAR, FAR, X])
    rows = local_flow(net, tokens_ref, here)
    across = qkv_ref.shape[1] // 2
    packed, at = [], 0
    for ref in (query_ref, key_ref, value_ref, gates_ref):
        wide = ref.shape[1] // 2
        for i in range(2):
            packed.append(net.copy(ref.at[:, pl.ds(i * wide, wide)], qkv_ref.at[:, pl.ds(i * across + at, wide)]))
        at += wide
    for copy in packed:
        copy.wait()
    net.local = [copy for copy in net.local if all(copy is not other for other in packed)]
    joined = weight_flow(net, qkv_ref, joined_ref, 0, 0, across, across)
    run(joined)
    rows[0].wait()
    rows[1].wait()
    net.local = net.local[2:]
    for copy in rows[2:]:
        net.arrived(copy)

    def norm(at):
        values = here[at, :].astype(F32)
        inverse = lax.rsqrt(jnp.mean(values * values, axis=1, keepdims=True) + EPS)
        normed[at, :] = (values * inverse * gain_ref[...]).astype(BF16)
        x_ref[at, :] = here[at, :]

    by_rows(here.shape[0], norm)
    gather = gather_flow(net, normed, all_ref)
    run(gather)
    across = out_ref.shape[0] // 2
    output = weight_flow(net, out_ref, output_ref, 1, 0, across, across)
    for flow in (joined, gather, output, joined, gather):
        run(flow)
    rows = local_flow(net, cotangent_ref, there)
    for flow in (joined, output, joined, output, output, output):
        run(flow)
    for copy in rows[:2]:
        copy.wait()
    net.local = [copy for copy in net.local if all(copy is not other for other in rows[:2])]
    for copy in rows[2:]:
        net.arrived(copy)
    net.copy(there, rows_ref)
    net.finish()


ANY = pl.BlockSpec(memory_space=pl.ANY)
VMEM = pl.BlockSpec(memory_space=pltpu.VMEM)


def sems(sends, locals_):
    return [pltpu.SemaphoreType.DMA((sends,)), pltpu.SemaphoreType.DMA((sends,)), pltpu.SemaphoreType.DMA((locals_,))]


def wire_call(kernel, name, number, specs, out_specs, shapes, scratch, sizes, cost, *args):
    return pl.pallas_call(
        functools.partial(kernel, sizes=sizes),
        in_specs=specs,
        out_specs=out_specs,
        out_shape=[jax.ShapeDtypeStruct(*shape) for shape in shapes],
        scratch_shapes=scratch,
        compiler_params=pltpu.CompilerParams(collective_id=number, has_side_effects=True, vmem_limit_bytes=VMEM_LIMIT),
        cost_estimate=pl.CostEstimate(flops=0, bytes_accessed=cost * 3 * 10**6, transcendentals=0),
        name=name,
    )(*args)


def begin(tokens, cotangent, gain, weights, out, sizes):
    rows, width = tokens.shape[0] // sizes["narrow"], gain.shape[0]
    wide = sum(w.shape[1] for w in weights)
    row = pltpu.VMEM((rows, width), BF16)
    return wire_call(
        begin_kernel, "begin", 1, [ANY, ANY, VMEM] + [ANY] * 4 + [VMEM], [VMEM, ANY, ANY, ANY, ANY],
        [
            ((rows, width), BF16), ((rows, width), BF16), ((4 * rows, width), BF16), ((width, wide), BF16),
            ((out.shape[0], width), BF16),
        ],
        [row, row, row, pltpu.VMEM((weights[0].shape[0], wide), BF16), *sems(48, 24)],
        sizes, 55, tokens, cotangent, gain[None], *weights, out,
    )


def keys_kernel(kv_ref, keys_ref, done, send, recv, local, *, sizes):
    net = Wires(send, recv, local, sizes)
    across = [FAR, ("wide", 3), (FAR, CORE), (("wide", 3), CORE)]
    net.greet([CORE] + across)
    count, width = kv_ref.shape
    size = width // 4
    part = lambda i, j: keys_ref.at[pl.ds(i, count), pl.ds(j * size, size)]
    base = pl.multiple_of(net.far * 2 * count, count)
    far = [net.make(kv_ref.at[:, pl.ds(j * size, size)], part(0, j ^ 1), FAR) for j in range(4)]
    on = [net.make(part(0, j ^ 1), part(count, j ^ 1), CORE) for j in range(4)]

    @pl.when(net.far == 0)
    def _():
        for copy in far:
            copy.start()

    net.copy(kv_ref, keys_ref.at[pl.ds(base, count), :])
    net.send(kv_ref, keys_ref.at[pl.ds(base + count, count), :], CORE)

    @pl.when(net.far == 1)
    def _():
        for copy, forward in zip(far, on):
            copy.wait_recv()
            forward.start()
        for to in across:
            pl.semaphore_signal(done, inc=1, device_id=net.peer(*to), device_id_type=pl.DeviceIdType.MESH)
        for forward in on:
            forward.wait()

    @pl.when(net.far == 0)
    def _():
        for copy in far:
            copy.wait_send()
        pl.semaphore_wait(done, len(across))

    net.sent = [copy for copy in net.sent if all(copy is not other for other in far + on)]
    net.finish()


def exchange_keys(kv, sizes):
    return wire_call(
        keys_kernel, "keys", 2, [VMEM], [ANY], [((4 * kv.shape[0], kv.shape[1]), BF16)],
        [pltpu.SemaphoreType.REGULAR, *sems(16, 4)], sizes, 45, kv,
    )[0]


def scatter_flow(net, partial_ref, first_ref, second_ref, send_ref, last_ref, total_ref):
    half = partial_ref.shape[0] // 8
    part = lambda i: partial_ref.at[pl.ds(i * half, half), :]
    slot = lambda ref, i: ref.at[pl.ds(i * half, half), :]
    to_z = [net.send(part(6), slot(first_ref, 1), NEAR), net.send(part(4), slot(first_ref, 0), NEAR)]
    to_y = [net.send(part(7), slot(second_ref, 1), Y), net.send(part(3), slot(second_ref, 0), Y)]
    yield

    def add(out_ref, to, i, ref, j):
        def body(at):
            move = lambda start: pl.ds(pl.multiple_of(at.start + start, 16), at.size)
            value = partial_ref[move(i * half), :].astype(F32) + ref[move(j * half), :].astype(F32)
            out_ref[move(to), :] = value.astype(out_ref.dtype)

        by_rows(half, body)

    net.arrived(to_z[0])
    add(send_ref, 0, 2, first_ref, 1)
    last_y = net.send(slot(send_ref, 0), slot(last_ref, 0), Y)
    net.arrived(to_y[0])
    add(send_ref, half, 5, second_ref, 1)
    last_z = net.send(slot(send_ref, 1), slot(last_ref, 1), NEAR)
    yield
    net.arrived(to_z[1])
    add(total_ref, 0, 0, first_ref, 0)
    net.arrived(to_y[1])
    add(total_ref, half, 1, second_ref, 0)
    yield
    net.arrived(last_y)
    net.arrived(last_z)
    yield


def middle_kernel(
    partial_ref, x_ref, gain_ref, gate_ref, up_ref, down_ref, gate_y_ref, up_y_ref, down_y_ref, gate_far_ref, up_far_ref, down_far_ref,
    gate_both_ref, up_both_ref, down_both_ref, middle_ref, all_ref, both_ref, last_ref,
    first, second, sums, last, total, normed, send, recv, local, *, sizes,
):
    net = Wires(send, recv, local, sizes)
    net.greet([Y, CORE, NEAR, FAR, X])
    scatter = scatter_flow(net, partial_ref, first, second, sums, last, total)
    run(scatter)
    across = gate_ref.shape[1] // 2
    flows = [
        weight_flow(net, gate_ref, both_ref, 0, 0, across, across, gate_y_ref, gate_far_ref, gate_both_ref),
        weight_flow(net, up_ref, both_ref, 0, 2 * across, 3 * across, across, up_y_ref, up_far_ref, up_both_ref),
        weight_flow(net, down_ref, last_ref, 1, 0, across, across, down_y_ref, down_far_ref, down_both_ref),
    ]
    for flow in flows:
        run(flow)
    run(scatter)
    run(scatter)
    run(scatter)

    def norm(at):
        values = x_ref[at, :].astype(F32) + total[at, :] + last[at, :].astype(F32)
        middle_ref[at, :] = values
        inverse = lax.rsqrt(jnp.mean(values * values, axis=1, keepdims=True) + EPS)
        normed[at, :] = (values * inverse * gain_ref[...]).astype(BF16)

    by_rows(normed.shape[0], norm)
    gather = gather_flow(net, normed, all_ref)
    run(gather)
    run(flows[0])
    run(gather)
    run(gather)
    run(flows[1])
    run(flows[2])
    net.finish()


def to_middle(partial, x, gain, gate, up, down, pieces, sizes):
    rows, width = x.shape
    buffer = lambda n, kind: pltpu.VMEM((n, width), kind)
    return wire_call(
        middle_kernel, "middle", 3, [VMEM] * 15, [VMEM, ANY, ANY, ANY],
        [((rows, width), F32), ((4 * rows, width), BF16), ((width, 2 * gate.shape[1]), BF16), ((down.shape[0], width), BF16)],
        [
            buffer(rows, BF16), buffer(rows, BF16), buffer(rows, BF16), buffer(rows, BF16), buffer(rows, F32), buffer(rows, BF16),
            *sems(64, 32),
        ],
        sizes, 80, partial, x, gain[None], gate, up, down, *pieces,
    )


def spread_flow(net, rows_ref, out_ref):
    rows, width = rows_ref.shape[0], out_ref.shape[1]
    half = width // 2
    base = pl.multiple_of(net.narrow * rows, rows)
    for distance, to in ((3, CORNER), (2, Y), (1, CORE), (0, None)):
        target = net.narrow if to is None else net.peer(*to)["narrow"]
        at = (2 * (distance % 2) + target // 2) * width
        for j in range(2):
            sub = net.x if j == 0 else 1 - net.x
            source = rows_ref.at[:, pl.ds(pl.multiple_of(at + j * half, half), half)]
            goal = out_ref.at[pl.ds(base, rows), pl.ds(pl.multiple_of(sub * half, half), half)]
            if to is None:
                net.copy(source, goal)
            else:
                net.send(source, goal, to)


def add_rows(target, terms):
    ref, (rows, cols) = target

    def body(at):
        move = lambda r: pl.ds(pl.multiple_of(at.start + r.start, 16), at.size)
        value = sum(term[move(r), c].astype(F32) for term, (r, c) in terms)
        ref[move(rows), cols] = value.astype(BF16)

    by_rows(rows.size, body)


class Gradient:
    def __init__(self, net, axis, step, across):
        self.net, self.axis, self.step, self.across = net, axis, step, across
        self.order = (1 - net.y, net.y)
        self.x, self.far = [], []

    def window(self, at, start, count, length=None):
        step = self.step if length is None else length
        hint = lambda v, unit: v if isinstance(v, int) else pl.multiple_of(v, unit)
        along, wide = pl.ds(hint(at, self.step), step), pl.ds(hint(start, self.across), count)
        return (along, wide) if self.axis == 0 else (wide, along)

    def start(self, g_ref, acc, from_core, given=False):
        self.acc, self.from_core = acc, from_core
        count = 4 * self.step
        own, other = (self.window(i * count, 0, 2 * self.across, count) for i in range(2))
        self.loaded = self.net.copy(g_ref.at[own], acc)
        self.core = None if given else self.net.send(g_ref.at[other], from_core, CORE)

    def wait_core(self):
        if self.loaded is not None:
            self.loaded.wait()
            self.net.local = [copy for copy in self.net.local if copy is not self.loaded]
        if self.core is not None:
            self.net.arrived(self.core)

    def core_to_x(self, from_x):
        self.wait_core()
        self.from_x = from_x
        for slot in self.order:
            place = self.window((2 * slot + 1) * self.step, 0, 2 * self.across)
            add_rows((self.acc, place), [(self.acc, place), (self.from_core, place)])
            goal = from_x.at[self.window(slot * self.step, 0, 2 * self.across)]
            self.x.append(self.net.send(self.acc.at[place], goal, X))

    def x_end(self, k, from_far=None):
        slot = self.order[k]
        self.net.arrived(self.x[k])
        for start in (self.across, 0):
            place = self.window(2 * slot * self.step, start, self.across)
            come = self.window(slot * self.step, start, self.across)
            add_rows((self.acc, place), [(self.acc, place), (self.from_core, place), (self.from_x, come)])
            if start and from_far is not None:
                self.from_far = from_far
                goal = from_far.at[self.window(slot * self.step, 0, self.across)]
                self.far.append(self.net.send(self.acc.at[place], goal, FAR))

    def far_end(self, k, result=None):
        slot = self.order[k]
        self.net.arrived(self.far[k])
        place = self.window(2 * slot * self.step, 0, self.across)
        come = self.window(slot * self.step, 0, self.across)
        add_rows((self.acc, place), [(self.acc, place), (self.from_far, come)])

    def to_owner(self, k, source, out):
        net, across = self.net, self.across
        goal = out.at[self.window(net.x * self.step, net.y * across, across)]
        if k == 0:
            self.out = out
            self.y = net.send(source, goal, Y)
        else:
            net.copy(source, goal)
            net.send(source, goal, X)

    def after_y(self):
        net, across = self.net, self.across
        net.arrived(self.y)
        place = self.out.at[self.window(net.x * self.step, (1 - net.y) * across, across)]
        net.send(place, place, X)

    def slot(self, k, stride, start, count):
        return self.window(stride * self.order[k] * self.step, start, count)


def row_back(grad, values, gain):
    inverse = lax.rsqrt(jnp.mean(values * values, axis=1, keepdims=True) + EPS)
    hat = values * inverse
    scaled = grad * gain
    inner = jnp.mean(scaled * hat, axis=1, keepdims=True)
    return jnp.sum(grad * hat, axis=0, keepdims=True), inverse * (scaled - hat * inner)


def turn_kernel(
    partial_ref, middle_ref, upstream_ref, gain_ref, down_ref, inputs_ref, gate_ref, up_ref,
    grad_ref, all_ref, term_ref, down_out, gate_out, up_keep, up_send,
    first, second, sums, last, total, low, *rest, sizes,
):
    buffers, (rows_two, gate_grads, up_grads, gate_other, up_other), (send, recv, local) = rest[:-8], rest[-8:-3], rest[-3:]
    net = Wires(send, recv, local, sizes)
    net.greet([Y, CORE, NEAR, FAR, X])
    scatter = scatter_flow(net, partial_ref, first, second, sums, last, total)
    run(scatter)
    step, across = low.shape[1] // sizes["narrow"] // 2, gate_ref.shape[1] // 2
    down, gate, up = (Gradient(net, axis, step, across) for axis in (1, 0, 0))
    down.start(down_ref, *buffers[0:2])
    gate.acc, gate.from_core = buffers[3:5]
    up.acc, up.from_core = buffers[6:8]
    loads = [net.copy(inputs_ref, rows_two), net.copy(gate_ref, gate_grads), net.copy(up_ref, up_grads)]
    for copy in loads:
        copy.wait()
    net.local = [copy for copy in net.local if all(copy is not other for other in loads)]
    half = rows_two.shape[1] // 2

    def dots(base, grads, target):
        def body(i, _):
            at = pl.multiple_of(i * step, step)
            part = dot_inner(rows_two[:, pl.ds(pl.multiple_of(base + at, step), step)], grads[...])
            target[pl.ds(at, step), :] = part.astype(BF16)
            return 0

        lax.fori_loop(0, half // step, body, 0)

    dots(half, gate_grads, gate_other)
    gate.loaded, gate.core = None, net.send(gate_other, gate.from_core, CORE)
    down.core_to_x(buffers[2])
    dots(0, gate_grads, gate.acc)
    gate.core_to_x(buffers[5])
    run(scatter)
    run(scatter)
    run(scatter)
    term_ref[...] = jnp.zeros_like(term_ref)

    def rows(at):
        grad = total[at, :] + last[at, :].astype(F32)
        term, change = row_back(grad, middle_ref[at, :], gain_ref[...])
        term_ref[...] += term
        value = upstream_ref[at, :].astype(F32) + change
        grad_ref[at, :] = value
        low[at, :] = value.astype(BF16)

    by_rows(low.shape[0], rows)
    gather = gather_flow(net, low, all_ref)
    run(gather)
    dots(half, up_grads, up_other)
    up.loaded, up.core = None, net.send(up_other, up.from_core, CORE)
    for k in range(2):
        down.x_end(k)
        net.copy(down.acc.at[down.slot(k, 2, 0, 2 * across)], down_out.at[down.slot(k, 1, 0, 2 * across)])
    run(gather)
    run(gather)
    dots(0, up_grads, up.acc)
    up.wait_core()
    for slot in range(2):
        for j, ref in ((1, up_send), (0, up_keep)):
            place = up.window((2 * slot + j) * step, 0, 2 * across)
            add_rows((up.acc, place), [(up.acc, place), (up.from_core, place)])
            net.copy(up.acc.at[place], ref.at[up.window(slot * step, 0, 2 * across)])
    for k in range(2):
        gate.x_end(k)
        net.copy(gate.acc.at[gate.slot(k, 2, 0, 2 * across)], gate_out.at[gate.slot(k, 1, 0, 2 * across)])
    net.finish()


def gradient_buffers(size, across, axis, count=4):
    shape = lambda a, b: pltpu.VMEM((a, b) if axis == 0 else (b, a), BF16)
    every = [shape(2 * size, 2 * across), shape(2 * size, 2 * across), shape(size, 2 * across), shape(size, across)]
    return every[:count]


def scatter_buffers(rows, width):
    buffer = lambda kind: pltpu.VMEM((rows, width), kind)
    return [buffer(BF16), buffer(BF16), buffer(BF16), buffer(BF16), buffer(F32)]


def turn(partial, middle, upstream, gain, down, inputs, gate, up, sizes):
    rows, width = middle.shape
    size, across = width // sizes["narrow"], down.shape[0] // 2
    return wire_call(
        turn_kernel, "turn", 4, [VMEM] * 4 + [ANY] * 4, [VMEM, ANY, VMEM, ANY, ANY, ANY, ANY],
        [
            ((rows, width), F32), ((4 * rows, width), BF16), ((1, width), F32),
            ((2 * across, size), BF16), ((size, 2 * across), BF16), ((size, 2 * across), BF16), ((size, 2 * across), BF16),
        ],
        [
            *scatter_buffers(rows, width), pltpu.VMEM((rows, width), BF16),
            *gradient_buffers(size, across, 1, 3), *gradient_buffers(size, across, 0, 3), *gradient_buffers(size, across, 0, 2),
            pltpu.VMEM(inputs.shape, BF16), *(pltpu.VMEM((n, 2 * across), BF16) for n in (gate.shape[0],) * 2 + (2 * size,) * 2),
            *sems(40, 24),
        ],
        sizes, 80, partial, middle, upstream, gain[None], down, inputs, gate, up,
    )


def owner_kernel(
    dkv_ref, partial_ref, middle_ref, down_ref, down_far_ref, gate_ref, gate_far_ref,
    mine_ref, layer_ref, down_out, gate_out,
    prompt_core, rest_core, prompt, prompt_far, first, second, sums, last, total, rows_low, down_sums, gate_sums,
    send, recv, local, *, sizes,
):
    net = Wires(send, recv, local, sizes)
    net.greet([Y, CORE, CORNER, NEAR, FAR, X])
    count, width = prompt.shape
    size = width // 4
    region = lambda i: dkv_ref.at[pl.ds(i * count, count), :]
    come = net.send(region(1), prompt_core, CORE)
    rest = net.send(region(3), rest_core, CORE)
    scatter = scatter_flow(net, partial_ref, first, second, sums, last, total)
    run(scatter)
    step, across = down_far_ref.shape[1] // 2, down_far_ref.shape[0]
    down, gate = (Gradient(net, axis, step, across) for axis in (1, 0))
    net.arrived(come)

    def add(at):
        prompt[at, :] = (dkv_ref[at, :].astype(F32) + prompt_core[at, :].astype(F32)).astype(BF16)

    by_rows(count, add)
    cols = lambda ref, j: ref.at[:, pl.ds(j * size, size)]
    far = [net.make(cols(prompt, j), cols(prompt_far, j ^ 1), FAR) for j in range(4)]

    @pl.when(net.far == 1)
    def _():
        for copy in far:
            copy.start()

    parts = ((down, down_sums, down_ref, down_far_ref, down_out), (gate, gate_sums, gate_ref, gate_far_ref, gate_out))
    for flow, total_ref, ref, far_ref, goal in parts:
        for k in range(2):
            place = flow.slot(k, 1, 0, across)
            add_rows((total_ref, place), [(ref, place), (far_ref, place)])
            flow.to_owner(k, total_ref.at[place], goal)
    run(scatter)
    run(scatter)
    run(scatter)

    def rows(at):
        rows_low[at, :] = (middle_ref[at, :] + total[at, :] + last[at, :].astype(F32)).astype(BF16)

    by_rows(rows_low.shape[0], rows)
    spread_flow(net, rows_low, layer_ref)
    down.after_y()
    gate.after_y()
    net.arrived(rest)

    @pl.when(net.far == 1)
    def _():
        def add(at):
            move = pl.ds(pl.multiple_of(at.start + 2 * count, 16), at.size)
            mine_ref[at, :] = dkv_ref[move, :].astype(F32) + rest_core[at, :].astype(F32)

        by_rows(count, add)
        for copy in far:
            copy.wait_send()

    @pl.when(net.far == 0)
    def _():
        for copy in far:
            copy.wait_recv()

        def add(at):
            mine_ref[at, :] = dkv_ref[at, :].astype(F32) + prompt_core[at, :].astype(F32) + prompt_far[at, :].astype(F32)

        by_rows(count, add)

    net.sent = [copy for copy in net.sent if all(copy is not other for other in far)]
    net.finish()


def to_owner(dkv, partial, middle, down, down_far, gate, gate_far, sizes):
    rows, width = middle.shape
    size, across = width // sizes["narrow"], gate_far.shape[1]
    count = dkv.shape[0] // 4
    block = lambda: pltpu.VMEM((count, dkv.shape[1]), BF16)
    return wire_call(
        owner_kernel, "owner", 5, [VMEM] * 7, [VMEM, ANY, ANY, ANY],
        [
            ((count, dkv.shape[1]), F32), ((sizes["narrow"] * rows, size), BF16), ((2 * across, size), BF16),
            ((size, 2 * across), BF16),
        ],
        [
            block(), block(), block(), block(), *scatter_buffers(rows, width), pltpu.VMEM((rows, width), BF16),
            pltpu.VMEM((across, size), BF16), pltpu.VMEM((size, across), BF16), *sems(40, 16),
        ],
        sizes, 80, dkv, partial, middle, down, down_far, gate, gate_far,
    )


SUMS = [CORE, Y, X, NEAR, FAR]


def end_kernel(
    partial_ref, x_ref, gain_ref, grad_ref, two_ref, query_ref, key_ref, up_ref, up_x_ref, qkv_core_ref, qkv_ref, out_ref,
    tokens_ref, gains_ref, qkv_out, out_out, up_out,
    first, second, sums, last, total, rows_low, vectors, up_sums, up_far, *rest, sizes,
):
    buffers, (send, recv, local) = rest[:-3], rest[-3:]
    net = Wires(send, recv, local, sizes)
    net.greet([Y, CORE, CORNER, NEAR, FAR, X])
    step = x_ref.shape[1] // sizes["narrow"] // 2
    qkv = Gradient(net, 0, step, qkv_ref.shape[1] // 2)
    out = Gradient(net, 1, step, out_ref.shape[0] // 2)
    qkv.start(qkv_ref, buffers[0], qkv_core_ref, True)
    out.start(out_ref, *buffers[3:5])
    scatter = scatter_flow(net, partial_ref, first, second, sums, last, total)
    run(scatter)
    up = Gradient(net, 0, step, up_ref.shape[1] // 2)
    qkv.core_to_x(buffers[1])
    out.core_to_x(buffers[5])

    def up_to_far(k):
        for start in (up.across, 0):
            place = up.slot(k, 1, start, up.across)
            add_rows((up_sums, place), [(up_ref, place), (up_x_ref, place)])
            if start:
                up.far.append(net.send(up_sums.at[place], up_far.at[up.slot(k, 1, 0, up.across)], FAR))

    run(scatter)
    qkv.x_end(0, buffers[2])
    up_to_far(0)
    run(scatter)
    qkv.x_end(1, buffers[2])
    up_to_far(1)
    run(scatter)
    width = x_ref.shape[1]
    size = query_ref.shape[1]
    block = width // sizes["narrow"]
    half = block // 2
    gains_ref[...] = jnp.zeros_like(gains_ref)

    def rows(at):
        grad = total[at, :] + last[at, :].astype(F32)
        term, change = row_back(grad, x_ref[at, :].astype(F32), gain_ref[...])
        gains_ref[:, :width] += term
        rows_low[at, :] = (grad_ref[at, :] + change).astype(BF16)

    by_rows(rows_low.shape[0], rows)
    for i, ref in enumerate((gains_ref, two_ref)):
        for slot in range(4):
            to = (2 * (slot % 2) + jnp.bitwise_xor(net.core, slot // 2)) * block + i * width
            for j in range(2):
                sub = net.x if j == 0 else 1 - net.x
                at = slot * block + j * half
                vectors[0, :, pl.ds(pl.multiple_of(to + sub * half, half), half)] = ref[:, at : at + half]
    vectors[0, :, 2 * width : 2 * width + size] = query_ref[...]
    vectors[0, :, 2 * width + size :] = key_ref[...]

    def add_gains():
        for i, to in enumerate(SUMS):
            copy = net.send(vectors.at[i], vectors.at[len(SUMS) + 1 + i], to)
            yield
            net.arrived(copy)
            vectors[i + 1] = vectors[i] + vectors[len(SUMS) + 1 + i]
        gains_ref[...] = vectors[len(SUMS)]
        yield

    def own(flow, k, ref):
        flow.far_end(k)
        flow.to_owner(k, flow.acc.at[flow.slot(k, 2, 0, flow.across)], ref)

    def own_up(k):
        net.arrived(up.far[k])
        place = up.slot(k, 1, 0, up.across)
        add_rows((up_sums, place), [(up_sums, place), (up_far, place)])
        up.to_owner(k, up_sums.at[place], up_out)

    gains = add_gains()
    run(gains)
    out.x_end(0, buffers[6])
    out.x_end(1, buffers[6])
    run(gains)
    spread_flow(net, rows_low, tokens_ref)
    own(qkv, 0, qkv_out)
    own_up(0)
    run(gains)
    own(qkv, 1, qkv_out)
    own_up(1)
    run(gains)
    own(out, 0, out_out)
    own(out, 1, out_out)
    up.after_y()
    qkv.after_y()
    out.after_y()
    run(gains)
    run(gains)
    net.finish()


def end(partial, x, gain, grad, two, query, key, up, up_x, qkv_core, qkv, out, sizes):
    rows, width = x.shape
    size = width // sizes["narrow"]
    wide, deep = qkv.shape[1], out.shape[0]
    length = 2 * width + 2 * query.shape[1]
    return wire_call(
        end_kernel, "end", 6, [VMEM] * 10 + [ANY] * 2, [ANY, VMEM, ANY, ANY, ANY],
        [((sizes["narrow"] * rows, size), BF16), ((1, length), F32), ((size, wide), BF16), ((deep, size), BF16),
         (up.shape, BF16)],
        [
            *scatter_buffers(rows, width), pltpu.VMEM((rows, width), BF16), pltpu.VMEM((2 * len(SUMS) + 1, 1, length), F32),
            pltpu.VMEM(up.shape, BF16), pltpu.VMEM((size, up.shape[1] // 2), BF16),
            *(v for i, v in enumerate(gradient_buffers(size, wide // 2, 0)) if i != 1), *gradient_buffers(size, deep // 2, 1),
            *sems(40, 16),
        ],
        sizes, 90, partial, x, gain[None], grad, two, query, key, up, up_x, qkv_core, qkv, out,
    )


def layout(lengths, index):
    order = jnp.arange(lengths.shape[0])
    ends = jnp.sum(jnp.where(order[None, :] <= order[:, None], lengths[None, :], 0), axis=1)[None, :]
    begins = ends - lengths[None, :]
    offset = index - PROMPT
    shift = jnp.sum(jnp.where((offset >= begins) & (offset < ends), begins, 0), axis=1, keepdims=True)
    return jnp.where(offset >= 0, PROMPT + shift, 0), index - shift


def make(sizes):
    n_dp, n_wide, n_narrow = sizes["dp"], sizes["wide"], sizes["narrow"]

    def over_y(values):
        return exchange(values, "narrow", 2, n_narrow)

    def over_z(values):
        return exchange(values, "wide", 1, n_wide)

    def over_x(values):
        return exchange(values, "dp", 1, n_dp)

    def over_core(values):
        return exchange(values, "narrow", 1, n_narrow)

    def over_far(values):
        return exchange(values, "wide", 2, n_wide)

    def over_groups(values, kind):
        distance = 2
        while distance < n_dp:
            values = values.astype(F32) + exchange(values.astype(kind), "dp", distance, n_dp).astype(F32)
            distance *= 2
        return values.astype(F32)

    def on_device(
        tokens, continuation_lengths, attention_gain, query_weight, key_weight, value_weight, head_gate, query_gain, key_gain,
        output_weight, feedforward_gain, gate_weight, up_weight, down_weight, cotangent,
    ):
        rows_wide, width_local = tokens.shape
        width = attention_gain.shape[0]
        size = query_gain.shape[0]
        heads = head_gate.shape[1]
        pairs = key_weight.shape[1] // size
        group_rows = rows_wide * n_wide
        rows_local = rows_wide // n_narrow
        x = lax.axis_index("dp") % 2
        z = lax.axis_index("wide")
        narrow = lax.axis_index("narrow")
        y, core = narrow // 2, narrow % 2
        z_near, z_far = z % 2, z // 2
        quarter = width_local // 2
        scale = size ** (-0.5)
        factor = scale * math.log2(math.e)
        log_two = math.log(2.0)

        def relative_vector(vector):
            values = jnp.transpose(vector.reshape(2, 2, 2, quarter), (1, 0, 2, 3))
            values = jnp.where(core == 0, values, values[::-1])
            return jnp.where(x == 0, values, values[:, :, ::-1]).reshape(width)

        def piece_of(weight, i, axis):
            half = weight.shape[1 - axis] // 2
            return cut(cut(weight, x * quarter, quarter, axis), i * half, half, 1 - axis)

        gain_one, gain_two = relative_vector(attention_gain), relative_vector(feedforward_gain)
        lane_pad = ((0, 0), (0, LANES - heads // 2))
        halves = lambda w, i: w[:, i * (w.shape[1] // 2) : (i + 1) * (w.shape[1] // 2)]
        gates = join([jnp.pad(halves(head_gate, i), lane_pad) for i in range(2)], 1)
        packed = (query_weight, key_weight, value_weight, gates)
        inputs, upstream, normed_all, joined_weight, out_weight = begin(tokens, cotangent, gain_one, packed, output_weight, sizes)

        def indices(row):
            part, at = row // rows_local, row % rows_local
            return ((z ^ (part // 2)) * n_narrow + (narrow ^ (2 * (part % 2)))) * rows_local + at

        my_index = indices(lax.broadcasted_iota(jnp.int32, (4 * rows_local, 1), 0))
        my_start, my_position = layout(continuation_lengths[0], my_index)
        frequency = THETA ** (-2.0 * jnp.arange(size // 2, dtype=F32) / size)
        angle = my_position.astype(F32) * frequency[None, :]
        cosine, sine = jnp.cos(angle), jnp.sin(angle)
        cosine = jnp.concatenate([cosine, cosine], axis=1)
        sine = jnp.concatenate([-sine, sine], axis=1)
        heads_index = indices(lax.broadcasted_iota(jnp.int32, (4, 1), 0) * rows_local)
        block = heads_index // rows_local
        first = layout(continuation_lengths[0], heads_index)[0] // rows_local
        prompt_blocks = PROMPT // rows_local
        in_prompt = block < prompt_blocks
        column = lax.broadcasted_iota(jnp.int32, (4, 5), 1)
        pick = lambda values: functools.reduce(lambda acc, item: jnp.where(column == item[0], item[1], acc), enumerate(values), 0)
        table = pick(
            [
                jnp.where(in_prompt, block // 2, prompt_blocks // 2),
                jnp.where(in_prompt, block // 2 * 2, first),
                block,
                2 * z_near + y,
                core,
            ]
        ).astype(jnp.int32)

        raw = dot_rows(normed_all, joined_weight)
        send = after((gate_weight, up_weight, down_weight), normed_all)
        axes = (0, 0, 1)
        from_far = [over_far(piece_of(w, y, axis)) for w, axis in zip(send, axes)]
        from_y = [over_y(piece_of(w, 1 - y, axis)) for w, axis in zip(after(send, raw), axes)]
        raw = after(raw, from_far[0], from_far[1])
        q, kv = post(raw, cosine, sine, query_gain, key_gain, heads, pairs, size, factor)
        part = rows_local // 2
        early = after(upstream, raw)
        upstream_y, upstream_z = over_y(early[:part]), over_z(early[part:])
        kv_all = exchange_keys(after(kv, *from_y, *from_far, upstream_y, upstream_z), sizes)
        from_both = [over_far(after(v, kv_all)) for v in from_y]

        come_z = over_z(join([upstream[:part], after(upstream_y, kv_all)]))
        come_y = over_y(join([upstream[part:], after(upstream_z, kv_all)]))
        upstream_all = join(
            [upstream, upstream_y, come_y[:part], come_z[:part], upstream_z, come_z[part:], come_y[part:]]
        )

        gated, context, inverse_total = attend(
            table, q, kv_all, my_index, my_start, raw, pairs, size
        )
        partial = dot_rows(gated, out_weight).astype(BF16)
        middle, normed_two_all, gate_up, down = to_middle(
            partial, inputs, gain_two, gate_weight, up_weight, down_weight, from_y + from_far + from_both, sizes
        )
        both = dot_rows(normed_two_all, gate_up)
        hidden_cols = gate_weight.shape[1]
        gate_pre, up_pre = both[:, :hidden_cols], both[:, hidden_cols:]
        gate_sigmoid = jax.nn.sigmoid(gate_pre)
        silu = gate_pre * gate_sigmoid
        hidden = (silu * up_pre).astype(BF16)
        hidden_grad = dot_trans(upstream_all, down)
        gate_grad = hidden_grad * up_pre * gate_sigmoid * (1.0 + gate_pre * (1.0 - gate_sigmoid))
        up_grad = hidden_grad * silu
        gate_low, up_low = gate_grad.astype(BF16), up_grad.astype(BF16)
        gate_up_low = join([gate_low, up_low], 1)
        partial = dot_trans(gate_up_low, gate_up).astype(BF16)
        down_sums = dot_inner(hidden, upstream_all).astype(BF16)
        mlp_partial = dot_rows(hidden, down).astype(BF16)
        partial = after(partial, mlp_partial)
        middle_grad, middle_all, two_term, down_part, gate_part, up_keep, up_send = turn(
            partial, middle, upstream, gain_two, down_sums, normed_two_all, gate_low, up_low, sizes
        )
        down_far = over_far(down_part[hidden_cols // 2 :])
        gate_far = over_far(gate_part[:, hidden_cols // 2 :])
        up_come = over_x(up_send)
        gated_grad = dot_trans(middle_all, out_weight)
        dq, dkv, logit_grad = attend_back(
            table, q, kv_all, my_index, my_start, raw, context, inverse_total, gated_grad, pairs, size
        )
        out_sums = dot_inner(gated, middle_all).astype(BF16)
        dkv_mine, layer_output, down_gradient, gate_gradient = to_owner(
            after(dkv, up_come, out_sums), mlp_partial, middle, down_part, down_far, gate_part, gate_far, sizes
        )
        low, query_term, key_term = project_back(
            dq, dkv_mine, raw, cosine, sine, query_gain, key_gain, logit_grad, heads, pairs, size, scale, log_two
        )
        half = width // 2
        qkv_sums = dot_inner(normed_all, low).astype(BF16)
        qkv_core = over_core(qkv_sums[half:])
        partial = dot_trans(after(low, qkv_sums), joined_weight).astype(BF16)
        tokens_gradient, gains, qkv_gradient, output_gradient, up_gradient = end(
            partial, inputs, gain_one, middle_grad, two_term, query_term, key_term, up_keep, up_come,
            qkv_core, qkv_sums, out_sums, sizes
        )
        tokens_gradient = tokens_gradient.astype(F32)
        gains = over_groups(gains[0], F32)
        qkv_gradient = over_groups(qkv_gradient, BF16)
        down_gradient, gate_gradient, up_gradient, output_gradient = (
            over_groups(v, BF16) for v in (down_gradient, gate_gradient, up_gradient, output_gradient)
        )
        block = qkv_gradient.shape[1] // 2
        query_cols, key_cols = heads // 2 * size, pairs // 2 * size
        take = lambda at, count: join([qkv_gradient[:, at + i * block : at + i * block + count] for i in range(2)], 1)
        query_gradient = take(0, query_cols)
        key_gradient = take(query_cols, key_cols)
        value_gradient = take(query_cols + key_cols, key_cols)
        head_gate_gradient = take(query_cols + 2 * key_cols, heads // 2)
        return (
            layer_output,
            tokens_gradient,
            gains[:width],
            query_gradient,
            key_gradient,
            value_gradient,
            head_gate_gradient,
            gains[2 * width : 2 * width + size],
            gains[2 * width + size :],
            output_gradient,
            gains[width : 2 * width],
            gate_gradient,
            up_gradient,
            down_gradient,
        )

    return on_device


def solution(mesh):
    rows, up, down = P(("dp", "wide"), "narrow"), P("narrow", "wide"), P("wide", "narrow")
    return jax.shard_map(
        make(dict(mesh.shape)),
        mesh=mesh,
        in_specs=(rows, P("dp", None), P(), up, up, up, up, P(), P(), down, P(), up, up, down, rows),
        out_specs=(rows, rows, P(), up, up, up, up, P(), P(), down, P(), up, up, down),
        check_vma=False,
    )
```

```python
import functools
import math

import jax
import jax.numpy as jnp
from jax import lax
from jax.experimental import pallas as pl
from jax.experimental.pallas import tpu as pltpu
from jax.sharding import PartitionSpec as P

PROMPT = 2048
EPS = 1e-06
THETA = 1000000.0
RELATIVE = (0, 2, 1, 3)
BF16 = jnp.bfloat16
F32 = jnp.float32
VMEM_LIMIT = 56 * 1024 * 1024
LANES = 128


def dot_rows(left, right):
    return jnp.dot(left, right, preferred_element_type=F32)


def dot_trans(left, right):
    return lax.dot_general(left, right, (((1,), (1,)), ((), ())), preferred_element_type=F32)


def dot_inner(left, right):
    return lax.dot_general(left, right, (((0,), (0,)), ((), ())), preferred_element_type=F32)


def exchange(values, axis, distance, size):
    return lax.ppermute(values, axis, [(i, i ^ distance) for i in range(size)])


def join(parts, axis=0):
    return jnp.concatenate(parts, axis=axis)


def cut(values, at, length, axis):
    return lax.dynamic_slice_in_dim(values, at, length, axis=axis)


def turn_pairs(values):
    step = values.shape[1] // 4
    return join([values[:, i * step : (i + 1) * step] for i in (1, 0, 3, 2)], 1)


def after(values, *others):
    return lax.optimization_barrier((values,) + others)[0]


def columns(heads, pairs, size):
    query, pair = heads // 2, pairs // 2
    block = (query + 2 * pair) * size + LANES
    of = lambda i, count, before: (i // count) * block + (before + i % count) * size
    return (
        [of(h, query, 0) for h in range(heads)],
        [of(p, pair, query) for p in range(pairs)],
        [of(p, pair, query + pair) for p in range(pairs)],
        [block - LANES, 2 * block - LANES],
    )


def post_kernel(raw_ref, cos_ref, sin_ref, query_gain_ref, key_gain_ref, q_ref, kv_ref, *, heads, pairs, size, factor):
    cosine = cos_ref[...]
    sine = sin_ref[...]
    query_at, key_at, value_at, _ = columns(heads, pairs, size)

    def turned(value, gain):
        inverse = lax.rsqrt(jnp.mean(value * value, axis=-1, keepdims=True) + EPS)
        normal = value * inverse * gain
        return normal * cosine + pltpu.roll(normal, size // 2, 1) * sine

    for h, at in enumerate(query_at):
        value = raw_ref[:, at : at + size]
        q_ref[:, h * size : (h + 1) * size] = (turned(value, query_gain_ref[...]) * factor).astype(BF16)
    for p, at in enumerate(key_at):
        kv_ref[:, p * size : (p + 1) * size] = turned(raw_ref[:, at : at + size], key_gain_ref[...]).astype(BF16)
    for p, at in enumerate(value_at):
        to = (pairs + p) * size
        kv_ref[:, to : to + size] = raw_ref[:, at : at + size].astype(BF16)


def post(raw, cosine, sine, query_gain, key_gain, heads, pairs, size, factor):
    rows, width = raw.shape
    step = 256
    return pl.pallas_call(
        functools.partial(post_kernel, heads=heads, pairs=pairs, size=size, factor=factor),
        grid=(rows // step,),
        in_specs=[
            pl.BlockSpec((step, width), lambda i: (i, 0)),
            pl.BlockSpec((step, size), lambda i: (i, 0)),
            pl.BlockSpec((step, size), lambda i: (i, 0)),
            pl.BlockSpec((1, size), lambda i: (0, 0)),
            pl.BlockSpec((1, size), lambda i: (0, 0)),
        ],
        out_specs=[
            pl.BlockSpec((step, heads * size), lambda i: (i, 0)),
            pl.BlockSpec((step, 2 * pairs * size), lambda i: (i, 0)),
        ],
        out_shape=[
            jax.ShapeDtypeStruct((rows, heads * size), BF16),
            jax.ShapeDtypeStruct((rows, 2 * pairs * size), BF16),
        ],
        cost_estimate=pl.CostEstimate(flops=rows * width * 20, bytes_accessed=rows * width * 8, transcendentals=0),
        name="post",
    )(raw, cosine, sine, query_gain[None], key_gain[None])


def back_kernel(
    dq_ref, dkv_ref, raw_ref, cos_ref, sin_ref, query_gain_ref, key_gain_ref, logit_ref, out_ref, gq_ref, gk_ref, *, heads, pairs, size, factor_q, factor_k
):
    cosine = cos_ref[...]
    sine = sin_ref[...]
    query_at, key_at, value_at, logit_at = columns(heads, pairs, size)

    @pl.when(pl.program_id(0) == 0)
    def _():
        gq_ref[...] = jnp.zeros_like(gq_ref)
        gk_ref[...] = jnp.zeros_like(gk_ref)

    def back(up, value, gain, total_ref):
        up = up * cosine - pltpu.roll(up, size // 2, 1) * sine
        inverse = lax.rsqrt(jnp.mean(value * value, axis=-1, keepdims=True) + EPS)
        hat = value * inverse
        total_ref[...] += jnp.sum(up * hat, axis=0, keepdims=True)
        scaled = up * gain
        return inverse * (scaled - hat * jnp.mean(scaled * hat, axis=-1, keepdims=True))

    for h, at in enumerate(query_at):
        up = dq_ref[:, h * size : (h + 1) * size] * factor_q
        out_ref[:, at : at + size] = back(up, raw_ref[:, at : at + size], query_gain_ref[...], gq_ref).astype(BF16)
    for p, at in enumerate(key_at):
        up = dkv_ref[:, p * size : (p + 1) * size].astype(F32) * factor_k
        out_ref[:, at : at + size] = back(up, raw_ref[:, at : at + size], key_gain_ref[...], gk_ref).astype(BF16)
    for p, at in enumerate(value_at):
        to = (pairs + p) * size
        out_ref[:, at : at + size] = dkv_ref[:, to : to + size].astype(BF16)
    for i, at in enumerate(logit_at):
        out_ref[:, at : at + LANES] = logit_ref[:, i * LANES : (i + 1) * LANES].astype(BF16)


def project_back(dq, dkv, raw, cosine, sine, query_gain, key_gain, logit_grad, heads, pairs, size, factor_q, factor_k):
    rows, width = raw.shape
    step = 256
    row = lambda cols: pl.BlockSpec((step, cols), lambda i: (i, 0))
    one = pl.BlockSpec((1, size), lambda i: (0, 0))
    return pl.pallas_call(
        functools.partial(back_kernel, heads=heads, pairs=pairs, size=size, factor_q=factor_q, factor_k=factor_k),
        grid=(rows // step,),
        in_specs=[row(heads * size), row(2 * pairs * size), row(width), row(size), row(size), one, one, row(2 * LANES)],
        out_specs=[row(width), one, one],
        out_shape=[
            jax.ShapeDtypeStruct((rows, width), BF16),
            jax.ShapeDtypeStruct((1, size), F32),
            jax.ShapeDtypeStruct((1, size), F32),
        ],
        cost_estimate=pl.CostEstimate(flops=rows * width * 30, bytes_accessed=rows * width * 12, transcendentals=0),
        name="project_back",
    )(dq, dkv, raw, cosine, sine, query_gain[None], key_gain[None], logit_grad)


def places(table_ref, stripe, step, length):
    turn = table_ref[stripe, 3]
    core = table_ref[stripe, 4]
    half = length // 2
    blocks = half // step

    def pair(i):
        at = jnp.bitwise_xor(i, turn) * step
        return pl.ds(pl.multiple_of(at, step), step), pl.ds(pl.multiple_of(at + half // 2, step), step)

    def single(b):
        part = b // blocks
        inner = b - part * blocks
        at = part * half + jnp.bitwise_xor(inner % 2, core) * (half // 2) + jnp.bitwise_xor(inner // 2, turn) * step
        return (pl.ds(pl.multiple_of(at, step), step),)

    return pair, single


def logit_of(head, heads, own_ref, other_ref):
    half = heads // 2
    at = head % half
    return (own_ref if head < half else other_ref)[:, at : at + 1]


def logit_specs(raw, heads, pairs, size, step):
    spec = lambda i: pl.BlockSpec((step, LANES), lambda s, t: (s, i))
    return [spec(at // LANES) for at in columns(heads, pairs, size)[3]]


def forward_kernel(table_ref, q_ref, kv_ref, row_ref, start_ref, own_ref, other_ref, gated_ref, context_ref, inverse_ref, *, pairs, repeat, size, step):
    stripe = pl.program_id(0)
    wide_blocks = table_ref[stripe, 0]
    low = table_ref[stripe, 1]
    high = table_ref[stripe, 2]
    pair, single = places(table_ref, stripe, step, kv_ref.shape[0])
    rows = row_ref[...]
    starts = start_ref[...]
    rows = jnp.concatenate([rows] * repeat, axis=0)
    starts = jnp.concatenate([starts] * repeat, axis=0)
    queries = [
        jnp.concatenate([q_ref[:, h * size : (h + 1) * size] for h in range(k * repeat, (k + 1) * repeat)], axis=0)
        for k in range(pairs)
    ]

    def seen(totals, where, first):
        outs = []
        for k in range(pairs):
            keys = join([kv_ref[at, k * size : (k + 1) * size] for at in where])
            weights = jnp.exp2(dot_trans(queries[k], keys))
            if first is not None:
                index = first + lax.broadcasted_iota(jnp.int32, weights.shape, 1)
                weights = jnp.where((index <= rows) & (index >= starts), weights, 0.0)
            values = join([kv_ref[at, (pairs + k) * size : (pairs + k + 1) * size] for at in where])
            values = jnp.concatenate([values, jnp.ones_like(values)], axis=1)
            outs.append(totals[k] + dot_rows(weights.astype(BF16), values))
        return tuple(outs)

    totals = tuple(jnp.zeros((query.shape[0], 2 * size), F32) for query in queries)
    totals = lax.fori_loop(0, wide_blocks, lambda i, t: seen(t, pair(i), None), totals)
    totals = lax.fori_loop(low, high + 1, lambda i, t: seen(t, single(i), i * step), totals)
    for k, total in enumerate(totals):
        inverse = 1.0 / total[:, size:]
        context = total[:, :size] * inverse
        for r in range(repeat):
            h = k * repeat + r
            part = context[r * step : (r + 1) * step]
            cols = slice(h * size, (h + 1) * size)
            gate = jax.nn.sigmoid(logit_of(h, pairs * repeat, own_ref, other_ref))
            gated_ref[:, cols] = (part * gate).astype(BF16)
            context_ref[:, cols] = part
            inverse_ref[:, cols] = inverse[r * step : (r + 1) * step]


def attend(table, q, kv, rows, starts, raw, pairs, size):
    length, cols = q.shape
    heads = cols // size
    step = length // table.shape[0]
    block = lambda width: pl.BlockSpec((step, width), lambda i, t: (i, 0))
    return pl.pallas_call(
        functools.partial(forward_kernel, pairs=pairs, repeat=heads // pairs, size=size, step=step),
        grid_spec=pltpu.PrefetchScalarGridSpec(
            num_scalar_prefetch=1,
            grid=(length // step,),
            in_specs=[
                block(cols),
                pl.BlockSpec(kv.shape, lambda i, t: (0, 0), pipeline_mode=pl.Buffered(1)),
                block(1),
                block(1),
                *logit_specs(raw, heads, pairs, size, step),
            ],
            out_specs=[block(cols), block(cols), block(cols)],
        ),
        out_shape=[
            jax.ShapeDtypeStruct((length, cols), BF16),
            jax.ShapeDtypeStruct((length, cols), F32),
            jax.ShapeDtypeStruct((length, cols), F32),
        ],
        compiler_params=pltpu.CompilerParams(vmem_limit_bytes=VMEM_LIMIT),
        cost_estimate=pl.CostEstimate(flops=20 * 10**9, bytes_accessed=12 * 10**6, transcendentals=7 * 10**6),
        name="attend",
    )(table, q, kv, rows, starts, raw, raw)


def backward_kernel(
    table_ref, q_ref, kv_ref, row_ref, start_ref, own_ref, other_ref, context_ref, inverse_ref, grad_ref,
    dq_ref, dkv_ref, dlogit_ref, sums_ref, *, pairs, repeat, size, step,
):
    stripe = pl.program_id(0)
    wide_blocks = table_ref[stripe, 0]
    low = table_ref[stripe, 1]
    high = table_ref[stripe, 2]
    pair, single = places(table_ref, stripe, step, kv_ref.shape[0])

    @pl.when(stripe == 0)
    def _():
        sums_ref[...] = jnp.zeros_like(sums_ref)

    dlogit_ref[...] = jnp.zeros_like(dlogit_ref)
    rows = jnp.concatenate([row_ref[0]] * repeat, axis=1)
    starts = jnp.concatenate([start_ref[0]] * repeat, axis=1)
    queries, all_grads, all_inners = [], [], []
    for k in range(pairs):
        heads = [k * repeat + r for r in range(repeat)]
        queries.append(jnp.concatenate([q_ref[:, h * size : (h + 1) * size] for h in heads], axis=0))
        grads, inners = [], []
        for h in heads:
            cols = slice(h * size, (h + 1) * size)
            up = grad_ref[:, cols]
            gate = jax.nn.sigmoid(logit_of(h, pairs * repeat, own_ref, other_ref))
            product = jnp.sum(up * context_ref[:, cols], axis=1, keepdims=True)
            half = pairs * repeat // 2
            at = h // half * LANES + h % half
            dlogit_ref[:, at : at + 1] = product * gate * (1.0 - gate)
            inverse = inverse_ref[:, cols]
            grads.append((up * gate * inverse).astype(BF16))
            inners.append(product * gate * inverse)
        all_grads.append(jnp.concatenate(grads, axis=0))
        all_inners.append(jnp.transpose(jnp.concatenate(inners, axis=0))[0:1])

    def seen(totals, where, first):
        outs = []
        for k in range(pairs):
            key_cols = slice(k * size, (k + 1) * size)
            value_cols = slice((pairs + k) * size, (pairs + k + 1) * size)
            keys = join([kv_ref[at, key_cols] for at in where])
            weights = jnp.exp2(dot_trans(keys, queries[k]))
            if first is not None:
                index = first + lax.broadcasted_iota(jnp.int32, weights.shape, 0)
                weights = jnp.where((index <= rows) & (index >= starts), weights, 0.0)
            changes = dot_trans(join([kv_ref[at, value_cols] for at in where]), all_grads[k])
            changes = (weights * (changes - all_inners[k])).astype(BF16)
            value_sums = dot_rows(weights.astype(BF16), all_grads[k])
            key_sums = dot_rows(changes, queries[k])
            for i, at in enumerate(where):
                sums_ref[at, value_cols] += value_sums[i * step : (i + 1) * step]
                sums_ref[at, key_cols] += key_sums[i * step : (i + 1) * step]
            outs.append(totals[k] + dot_inner(changes, keys))
        return tuple(outs)

    totals = tuple(jnp.zeros((query.shape[0], size), F32) for query in queries)
    totals = lax.fori_loop(0, wide_blocks, lambda i, t: seen(t, pair(i), None), totals)
    totals = lax.fori_loop(low, high + 1, lambda i, t: seen(t, single(i), i * step), totals)
    for k, total in enumerate(totals):
        for r in range(repeat):
            h = k * repeat + r
            dq_ref[:, h * size : (h + 1) * size] = total[r * step : (r + 1) * step]

    @pl.when(stripe == pl.num_programs(0) - 1)
    def _():
        dkv_ref[...] = sums_ref[...].astype(BF16)


def attend_back(table, q, kv, rows, starts, raw, context, inverse, grad, pairs, size):
    length, cols = q.shape
    heads = cols // size
    step = length // table.shape[0]
    block = lambda width: pl.BlockSpec((step, width), lambda i, t: (i, 0))
    whole = pl.BlockSpec(kv.shape, lambda i, t: (0, 0), pipeline_mode=pl.Buffered(1))
    lane = pl.BlockSpec((1, 1, step), lambda i, t: (i, 0, 0))
    logits = logit_specs(raw, heads, pairs, size, step)
    return pl.pallas_call(
        functools.partial(backward_kernel, pairs=pairs, repeat=heads // pairs, size=size, step=step),
        grid_spec=pltpu.PrefetchScalarGridSpec(
            num_scalar_prefetch=1,
            grid=(length // step,),
            in_specs=[block(cols), whole, lane, lane, *logits, block(cols), block(cols), block(cols)],
            out_specs=[block(cols), whole, block(2 * LANES)],
            scratch_shapes=[pltpu.VMEM(kv.shape, F32)],
        ),
        out_shape=[
            jax.ShapeDtypeStruct((length, cols), F32),
            jax.ShapeDtypeStruct(kv.shape, BF16),
            jax.ShapeDtypeStruct((length, 2 * LANES), F32),
        ],
        compiler_params=pltpu.CompilerParams(vmem_limit_bytes=VMEM_LIMIT),
        cost_estimate=pl.CostEstimate(flops=50 * 10**9, bytes_accessed=20 * 10**6, transcendentals=7 * 10**6),
        name="attend_back",
    )(table, q, kv, rows.reshape(-1, 1, step), starts.reshape(-1, 1, step), raw, raw, context, inverse, grad)


class Wires:
    def __init__(self, send_sems, recv_sems, local_sems, sizes):
        self.send_sems, self.recv_sems, self.local_sems = send_sems, recv_sems, local_sems
        self.sizes = sizes
        self.sent, self.local, self.open = [], [], []
        self.locals_used, self.sends_used = 0, 0
        self.dp, self.wide, self.narrow = (lax.axis_index(a) for a in ("dp", "wide", "narrow"))
        self.y, self.core = self.narrow // 2, self.narrow % 2
        self.x, self.far = self.dp % 2, self.wide // 2

    def peer(self, *to):
        if isinstance(to[0], tuple):
            return {axis: at for part in to for axis, at in self.peer(*part).items()}
        axis, distance = to
        at = {"dp": self.dp, "wide": self.wide, "narrow": self.narrow}[axis]
        bit = at // distance % 2
        return {axis: at + distance * (1 - 2 * bit) if distance < 3 else 3 - at}

    def greet(self, peers):
        barrier = pltpu.get_barrier_semaphore()
        for to in peers:
            pl.semaphore_signal(barrier, inc=1, device_id=self.peer(*to), device_id_type=pl.DeviceIdType.MESH)
        pl.semaphore_wait(barrier, len(peers))

    def make(self, source, target, to):
        i = self.sends_used
        self.sends_used += 1
        copy = pltpu.make_async_remote_copy(
            src_ref=source, dst_ref=target, send_sem=self.send_sems.at[i], recv_sem=self.recv_sems.at[i],
            device_id=self.peer(*to), device_id_type=pl.DeviceIdType.MESH,
        )
        self.sent.append(copy)
        return copy

    def send(self, source, target, to):
        copy = self.make(source, target, to)
        copy.start()
        self.open.append(copy)
        return copy

    def arrived(self, copy):
        copy.wait_recv()
        self.open = [other for other in self.open if other is not copy]

    def copy(self, source, target):
        copy = pltpu.make_async_copy(source, target, self.local_sems.at[self.locals_used])
        self.locals_used += 1
        copy.start()
        self.local.append(copy)
        return copy

    def finish(self):
        for copy in list(self.open):
            self.arrived(copy)
        for copy in self.sent:
            copy.wait_send()
        for copy in self.local:
            copy.wait()


Y, CORE, CORNER, NEAR, FAR, X = ("narrow", 2), ("narrow", 1), ("narrow", 3), ("wide", 1), ("wide", 2), ("dp", 1)


def local_flow(net, values_ref, rows_ref):
    rows, width = rows_ref.shape[0], values_ref.shape[1]
    half = width // 2
    out = []
    for distance, to in ((0, None), (1, CORE), (2, Y), (3, CORNER)):
        target = net.narrow if to is None else net.peer(*to)["narrow"]
        at = (2 * (distance % 2) + net.y) * width
        for j in range(2):
            sub = net.x if j == 0 else 1 - net.x
            source = values_ref.at[pl.ds(pl.multiple_of(target * rows, rows), rows), pl.ds(pl.multiple_of(sub * half, half), half)]
            goal = rows_ref.at[:, pl.ds(pl.multiple_of(at + j * half, half), half)]
            out.append(net.copy(source, goal) if to is None else net.send(source, goal, to))
    return out


def gather_flow(net, values_ref, all_ref):
    rows = values_ref.shape[0]
    half = rows // 2
    part = lambda i: all_ref.at[pl.ds(i * half, half), :]
    first, second = values_ref.at[pl.ds(0, half), :], values_ref.at[pl.ds(half, half), :]
    first_y = net.send(first, part(2), Y)
    second_z = net.send(second, part(5), NEAR)
    net.send(first, part(4), NEAR)
    net.send(second, part(3), Y)
    net.copy(values_ref, all_ref.at[pl.ds(0, rows), :])
    yield
    net.arrived(first_y)
    net.send(part(2), part(6), NEAR)
    yield
    net.arrived(second_z)
    net.send(part(5), part(7), Y)
    yield


def weight_flow(net, source_ref, out_ref, axis, own, other, across, from_y=None, from_far=None, from_both=None, their_y=None, their_far=None):
    step = source_ref.shape[axis] // 2
    count = source_ref.shape[axis]

    def window(ref, at, start):
        long, wide = pl.ds(pl.multiple_of(at, step), step), pl.ds(start, across)
        return ref.at[long, wide] if axis == 0 else ref.at[wide, long]

    y, x = net.y, net.x
    piece = lambda sub, half: window(source_ref, sub * step, pl.multiple_of(half * across, across))
    place = lambda slot, j, start: window(out_ref, slot * count + j * step, start)
    mine, rest = piece(x, y), piece(1 - x, y)
    net.copy(mine, place(y, 0, own))
    net.copy(rest, place(y, 1, own))
    if from_y is None:
        come_y = net.send(piece(x, 1 - y), place(y, 0, own), Y)
    else:
        net.copy(from_y, place(1 - y, 0, own))
    if from_far is None:
        come_far = net.send(mine, place(y, 0, other), FAR)
    else:
        net.copy(from_far, place(y, 0, other))
    net.send(mine, place(2 + y, 0, own), CORE)
    net.send(rest, place(2 + y, 1, own), CORE)
    if from_y is None:
        yield
        net.arrived(come_y)
        from_y = place(1 - y, 0, own)
    if from_both is None:
        come_both = net.send(from_y, place(1 - y, 0, other), FAR)
    else:
        net.copy(from_both, place(1 - y, 0, other))
    given = their_y is not None
    if given:
        for ref, slot, start in ((their_y, 1 - y, own), (their_far, y, other)):
            net.copy(ref, place(slot, 1, start))
            net.send(ref, place(slot + 2, 1, start), CORE)
    else:
        their_y = net.send(from_y, place(1 - y, 1, own), X)
    net.send(from_y, place(3 - y, 0, own), CORE)
    if from_far is None:
        yield
        net.arrived(come_far)
        from_far = place(y, 0, other)
    if not given:
        their_far = net.send(from_far, place(y, 1, other), X)
    net.send(from_far, place(2 + y, 0, other), CORE)
    if from_both is None:
        yield
        net.arrived(come_both)
        from_both = place(1 - y, 0, other)
    their_both = net.send(from_both, place(1 - y, 1, other), X)
    net.send(from_both, place(3 - y, 0, other), CORE)
    yield
    waiting = ((their_y, 1 - y, own), (their_far, y, other), (their_both, 1 - y, other))
    for copy, slot, start in waiting[2 * given :]:
        net.arrived(copy)
        net.send(place(slot, 1, start), place(slot + 2, 1, start), CORE)
    yield


def run(flow):
    return next(flow, None)


def by_rows(count, body):
    step = 16
    lax.fori_loop(0, count // step, lambda i, _: (body(pl.ds(pl.multiple_of(i * step, step), step)), 0)[1], 0)


def begin_kernel(
    tokens_ref, cotangent_ref, gain_ref, query_ref, key_ref, value_ref, gates_ref, out_ref,
    x_ref, rows_ref, all_ref, joined_ref, output_ref, here, normed, there, qkv_ref, send, recv, local, *, sizes,
):
    net = Wires(send, recv, local, sizes)
    net.greet([Y, CORE, CORNER, NEAR, FAR, X])
    rows = local_flow(net, tokens_ref, here)
    across = qkv_ref.shape[1] // 2
    packed, at = [], 0
    for ref in (query_ref, key_ref, value_ref, gates_ref):
        wide = ref.shape[1] // 2
        for i in range(2):
            packed.append(net.copy(ref.at[:, pl.ds(i * wide, wide)], qkv_ref.at[:, pl.ds(i * across + at, wide)]))
        at += wide
    for copy in packed:
        copy.wait()
    net.local = [copy for copy in net.local if all(copy is not other for other in packed)]
    joined = weight_flow(net, qkv_ref, joined_ref, 0, 0, across, across)
    run(joined)
    rows[0].wait()
    rows[1].wait()
    net.local = net.local[2:]
    for copy in rows[2:]:
        net.arrived(copy)

    def norm(at):
        values = here[at, :].astype(F32)
        inverse = lax.rsqrt(jnp.mean(values * values, axis=1, keepdims=True) + EPS)
        normed[at, :] = (values * inverse * gain_ref[...]).astype(BF16)
        x_ref[at, :] = here[at, :]

    by_rows(here.shape[0], norm)
    gather = gather_flow(net, normed, all_ref)
    run(gather)
    across = out_ref.shape[0] // 2
    output = weight_flow(net, out_ref, output_ref, 1, 0, across, across)
    for flow in (joined, gather, output, joined, gather):
        run(flow)
    rows = local_flow(net, cotangent_ref, there)
    for flow in (joined, output, joined, output, output, output):
        run(flow)
    for copy in rows[:2]:
        copy.wait()
    net.local = [copy for copy in net.local if all(copy is not other for other in rows[:2])]
    for copy in rows[2:]:
        net.arrived(copy)
    net.copy(there, rows_ref)
    net.finish()


ANY = pl.BlockSpec(memory_space=pl.ANY)
VMEM = pl.BlockSpec(memory_space=pltpu.VMEM)


def sems(sends, locals_):
    return [pltpu.SemaphoreType.DMA((sends,)), pltpu.SemaphoreType.DMA((sends,)), pltpu.SemaphoreType.DMA((locals_,))]


def wire_call(kernel, name, number, specs, out_specs, shapes, scratch, sizes, cost, *args):
    return pl.pallas_call(
        functools.partial(kernel, sizes=sizes),
        in_specs=specs,
        out_specs=out_specs,
        out_shape=[jax.ShapeDtypeStruct(*shape) for shape in shapes],
        scratch_shapes=scratch,
        compiler_params=pltpu.CompilerParams(collective_id=number, has_side_effects=True, vmem_limit_bytes=VMEM_LIMIT),
        cost_estimate=pl.CostEstimate(flops=0, bytes_accessed=cost * 3 * 10**6, transcendentals=0),
        name=name,
    )(*args)


def begin(tokens, cotangent, gain, weights, out, sizes):
    rows, width = tokens.shape[0] // sizes["narrow"], gain.shape[0]
    wide = sum(w.shape[1] for w in weights)
    row = pltpu.VMEM((rows, width), BF16)
    return wire_call(
        begin_kernel, "begin", 1, [ANY, ANY, VMEM] + [ANY] * 4 + [VMEM], [VMEM, ANY, ANY, ANY, ANY],
        [
            ((rows, width), BF16), ((rows, width), BF16), ((4 * rows, width), BF16), ((width, wide), BF16),
            ((out.shape[0], width), BF16),
        ],
        [row, row, row, pltpu.VMEM((weights[0].shape[0], wide), BF16), *sems(48, 24)],
        sizes, 55, tokens, cotangent, gain[None], *weights, out,
    )


def keys_kernel(kv_ref, keys_ref, done, send, recv, local, *, sizes):
    net = Wires(send, recv, local, sizes)
    across = [FAR, ("wide", 3), (FAR, CORE), (("wide", 3), CORE)]
    net.greet([CORE] + across)
    count, width = kv_ref.shape
    size = width // 4
    part = lambda i, j: keys_ref.at[pl.ds(i, count), pl.ds(j * size, size)]
    base = pl.multiple_of(net.far * 2 * count, count)
    far = [net.make(kv_ref.at[:, pl.ds(j * size, size)], part(0, j ^ 1), FAR) for j in range(4)]
    on = [net.make(part(0, j ^ 1), part(count, j ^ 1), CORE) for j in range(4)]

    @pl.when(net.far == 0)
    def _():
        for copy in far:
            copy.start()

    net.copy(kv_ref, keys_ref.at[pl.ds(base, count), :])
    net.send(kv_ref, keys_ref.at[pl.ds(base + count, count), :], CORE)

    @pl.when(net.far == 1)
    def _():
        for copy, forward in zip(far, on):
            copy.wait_recv()
            forward.start()
        for to in across:
            pl.semaphore_signal(done, inc=1, device_id=net.peer(*to), device_id_type=pl.DeviceIdType.MESH)
        for forward in on:
            forward.wait()

    @pl.when(net.far == 0)
    def _():
        for copy in far:
            copy.wait_send()
        pl.semaphore_wait(done, len(across))

    net.sent = [copy for copy in net.sent if all(copy is not other for other in far + on)]
    net.finish()


def exchange_keys(kv, sizes):
    return wire_call(
        keys_kernel, "keys", 2, [VMEM], [ANY], [((4 * kv.shape[0], kv.shape[1]), BF16)],
        [pltpu.SemaphoreType.REGULAR, *sems(16, 4)], sizes, 45, kv,
    )[0]


def scatter_flow(net, partial_ref, first_ref, second_ref, send_ref, last_ref, total_ref):
    half = partial_ref.shape[0] // 8
    part = lambda i: partial_ref.at[pl.ds(i * half, half), :]
    slot = lambda ref, i: ref.at[pl.ds(i * half, half), :]
    to_z = [net.send(part(6), slot(first_ref, 1), NEAR), net.send(part(4), slot(first_ref, 0), NEAR)]
    to_y = [net.send(part(7), slot(second_ref, 1), Y), net.send(part(3), slot(second_ref, 0), Y)]
    yield

    def add(out_ref, to, i, ref, j):
        def body(at):
            move = lambda start: pl.ds(pl.multiple_of(at.start + start, 16), at.size)
            value = partial_ref[move(i * half), :].astype(F32) + ref[move(j * half), :].astype(F32)
            out_ref[move(to), :] = value.astype(out_ref.dtype)

        by_rows(half, body)

    net.arrived(to_z[0])
    add(send_ref, 0, 2, first_ref, 1)
    last_y = net.send(slot(send_ref, 0), slot(last_ref, 0), Y)
    net.arrived(to_y[0])
    add(send_ref, half, 5, second_ref, 1)
    last_z = net.send(slot(send_ref, 1), slot(last_ref, 1), NEAR)
    yield
    net.arrived(to_z[1])
    add(total_ref, 0, 0, first_ref, 0)
    net.arrived(to_y[1])
    add(total_ref, half, 1, second_ref, 0)
    yield
    net.arrived(last_y)
    net.arrived(last_z)
    yield


def middle_kernel(
    partial_ref, x_ref, gain_ref, gate_ref, up_ref, down_ref, gate_y_ref, up_y_ref, down_y_ref, gate_far_ref, up_far_ref, down_far_ref,
    gate_both_ref, up_both_ref, down_both_ref, middle_ref, all_ref, both_ref, last_ref,
    first, second, sums, last, total, normed, send, recv, local, *, sizes,
):
    net = Wires(send, recv, local, sizes)
    net.greet([Y, CORE, NEAR, FAR, X])
    scatter = scatter_flow(net, partial_ref, first, second, sums, last, total)
    run(scatter)
    across = gate_ref.shape[1] // 2
    flows = [
        weight_flow(net, gate_ref, both_ref, 0, 0, across, across, gate_y_ref, gate_far_ref, gate_both_ref),
        weight_flow(net, up_ref, both_ref, 0, 2 * across, 3 * across, across, up_y_ref, up_far_ref, up_both_ref),
        weight_flow(net, down_ref, last_ref, 1, 0, across, across, down_y_ref, down_far_ref, down_both_ref),
    ]
    for flow in flows:
        run(flow)
    run(scatter)
    run(scatter)
    run(scatter)

    def norm(at):
        values = x_ref[at, :].astype(F32) + total[at, :] + last[at, :].astype(F32)
        middle_ref[at, :] = values
        inverse = lax.rsqrt(jnp.mean(values * values, axis=1, keepdims=True) + EPS)
        normed[at, :] = (values * inverse * gain_ref[...]).astype(BF16)

    by_rows(normed.shape[0], norm)
    gather = gather_flow(net, normed, all_ref)
    run(gather)
    run(flows[0])
    run(gather)
    run(gather)
    run(flows[1])
    run(flows[2])
    net.finish()


def to_middle(partial, x, gain, gate, up, down, pieces, sizes):
    rows, width = x.shape
    buffer = lambda n, kind: pltpu.VMEM((n, width), kind)
    return wire_call(
        middle_kernel, "middle", 3, [VMEM] * 15, [VMEM, ANY, ANY, ANY],
        [((rows, width), F32), ((4 * rows, width), BF16), ((width, 2 * gate.shape[1]), BF16), ((down.shape[0], width), BF16)],
        [
            buffer(rows, BF16), buffer(rows, BF16), buffer(rows, BF16), buffer(rows, BF16), buffer(rows, F32), buffer(rows, BF16),
            *sems(64, 32),
        ],
        sizes, 80, partial, x, gain[None], gate, up, down, *pieces,
    )


def spread_flow(net, rows_ref, out_ref):
    rows, width = rows_ref.shape[0], out_ref.shape[1]
    half = width // 2
    base = pl.multiple_of(net.narrow * rows, rows)
    for distance, to in ((3, CORNER), (2, Y), (1, CORE), (0, None)):
        target = net.narrow if to is None else net.peer(*to)["narrow"]
        at = (2 * (distance % 2) + target // 2) * width
        for j in range(2):
            sub = net.x if j == 0 else 1 - net.x
            source = rows_ref.at[:, pl.ds(pl.multiple_of(at + j * half, half), half)]
            goal = out_ref.at[pl.ds(base, rows), pl.ds(pl.multiple_of(sub * half, half), half)]
            if to is None:
                net.copy(source, goal)
            else:
                net.send(source, goal, to)


def add_rows(target, terms):
    ref, (rows, cols) = target

    def body(at):
        move = lambda r: pl.ds(pl.multiple_of(at.start + r.start, 16), at.size)
        value = sum(term[move(r), c].astype(F32) for term, (r, c) in terms)
        ref[move(rows), cols] = value.astype(BF16)

    by_rows(rows.size, body)


class Gradient:
    def __init__(self, net, axis, step, across):
        self.net, self.axis, self.step, self.across = net, axis, step, across
        self.order = (1 - net.y, net.y)
        self.x, self.far = [], []

    def window(self, at, start, count, length=None):
        step = self.step if length is None else length
        hint = lambda v, unit: v if isinstance(v, int) else pl.multiple_of(v, unit)
        along, wide = pl.ds(hint(at, self.step), step), pl.ds(hint(start, self.across), count)
        return (along, wide) if self.axis == 0 else (wide, along)

    def start(self, g_ref, acc, from_core, given=False):
        self.acc, self.from_core = acc, from_core
        count = 4 * self.step
        own, other = (self.window(i * count, 0, 2 * self.across, count) for i in range(2))
        self.loaded = self.net.copy(g_ref.at[own], acc)
        self.core = None if given else self.net.send(g_ref.at[other], from_core, CORE)

    def wait_core(self):
        if self.loaded is not None:
            self.loaded.wait()
            self.net.local = [copy for copy in self.net.local if copy is not self.loaded]
        if self.core is not None:
            self.net.arrived(self.core)

    def core_to_x(self, from_x):
        self.wait_core()
        self.from_x = from_x
        for slot in self.order:
            place = self.window((2 * slot + 1) * self.step, 0, 2 * self.across)
            add_rows((self.acc, place), [(self.acc, place), (self.from_core, place)])
            goal = from_x.at[self.window(slot * self.step, 0, 2 * self.across)]
            self.x.append(self.net.send(self.acc.at[place], goal, X))

    def x_end(self, k, from_far=None):
        slot = self.order[k]
        self.net.arrived(self.x[k])
        for start in (self.across, 0):
            place = self.window(2 * slot * self.step, start, self.across)
            come = self.window(slot * self.step, start, self.across)
            add_rows((self.acc, place), [(self.acc, place), (self.from_core, place), (self.from_x, come)])
            if start and from_far is not None:
                self.from_far = from_far
                goal = from_far.at[self.window(slot * self.step, 0, self.across)]
                self.far.append(self.net.send(self.acc.at[place], goal, FAR))

    def far_end(self, k, result=None):
        slot = self.order[k]
        self.net.arrived(self.far[k])
        place = self.window(2 * slot * self.step, 0, self.across)
        come = self.window(slot * self.step, 0, self.across)
        add_rows((self.acc, place), [(self.acc, place), (self.from_far, come)])

    def to_owner(self, k, source, out):
        net, across = self.net, self.across
        goal = out.at[self.window(net.x * self.step, net.y * across, across)]
        if k == 0:
            self.out = out
            self.y = net.send(source, goal, Y)
        else:
            net.copy(source, goal)
            net.send(source, goal, X)

    def after_y(self):
        net, across = self.net, self.across
        net.arrived(self.y)
        place = self.out.at[self.window(net.x * self.step, (1 - net.y) * across, across)]
        net.send(place, place, X)

    def slot(self, k, stride, start, count):
        return self.window(stride * self.order[k] * self.step, start, count)


def row_back(grad, values, gain):
    inverse = lax.rsqrt(jnp.mean(values * values, axis=1, keepdims=True) + EPS)
    hat = values * inverse
    scaled = grad * gain
    inner = jnp.mean(scaled * hat, axis=1, keepdims=True)
    return jnp.sum(grad * hat, axis=0, keepdims=True), inverse * (scaled - hat * inner)


def turn_kernel(
    partial_ref, middle_ref, upstream_ref, gain_ref, down_ref, inputs_ref, gate_ref, up_ref,
    grad_ref, all_ref, term_ref, down_out, gate_out, up_keep, up_send,
    first, second, sums, last, total, low, *rest, sizes,
):
    buffers, (rows_two, gate_grads, up_grads, gate_other, up_other), (send, recv, local) = rest[:-8], rest[-8:-3], rest[-3:]
    net = Wires(send, recv, local, sizes)
    net.greet([Y, CORE, NEAR, FAR, X])
    scatter = scatter_flow(net, partial_ref, first, second, sums, last, total)
    run(scatter)
    step, across = low.shape[1] // sizes["narrow"] // 2, gate_ref.shape[1] // 2
    down, gate, up = (Gradient(net, axis, step, across) for axis in (1, 0, 0))
    down.start(down_ref, *buffers[0:2])
    gate.acc, gate.from_core = buffers[3:5]
    up.acc, up.from_core = buffers[6:8]
    loads = [net.copy(inputs_ref, rows_two), net.copy(gate_ref, gate_grads), net.copy(up_ref, up_grads)]
    for copy in loads:
        copy.wait()
    net.local = [copy for copy in net.local if all(copy is not other for other in loads)]
    half = rows_two.shape[1] // 2

    def dots(base, grads, target):
        def body(i, _):
            at = pl.multiple_of(i * step, step)
            part = dot_inner(rows_two[:, pl.ds(pl.multiple_of(base + at, step), step)], grads[...])
            target[pl.ds(at, step), :] = part.astype(BF16)
            return 0

        lax.fori_loop(0, half // step, body, 0)

    dots(half, gate_grads, gate_other)
    gate.loaded, gate.core = None, net.send(gate_other, gate.from_core, CORE)
    down.core_to_x(buffers[2])
    dots(0, gate_grads, gate.acc)
    gate.core_to_x(buffers[5])
    run(scatter)
    run(scatter)
    run(scatter)
    term_ref[...] = jnp.zeros_like(term_ref)

    def rows(at):
        grad = total[at, :] + last[at, :].astype(F32)
        term, change = row_back(grad, middle_ref[at, :], gain_ref[...])
        term_ref[...] += term
        value = upstream_ref[at, :].astype(F32) + change
        grad_ref[at, :] = value
        low[at, :] = value.astype(BF16)

    by_rows(low.shape[0], rows)
    gather = gather_flow(net, low, all_ref)
    run(gather)
    dots(half, up_grads, up_other)
    up.loaded, up.core = None, net.send(up_other, up.from_core, CORE)
    for k in range(2):
        down.x_end(k)
        net.copy(down.acc.at[down.slot(k, 2, 0, 2 * across)], down_out.at[down.slot(k, 1, 0, 2 * across)])
    run(gather)
    run(gather)
    dots(0, up_grads, up.acc)
    up.wait_core()
    for slot in range(2):
        for j, ref in ((1, up_send), (0, up_keep)):
            place = up.window((2 * slot + j) * step, 0, 2 * across)
            add_rows((up.acc, place), [(up.acc, place), (up.from_core, place)])
            net.copy(up.acc.at[place], ref.at[up.window(slot * step, 0, 2 * across)])
    for k in range(2):
        gate.x_end(k)
        net.copy(gate.acc.at[gate.slot(k, 2, 0, 2 * across)], gate_out.at[gate.slot(k, 1, 0, 2 * across)])
    net.finish()


def gradient_buffers(size, across, axis, count=4):
    shape = lambda a, b: pltpu.VMEM((a, b) if axis == 0 else (b, a), BF16)
    every = [shape(2 * size, 2 * across), shape(2 * size, 2 * across), shape(size, 2 * across), shape(size, across)]
    return every[:count]


def scatter_buffers(rows, width):
    buffer = lambda kind: pltpu.VMEM((rows, width), kind)
    return [buffer(BF16), buffer(BF16), buffer(BF16), buffer(BF16), buffer(F32)]


def turn(partial, middle, upstream, gain, down, inputs, gate, up, sizes):
    rows, width = middle.shape
    size, across = width // sizes["narrow"], down.shape[0] // 2
    return wire_call(
        turn_kernel, "turn", 4, [VMEM] * 4 + [ANY] * 4, [VMEM, ANY, VMEM, ANY, ANY, ANY, ANY],
        [
            ((rows, width), F32), ((4 * rows, width), BF16), ((1, width), F32),
            ((2 * across, size), BF16), ((size, 2 * across), BF16), ((size, 2 * across), BF16), ((size, 2 * across), BF16),
        ],
        [
            *scatter_buffers(rows, width), pltpu.VMEM((rows, width), BF16),
            *gradient_buffers(size, across, 1, 3), *gradient_buffers(size, across, 0, 3), *gradient_buffers(size, across, 0, 2),
            pltpu.VMEM(inputs.shape, BF16), *(pltpu.VMEM((n, 2 * across), BF16) for n in (gate.shape[0],) * 2 + (2 * size,) * 2),
            *sems(40, 24),
        ],
        sizes, 80, partial, middle, upstream, gain[None], down, inputs, gate, up,
    )


def owner_kernel(
    dkv_ref, partial_ref, middle_ref, down_ref, down_far_ref, gate_ref, gate_far_ref,
    mine_ref, layer_ref, down_out, gate_out,
    prompt_core, rest_core, prompt, prompt_far, first, second, sums, last, total, rows_low, down_sums, gate_sums,
    send, recv, local, *, sizes,
):
    net = Wires(send, recv, local, sizes)
    net.greet([Y, CORE, CORNER, NEAR, FAR, X])
    count, width = prompt.shape
    size = width // 4
    region = lambda i: dkv_ref.at[pl.ds(i * count, count), :]
    come = net.send(region(1), prompt_core, CORE)
    rest = net.send(region(3), rest_core, CORE)
    scatter = scatter_flow(net, partial_ref, first, second, sums, last, total)
    run(scatter)
    step, across = down_far_ref.shape[1] // 2, down_far_ref.shape[0]
    down, gate = (Gradient(net, axis, step, across) for axis in (1, 0))
    net.arrived(come)

    def add(at):
        prompt[at, :] = (dkv_ref[at, :].astype(F32) + prompt_core[at, :].astype(F32)).astype(BF16)

    by_rows(count, add)
    cols = lambda ref, j: ref.at[:, pl.ds(j * size, size)]
    far = [net.make(cols(prompt, j), cols(prompt_far, j ^ 1), FAR) for j in range(4)]

    @pl.when(net.far == 1)
    def _():
        for copy in far:
            copy.start()

    parts = ((down, down_sums, down_ref, down_far_ref, down_out), (gate, gate_sums, gate_ref, gate_far_ref, gate_out))
    for flow, total_ref, ref, far_ref, goal in parts:
        for k in range(2):
            place = flow.slot(k, 1, 0, across)
            add_rows((total_ref, place), [(ref, place), (far_ref, place)])
            flow.to_owner(k, total_ref.at[place], goal)
    run(scatter)
    run(scatter)
    run(scatter)

    def rows(at):
        rows_low[at, :] = (middle_ref[at, :] + total[at, :] + last[at, :].astype(F32)).astype(BF16)

    by_rows(rows_low.shape[0], rows)
    spread_flow(net, rows_low, layer_ref)
    down.after_y()
    gate.after_y()
    net.arrived(rest)

    @pl.when(net.far == 1)
    def _():
        def add(at):
            move = pl.ds(pl.multiple_of(at.start + 2 * count, 16), at.size)
            mine_ref[at, :] = dkv_ref[move, :].astype(F32) + rest_core[at, :].astype(F32)

        by_rows(count, add)
        for copy in far:
            copy.wait_send()

    @pl.when(net.far == 0)
    def _():
        for copy in far:
            copy.wait_recv()

        def add(at):
            mine_ref[at, :] = dkv_ref[at, :].astype(F32) + prompt_core[at, :].astype(F32) + prompt_far[at, :].astype(F32)

        by_rows(count, add)

    net.sent = [copy for copy in net.sent if all(copy is not other for other in far)]
    net.finish()


def to_owner(dkv, partial, middle, down, down_far, gate, gate_far, sizes):
    rows, width = middle.shape
    size, across = width // sizes["narrow"], gate_far.shape[1]
    count = dkv.shape[0] // 4
    block = lambda: pltpu.VMEM((count, dkv.shape[1]), BF16)
    return wire_call(
        owner_kernel, "owner", 5, [VMEM] * 7, [VMEM, ANY, ANY, ANY],
        [
            ((count, dkv.shape[1]), F32), ((sizes["narrow"] * rows, size), BF16), ((2 * across, size), BF16),
            ((size, 2 * across), BF16),
        ],
        [
            block(), block(), block(), block(), *scatter_buffers(rows, width), pltpu.VMEM((rows, width), BF16),
            pltpu.VMEM((across, size), BF16), pltpu.VMEM((size, across), BF16), *sems(40, 16),
        ],
        sizes, 80, dkv, partial, middle, down, down_far, gate, gate_far,
    )


SUMS = [CORE, Y, X, NEAR, FAR]


def end_kernel(
    partial_ref, x_ref, gain_ref, grad_ref, two_ref, query_ref, key_ref, up_ref, up_x_ref, qkv_core_ref, qkv_ref, out_ref,
    tokens_ref, gains_ref, qkv_out, out_out, up_out,
    first, second, sums, last, total, rows_low, vectors, up_sums, up_far, *rest, sizes,
):
    buffers, (send, recv, local) = rest[:-3], rest[-3:]
    net = Wires(send, recv, local, sizes)
    net.greet([Y, CORE, CORNER, NEAR, FAR, X])
    step = x_ref.shape[1] // sizes["narrow"] // 2
    qkv = Gradient(net, 0, step, qkv_ref.shape[1] // 2)
    out = Gradient(net, 1, step, out_ref.shape[0] // 2)
    qkv.start(qkv_ref, buffers[0], qkv_core_ref, True)
    out.start(out_ref, *buffers[3:5])
    scatter = scatter_flow(net, partial_ref, first, second, sums, last, total)
    run(scatter)
    up = Gradient(net, 0, step, up_ref.shape[1] // 2)
    qkv.core_to_x(buffers[1])
    out.core_to_x(buffers[5])

    def up_to_far(k):
        for start in (up.across, 0):
            place = up.slot(k, 1, start, up.across)
            add_rows((up_sums, place), [(up_ref, place), (up_x_ref, place)])
            if start:
                up.far.append(net.send(up_sums.at[place], up_far.at[up.slot(k, 1, 0, up.across)], FAR))

    run(scatter)
    qkv.x_end(0, buffers[2])
    up_to_far(0)
    run(scatter)
    qkv.x_end(1, buffers[2])
    up_to_far(1)
    run(scatter)
    width = x_ref.shape[1]
    size = query_ref.shape[1]
    block = width // sizes["narrow"]
    half = block // 2
    gains_ref[...] = jnp.zeros_like(gains_ref)

    def rows(at):
        grad = total[at, :] + last[at, :].astype(F32)
        term, change = row_back(grad, x_ref[at, :].astype(F32), gain_ref[...])
        gains_ref[:, :width] += term
        rows_low[at, :] = (grad_ref[at, :] + change).astype(BF16)

    by_rows(rows_low.shape[0], rows)
    for i, ref in enumerate((gains_ref, two_ref)):
        for slot in range(4):
            to = (2 * (slot % 2) + jnp.bitwise_xor(net.core, slot // 2)) * block + i * width
            for j in range(2):
                sub = net.x if j == 0 else 1 - net.x
                at = slot * block + j * half
                vectors[0, :, pl.ds(pl.multiple_of(to + sub * half, half), half)] = ref[:, at : at + half]
    vectors[0, :, 2 * width : 2 * width + size] = query_ref[...]
    vectors[0, :, 2 * width + size :] = key_ref[...]

    def add_gains():
        for i, to in enumerate(SUMS):
            copy = net.send(vectors.at[i], vectors.at[len(SUMS) + 1 + i], to)
            yield
            net.arrived(copy)
            vectors[i + 1] = vectors[i] + vectors[len(SUMS) + 1 + i]
        gains_ref[...] = vectors[len(SUMS)]
        yield

    def own(flow, k, ref):
        flow.far_end(k)
        flow.to_owner(k, flow.acc.at[flow.slot(k, 2, 0, flow.across)], ref)

    def own_up(k):
        net.arrived(up.far[k])
        place = up.slot(k, 1, 0, up.across)
        add_rows((up_sums, place), [(up_sums, place), (up_far, place)])
        up.to_owner(k, up_sums.at[place], up_out)

    gains = add_gains()
    run(gains)
    out.x_end(0, buffers[6])
    out.x_end(1, buffers[6])
    run(gains)
    spread_flow(net, rows_low, tokens_ref)
    own(qkv, 0, qkv_out)
    own_up(0)
    run(gains)
    own(qkv, 1, qkv_out)
    own_up(1)
    run(gains)
    own(out, 0, out_out)
    own(out, 1, out_out)
    up.after_y()
    qkv.after_y()
    out.after_y()
    run(gains)
    run(gains)
    net.finish()


def end(partial, x, gain, grad, two, query, key, up, up_x, qkv_core, qkv, out, sizes):
    rows, width = x.shape
    size = width // sizes["narrow"]
    wide, deep = qkv.shape[1], out.shape[0]
    length = 2 * width + 2 * query.shape[1]
    return wire_call(
        end_kernel, "end", 6, [VMEM] * 10 + [ANY] * 2, [ANY, VMEM, ANY, ANY, ANY],
        [((sizes["narrow"] * rows, size), BF16), ((1, length), F32), ((size, wide), BF16), ((deep, size), BF16),
         (up.shape, BF16)],
        [
            *scatter_buffers(rows, width), pltpu.VMEM((rows, width), BF16), pltpu.VMEM((2 * len(SUMS) + 1, 1, length), F32),
            pltpu.VMEM(up.shape, BF16), pltpu.VMEM((size, up.shape[1] // 2), BF16),
            *(v for i, v in enumerate(gradient_buffers(size, wide // 2, 0)) if i != 1), *gradient_buffers(size, deep // 2, 1),
            *sems(40, 16),
        ],
        sizes, 90, partial, x, gain[None], grad, two, query, key, up, up_x, qkv_core, qkv, out,
    )


def layout(lengths, index):
    order = jnp.arange(lengths.shape[0])
    ends = jnp.sum(jnp.where(order[None, :] <= order[:, None], lengths[None, :], 0), axis=1)[None, :]
    begins = ends - lengths[None, :]
    offset = index - PROMPT
    shift = jnp.sum(jnp.where((offset >= begins) & (offset < ends), begins, 0), axis=1, keepdims=True)
    return jnp.where(offset >= 0, PROMPT + shift, 0), index - shift


def make(sizes):
    n_dp, n_wide, n_narrow = sizes["dp"], sizes["wide"], sizes["narrow"]

    def over_y(values):
        return exchange(values, "narrow", 2, n_narrow)

    def over_z(values):
        return exchange(values, "wide", 1, n_wide)

    def over_x(values):
        return exchange(values, "dp", 1, n_dp)

    def over_core(values):
        return exchange(values, "narrow", 1, n_narrow)

    def over_far(values):
        return exchange(values, "wide", 2, n_wide)

    def over_groups(values, kind):
        distance = 2
        while distance < n_dp:
            values = values.astype(F32) + exchange(values.astype(kind), "dp", distance, n_dp).astype(F32)
            distance *= 2
        return values.astype(F32)

    def on_device(
        tokens, continuation_lengths, attention_gain, query_weight, key_weight, value_weight, head_gate, query_gain, key_gain,
        output_weight, feedforward_gain, gate_weight, up_weight, down_weight, cotangent,
    ):
        rows_wide, width_local = tokens.shape
        width = attention_gain.shape[0]
        size = query_gain.shape[0]
        heads = head_gate.shape[1]
        pairs = key_weight.shape[1] // size
        group_rows = rows_wide * n_wide
        rows_local = rows_wide // n_narrow
        x = lax.axis_index("dp") % 2
        z = lax.axis_index("wide")
        narrow = lax.axis_index("narrow")
        y, core = narrow // 2, narrow % 2
        z_near, z_far = z % 2, z // 2
        quarter = width_local // 2
        scale = size ** (-0.5)
        factor = scale * math.log2(math.e)
        log_two = math.log(2.0)

        def relative_vector(vector):
            values = jnp.transpose(vector.reshape(2, 2, 2, quarter), (1, 0, 2, 3))
            values = jnp.where(core == 0, values, values[::-1])
            return jnp.where(x == 0, values, values[:, :, ::-1]).reshape(width)

        def piece_of(weight, i, axis):
            half = weight.shape[1 - axis] // 2
            return cut(cut(weight, x * quarter, quarter, axis), i * half, half, 1 - axis)

        gain_one, gain_two = relative_vector(attention_gain), relative_vector(feedforward_gain)
        lane_pad = ((0, 0), (0, LANES - heads // 2))
        halves = lambda w, i: w[:, i * (w.shape[1] // 2) : (i + 1) * (w.shape[1] // 2)]
        gates = join([jnp.pad(halves(head_gate, i), lane_pad) for i in range(2)], 1)
        packed = (query_weight, key_weight, value_weight, gates)
        inputs, upstream, normed_all, joined_weight, out_weight = begin(tokens, cotangent, gain_one, packed, output_weight, sizes)

        def indices(row):
            part, at = row // rows_local, row % rows_local
            return ((z ^ (part // 2)) * n_narrow + (narrow ^ (2 * (part % 2)))) * rows_local + at

        my_index = indices(lax.broadcasted_iota(jnp.int32, (4 * rows_local, 1), 0))
        my_start, my_position = layout(continuation_lengths[0], my_index)
        frequency = THETA ** (-2.0 * jnp.arange(size // 2, dtype=F32) / size)
        angle = my_position.astype(F32) * frequency[None, :]
        cosine, sine = jnp.cos(angle), jnp.sin(angle)
        cosine = jnp.concatenate([cosine, cosine], axis=1)
        sine = jnp.concatenate([-sine, sine], axis=1)
        heads_index = indices(lax.broadcasted_iota(jnp.int32, (4, 1), 0) * rows_local)
        block = heads_index // rows_local
        first = layout(continuation_lengths[0], heads_index)[0] // rows_local
        prompt_blocks = PROMPT // rows_local
        in_prompt = block < prompt_blocks
        column = lax.broadcasted_iota(jnp.int32, (4, 5), 1)
        pick = lambda values: functools.reduce(lambda acc, item: jnp.where(column == item[0], item[1], acc), enumerate(values), 0)
        table = pick(
            [
                jnp.where(in_prompt, block // 2, prompt_blocks // 2),
                jnp.where(in_prompt, block // 2 * 2, first),
                block,
                2 * z_near + y,
                core,
            ]
        ).astype(jnp.int32)

        raw = dot_rows(normed_all, joined_weight)
        send = after((gate_weight, up_weight, down_weight), normed_all)
        axes = (0, 0, 1)
        from_far = [over_far(piece_of(w, y, axis)) for w, axis in zip(send, axes)]
        from_y = [over_y(piece_of(w, 1 - y, axis)) for w, axis in zip(after(send, raw), axes)]
        raw = after(raw, *from_far)
        q, kv = post(raw, cosine, sine, query_gain, key_gain, heads, pairs, size, factor)
        part = rows_local // 2
        early = after(upstream, raw)
        upstream_y, upstream_z = over_y(early[:part]), over_z(early[part:])
        kv_all = exchange_keys(after(kv, *from_y, *from_far, upstream_y, upstream_z), sizes)
        from_both = [over_far(after(v, kv_all)) for v in from_y]

        come_z = over_z(join([upstream[:part], after(upstream_y, kv_all)]))
        come_y = over_y(join([upstream[part:], after(upstream_z, kv_all)]))
        upstream_all = join(
            [upstream, upstream_y, come_y[:part], come_z[:part], upstream_z, come_z[part:], come_y[part:]]
        )

        gated, context, inverse_total = attend(
            table, q, kv_all, my_index, my_start, raw, pairs, size
        )
        partial = dot_rows(gated, out_weight).astype(BF16)
        middle, normed_two_all, gate_up, down = to_middle(
            partial, inputs, gain_two, gate_weight, up_weight, down_weight, from_y + from_far + from_both, sizes
        )
        both = dot_rows(normed_two_all, gate_up)
        hidden_cols = gate_weight.shape[1]
        gate_pre, up_pre = both[:, :hidden_cols], both[:, hidden_cols:]
        gate_sigmoid = jax.nn.sigmoid(gate_pre)
        silu = gate_pre * gate_sigmoid
        hidden = (silu * up_pre).astype(BF16)
        hidden_grad = dot_trans(upstream_all, down)
        gate_grad = hidden_grad * up_pre * gate_sigmoid * (1.0 + gate_pre * (1.0 - gate_sigmoid))
        up_grad = hidden_grad * silu
        gate_low, up_low = gate_grad.astype(BF16), up_grad.astype(BF16)
        gate_up_low = join([gate_low, up_low], 1)
        partial = dot_trans(gate_up_low, gate_up).astype(BF16)
        down_sums = dot_inner(hidden, upstream_all).astype(BF16)
        mlp_partial = dot_rows(hidden, down).astype(BF16)
        partial = after(partial, mlp_partial)
        middle_grad, middle_all, two_term, down_part, gate_part, up_keep, up_send = turn(
            partial, middle, upstream, gain_two, down_sums, normed_two_all, gate_low, up_low, sizes
        )
        down_far = over_far(down_part[hidden_cols // 2 :])
        gate_far = over_far(gate_part[:, hidden_cols // 2 :])
        up_come = over_x(up_send)
        gated_grad = dot_trans(middle_all, out_weight)
        dq, dkv, logit_grad = attend_back(
            table, q, kv_all, my_index, my_start, raw, context, inverse_total, gated_grad, pairs, size
        )
        out_sums = dot_inner(gated, middle_all).astype(BF16)
        dkv_mine, layer_output, down_gradient, gate_gradient = to_owner(
            after(dkv, up_come, out_sums), mlp_partial, middle, down_part, down_far, gate_part, gate_far, sizes
        )
        low, query_term, key_term = project_back(
            dq, dkv_mine, raw, cosine, sine, query_gain, key_gain, logit_grad, heads, pairs, size, scale, log_two
        )
        half = width // 2
        qkv_sums = dot_inner(normed_all, low).astype(BF16)
        qkv_core = over_core(qkv_sums[half:])
        partial = dot_trans(after(low, qkv_sums), joined_weight).astype(BF16)
        tokens_gradient, gains, qkv_gradient, output_gradient, up_gradient = end(
            partial, inputs, gain_one, middle_grad, two_term, query_term, key_term, up_keep, up_come,
            qkv_core, qkv_sums, out_sums, sizes
        )
        tokens_gradient = tokens_gradient.astype(F32)
        gains = over_groups(gains[0], F32)
        qkv_gradient = over_groups(qkv_gradient, BF16)
        down_gradient, gate_gradient, up_gradient, output_gradient = (
            over_groups(v, BF16) for v in (down_gradient, gate_gradient, up_gradient, output_gradient)
        )
        block = qkv_gradient.shape[1] // 2
        query_cols, key_cols = heads // 2 * size, pairs // 2 * size
        take = lambda at, count: join([qkv_gradient[:, at + i * block : at + i * block + count] for i in range(2)], 1)
        query_gradient = take(0, query_cols)
        key_gradient = take(query_cols, key_cols)
        value_gradient = take(query_cols + key_cols, key_cols)
        head_gate_gradient = take(query_cols + 2 * key_cols, heads // 2)
        return (
            layer_output,
            tokens_gradient,
            gains[:width],
            query_gradient,
            key_gradient,
            value_gradient,
            head_gate_gradient,
            gains[2 * width : 2 * width + size],
            gains[2 * width + size :],
            output_gradient,
            gains[width : 2 * width],
            gate_gradient,
            up_gradient,
            down_gradient,
        )

    return on_device


def solution(mesh):
    rows, up, down = P(("dp", "wide"), "narrow"), P("narrow", "wide"), P("wide", "narrow")
    return jax.shard_map(
        make(dict(mesh.shape)),
        mesh=mesh,
        in_specs=(rows, P("dp", None), P(), up, up, up, up, P(), P(), down, P(), up, up, down, rows),
        out_specs=(rows, rows, P(), up, up, up, up, P(), P(), down, P(), up, up, down),
        check_vma=False,
    )
```
